32 devices in a mesh: dp: 8 (over z, y), seq: 4 (over x, core).
Axes of the slice: x: 2, y: 2, z: 4, core: 2. Of those that a mesh axis runs over, the one named last changes fastest.
Arguments:
- hidden_in: bfloat16 [8, 2048, 768], P('dp', 'seq'), may hold values from -6 to 6
- prev_logits: float32 [8, 2048, 12], P('dp', 'seq'), may hold values from -6 to 6
- segments: int32 [8, 2048], P('dp'), may hold values from 0 to 15, never falling along the last dimension, each value on 1 to 1024 neighbouring positions
- routes: int32 [8, 2048, 2], P('dp', 'seq'), may hold values from 0 to 11, all different within a row; in each aligned block of 512 rows (0 to 511, 512 to 1023, ..., all dimensions but the last counted through in order) at most 128 rows name the same one
- attn_gain: bfloat16 [768], P('dp'), may hold values from 0.5 to 1.5
- w_qkv: bfloat16 [768, 2304], P('dp'), may hold values from -0.21875 to 0.21875
- w_out: bfloat16 [768, 768], P('dp'), may hold values from -1.75 to 1.75
- moe_gain: bfloat16 [768], P('dp'), may hold values from 0.5 to 1.5
- w_router: bfloat16 [768, 12], P('dp'), may hold values from -0.109375 to 0.109375
- w_carry: bfloat16 [12, 12], replicated, may hold values from -0.875 to 0.875
- const_vec: bfloat16 [2, 768], P(None, 'dp'), may hold values from -6 to 6
- const_mix: bfloat16 [2, 2, 768], P(None, None, 'dp'), may hold values from -0.21875 to 0.21875
- experts: bfloat16 [3, 16384, 768], P(None, 'dp'), may hold values from -0.21875 to 0.21875
- cotangent: bfloat16 [8, 2048, 768], P('dp', 'seq'), may hold values from -6 to 6
Outputs:
- block_out: bfloat16 [8, 2048, 768], P('dp', 'seq')
- d_input: float32 [8, 2048, 768], P('dp', 'seq')
- d_prev: float32 [8, 2048, 12], P('dp', 'seq')
- d_attn_gain: float32 [768], P('dp')
- d_w_qkv: float32 [768, 2304], P('dp')
- d_w_out: float32 [768, 768], P('dp')
- d_moe_gain: float32 [768], P('dp')
- d_w_router: float32 [768, 12], P('dp')
- d_w_carry: float32 [12, 12], replicated
- d_const_vec: float32 [2, 768], P(None, 'dp')
- d_const_mix: float32 [2, 2, 768], P(None, None, 'dp')
- d_experts: float32 [3, 16384, 768], P(None, 'dp')
The draws below stay inside these ranges and needn't reach their ends.
Inputs may be any that keep to these rules, and one draw needn't show every extreme that they name: `routes`: each token names two different experts: numbers below 8 are feed-forward experts, 8 the zero expert, 9 the copy expert, 10 and 11 the constant experts. Among the 512 tokens of one device no expert is named more than 128 times, and some expert of some device is named exactly 128 times. `segments`: within a sequence the numbers start at 0 and never fall; a document has 1 to 1024 tokens, and one has exactly that many.
All inputs are finite; a program needn't handle non-finite values.
Results may differ from the reference program's by a relative error of at most 0.013.
The reference program's roundings to bfloat16 on the way count: a program that leaves them out, or rounds other values in their place, can miss the bound.
Values may be sent and summed in bfloat16 or wider, within the bound.
A program may use at most 192 MiB of HBM per device.

```python
import math
import jax
import jax.numpy as jnp
import numpy as np
from jax import lax

D = 768
H = 12
HD = 64
FF = 2048
E = 8
EALL = 12
TOK_DEV = 512
CAP = 128
LENGTH = 2048
NSEQS = 8
DOCS = 16
OWNERS = 1
N_SEQ = 4


def steps_of(own_key, dims, shards, low, largest):
    loudness, own = 1.0, jax.random.fold_in(own_key, 6)
    for dim, shards_of in shards:
        heights = jnp.exp(jax.random.uniform(jax.random.fold_in(own, dim), (shards_of,), jnp.float32, low / len(shards), largest / len(shards)))
        loudness = loudness * jnp.repeat(heights, dims[dim] // shards_of).reshape([-1 if axis == dim else 1 for axis in range(len(dims))])
    return loudness


def split_up(count, total, most, slope):
    portions = [(1 << 20) // math.isqrt(rank ** slope) + 1 for rank in range(2, count + 1)]
    spare, given = total - most - (count - 1), [1] * (count - 1)
    while spare > 0:
        candidates = [i for i in range(count - 1) if given[i] < most]
        whole, remaining = sum([portions[i] for i in candidates]), spare
        for i in candidates:
            addition = min(most - given[i], max(1, remaining * portions[i] // whole), spare)
            given[i] = given[i] + addition
            spare = spare - addition
    return np.array([most] + given)


def ragged_sizes(own_key, amount, total, bound, skew):
    if amount == 2:
        one = jax.random.randint(own_key, (), max(1, total - bound), min(bound, total - 1) + 1)
        return jnp.stack([one, total - one])
    tallies = jnp.asarray(split_up(amount, total, bound, skew), jnp.int32)
    couples = (amount - 1) // 2
    giver, receiver = tallies[1:1 + 2 * couples:2], tallies[2:2 + 2 * couples:2]
    slack = jnp.minimum(giver - 1, bound - receiver)
    moved = jax.random.randint(jax.random.fold_in(own_key, 1), (couples,), 0, 1 << 20) % (slack + 1)
    tallies = tallies.at[1:1 + 2 * couples:2].set(giver - moved).at[2:2 + 2 * couples:2].set(receiver + moved)
    return tallies[jax.random.permutation(jax.random.fold_in(own_key, 2), amount)]


def routed_block(key, own, number, rows, amount, top, most, lean):
    ranking = jax.random.permutation(key, amount)
    packed, common = portions_of(amount, rows * top, most, lean, True), portions_of(amount, rows * top, most, lean, False)
    places = jnp.arange(amount)

    def named(lengths, turn):
        used = int((lengths > 0).sum())
        fixed = max(1, used // 4)
        shifted = fixed + (places - fixed + turn * (used - fixed)) % max(1, amount - fixed)
        return jnp.zeros((amount,), jnp.int32).at[ranking[jnp.where(places < fixed, places, shifted)]].set(jnp.asarray(lengths, jnp.int32))

    lengths = jnp.where(number % 4 == 0, named(packed, number // 4), named(common, number - number // 4 - 1))
    mixed = jax.random.permutation(jax.random.fold_in(own, 3), amount)
    donor, sink = mixed[0:amount // 2 * 2:2], mixed[1:amount // 2 * 2:2]
    slack = jnp.minimum(lengths[donor] - 1, most - lengths[sink]) // 2
    slack = jnp.where((donor == ranking[0]) | (sink == ranking[0]) | (lengths[sink] == 0), 0, jnp.maximum(slack, 0))
    shifted = jax.random.randint(jax.random.fold_in(own, 4), (amount // 2,), 0, 1 << 20) % (slack + 1)
    lengths = lengths.at[donor].add(-shifted).at[sink].add(shifted)
    items = jnp.searchsorted(jnp.cumsum(lengths), jnp.arange(rows * top), side="right").astype(jnp.int32)
    listing = items.reshape(top, rows).T
    listing = listing[jax.random.permutation(jax.random.fold_in(own, 1), rows)]
    turn = jax.random.randint(jax.random.fold_in(own, 2), (rows, 1), 0, top)
    return jnp.take_along_axis(listing, (jnp.arange(top)[None, :] + turn) % top, axis=1)


def portions_of(count, total, bound, slope, full):
    weights = [(1 << 20) // math.isqrt(rank ** slope) + 1 for rank in range(1, count + 1)]
    largest = bound if full else min(bound, max(-(-total // count), total * weights[0] // sum(weights)))
    least = 1 if total - largest >= count - 1 else 0
    counts, surplus = [largest] + [least] * (count - 1), total - largest - least * (count - 1)
    while surplus > 0:
        candidates = [i for i in range(1, count) if counts[i] < largest] or [i for i in range(1, count) if counts[i] < bound]
        mass, budget = sum([weights[i] for i in candidates]), surplus
        for i in candidates:
            addition = min(bound - counts[i], max(1, budget * weights[i] // mass), surplus)
            counts[i] = counts[i] + addition
            surplus = surplus - addition
    return np.array(counts)


def normal_values(key, extent, spread, limit, shards=(), held_as=jnp.bfloat16):
    factor_of = steps_of(key, extent, shards, -0.22, 0.18) if shards else 1.0
    entries = jax.random.normal(key, extent, jnp.float32) * spread * factor_of
    return jnp.minimum(jnp.maximum(entries, -limit), limit).astype(held_as)


def setup_inputs(seed: int = 0) -> dict:
    splits = jax.random.split(jax.random.key(seed), 15)
    hidden_in = normal_values(splits[0], (NSEQS, LENGTH, D), 1.0, 6.0, ((0, 8), (1, 4)))
    prev_logits = normal_values(splits[1], (NSEQS, LENGTH, EALL), 1.0, 6.0, ((0, 8), (1, 4)), jnp.float32)
    segments = jax.vmap(lambda own: jnp.searchsorted(jnp.cumsum(ragged_sizes(own, DOCS, LENGTH, LENGTH // 2, 2)), jnp.arange(LENGTH), side="right"))(jax.random.split(splits[2], NSEQS)).reshape((NSEQS, LENGTH)).astype(jnp.int32)
    routes_keys = jax.random.split(jax.random.fold_in(splits[3], 1), NSEQS * LENGTH // TOK_DEV)
    routes_turns = jax.random.permutation(jax.random.fold_in(splits[3], 3), NSEQS * LENGTH // TOK_DEV)
    routes = jax.vmap(lambda own, number: routed_block(jax.random.fold_in(splits[3], 2), own, number, TOK_DEV, EALL, 2, CAP, 1))(routes_keys, routes_turns).reshape((NSEQS, LENGTH, 2))
    attn_gain = jnp.clip(1.0 + 0.1 * jax.random.normal(splits[4], (D,), jnp.float32), 0.5, 1.5).astype(jnp.bfloat16)
    w_qkv = normal_values(splits[5], (D, 3 * D), D ** -0.5, 0.21875, ((0, 8),))
    w_out = normal_values(splits[6], (D, D), (D // 64) ** -0.5, 1.75, ((0, 8),))
    moe_gain = jnp.clip(1.0 + 0.1 * jax.random.normal(splits[7], (D,), jnp.float32), 0.5, 1.5).astype(jnp.bfloat16)
    w_router = normal_values(splits[8], (D, EALL), (4 * D) ** -0.5, 0.109375, ((0, 8),))
    w_carry = normal_values(splits[9], (EALL, EALL), (4 * EALL) ** -0.5, 0.875)
    const_vec = normal_values(splits[10], (2, D), 1.0, 6.0, ((1, 8),))
    const_mix = normal_values(splits[11], (2, 2, D), D ** -0.5, 0.21875, ((2, 8),))
    experts = normal_values(splits[12], (3, E * FF, D), D ** -0.5, 0.21875, ((1, 8),))
    cotangent = normal_values(splits[13], (NSEQS, LENGTH, D), 1.0, 6.0, ((0, 8), (1, 4)))
    return {"hidden_in": hidden_in, "prev_logits": prev_logits, "segments": segments, "routes": routes, "attn_gain": attn_gain, "w_qkv": w_qkv, "w_out": w_out, "moe_gain": moe_gain, "w_router": w_router, "w_carry": w_carry, "const_vec": const_vec, "const_mix": const_mix, "experts": experts, "cotangent": cotangent}


@jax.custom_vjp
def low(v):
    return lax.optimization_barrier(v.astype(jnp.bfloat16)).astype(jnp.float32)

@jax.custom_vjp
def low_back(v):
    return v

def low_keep(v):
    return (low(v), None)

def low_pass(kept, grad):
    return (grad,)

def back_keep(v):
    return (v, None)

def back_low(kept, grad):
    return (low(grad),)
low.defvjp(low_keep, low_pass)
low_back.defvjp(back_keep, back_low)
exact_prec = lax.Precision.HIGHEST
neg_large = -1e+30

def rms_scale(values, gain_vec):
    mean_square = lax.optimization_barrier(jnp.mean(values * values, axis=-1, keepdims=True))
    return values * lax.rsqrt(mean_square + 1e-06) * gain_vec

def rope_tables(positions):
    freq_index = jnp.arange(HD // 2, dtype=jnp.float32)
    inv_freq = jnp.exp(freq_index * (-2.0 * math.log(10000.0) / HD))
    angles = positions.astype(jnp.float32)[:, None] * inv_freq[None, :]
    return (jnp.cos(angles)[:, None, :], jnp.sin(angles)[:, None, :])

def rotate_half(values, cos_part, sin_part):
    half_size = values.shape[-1] // 2
    first_half = values[..., :half_size]
    second_half = values[..., half_size:]
    return jnp.concatenate([first_half * cos_part - second_half * sin_part, first_half * sin_part + second_half * cos_part], axis=-1)

def slot_layout(route_rows, slots_each):
    flat_routes = route_rows.reshape(-1)
    expert_hot = (flat_routes[:, None] == jnp.arange(E, dtype=jnp.int32)[None, :]).astype(jnp.int32)
    ranks = lax.optimization_barrier(jnp.sum((jnp.cumsum(expert_hot, axis=0) - expert_hot) * expert_hot, axis=1)).astype(jnp.int32)
    return jnp.where(flat_routes < E, flat_routes * slots_each + ranks, E * slots_each).astype(jnp.int32)

def combine(normed, logits, vec_f, mix_f, ffn_rows, route_rows):
    tok_count = normed.shape[0]
    chosen = jnp.take_along_axis(logits, route_rows, axis=1)
    gate_exp = jnp.exp(chosen - lax.optimization_barrier(jnp.max(chosen, axis=1, keepdims=True)))
    gates = gate_exp / lax.optimization_barrier(jnp.sum(gate_exp, axis=1, keepdims=True))
    const_logits = jnp.einsum('td,jcd->tjc', normed, mix_f, precision=exact_prec)
    const_exp = jnp.exp(const_logits - lax.optimization_barrier(jnp.max(const_logits, axis=2, keepdims=True)))
    alphas = const_exp / lax.optimization_barrier(jnp.sum(const_exp, axis=2, keepdims=True))
    const_out = alphas[:, :, 0:1] * normed[:, None, :] + alphas[:, :, 1:2] * vec_f[None, :, :]
    slot_rows = ffn_rows.reshape(tok_count, 2, normed.shape[1])
    route_cube = route_rows[:, :, None]
    slot_rows = slot_rows + jnp.where(route_cube == E + 1, normed[:, None, :], 0.0)
    slot_rows = slot_rows + jnp.where(route_cube == E + 2, const_out[:, 0:1, :], 0.0)
    slot_rows = slot_rows + jnp.where(route_cube == E + 3, const_out[:, 1:2, :], 0.0)
    return lax.optimization_barrier(jnp.sum(gates[:, :, None] * slot_rows, axis=1))

def expert_rows(normed_low, route_rows, experts_f):
    seq_len = normed_low.shape[0]
    per_expert = N_SEQ * CAP
    piece_size = FF // OWNERS
    slot_index = slot_layout(route_rows, per_expert)
    token_of = (jnp.arange(2 * seq_len, dtype=jnp.int32) // 2).astype(jnp.int32)
    buffer_rows = jnp.zeros((E * per_expert + 1, D), jnp.float32).at[slot_index].add(normed_low[token_of])
    grouped = buffer_rows[:E * per_expert].reshape(E, 1, per_expert, D)
    pieces_in = low_back(jnp.broadcast_to(grouped, (E, OWNERS, per_expert, D)))
    weights_split = experts_f.reshape(3, E, OWNERS, piece_size, D)
    gate_pre = low_back(jnp.einsum('eond,eofd->eonf', pieces_in, weights_split[0], precision=exact_prec))
    up_pre = low_back(jnp.einsum('eond,eofd->eonf', pieces_in, weights_split[1], precision=exact_prec))
    hidden = low(jax.nn.silu(gate_pre) * up_pre)
    partial_out = low(jnp.einsum('eonf,eofd->eond', hidden, weights_split[2], precision=exact_prec))
    expert_out = low_back(lax.optimization_barrier(jnp.sum(partial_out, axis=1))).reshape(E * per_expert, D)
    padded = jnp.concatenate([expert_out, jnp.zeros((1, D), jnp.float32)], axis=0)
    return padded[slot_index]

def layer(tokens_f, prev_f, seg_row, route_rows, params):
    attn_gain_f, w_qkv_f, w_out_f, moe_gain_f, w_router_f, w_carry_f, vec_f, mix_f, experts_f = params
    seq_len = tokens_f.shape[0]
    attn_in = low(rms_scale(tokens_f, attn_gain_f))
    qkv_pre = low_back(jnp.dot(attn_in, w_qkv_f, precision=exact_prec)).reshape(seq_len, 3, H, HD)
    positions = jnp.arange(seq_len, dtype=jnp.int32)
    cos_part, sin_part = rope_tables(positions)
    queries = low(low_back(rotate_half(qkv_pre[:, 0], cos_part, sin_part)))
    keys_all = low(low_back(rotate_half(qkv_pre[:, 1], cos_part, sin_part)))
    values_all = low(low_back(qkv_pre[:, 2]))
    block_rows = min(512, seq_len)
    count_blocks = seq_len // block_rows

    def attend_block(block_args):
        q_blk, pos_blk, seg_blk = block_args
        scores = low_back(jnp.einsum('qhd,khd->hqk', q_blk, keys_all, precision=exact_prec) * 0.125)
        allowed = (positions[None, :] <= pos_blk[:, None]) & (seg_row[None, :] == seg_blk[:, None])
        scores = jnp.where(allowed[None], scores, neg_large)
        top_score = lax.optimization_barrier(jnp.max(scores, axis=-1, keepdims=True))
        weights = jnp.exp(scores - top_score)
        probs = weights / lax.optimization_barrier(jnp.sum(weights, axis=-1, keepdims=True))
        return jnp.einsum('hqk,khd->qhd', low(probs), values_all, precision=exact_prec)
    attended = lax.map(jax.checkpoint(attend_block), (queries.reshape(count_blocks, block_rows, H, HD), positions.reshape(count_blocks, block_rows), seg_row.reshape(count_blocks, block_rows)))
    attn_heads = low(low_back(attended.reshape(seq_len, H * HD)))
    attn_out = low_back(jnp.dot(attn_heads, w_out_f, precision=exact_prec))
    resid_mid = tokens_f + attn_out
    normed = rms_scale(resid_mid, moe_gain_f)
    normed_low = low(normed)
    logits = jnp.dot(normed_low, w_router_f, precision=exact_prec) + jnp.dot(prev_f, w_carry_f, precision=exact_prec)
    ffn_rows = expert_rows(normed_low, route_rows, experts_f)
    return resid_mid + combine(normed, logits, vec_f, mix_f, ffn_rows, route_rows)

def reference(hidden_in, prev_logits, segments, routes, attn_gain, w_qkv, w_out, moe_gain, w_router, w_carry, const_vec, const_mix, experts, cotangent):
    params = tuple((weight_arr.astype(jnp.float32) for weight_arr in (attn_gain, w_qkv, w_out, moe_gain, w_router, w_carry, const_vec, const_mix, experts)))

    def one_sequence(grad_acc, seq_item):
        tokens_in, prev_in, seg_row, route_rows, cot_in = seq_item

        def forward_fn(tokens_f, prev_f, params_in):
            return layer(tokens_f, prev_f, seg_row, route_rows, params_in)
        result, pull_back = jax.vjp(forward_fn, tokens_in.astype(jnp.float32), prev_in, params)
        grad_tokens, grad_prev, grad_params = pull_back(cot_in.astype(jnp.float32))
        new_acc = tuple((acc_item + grad_item for acc_item, grad_item in zip(grad_acc, grad_params)))
        return (new_acc, (result.astype(jnp.bfloat16), grad_tokens, grad_prev))
    zero_acc = tuple((jnp.zeros(param_arr.shape, jnp.float32) for param_arr in params))
    grad_sums, (block_out, d_input, d_prev) = lax.scan(one_sequence, zero_acc, (hidden_in, prev_logits, segments, routes, cotangent))
    return (block_out, d_input, d_prev, grad_sums[0], grad_sums[1], grad_sums[2], grad_sums[3], grad_sums[4], grad_sums[5], grad_sums[6], grad_sums[7], grad_sums[8])
```

```python
import functools
import math

import jax
import jax.numpy as jnp
from jax import lax
from jax.experimental import pallas as pl
from jax.experimental.pallas import tpu as pltpu
from jax.sharding import PartitionSpec as P

D = 768
H = 12
HD = 64
E = 8
CAP = 128
BLK = 256

exact_prec = lax.Precision.HIGHEST
neg_large = -1e30
score_scale = 0.125 * math.log2(math.e)
f32 = jnp.float32
bf16 = jnp.bfloat16

NN = (((1,), (0,)), ((), ()))
NT = (((1,), (1,)), ((), ()))
TN = (((0,), (0,)), ((), ()))


def mm(a, b, dims):
    return lax.dot_general(a, b, dims, preferred_element_type=f32)


def swap(value, axis, bit):
    size = lax.axis_size(axis)
    return lax.ppermute(value, axis, [(i, i ^ bit) for i in range(size)])


def bits_high_first(size):
    bit = size // 2
    while bit >= 1:
        yield bit
        bit //= 2


def gather_relative(value, axis):
    held = {0: value}
    for bit in bits_high_first(lax.axis_size(axis)):
        for place in list(held):
            held[place ^ bit] = swap(held[place], axis, bit)
    return [held[place] for place in range(len(held))]


def sum_relative(blocks, axis):
    held = {place: block.astype(f32) for place, block in enumerate(blocks)}
    bit = 1
    while bit < lax.axis_size(axis):
        for place in [p for p in held if p & bit]:
            arrived = swap(held.pop(place).astype(bf16), axis, bit)
            held[place ^ bit] = held[place ^ bit] + arrived.astype(f32)
        bit *= 2
    return held[0]


def qkv_kernel(me_ref, h_ref, gain_ref, w_ref, cos_ref, sin_ref, attn_ref, out_ref, wt_ref):
    @pl.when((pl.program_id(0) == 0) & (pl.program_id(1) == 0))
    def _():
        wt_ref[...] = w_ref[...].T

    x = h_ref[0].astype(f32)
    mean_square = jnp.mean(x * x, axis=-1, keepdims=True)
    attn = (x * lax.rsqrt(mean_square + 1e-06) * gain_ref[...]).astype(bf16)
    attn_ref[...] = attn
    y = mm(wt_ref[...], attn, NT)
    cos, sin = cos_ref[...], sin_ref[...]
    rows = y.shape[0]
    half = HD // 2
    for head in range(2 * rows // (3 * HD)):
        a = y[head * HD : head * HD + half]
        b = y[head * HD + half : (head + 1) * HD]
        out_ref[head * HD : head * HD + half] = (a * cos - b * sin).astype(bf16)
        out_ref[head * HD + half : (head + 1) * HD] = (a * sin + b * cos).astype(bf16)
    out_ref[2 * rows // 3 :] = y[2 * rows // 3 :].astype(bf16)


def qkv_call(me, blocks, gain, w, cos_t, sin_t):
    parts, tok, _ = blocks.shape
    seq_len, width = parts * tok, w.shape[1]
    per = tok // BLK
    return pl.pallas_call(
        qkv_kernel,
        out_shape=(
            jax.ShapeDtypeStruct((seq_len, D), bf16),
            jax.ShapeDtypeStruct((width, seq_len), bf16),
        ),
        grid_spec=pltpu.PrefetchScalarGridSpec(
            num_scalar_prefetch=1,
            grid=(parts, per),
            in_specs=[
                pl.BlockSpec((1, BLK, D), lambda b, t, me_ref: (b ^ me_ref[0], t, 0)),
                pl.BlockSpec((1, D), lambda b, t, me_ref: (0, 0)),
                pl.BlockSpec((D, width), lambda b, t, me_ref: (0, 0)),
                pl.BlockSpec((HD // 2, BLK), lambda b, t, me_ref: (0, b * per + t)),
                pl.BlockSpec((HD // 2, BLK), lambda b, t, me_ref: (0, b * per + t)),
            ],
            out_specs=[
                pl.BlockSpec((BLK, D), lambda b, t, me_ref: (b * per + t, 0)),
                pl.BlockSpec((width, BLK), lambda b, t, me_ref: (0, b * per + t)),
            ],
            scratch_shapes=[pltpu.VMEM((width, D), bf16)],
        ),
        name="qkv",
    )(me, blocks, gain, w, cos_t, sin_t)


def allowed_block(key_block, query_block, start_row):
    key_pos = key_block * BLK + lax.broadcasted_iota(jnp.int32, (BLK, BLK), 0)
    query_pos = query_block * BLK + lax.broadcasted_iota(jnp.int32, (BLK, BLK), 1)
    return (key_pos >= start_row) & (key_pos <= query_pos)


def attn_kernel(lo_ref, qkv_ref, start_ref, out_ref, exact_ref, log_ref, keys_ref):
    heads, seq_len, _ = keys_ref.shape
    width = heads * HD
    qb = pl.program_id(0)

    @pl.when(qb == 0)
    def _():
        for h in range(heads):
            keys_ref[h] = qkv_ref[width + h * HD : width + (h + 1) * HD, :].T

    here = pl.ds(pl.multiple_of(qb * BLK, BLK), BLK)
    start_row = start_ref[...]

    def step(kb, carry):
        there = pl.ds(pl.multiple_of(kb * BLK, BLK), BLK)
        allowed = allowed_block(kb, qb, start_row)
        new = []
        for h in range(heads):
            top, total, acc = carry[h]
            scores = mm(keys_ref[h, there, :], qkv_ref[h * HD : (h + 1) * HD, here], NN)
            scores = jnp.where(allowed, scores * score_scale, neg_large)
            new_top = jnp.maximum(top, jnp.max(scores, axis=0, keepdims=True))
            fade = jnp.exp2(top - new_top)
            weights = jnp.exp2(scores - new_top)
            total = total * fade + jnp.sum(weights, axis=0, keepdims=True)
            values = qkv_ref[2 * width + h * HD : 2 * width + (h + 1) * HD, there]
            acc = acc * fade + mm(values, weights.astype(bf16), NN)
            new.append((new_top, total, acc))
        return tuple(new)

    first = tuple(
        (
            jnp.full((1, BLK), neg_large, f32),
            jnp.zeros((1, BLK), f32),
            jnp.zeros((HD, BLK), f32),
        )
        for _ in range(heads)
    )
    done = lax.fori_loop(lo_ref[qb], qb + 1, step, first)
    for h in range(heads):
        top, total, acc = done[h]
        attended = acc / total
        exact_ref[h * HD : (h + 1) * HD, :] = attended
        out_ref[0, h * HD : (h + 1) * HD, :] = attended.astype(bf16)
        log_ref[h : h + 1, :] = top + jnp.log2(total)


def attn_call(lows, qkv, start_row, tok):
    width3, seq_len = qkv.shape
    width = width3 // 3
    heads = width // HD
    per = tok // BLK
    return pl.pallas_call(
        attn_kernel,
        out_shape=(
            jax.ShapeDtypeStruct((seq_len // tok, width, tok), bf16),
            jax.ShapeDtypeStruct((width, seq_len), f32),
            jax.ShapeDtypeStruct((heads, seq_len), f32),
        ),
        grid_spec=pltpu.PrefetchScalarGridSpec(
            num_scalar_prefetch=1,
            grid=(seq_len // BLK,),
            in_specs=[
                pl.BlockSpec((width3, seq_len), lambda i, lo: (0, 0)),
                pl.BlockSpec((1, BLK), lambda i, lo: (0, i)),
            ],
            out_specs=[
                pl.BlockSpec((1, width, BLK), lambda i, lo: (i // per, 0, i % per)),
                pl.BlockSpec((width, BLK), lambda i, lo: (0, i)),
                pl.BlockSpec((heads, BLK), lambda i, lo: (0, i)),
            ],
            scratch_shapes=[pltpu.VMEM((heads, seq_len, HD), bf16)],
        ),
        name="attend",
    )(lows, qkv, start_row)


def attn_back_kernel(
    lo_ref, qkv_ref, go_ref, exact_ref, log_ref, start_ref, cos_ref, sin_ref, out_ref,
    keys_ref, values_ref, dk_ref, dv_ref,
):
    heads, seq_len, _ = keys_ref.shape
    width = heads * HD
    half = HD // 2
    qb = pl.program_id(0)

    @pl.when(qb == 0)
    def _():
        for h in range(heads):
            keys_ref[h] = qkv_ref[width + h * HD : width + (h + 1) * HD, :].T
            values_ref[h] = qkv_ref[2 * width + h * HD : 2 * width + (h + 1) * HD, :].T
        dk_ref[...] = jnp.zeros_like(dk_ref)
        dv_ref[...] = jnp.zeros_like(dv_ref)

    here = pl.ds(pl.multiple_of(qb * BLK, BLK), BLK)
    start_row = start_ref[...]
    grad = go_ref[0]
    deltas = [
        jnp.sum(
            exact_ref[h * HD : (h + 1) * HD, :] * grad[h * HD : (h + 1) * HD].astype(f32),
            axis=0,
            keepdims=True,
        )
        for h in range(heads)
    ]

    def step(kb, carry):
        there = pl.ds(pl.multiple_of(kb * BLK, BLK), BLK)
        allowed = allowed_block(kb, qb, start_row)
        new = []
        for h in range(heads):
            rows = slice(h * HD, (h + 1) * HD)
            queries = qkv_ref[rows, here]
            scores = mm(keys_ref[h, there, :], queries, NN)
            scores = jnp.where(allowed, scores * score_scale, neg_large)
            probs = jnp.exp2(scores - log_ref[h : h + 1, :])
            grad_probs = mm(values_ref[h, there, :], grad[rows], NN)
            grad_scores = (probs * (grad_probs - deltas[h])).astype(bf16)
            dv_ref[rows, there] += mm(grad[rows], probs.astype(bf16), NT)
            dk_ref[rows, there] += mm(queries, grad_scores, NT)
            keys = qkv_ref[width + h * HD : width + (h + 1) * HD, there]
            new.append(carry[h] + mm(keys, grad_scores, NN))
        return tuple(new)

    grads = lax.fori_loop(
        lo_ref[qb], qb + 1, step, tuple(jnp.zeros((HD, BLK), f32) for _ in range(heads))
    )

    def turn_back(value, cos, sin):
        value = value.astype(bf16).astype(f32)
        a, b = value[:half], value[half:]
        return (a * cos + b * sin).astype(bf16), (b * cos - a * sin).astype(bf16)

    for h in range(heads):
        a, b = turn_back(grads[h] * 0.125, cos_ref[:, here], sin_ref[:, here])
        out_ref[h * HD : h * HD + half, here] = a
        out_ref[h * HD + half : (h + 1) * HD, here] = b

    @pl.when(qb == pl.num_programs(0) - 1)
    def _():
        cos, sin = cos_ref[...], sin_ref[...]
        for h in range(heads):
            a, b = turn_back(dk_ref[h * HD : (h + 1) * HD, :] * 0.125, cos, sin)
            out_ref[width + h * HD : width + h * HD + half, :] = a
            out_ref[width + h * HD + half : width + (h + 1) * HD, :] = b
        out_ref[2 * width :, :] = dv_ref[...].astype(bf16)


def attn_back_call(lows, qkv, grad_out, exact, logs, start_row, cos_t, sin_t):
    width3, seq_len = qkv.shape
    width = width3 // 3
    heads = width // HD
    per = grad_out.shape[2] // BLK
    return pl.pallas_call(
        attn_back_kernel,
        out_shape=jax.ShapeDtypeStruct((width3, seq_len), bf16),
        grid_spec=pltpu.PrefetchScalarGridSpec(
            num_scalar_prefetch=1,
            grid=(seq_len // BLK,),
            in_specs=[
                pl.BlockSpec((width3, seq_len), lambda i, lo: (0, 0)),
                pl.BlockSpec((1, width, BLK), lambda i, lo: (i // per, 0, i % per)),
                pl.BlockSpec((width, BLK), lambda i, lo: (0, i)),
                pl.BlockSpec((heads, BLK), lambda i, lo: (0, i)),
                pl.BlockSpec((1, BLK), lambda i, lo: (0, i)),
                pl.BlockSpec((HD // 2, seq_len), lambda i, lo: (0, 0)),
                pl.BlockSpec((HD // 2, seq_len), lambda i, lo: (0, 0)),
            ],
            out_specs=pl.BlockSpec((width3, seq_len), lambda i, lo: (0, 0)),
            scratch_shapes=[
                pltpu.VMEM((heads, seq_len, HD), bf16),
                pltpu.VMEM((heads, seq_len, HD), bf16),
                pltpu.VMEM((width, seq_len), f32),
                pltpu.VMEM((width, seq_len), f32),
            ],
        ),
        name="attend_back",
    )(lows, qkv, grad_out, exact, logs, start_row, cos_t, sin_t)


def expert_kernel(
    x_ref, g_ref, gate_ref, w_ref, out_ref, piece_ref, dot_ref, dw_ref, gs_ref, oacc_ref, pacc_ref
):
    i = pl.program_id(0)

    @pl.when(i == 0)
    def _():
        gs_ref[...] = (g_ref[...].astype(f32) * gate_ref[...]).astype(bf16)
        oacc_ref[...] = jnp.zeros_like(oacc_ref)
        pacc_ref[...] = jnp.zeros_like(pacc_ref)

    x, gs = x_ref[...], gs_ref[...]
    gate_pre = mm(x, w_ref[0], NT)
    up_pre = mm(x, w_ref[1], NT)
    sig = 1.0 / (1.0 + jnp.exp(-gate_pre))
    silu = gate_pre * sig
    hidden = (silu * up_pre).astype(bf16)
    oacc_ref[...] += mm(hidden, w_ref[2], NN)
    dw_ref[2] = mm(hidden, gs, TN).astype(dw_ref.dtype)
    grad_hidden = mm(gs, w_ref[2], NT)
    grad_gate = (grad_hidden * up_pre * sig * (1.0 + gate_pre * (1.0 - sig))).astype(bf16)
    grad_up = (grad_hidden * silu).astype(bf16)
    pacc_ref[...] += mm(grad_gate, w_ref[0], NN) + mm(grad_up, w_ref[1], NN)
    dw_ref[0] = mm(grad_gate, x, TN).astype(dw_ref.dtype)
    dw_ref[1] = mm(grad_up, x, TN).astype(dw_ref.dtype)

    @pl.when(i == pl.num_programs(0) - 1)
    def _():
        out = oacc_ref[...].astype(bf16)
        out_ref[...] = out
        piece_ref[...] = pacc_ref[...].astype(bf16)
        dot_ref[...] = jnp.sum(out.astype(f32) * g_ref[...].astype(f32), axis=-1, keepdims=True)


def expert_plain(x, g, gate, weights):
    gs = (g.astype(f32) * gate).astype(bf16)
    gate_pre = mm(x, weights[0], NT)
    up_pre = mm(x, weights[1], NT)
    sig = 1.0 / (1.0 + jnp.exp(-gate_pre))
    silu = gate_pre * sig
    hidden = (silu * up_pre).astype(bf16)
    out = mm(hidden, weights[2], NN).astype(bf16)
    grad_hidden = mm(gs, weights[2], NT)
    grad_gate = (grad_hidden * up_pre * sig * (1.0 + gate_pre * (1.0 - sig))).astype(bf16)
    grad_up = (grad_hidden * silu).astype(bf16)
    piece = (mm(grad_gate, weights[0], NN) + mm(grad_up, weights[1], NN)).astype(bf16)
    dw = jnp.stack([mm(grad_gate, x, TN), mm(grad_up, x, TN), mm(hidden, gs, TN)]).astype(bf16)
    dots = jnp.sum(out.astype(f32) * g.astype(f32), axis=-1, keepdims=True)
    return out, piece, dots, dw


def expert_call(x, g, gate, weights):
    rows, units = x.shape[0], weights.shape[1]
    if rows > 1024:
        return expert_plain(x, g, gate, weights)
    tile = min(256, units)
    whole = pl.BlockSpec((rows, D), lambda i: (0, 0))
    column = pl.BlockSpec((rows, 1), lambda i: (0, 0))
    return pl.pallas_call(
        expert_kernel,
        out_shape=(
            jax.ShapeDtypeStruct((rows, D), bf16),
            jax.ShapeDtypeStruct((rows, D), bf16),
            jax.ShapeDtypeStruct((rows, 1), f32),
            jax.ShapeDtypeStruct(weights.shape, bf16),
        ),
        grid=(units // tile,),
        in_specs=[whole, whole, column, pl.BlockSpec((3, tile, D), lambda i: (0, i, 0))],
        out_specs=[whole, whole, column, pl.BlockSpec((3, tile, D), lambda i: (0, i, 0))],
        scratch_shapes=[
            pltpu.VMEM((rows, D), bf16),
            pltpu.VMEM((rows, D), f32),
            pltpu.VMEM((rows, D), f32),
        ],
        name="experts",
    )(x, g, gate, weights)


def rope_tables(seq_len):
    freq_index = jnp.arange(HD // 2, dtype=f32)
    inv_freq = jnp.exp(freq_index * (-2.0 * math.log(10000.0) / HD))
    angles = jnp.arange(seq_len, dtype=jnp.int32).astype(f32)[None, :] * inv_freq[:, None]
    return jnp.cos(angles), jnp.sin(angles)


def norm_back(values, gain, grad):
    rate = lax.rsqrt(jnp.mean(values * values, axis=-1, keepdims=True) + 1e-06)
    scaled = gain * grad
    inner = jnp.mean(values * scaled, axis=-1, keepdims=True)
    return rate * scaled - values * (rate * rate * rate) * inner, rate


def per_device(
    hidden_in,
    prev_logits,
    segments,
    routes,
    attn_gain,
    w_qkv,
    w_out,
    moe_gain,
    w_router,
    w_carry,
    const_vec,
    const_mix,
    experts,
    cotangent,
):
    n_seq, n_dp = lax.axis_size("seq"), lax.axis_size("dp")
    owners = n_dp // E
    me = lax.axis_index("seq")
    me_arr = me.astype(jnp.int32).reshape(1)
    tok = hidden_in.shape[1]
    seq_len = tok * n_seq
    shard = w_qkv.shape[0]
    heads_here = H // n_seq
    width = heads_here * HD
    hidden = hidden_in[0]
    tokens_f = hidden.astype(f32)
    grad_low = cotangent[0]
    grad_top = grad_low.astype(f32)
    prev_rows = prev_logits[0]
    route_rows = routes[0]
    carry_f = w_carry.astype(f32)

    blocks = jnp.stack(gather_relative(hidden, "seq"))
    w_mine = lax.dynamic_slice_in_dim(
        w_qkv.reshape(shard, 3, n_seq, width), me, 1, axis=2
    ).reshape(shard, 3 * width)
    small = jnp.concatenate(
        [
            attn_gain[:, None],
            moe_gain[:, None],
            const_vec.T,
            const_mix.reshape(4, shard).T,
            w_router,
        ],
        axis=1,
    )
    first = lax.all_gather(jnp.concatenate([w_mine, small], axis=1), "dp", axis=0, tiled=True)
    w_slice = first[:, : 3 * width]
    small_t = first[:, 3 * width :].astype(f32).T
    gain_one, gain_two = small_t[0:1], small_t[1:2]
    vec_f, mix_f, router_t = small_t[2:4], small_t[4:8], small_t[8:20]
    dp_me = lax.axis_index("dp")
    out_parts = [w_out] + [
        lax.ppermute(w_out, "dp", [(i, (i + k) % n_dp) for i in range(n_dp)])
        for k in range(1, n_dp)
    ]
    out_weight = jnp.zeros((n_dp, shard, D), bf16)
    for k, part in enumerate(out_parts):
        out_weight = lax.dynamic_update_index_in_dim(
            out_weight, part, lax.rem(dp_me + n_dp - k, n_dp), 0
        )
    out_weight = out_weight.reshape(D, D)

    named = [
        (route_rows[:, k : k + 1] == jnp.arange(E, dtype=jnp.int32)[None, :]) for k in range(2)
    ]
    earlier = (
        jnp.arange(tok, dtype=jnp.int32)[None, :] < jnp.arange(tok, dtype=jnp.int32)[:, None]
    ).astype(bf16)
    ranks = mm(earlier, (named[0] | named[1]).astype(bf16), NN)
    slot_of = [
        jnp.where(
            route_rows[:, k] < E,
            route_rows[:, k] * CAP
            + jnp.sum(jnp.where(named[k], ranks, 0.0), axis=1).astype(jnp.int32),
            E * CAP,
        )
        for k in range(2)
    ]
    slots = jnp.arange(E * CAP, dtype=jnp.int32)[None, :]
    picks = [slot_of[k][:, None] == slots for k in range(2)]
    pick_low = [p.astype(bf16) for p in picks]
    pick_any = (picks[0] | picks[1]).astype(bf16)

    def dispatch(rows):
        grouped = mm(pick_any, rows, TN).astype(bf16).reshape(E, CAP, D)
        return lax.all_to_all(
            jnp.repeat(grouped, owners, axis=0), "dp", split_axis=0, concat_axis=0, tiled=True
        )

    def back_to_source(values):
        return lax.all_to_all(values, "dp", split_axis=0, concat_axis=0, tiled=True)

    arrived_grad = dispatch(grad_low)

    cos_t, sin_t = rope_tables(seq_len)
    seg_row = segments[0]
    doc_ids = jnp.arange(16, dtype=jnp.int32)
    doc_start = jnp.sum((seg_row[None, :] < doc_ids[:, None]).astype(jnp.int32), axis=1)
    start = jnp.sum(jnp.where(seg_row[None, :] == doc_ids[:, None], doc_start[:, None], 0), axis=0)
    start_row = start.astype(jnp.int32)[None, :]
    lows = start[::BLK].astype(jnp.int32) // BLK
    attn_in, qkv = qkv_call(me_arr, blocks, gain_one, w_slice, cos_t, sin_t)
    attended, attended_exact, logs = attn_call(lows, qkv, start_row, tok)
    heads_t = lax.all_to_all(attended, "seq", split_axis=0, concat_axis=0, tiled=True).reshape(
        D, tok
    )

    resid_mid = tokens_f + mm(heads_t, out_weight, TN)
    rate_two = lax.rsqrt(jnp.mean(resid_mid * resid_mid, axis=-1, keepdims=True) + 1e-06)
    normed = resid_mid * rate_two * gain_two
    normed_low = normed.astype(bf16)
    logits = mm(normed_low, router_t.astype(bf16), NT) + jnp.dot(
        prev_rows, carry_f, precision=exact_prec
    )
    all_ids = jnp.arange(H, dtype=jnp.int32)[None, :]
    hot = [route_rows[:, k : k + 1] == all_ids for k in range(2)]
    chosen = [jnp.sum(jnp.where(hot[k], logits, 0.0), axis=1, keepdims=True) for k in range(2)]
    top_logit = jnp.maximum(chosen[0], chosen[1])
    gate_exp = [jnp.exp(c - top_logit) for c in chosen]
    gate_sum = gate_exp[0] + gate_exp[1]
    gates = [g / gate_sum for g in gate_exp]

    arrived = dispatch(normed_low)
    gate_slots = jnp.sum(
        jnp.where(picks[0], gates[0], 0.0) + jnp.where(picks[1], gates[1], 0.0), axis=0
    ).reshape(E, 1, CAP)
    arrived_gate = lax.all_to_all(
        jnp.repeat(gate_slots, owners, axis=0), "dp", split_axis=0, concat_axis=0, tiled=True
    )
    rows = n_dp * CAP
    partial, piece, dots, dw = expert_call(
        arrived.reshape(rows, D),
        arrived_grad.reshape(rows, D),
        arrived_gate.reshape(rows, 1),
        experts,
    )
    back_piece = back_to_source(piece.reshape(n_dp, CAP, D))
    back_dots = back_to_source(dots.reshape(n_dp, 1, CAP))
    partial, back_piece = lax.optimization_barrier((partial, back_piece))
    back_out = back_to_source(partial.reshape(n_dp, CAP, D))

    def owner_rows(values, owner):
        return values.reshape(E, owners, CAP, -1)[:, owner].reshape(E * CAP, -1)

    half = dw.shape[1] // 2
    core = me & 1
    kept = lax.dynamic_slice_in_dim(dw, core * half, half, 1)
    given = lax.dynamic_slice_in_dim(dw, (1 - core) * half, half, 1)
    summed = (kept.astype(f32) + swap(given, "seq", 1).astype(f32)).astype(bf16)
    bit = 2
    total = summed.astype(f32)
    while bit < n_seq:
        low = total.astype(bf16)
        total = low.astype(f32) + swap(low, "seq", bit).astype(f32)
        bit *= 2
    mine = total.astype(bf16)
    other = swap(mine, "seq", 1)
    d_experts = jnp.concatenate(
        [jnp.where(core == 0, mine, other), jnp.where(core == 0, other, mine)], axis=1
    ).astype(f32)

    const_logits = lax.dot_general(normed, mix_f, NT, precision=exact_prec)
    grad_normed_dot = jnp.sum(grad_top * normed, axis=1, keepdims=True)
    grad_vec_dot = lax.dot_general(grad_top, vec_f, NT, precision=exact_prec)
    alphas = []
    for j in range(2):
        pair = const_logits[:, 2 * j : 2 * j + 2]
        pair_exp = jnp.exp(pair - jnp.max(pair, axis=1, keepdims=True))
        alphas.append(pair_exp / jnp.sum(pair_exp, axis=1, keepdims=True))
    const_dot = [
        alphas[j][:, 0:1] * grad_normed_dot + alphas[j][:, 1:2] * grad_vec_dot[:, j : j + 1]
        for j in range(2)
    ]
    slot_dots = jnp.sum(back_dots.reshape(E, owners, CAP), axis=1).reshape(1, E * CAP)
    out_dots = []
    for k in range(2):
        route = route_rows[:, k : k + 1]
        value = jnp.sum(jnp.where(picks[k], slot_dots, 0.0), axis=1, keepdims=True)
        value = value + jnp.where(route == E + 1, grad_normed_dot, 0.0)
        for j in range(2):
            value = value + jnp.where(route == E + 2 + j, const_dot[j], 0.0)
        out_dots.append(value)
    mean_dot = gates[0] * out_dots[0] + gates[1] * out_dots[1]
    grad_logits = sum(
        jnp.where(hot[k], gates[k] * (out_dots[k] - mean_dot), 0.0) for k in range(2)
    )

    def gate_of(expert):
        return sum(
            jnp.where(route_rows[:, k : k + 1] == expert, gates[k], 0.0) for k in range(2)
        )

    copy_gate = gate_of(E + 1)
    const_gate = [gate_of(E + 2 + j) for j in range(2)]
    mix_grads = []
    for j in range(2):
        terms = [grad_normed_dot, grad_vec_dot[:, j : j + 1]]
        for c in range(2):
            mix_grads.append(
                const_gate[j] * alphas[j][:, c : c + 1] * (terms[c] - const_dot[j])
            )
    mix_grads = jnp.concatenate(mix_grads, axis=1)
    normed_gate = copy_gate + sum(const_gate[j] * alphas[j][:, 0:1] for j in range(2))
    vec_gate = jnp.concatenate([const_gate[j] * alphas[j][:, 1:2] for j in range(2)], axis=1)

    mixed = normed * normed_gate + jnp.dot(vec_gate, vec_f, precision=exact_prec)
    for k in range(2):
        picked = sum(mm(pick_low[k], owner_rows(back_out, o), NN) for o in range(owners))
        mixed = mixed + gates[k] * picked
    block_out = (resid_mid + mixed).astype(bf16)

    grad_normed = grad_top * normed_gate
    grad_normed = grad_normed + jnp.dot(
        jnp.concatenate([grad_logits, mix_grads], axis=1),
        jnp.concatenate([router_t, mix_f], axis=0),
        precision=exact_prec,
    )
    for o in range(owners):
        grad_normed = grad_normed + mm(pick_any, owner_rows(back_piece, o), NN)
    grad_mid, _ = norm_back(resid_mid, gain_two, grad_normed)
    grad_resid = grad_top + grad_mid
    grad_attn = grad_resid.astype(bf16)
    grad_heads = mm(out_weight, grad_attn, NT).astype(bf16)
    grad_out = lax.all_to_all(
        grad_heads.reshape(n_seq, width, tok), "seq", split_axis=0, concat_axis=0, tiled=True
    )

    d_prev = jnp.dot(grad_logits, carry_f.T, precision=exact_prec)
    grad_router = jnp.dot(grad_logits.T, normed_low.astype(f32), precision=exact_prec)
    grad_carry = jnp.dot(prev_rows.T, grad_logits, precision=exact_prec)
    grad_gain_two = jnp.sum(grad_normed * resid_mid * rate_two, axis=0, keepdims=True)
    grad_vec = jnp.dot(vec_gate.T, grad_top, precision=exact_prec)
    grad_mix = jnp.dot(mix_grads.T, normed, precision=exact_prec)
    packed = jnp.concatenate([grad_router, grad_gain_two, grad_vec, grad_mix], axis=0)
    lines = packed.shape[0]
    packed = packed.reshape(lines, n_dp, shard).swapaxes(0, 1).reshape(n_dp, lines * shard)
    packed = jnp.concatenate(
        [packed, jnp.broadcast_to(grad_carry.reshape(1, H * H), (n_dp, H * H))], axis=1
    )
    packed = lax.all_to_all(packed, "dp", split_axis=0, concat_axis=0, tiled=True)
    packed = jnp.sum(packed, axis=0, keepdims=True)
    for bit in bits_high_first(n_seq):
        packed = packed + swap(packed, "seq", bit)
    lined = packed[0, : lines * shard].reshape(lines, shard)
    d_router, d_moe_gain = lined[:H].T, lined[H]
    d_vec, d_mix = lined[H + 1 : H + 3], lined[H + 3 : H + 7].reshape(2, 2, shard)
    d_carry = packed[0, lines * shard :].reshape(H, H)

    grad_out_w = mm(heads_t, grad_attn, NN)
    blocks_out = grad_out_w.reshape(D, n_seq, width).swapaxes(0, 1)
    blocks_out = blocks_out[jnp.arange(n_seq) ^ me]
    mine_out = sum_relative([blocks_out[r] for r in range(n_seq)], "seq").astype(bf16)

    def reduce_rows(value):
        value = value.reshape(n_dp, -1, value.shape[-1])
        value = lax.all_to_all(value, "dp", split_axis=0, concat_axis=0, tiled=True)
        return jnp.sum(value.astype(f32), axis=0)

    def collect_columns(value):
        parts = jnp.stack(gather_relative(value, "seq"))
        return parts[jnp.arange(n_seq) ^ me]

    d_out = collect_columns(reduce_rows(mine_out)).swapaxes(0, 1).reshape(shard, D)

    grad_qkv = attn_back_call(
        lows, qkv, grad_out, attended_exact, logs, start_row, cos_t, sin_t
    )
    grad_w = lax.dot_general(
        attn_in, grad_qkv, (((0,), (1,)), ((), ())), preferred_element_type=f32
    )
    rows_w = collect_columns(reduce_rows(grad_w.astype(bf16)))
    d_qkv = (
        rows_w.reshape(n_seq, shard, 3, width).transpose(1, 2, 0, 3).reshape(shard, 3 * D)
    )
    d_attn_gain = jnp.sum(d_qkv * w_qkv.astype(f32), axis=1) / attn_gain.astype(f32)

    grad_in = lax.dot_general(
        grad_qkv, w_slice, (((0,), (1,)), ((), ())), preferred_element_type=f32
    ).astype(bf16)
    grad_in = grad_in.reshape(n_seq, tok, D)[jnp.arange(n_seq) ^ me]
    grad_attn_in = sum_relative([grad_in[r] for r in range(n_seq)], "seq")
    grad_first, _ = norm_back(tokens_f, gain_one, grad_attn_in)
    d_input = grad_resid + grad_first
    return (
        block_out[None],
        d_input[None],
        d_prev[None],
        d_attn_gain,
        d_qkv,
        d_out,
        d_moe_gain,
        d_router,
        d_carry,
        d_vec,
        d_mix,
        d_experts,
    )


def solution(mesh):
    return jax.shard_map(
        per_device,
        mesh=mesh,
        in_specs=(
            P("dp", "seq", None),
            P("dp", "seq", None),
            P("dp", None),
            P("dp", "seq", None),
            P("dp"),
            P("dp", None),
            P("dp", None),
            P("dp"),
            P("dp", None),
            P(),
            P(None, "dp"),
            P(None, None, "dp"),
            P(None, "dp", None),
            P("dp", "seq", None),
        ),
        out_specs=(
            P("dp", "seq", None),
            P("dp", "seq", None),
            P("dp", "seq", None),
            P("dp"),
            P("dp", None),
            P("dp", None),
            P("dp"),
            P("dp", None),
            P(),
            P(None, "dp"),
            P(None, None, "dp"),
            P(None, "dp", None),
        ),
        check_vma=False,
    )
```

```python
import functools
import math

import jax
import jax.numpy as jnp
from jax import lax
from jax.experimental import pallas as pl
from jax.experimental.pallas import tpu as pltpu
from jax.sharding import PartitionSpec as P

D = 768
H = 12
HD = 64
E = 8
CAP = 128
BLK = 256

exact_prec = lax.Precision.HIGHEST
neg_large = -1e30
score_scale = 0.125 * math.log2(math.e)
f32 = jnp.float32
bf16 = jnp.bfloat16

NN = (((1,), (0,)), ((), ()))
NT = (((1,), (1,)), ((), ()))
TN = (((0,), (0,)), ((), ()))


def mm(a, b, dims):
    return lax.dot_general(a, b, dims, preferred_element_type=f32)


def swap(value, axis, bit):
    size = lax.axis_size(axis)
    return lax.ppermute(value, axis, [(i, i ^ bit) for i in range(size)])


def bits_high_first(size):
    bit = size // 2
    while bit >= 1:
        yield bit
        bit //= 2


def gather_relative(value, axis):
    held = {0: value}
    for bit in bits_high_first(lax.axis_size(axis)):
        for place in list(held):
            held[place ^ bit] = swap(held[place], axis, bit)
    return [held[place] for place in range(len(held))]


def sum_relative(blocks, axis):
    held = {place: block.astype(f32) for place, block in enumerate(blocks)}
    bit = 1
    while bit < lax.axis_size(axis):
        for place in [p for p in held if p & bit]:
            arrived = swap(held.pop(place).astype(bf16), axis, bit)
            held[place ^ bit] = held[place ^ bit] + arrived.astype(f32)
        bit *= 2
    return held[0]


MESH = pl.DeviceIdType.MESH
SMALL = 32


def greet(peers):
    barrier = pltpu.get_barrier_semaphore()
    for peer in peers:
        pl.semaphore_signal(barrier, inc=1, device_id=peer, device_id_type=MESH)
    pl.semaphore_wait(barrier, len(peers))


def start_kernel(
    n_seq, n_dp, h_ref, w_ref, again_ref, mgain_ref, vec_ref, mix_ref, router_ref,
    all_ref, slice_ref, small_ref,
    small_buf, h_send, h_recv, w_send, w_recv, s_send, s_recv,
):
    me, dp = lax.axis_index("seq"), lax.axis_index("dp")
    shard, width3 = slice_ref.shape[1], slice_ref.shape[2]
    width = width3 // 3
    seq_bits = list(bits_high_first(n_seq))
    greet(
        [{"seq": me ^ bit} for bit in seq_bits]
        + [{"dp": lax.rem(dp + k, n_dp)} for k in range(1, n_dp)]
    )

    def put(place, bit, index):
        return pltpu.make_async_remote_copy(
            src_ref=h_ref if place == 0 else all_ref.at[me ^ place],
            dst_ref=all_ref.at[me ^ place],
            send_sem=h_send.at[index],
            recv_sem=h_recv.at[index],
            device_id={"seq": me ^ bit},
            device_id_type=MESH,
        )

    plan, arrival = [], {}
    order = [(0, bit) for bit in seq_bits]
    while order:
        place, bit = order.pop(0)
        copy = put(place, bit, len(plan))
        arrival[place ^ bit] = copy
        plan.append((place, copy))
        order += [(place ^ bit, low) for low in seq_bits if low < bit]
    for place, copy in plan:
        if place == 0:
            copy.start()

    for j in range(n_seq):

        @pl.when(me == j)
        def _():
            for c in range(3):
                left = c * width * n_seq + j * width
                slice_ref[dp, :, c * width : (c + 1) * width] = w_ref[:, left : left + width]

    small_buf[dp] = jnp.zeros(small_buf.shape[1:], bf16)
    small_buf[dp, 0:1, :] = again_ref[...]
    small_buf[dp, 1:2, :] = mgain_ref[...]
    small_buf[dp, 2:4, :] = vec_ref[...]
    small_buf[dp, 4:6, :] = mix_ref[0]
    small_buf[dp, 6:8, :] = mix_ref[1]
    small_buf[dp, 8 : 8 + H, :] = router_ref[...].astype(f32).T.astype(bf16)
    copies = []
    for k in range(1, n_dp):
        target = {"dp": lax.rem(dp + k, n_dp)}
        for ref, send, recv in ((slice_ref, w_send, w_recv), (small_buf, s_send, s_recv)):
            copy = pltpu.make_async_remote_copy(
                src_ref=ref.at[dp],
                dst_ref=ref.at[dp],
                send_sem=send.at[k],
                recv_sem=recv.at[k],
                device_id=target,
                device_id_type=MESH,
            )
            copy.start()
            copies.append(copy)
    all_ref[me] = h_ref[...]
    for place, copy in plan:
        if place != 0:
            arrival[place].wait_recv()
            copy.start()
    for place in arrival:
        if not any(p == place for p, _ in plan):
            arrival[place].wait_recv()
    for _, copy in plan:
        copy.wait_send()
    for copy in copies:
        copy.wait()
    small_ref[...] = jnp.concatenate(
        [small_buf[i].astype(f32) for i in range(n_dp)], axis=1
    )


def start_call(n_seq, n_dp, hidden, w_qkv, attn_gain, moe_gain, vec, mix, router):
    tok, shard = hidden.shape[0], w_qkv.shape[0]
    width3 = w_qkv.shape[1] // n_seq
    vmem = pl.BlockSpec(memory_space=pltpu.VMEM)
    hops = n_seq - 1
    dma = pltpu.SemaphoreType.DMA
    return pl.pallas_call(
        functools.partial(start_kernel, n_seq, n_dp),
        out_shape=(
            jax.ShapeDtypeStruct((n_seq, tok, D), bf16),
            jax.ShapeDtypeStruct((n_dp, shard, width3), bf16),
            jax.ShapeDtypeStruct((SMALL, D), f32),
        ),
        in_specs=[vmem] * 7,
        out_specs=[vmem] * 3,
        scratch_shapes=[
            pltpu.VMEM((n_dp, SMALL, shard), bf16),
            dma((hops,)),
            dma((hops,)),
            dma((n_dp,)),
            dma((n_dp,)),
            dma((n_dp,)),
            dma((n_dp,)),
        ],
        compiler_params=pltpu.CompilerParams(collective_id=0, has_side_effects=True),
        name="start",
    )(hidden, w_qkv, attn_gain[None], moe_gain[None], vec, mix, router)


def qkv_kernel(h_ref, gain_ref, w_ref, cos_ref, sin_ref, attn_ref, out_ref, wt_ref):
    @pl.when((pl.program_id(0) == 0) & (pl.program_id(1) == 0))
    def _():
        wt_ref[...] = w_ref[...].reshape(D, w_ref.shape[2]).T

    x = h_ref[0].astype(f32)
    mean_square = jnp.mean(x * x, axis=-1, keepdims=True)
    attn = (x * lax.rsqrt(mean_square + 1e-06) * gain_ref[...]).astype(bf16)
    attn_ref[...] = attn
    y = mm(wt_ref[...], attn, NT)
    cos, sin = cos_ref[...], sin_ref[...]
    rows = y.shape[0]
    half = HD // 2
    for head in range(2 * rows // (3 * HD)):
        a = y[head * HD : head * HD + half]
        b = y[head * HD + half : (head + 1) * HD]
        out_ref[head * HD : head * HD + half] = (a * cos - b * sin).astype(bf16)
        out_ref[head * HD + half : (head + 1) * HD] = (a * sin + b * cos).astype(bf16)
    out_ref[2 * rows // 3 :] = y[2 * rows // 3 :].astype(bf16)


def qkv_call(blocks, gain, w, cos_t, sin_t):
    parts, tok, _ = blocks.shape
    seq_len, width = parts * tok, w.shape[2]
    per = tok // BLK
    return pl.pallas_call(
        qkv_kernel,
        out_shape=(
            jax.ShapeDtypeStruct((seq_len, D), bf16),
            jax.ShapeDtypeStruct((width, seq_len), bf16),
            jax.ShapeDtypeStruct((width, D), bf16),
        ),
        grid=(parts, per),
        in_specs=[
            pl.BlockSpec((1, BLK, D), lambda b, t: (b, t, 0)),
            pl.BlockSpec((1, D), lambda b, t: (0, 0)),
            pl.BlockSpec(w.shape, lambda b, t: (0, 0, 0)),
            pl.BlockSpec((HD // 2, BLK), lambda b, t: (0, b * per + t)),
            pl.BlockSpec((HD // 2, BLK), lambda b, t: (0, b * per + t)),
        ],
        out_specs=[
            pl.BlockSpec((BLK, D), lambda b, t: (b * per + t, 0)),
            pl.BlockSpec((width, BLK), lambda b, t: (0, b * per + t)),
            pl.BlockSpec((width, D), lambda b, t: (0, 0)),
        ],
        name="qkv",
    )(blocks, gain, w, cos_t, sin_t)


def allowed_block(key_block, query_block, start_row):
    key_pos = key_block * BLK + lax.broadcasted_iota(jnp.int32, (BLK, BLK), 0)
    query_pos = query_block * BLK + lax.broadcasted_iota(jnp.int32, (BLK, BLK), 1)
    return (key_pos >= start_row) & (key_pos <= query_pos)


def attn_kernel(lo_ref, qkv_ref, start_ref, out_ref, exact_ref, log_ref, keys_ref):
    heads, seq_len, _ = keys_ref.shape
    width = heads * HD
    qb = pl.program_id(0)

    @pl.when(qb == 0)
    def _():
        for h in range(heads):
            keys_ref[h] = qkv_ref[width + h * HD : width + (h + 1) * HD, :].T

    here = pl.ds(pl.multiple_of(qb * BLK, BLK), BLK)
    start_row = start_ref[...]

    def step(kb, carry):
        there = pl.ds(pl.multiple_of(kb * BLK, BLK), BLK)
        allowed = allowed_block(kb, qb, start_row)
        new = []
        for h in range(heads):
            top, total, acc = carry[h]
            scores = mm(keys_ref[h, there, :], qkv_ref[h * HD : (h + 1) * HD, here], NN)
            scores = jnp.where(allowed, scores * score_scale, neg_large)
            new_top = jnp.maximum(top, jnp.max(scores, axis=0, keepdims=True))
            fade = jnp.exp2(top - new_top)
            weights = jnp.exp2(scores - new_top)
            total = total * fade + jnp.sum(weights, axis=0, keepdims=True)
            values = qkv_ref[2 * width + h * HD : 2 * width + (h + 1) * HD, there]
            acc = acc * fade + mm(values, weights.astype(bf16), NN)
            new.append((new_top, total, acc))
        return tuple(new)

    first = tuple(
        (
            jnp.full((1, BLK), neg_large, f32),
            jnp.zeros((1, BLK), f32),
            jnp.zeros((HD, BLK), f32),
        )
        for _ in range(heads)
    )
    done = lax.fori_loop(lo_ref[qb], qb + 1, step, first)
    for h in range(heads):
        top, total, acc = done[h]
        attended = acc / total
        exact_ref[h * HD : (h + 1) * HD, :] = attended
        out_ref[0, h * HD : (h + 1) * HD, :] = attended.astype(bf16)
        log_ref[h : h + 1, :] = top + jnp.log2(total)


def attn_call(lows, qkv, start_row, tok):
    width3, seq_len = qkv.shape
    width = width3 // 3
    heads = width // HD
    per = tok // BLK
    return pl.pallas_call(
        attn_kernel,
        out_shape=(
            jax.ShapeDtypeStruct((seq_len // tok, width, tok), bf16),
            jax.ShapeDtypeStruct((width, seq_len), f32),
            jax.ShapeDtypeStruct((heads, seq_len), f32),
        ),
        grid_spec=pltpu.PrefetchScalarGridSpec(
            num_scalar_prefetch=1,
            grid=(seq_len // BLK,),
            in_specs=[
                pl.BlockSpec((width3, seq_len), lambda i, lo: (0, 0)),
                pl.BlockSpec((1, BLK), lambda i, lo: (0, i)),
            ],
            out_specs=[
                pl.BlockSpec((1, width, BLK), lambda i, lo: (i // per, 0, i % per)),
                pl.BlockSpec((width, BLK), lambda i, lo: (0, i)),
                pl.BlockSpec((heads, BLK), lambda i, lo: (0, i)),
            ],
            scratch_shapes=[pltpu.VMEM((heads, seq_len, HD), bf16)],
        ),
        name="attend",
    )(lows, qkv, start_row)


def attn_back_kernel(
    lo_ref, qkv_ref, go_ref, exact_ref, log_ref, start_ref, cos_ref, sin_ref, out_ref,
    keys_ref, values_ref, dk_ref, dv_ref,
):
    heads, seq_len, _ = keys_ref.shape
    width = heads * HD
    half = HD // 2
    qb = pl.program_id(0)

    @pl.when(qb == 0)
    def _():
        for h in range(heads):
            keys_ref[h] = qkv_ref[width + h * HD : width + (h + 1) * HD, :].T
            values_ref[h] = qkv_ref[2 * width + h * HD : 2 * width + (h + 1) * HD, :].T
        dk_ref[...] = jnp.zeros_like(dk_ref)
        dv_ref[...] = jnp.zeros_like(dv_ref)

    here = pl.ds(pl.multiple_of(qb * BLK, BLK), BLK)
    start_row = start_ref[...]
    grad = go_ref[0]
    deltas = [
        jnp.sum(
            exact_ref[h * HD : (h + 1) * HD, :] * grad[h * HD : (h + 1) * HD].astype(f32),
            axis=0,
            keepdims=True,
        )
        for h in range(heads)
    ]

    def step(kb, carry):
        there = pl.ds(pl.multiple_of(kb * BLK, BLK), BLK)
        allowed = allowed_block(kb, qb, start_row)
        new = []
        for h in range(heads):
            rows = slice(h * HD, (h + 1) * HD)
            queries = qkv_ref[rows, here]
            scores = mm(keys_ref[h, there, :], queries, NN)
            scores = jnp.where(allowed, scores * score_scale, neg_large)
            probs = jnp.exp2(scores - log_ref[h : h + 1, :])
            grad_probs = mm(values_ref[h, there, :], grad[rows], NN)
            grad_scores = (probs * (grad_probs - deltas[h])).astype(bf16)
            dv_ref[rows, there] += mm(grad[rows], probs.astype(bf16), NT)
            dk_ref[rows, there] += mm(queries, grad_scores, NT)
            keys = qkv_ref[width + h * HD : width + (h + 1) * HD, there]
            new.append(carry[h] + mm(keys, grad_scores, NN))
        return tuple(new)

    grads = lax.fori_loop(
        lo_ref[qb], qb + 1, step, tuple(jnp.zeros((HD, BLK), f32) for _ in range(heads))
    )

    def turn_back(value, cos, sin):
        value = value.astype(bf16).astype(f32)
        a, b = value[:half], value[half:]
        return (a * cos + b * sin).astype(bf16), (b * cos - a * sin).astype(bf16)

    for h in range(heads):
        a, b = turn_back(grads[h] * 0.125, cos_ref[:, here], sin_ref[:, here])
        out_ref[h * HD : h * HD + half, here] = a
        out_ref[h * HD + half : (h + 1) * HD, here] = b

    @pl.when(qb == pl.num_programs(0) - 1)
    def _():
        cos, sin = cos_ref[...], sin_ref[...]
        for h in range(heads):
            a, b = turn_back(dk_ref[h * HD : (h + 1) * HD, :] * 0.125, cos, sin)
            out_ref[width + h * HD : width + h * HD + half, :] = a
            out_ref[width + h * HD + half : width + (h + 1) * HD, :] = b
        out_ref[2 * width :, :] = dv_ref[...].astype(bf16)


def attn_back_call(lows, qkv, grad_out, exact, logs, start_row, cos_t, sin_t):
    width3, seq_len = qkv.shape
    width = width3 // 3
    heads = width // HD
    per = grad_out.shape[2] // BLK
    return pl.pallas_call(
        attn_back_kernel,
        out_shape=jax.ShapeDtypeStruct((width3, seq_len), bf16),
        grid_spec=pltpu.PrefetchScalarGridSpec(
            num_scalar_prefetch=1,
            grid=(seq_len // BLK,),
            in_specs=[
                pl.BlockSpec((width3, seq_len), lambda i, lo: (0, 0)),
                pl.BlockSpec((1, width, BLK), lambda i, lo: (i // per, 0, i % per)),
                pl.BlockSpec((width, BLK), lambda i, lo: (0, i)),
                pl.BlockSpec((heads, BLK), lambda i, lo: (0, i)),
                pl.BlockSpec((1, BLK), lambda i, lo: (0, i)),
                pl.BlockSpec((HD // 2, seq_len), lambda i, lo: (0, 0)),
                pl.BlockSpec((HD // 2, seq_len), lambda i, lo: (0, 0)),
            ],
            out_specs=pl.BlockSpec((width3, seq_len), lambda i, lo: (0, 0)),
            scratch_shapes=[
                pltpu.VMEM((heads, seq_len, HD), bf16),
                pltpu.VMEM((heads, seq_len, HD), bf16),
                pltpu.VMEM((width, seq_len), f32),
                pltpu.VMEM((width, seq_len), f32),
            ],
        ),
        name="attend_back",
    )(lows, qkv, grad_out, exact, logs, start_row, cos_t, sin_t)


def expert_kernel(
    x_ref, g_ref, gate_ref, w_ref, out_ref, piece_ref, dot_ref, dw_ref, gs_ref, oacc_ref, pacc_ref
):
    i = pl.program_id(0)

    @pl.when(i == 0)
    def _():
        gs_ref[...] = (g_ref[...].astype(f32) * gate_ref[...]).astype(bf16)
        oacc_ref[...] = jnp.zeros_like(oacc_ref)
        pacc_ref[...] = jnp.zeros_like(pacc_ref)

    x, gs = x_ref[...], gs_ref[...]
    gate_pre = mm(x, w_ref[0], NT)
    up_pre = mm(x, w_ref[1], NT)
    sig = 1.0 / (1.0 + jnp.exp(-gate_pre))
    silu = gate_pre * sig
    hidden = (silu * up_pre).astype(bf16)
    oacc_ref[...] += mm(hidden, w_ref[2], NN)
    dw_ref[2] = mm(hidden, gs, TN).astype(dw_ref.dtype)
    grad_hidden = mm(gs, w_ref[2], NT)
    grad_gate = (grad_hidden * up_pre * sig * (1.0 + gate_pre * (1.0 - sig))).astype(bf16)
    grad_up = (grad_hidden * silu).astype(bf16)
    pacc_ref[...] += mm(grad_gate, w_ref[0], NN) + mm(grad_up, w_ref[1], NN)
    dw_ref[0] = mm(grad_gate, x, TN).astype(dw_ref.dtype)
    dw_ref[1] = mm(grad_up, x, TN).astype(dw_ref.dtype)

    @pl.when(i == pl.num_programs(0) - 1)
    def _():
        out = oacc_ref[...].astype(bf16)
        out_ref[...] = out
        piece_ref[...] = pacc_ref[...].astype(bf16)
        dot_ref[...] = jnp.sum(out.astype(f32) * g_ref[...].astype(f32), axis=-1, keepdims=True)


def expert_plain(x, g, gate, weights):
    gs = (g.astype(f32) * gate).astype(bf16)
    gate_pre = mm(x, weights[0], NT)
    up_pre = mm(x, weights[1], NT)
    sig = 1.0 / (1.0 + jnp.exp(-gate_pre))
    silu = gate_pre * sig
    hidden = (silu * up_pre).astype(bf16)
    out = mm(hidden, weights[2], NN).astype(bf16)
    grad_hidden = mm(gs, weights[2], NT)
    grad_gate = (grad_hidden * up_pre * sig * (1.0 + gate_pre * (1.0 - sig))).astype(bf16)
    grad_up = (grad_hidden * silu).astype(bf16)
    piece = (mm(grad_gate, weights[0], NN) + mm(grad_up, weights[1], NN)).astype(bf16)
    dw = jnp.stack([mm(grad_gate, x, TN), mm(grad_up, x, TN), mm(hidden, gs, TN)]).astype(bf16)
    dots = jnp.sum(out.astype(f32) * g.astype(f32), axis=-1, keepdims=True)
    return out, piece, dots, dw


def expert_call(x, g, gate, weights):
    rows, units = x.shape[0], weights.shape[1]
    if rows > 1024:
        return expert_plain(x, g, gate, weights)
    tile = min(256, units)
    whole = pl.BlockSpec((rows, D), lambda i: (0, 0))
    column = pl.BlockSpec((rows, 1), lambda i: (0, 0))
    return pl.pallas_call(
        expert_kernel,
        out_shape=(
            jax.ShapeDtypeStruct((rows, D), bf16),
            jax.ShapeDtypeStruct((rows, D), bf16),
            jax.ShapeDtypeStruct((rows, 1), f32),
            jax.ShapeDtypeStruct(weights.shape, bf16),
        ),
        grid=(units // tile,),
        in_specs=[whole, whole, column, pl.BlockSpec((3, tile, D), lambda i: (0, i, 0))],
        out_specs=[whole, whole, column, pl.BlockSpec((3, tile, D), lambda i: (0, i, 0))],
        scratch_shapes=[
            pltpu.VMEM((rows, D), bf16),
            pltpu.VMEM((rows, D), f32),
            pltpu.VMEM((rows, D), f32),
        ],
        name="experts",
    )(x, g, gate, weights)


def tail_kernel(
    n_seq, n_dp, g_ref, a_ref, wt_ref, h_ref, resid_ref, gain_ref, wq_ref,
    din_ref, dw_ref, dgain_ref,
    core_out, core_in, x_out, x_in, part_ref, w_out_buf, w_in, row_buf, row_in,
    c_send, c_recv, x_send, x_recv, w_send, w_recv, r_send, r_recv,
):
    me, dp = lax.axis_index("seq"), lax.axis_index("dp")
    tok = h_ref.shape[0]
    shard, width3 = w_in.shape[1], w_in.shape[2]
    width = width3 // 3
    bits = list(bits_high_first(n_seq))[::-1]
    greet(
        [{"seq": me ^ place} for place in range(1, n_seq)]
        + [{"dp": lax.rem(dp + k, n_dp)} for k in range(1, n_dp)]
    )

    def term(place):
        columns = pl.ds(pl.multiple_of((me ^ place) * tok, tok), tok)
        return mm(g_ref[:, columns], wt_ref[...], TN)

    def send(src, dst, sems, index, target):
        copy = pltpu.make_async_remote_copy(
            src_ref=src, dst_ref=dst, send_sem=sems[0].at[index], recv_sem=sems[1].at[index],
            device_id=target, device_id_type=MESH,
        )
        copy.start()
        return copy

    pairs = n_seq // 2
    core_copies = []
    for i in range(pairs):
        core_out[i] = term(2 * i + 1).astype(bf16)
        core_copies.append(
            send(core_out.at[i], core_in.at[i], (c_send, c_recv), i, {"seq": me ^ 1})
        )
    turned = mm(g_ref[...], a_ref[...], NN)
    w_out_buf[...] = turned.T.astype(bf16).reshape(n_dp, shard, width3)
    w_in[dp] = w_out_buf[dp]
    w_copies = [
        send(
            w_out_buf.at[lax.rem(dp + k, n_dp)], w_in.at[dp], (w_send, w_recv), k,
            {"dp": lax.rem(dp + k, n_dp)},
        )
        for k in range(1, n_dp)
    ]
    x_copies = []
    for i in range(pairs - 1, -1, -1):
        part = term(2 * i)
        core_copies[i].wait_recv()
        part = part + core_in[i].astype(f32)
        if i == 0:
            part_ref[...] = part
        else:
            x_out[i - 1] = part.astype(bf16)
            x_copies.append(
                send(x_out.at[i - 1], x_in.at[i - 1], (x_send, x_recv), i - 1,
                     {"seq": me ^ (2 * i)})
            )
    for copy in w_copies:
        copy.wait_recv()
    rows = jnp.sum(w_in[...].astype(f32), axis=0)
    row_buf[...] = rows.astype(bf16)
    row_in[me] = row_buf[...]
    row_copies = [
        send(row_buf, row_in.at[me], (r_send, r_recv), place, {"seq": me ^ place})
        for place in range(1, n_seq)
    ]
    for copy in x_copies:
        copy.wait_recv()
    grad = part_ref[...]
    for i in range(pairs - 1):
        grad = grad + x_in[i].astype(f32)
    values = h_ref[...].astype(f32)
    back, _ = norm_back(values, gain_ref[...], grad)
    din_ref[...] = resid_ref[...] + back
    for copy in row_copies:
        copy.wait_recv()
    for j in range(n_seq):
        block = row_in[j].astype(f32)
        for c in range(3):
            left = c * width * n_seq + j * width
            dw_ref[:, left : left + width] = block[:, c * width : (c + 1) * width]
    dgain_ref[...] = jnp.sum(dw_ref[...] * wq_ref[...].astype(f32), axis=1, keepdims=True)
    for copy in core_copies + w_copies + x_copies + row_copies:
        copy.wait_send()


def tail_call(n_seq, n_dp, grad_qkv, attn_in, w_turned, hidden, grad_resid, gain, w_qkv):
    tok, shard = hidden.shape[0], w_qkv.shape[0]
    width3 = grad_qkv.shape[0]
    pairs = n_seq // 2
    vmem = pl.BlockSpec(memory_space=pltpu.VMEM)
    dma = pltpu.SemaphoreType.DMA
    return pl.pallas_call(
        functools.partial(tail_kernel, n_seq, n_dp),
        out_shape=(
            jax.ShapeDtypeStruct((tok, D), f32),
            jax.ShapeDtypeStruct(w_qkv.shape, f32),
            jax.ShapeDtypeStruct((shard, 1), f32),
        ),
        in_specs=[vmem] * 7,
        out_specs=[vmem] * 3,
        scratch_shapes=[
            pltpu.VMEM((pairs, tok, D), bf16),
            pltpu.VMEM((pairs, tok, D), bf16),
            pltpu.VMEM((pairs - 1, tok, D), bf16),
            pltpu.VMEM((pairs - 1, tok, D), bf16),
            pltpu.VMEM((tok, D), f32),
            pltpu.VMEM((n_dp, shard, width3), bf16),
            pltpu.VMEM((n_dp, shard, width3), bf16),
            pltpu.VMEM((shard, width3), bf16),
            pltpu.VMEM((n_seq, shard, width3), bf16),
            dma((pairs,)),
            dma((pairs,)),
            dma((pairs,)),
            dma((pairs,)),
            dma((n_dp,)),
            dma((n_dp,)),
            dma((n_seq,)),
            dma((n_seq,)),
        ],
        compiler_params=pltpu.CompilerParams(collective_id=1, has_side_effects=True),
        name="tail",
    )(grad_qkv, attn_in, w_turned, hidden, grad_resid, gain, w_qkv)


def rope_tables(seq_len):
    freq_index = jnp.arange(HD // 2, dtype=f32)
    inv_freq = jnp.exp(freq_index * (-2.0 * math.log(10000.0) / HD))
    angles = jnp.arange(seq_len, dtype=jnp.int32).astype(f32)[None, :] * inv_freq[:, None]
    return jnp.cos(angles), jnp.sin(angles)


def norm_back(values, gain, grad):
    rate = lax.rsqrt(jnp.mean(values * values, axis=-1, keepdims=True) + 1e-06)
    scaled = gain * grad
    inner = jnp.mean(values * scaled, axis=-1, keepdims=True)
    return rate * scaled - values * (rate * rate * rate) * inner, rate


def per_device(
    hidden_in,
    prev_logits,
    segments,
    routes,
    attn_gain,
    w_qkv,
    w_out,
    moe_gain,
    w_router,
    w_carry,
    const_vec,
    const_mix,
    experts,
    cotangent,
):
    n_seq, n_dp = lax.axis_size("seq"), lax.axis_size("dp")
    owners = n_dp // E
    me = lax.axis_index("seq")
    tok = hidden_in.shape[1]
    seq_len = tok * n_seq
    shard = w_qkv.shape[0]
    heads_here = H // n_seq
    width = heads_here * HD
    hidden = hidden_in[0]
    tokens_f = hidden.astype(f32)
    grad_low = cotangent[0]
    grad_top = grad_low.astype(f32)
    prev_rows = prev_logits[0]
    route_rows = routes[0]
    carry_f = w_carry.astype(f32)

    blocks, w_slice, small_t = start_call(
        n_seq, n_dp, hidden, w_qkv, attn_gain, moe_gain, const_vec, const_mix, w_router
    )
    gain_one, gain_two = small_t[0:1], small_t[1:2]
    vec_f, mix_f, router_t = small_t[2:4], small_t[4:8], small_t[8:20]
    dp_me = lax.axis_index("dp")
    out_parts = [w_out] + [
        lax.ppermute(w_out, "dp", [(i, (i + k) % n_dp) for i in range(n_dp)])
        for k in range(1, n_dp)
    ]
    out_weight = jnp.zeros((n_dp, shard, D), bf16)
    for k, part in enumerate(out_parts):
        out_weight = lax.dynamic_update_index_in_dim(
            out_weight, part, lax.rem(dp_me + n_dp - k, n_dp), 0
        )
    out_weight = out_weight.reshape(D, D)

    named = [
        (route_rows[:, k : k + 1] == jnp.arange(E, dtype=jnp.int32)[None, :]) for k in range(2)
    ]
    earlier = (
        jnp.arange(tok, dtype=jnp.int32)[None, :] < jnp.arange(tok, dtype=jnp.int32)[:, None]
    ).astype(bf16)
    ranks = mm(earlier, (named[0] | named[1]).astype(bf16), NN)
    slot_of = [
        jnp.where(
            route_rows[:, k] < E,
            route_rows[:, k] * CAP
            + jnp.sum(jnp.where(named[k], ranks, 0.0), axis=1).astype(jnp.int32),
            E * CAP,
        )
        for k in range(2)
    ]
    slots = jnp.arange(E * CAP, dtype=jnp.int32)[None, :]
    picks = [slot_of[k][:, None] == slots for k in range(2)]
    pick_low = [p.astype(bf16) for p in picks]
    pick_any = (picks[0] | picks[1]).astype(bf16)

    def dispatch(rows):
        grouped = mm(pick_any, rows, TN).astype(bf16).reshape(E, CAP, D)
        return lax.all_to_all(
            jnp.repeat(grouped, owners, axis=0), "dp", split_axis=0, concat_axis=0, tiled=True
        )

    def back_to_source(values):
        return lax.all_to_all(values, "dp", split_axis=0, concat_axis=0, tiled=True)

    arrived_grad = dispatch(grad_low)

    cos_t, sin_t = rope_tables(seq_len)
    seg_row = segments[0]
    doc_ids = jnp.arange(16, dtype=jnp.int32)
    doc_start = jnp.sum((seg_row[None, :] < doc_ids[:, None]).astype(jnp.int32), axis=1)
    start = jnp.sum(jnp.where(seg_row[None, :] == doc_ids[:, None], doc_start[:, None], 0), axis=0)
    start_row = start.astype(jnp.int32)[None, :]
    lows = start[::BLK].astype(jnp.int32) // BLK
    attn_in, qkv, w_turned = qkv_call(blocks, gain_one, w_slice, cos_t, sin_t)
    attended, attended_exact, logs = attn_call(lows, qkv, start_row, tok)
    heads_t = lax.all_to_all(attended, "seq", split_axis=0, concat_axis=0, tiled=True).reshape(
        D, tok
    )

    resid_mid = tokens_f + mm(heads_t, out_weight, TN)
    rate_two = lax.rsqrt(jnp.mean(resid_mid * resid_mid, axis=-1, keepdims=True) + 1e-06)
    normed = resid_mid * rate_two * gain_two
    normed_low = normed.astype(bf16)
    logits = mm(normed_low, router_t.astype(bf16), NT) + jnp.dot(
        prev_rows, carry_f, precision=exact_prec
    )
    all_ids = jnp.arange(H, dtype=jnp.int32)[None, :]
    hot = [route_rows[:, k : k + 1] == all_ids for k in range(2)]
    chosen = [jnp.sum(jnp.where(hot[k], logits, 0.0), axis=1, keepdims=True) for k in range(2)]
    top_logit = jnp.maximum(chosen[0], chosen[1])
    gate_exp = [jnp.exp(c - top_logit) for c in chosen]
    gate_sum = gate_exp[0] + gate_exp[1]
    gates = [g / gate_sum for g in gate_exp]

    arrived = dispatch(normed_low)
    gate_slots = jnp.sum(
        jnp.where(picks[0], gates[0], 0.0) + jnp.where(picks[1], gates[1], 0.0), axis=0
    ).reshape(E, 1, CAP)
    arrived_gate = lax.all_to_all(
        jnp.repeat(gate_slots, owners, axis=0), "dp", split_axis=0, concat_axis=0, tiled=True
    )
    rows = n_dp * CAP
    partial, piece, dots, dw = expert_call(
        arrived.reshape(rows, D),
        arrived_grad.reshape(rows, D),
        arrived_gate.reshape(rows, 1),
        experts,
    )
    back_piece = back_to_source(piece.reshape(n_dp, CAP, D))
    back_dots = back_to_source(dots.reshape(n_dp, 1, CAP))
    partial, back_piece = lax.optimization_barrier((partial, back_piece))
    back_out = back_to_source(partial.reshape(n_dp, CAP, D))

    def owner_rows(values, owner):
        return values.reshape(E, owners, CAP, -1)[:, owner].reshape(E * CAP, -1)

    half = dw.shape[1] // 2
    core = me & 1
    kept = lax.dynamic_slice_in_dim(dw, core * half, half, 1)
    given = lax.dynamic_slice_in_dim(dw, (1 - core) * half, half, 1)
    summed = (kept.astype(f32) + swap(given, "seq", 1).astype(f32)).astype(bf16)
    bit = 2
    total = summed.astype(f32)
    while bit < n_seq:
        low = total.astype(bf16)
        total = low.astype(f32) + swap(low, "seq", bit).astype(f32)
        bit *= 2
    mine = total.astype(bf16)
    other = swap(mine, "seq", 1)
    d_experts = jnp.concatenate(
        [jnp.where(core == 0, mine, other), jnp.where(core == 0, other, mine)], axis=1
    ).astype(f32)

    const_logits = lax.dot_general(normed, mix_f, NT, precision=exact_prec)
    grad_normed_dot = jnp.sum(grad_top * normed, axis=1, keepdims=True)
    grad_vec_dot = lax.dot_general(grad_top, vec_f, NT, precision=exact_prec)
    alphas = []
    for j in range(2):
        pair = const_logits[:, 2 * j : 2 * j + 2]
        pair_exp = jnp.exp(pair - jnp.max(pair, axis=1, keepdims=True))
        alphas.append(pair_exp / jnp.sum(pair_exp, axis=1, keepdims=True))
    const_dot = [
        alphas[j][:, 0:1] * grad_normed_dot + alphas[j][:, 1:2] * grad_vec_dot[:, j : j + 1]
        for j in range(2)
    ]
    slot_dots = jnp.sum(back_dots.reshape(E, owners, CAP), axis=1).reshape(1, E * CAP)
    out_dots = []
    for k in range(2):
        route = route_rows[:, k : k + 1]
        value = jnp.sum(jnp.where(picks[k], slot_dots, 0.0), axis=1, keepdims=True)
        value = value + jnp.where(route == E + 1, grad_normed_dot, 0.0)
        for j in range(2):
            value = value + jnp.where(route == E + 2 + j, const_dot[j], 0.0)
        out_dots.append(value)
    mean_dot = gates[0] * out_dots[0] + gates[1] * out_dots[1]
    grad_logits = sum(
        jnp.where(hot[k], gates[k] * (out_dots[k] - mean_dot), 0.0) for k in range(2)
    )

    def gate_of(expert):
        return sum(
            jnp.where(route_rows[:, k : k + 1] == expert, gates[k], 0.0) for k in range(2)
        )

    copy_gate = gate_of(E + 1)
    const_gate = [gate_of(E + 2 + j) for j in range(2)]
    mix_grads = []
    for j in range(2):
        terms = [grad_normed_dot, grad_vec_dot[:, j : j + 1]]
        for c in range(2):
            mix_grads.append(
                const_gate[j] * alphas[j][:, c : c + 1] * (terms[c] - const_dot[j])
            )
    mix_grads = jnp.concatenate(mix_grads, axis=1)
    normed_gate = copy_gate + sum(const_gate[j] * alphas[j][:, 0:1] for j in range(2))
    vec_gate = jnp.concatenate([const_gate[j] * alphas[j][:, 1:2] for j in range(2)], axis=1)

    mixed = normed * normed_gate + jnp.dot(vec_gate, vec_f, precision=exact_prec)
    for k in range(2):
        picked = sum(mm(pick_low[k], owner_rows(back_out, o), NN) for o in range(owners))
        mixed = mixed + gates[k] * picked
    block_out = (resid_mid + mixed).astype(bf16)

    grad_normed = grad_top * normed_gate
    grad_normed = grad_normed + jnp.dot(
        jnp.concatenate([grad_logits, mix_grads], axis=1),
        jnp.concatenate([router_t, mix_f], axis=0),
        precision=exact_prec,
    )
    for o in range(owners):
        grad_normed = grad_normed + mm(pick_any, owner_rows(back_piece, o), NN)
    grad_mid, _ = norm_back(resid_mid, gain_two, grad_normed)
    grad_resid = grad_top + grad_mid
    grad_attn = grad_resid.astype(bf16)
    grad_heads = mm(out_weight, grad_attn, NT).astype(bf16)
    grad_out = lax.all_to_all(
        grad_heads.reshape(n_seq, width, tok), "seq", split_axis=0, concat_axis=0, tiled=True
    )

    d_prev = jnp.dot(grad_logits, carry_f.T, precision=exact_prec)
    grad_router = jnp.dot(grad_logits.T, normed_low.astype(f32), precision=exact_prec)
    grad_carry = jnp.dot(prev_rows.T, grad_logits, precision=exact_prec)
    grad_gain_two = jnp.sum(grad_normed * resid_mid * rate_two, axis=0, keepdims=True)
    grad_vec = jnp.dot(vec_gate.T, grad_top, precision=exact_prec)
    grad_mix = jnp.dot(mix_grads.T, normed, precision=exact_prec)
    packed = jnp.concatenate([grad_router, grad_gain_two, grad_vec, grad_mix], axis=0)
    lines = packed.shape[0]
    packed = packed.reshape(lines, n_dp, shard).swapaxes(0, 1).reshape(n_dp, lines * shard)
    packed = jnp.concatenate(
        [packed, jnp.broadcast_to(grad_carry.reshape(1, H * H), (n_dp, H * H))], axis=1
    )
    packed = lax.all_to_all(packed, "dp", split_axis=0, concat_axis=0, tiled=True)
    packed = jnp.sum(packed, axis=0, keepdims=True)
    for bit in bits_high_first(n_seq):
        packed = packed + swap(packed, "seq", bit)
    lined = packed[0, : lines * shard].reshape(lines, shard)
    d_router, d_moe_gain = lined[:H].T, lined[H]
    d_vec, d_mix = lined[H + 1 : H + 3], lined[H + 3 : H + 7].reshape(2, 2, shard)
    d_carry = packed[0, lines * shard :].reshape(H, H)

    grad_out_w = mm(heads_t, grad_attn, NN)
    blocks_out = grad_out_w.reshape(D, n_seq, width).swapaxes(0, 1)
    blocks_out = blocks_out[jnp.arange(n_seq) ^ me]
    mine_out = sum_relative([blocks_out[r] for r in range(n_seq)], "seq").astype(bf16)

    def reduce_rows(value):
        value = value.reshape(n_dp, -1, value.shape[-1])
        value = lax.all_to_all(value, "dp", split_axis=0, concat_axis=0, tiled=True)
        return jnp.sum(value.astype(f32), axis=0)

    def collect_columns(value):
        parts = jnp.stack(gather_relative(value, "seq"))
        return parts[jnp.arange(n_seq) ^ me]

    d_out = collect_columns(reduce_rows(mine_out)).swapaxes(0, 1).reshape(shard, D)

    grad_qkv = attn_back_call(
        lows, qkv, grad_out, attended_exact, logs, start_row, cos_t, sin_t
    )
    d_input, d_qkv, gain_sum = tail_call(
        n_seq, n_dp, grad_qkv, attn_in, w_turned, hidden, grad_resid, gain_one, w_qkv
    )
    d_attn_gain = gain_sum[:, 0] / attn_gain.astype(f32)
    return (
        block_out[None],
        d_input[None],
        d_prev[None],
        d_attn_gain,
        d_qkv,
        d_out,
        d_moe_gain,
        d_router,
        d_carry,
        d_vec,
        d_mix,
        d_experts,
    )


def solution(mesh):
    return jax.shard_map(
        per_device,
        mesh=mesh,
        in_specs=(
            P("dp", "seq", None),
            P("dp", "seq", None),
            P("dp", None),
            P("dp", "seq", None),
            P("dp"),
            P("dp", None),
            P("dp", None),
            P("dp"),
            P("dp", None),
            P(),
            P(None, "dp"),
            P(None, None, "dp"),
            P(None, "dp", None),
            P("dp", "seq", None),
        ),
        out_specs=(
            P("dp", "seq", None),
            P("dp", "seq", None),
            P("dp", "seq", None),
            P("dp"),
            P("dp", None),
            P("dp", None),
            P("dp"),
            P("dp", None),
            P(),
            P(None, "dp"),
            P(None, None, "dp"),
            P(None, "dp", None),
        ),
        check_vma=False,
    )
```

```python
import functools
import math

import jax
import jax.numpy as jnp
from jax import lax
from jax.experimental import pallas as pl
from jax.experimental.pallas import tpu as pltpu
from jax.sharding import PartitionSpec as P

D = 768
H = 12
HD = 64
E = 8
CAP = 128
BLK = 256
N_CROSS = 1

exact_prec = lax.Precision.HIGHEST
neg_large = -1e30
score_scale = 0.125 * math.log2(math.e)
f32 = jnp.float32
bf16 = jnp.bfloat16

NN = (((1,), (0,)), ((), ()))
NT = (((1,), (1,)), ((), ()))
TN = (((0,), (0,)), ((), ()))


def mm(a, b, dims):
    return lax.dot_general(a, b, dims, preferred_element_type=f32)


def swap(value, axis, bit):
    size = lax.axis_size(axis)
    return lax.ppermute(value, axis, [(i, i ^ bit) for i in range(size)])


def bits_high_first(size):
    bit = size // 2
    while bit >= 1:
        yield bit
        bit //= 2


MESH = pl.DeviceIdType.MESH
SMALL = 32


def greet(peers):
    barrier = pltpu.get_barrier_semaphore()
    for peer in peers:
        pl.semaphore_signal(barrier, inc=1, device_id=peer, device_id_type=MESH)
    pl.semaphore_wait(barrier, len(peers))


def one_hot(condition):
    return jnp.where(condition, 1.0, 0.0).astype(bf16)


def picks_of(slot_ref):
    tok = slot_ref.shape[0]
    slots = lax.broadcasted_iota(jnp.int32, (tok, E * CAP), 1)
    return [slot_ref[:, k : k + 1] == slots for k in range(2)]


def make_slots(route_ref, cot_ref, slot_ref, g_ref):
    tok = route_ref.shape[0]
    ids = lax.broadcasted_iota(jnp.int32, (tok, E), 1)
    named = [route_ref[:, k : k + 1] == ids for k in range(2)]
    earlier = lax.broadcasted_iota(jnp.int32, (tok, tok), 1) < lax.broadcasted_iota(
        jnp.int32, (tok, tok), 0
    )
    ranks = mm(one_hot(earlier), one_hot(named[0] | named[1]), NN)
    for k in range(2):
        route = route_ref[:, k : k + 1]
        rank = jnp.sum(jnp.where(named[k], ranks, 0.0), axis=1, keepdims=True)
        slot_ref[:, k : k + 1] = jnp.where(
            route < E, route * CAP + rank.astype(jnp.int32), E * CAP
        )
    picks = picks_of(slot_ref)
    rows = mm(one_hot(picks[0] | picks[1]), cot_ref[...], TN)
    g_ref[...] = rows.astype(bf16).reshape(g_ref.shape)


def start_kernel(
    n_seq, n_dp, h_ref, w_ref, again_ref, mgain_ref, vec_ref, mix_ref, router_ref,
    route_ref, cot_ref,
    all_ref, slice_ref, small_ref, slot_ref, *refs,
):
    g_refs, refs = refs[:n_dp], refs[n_dp:]
    g_buf, small_buf, h_send, h_recv, w_send, w_recv, s_send, s_recv = refs
    owners = n_dp // E
    me, dp = lax.axis_index("seq"), lax.axis_index("dp")
    shard, width3 = slice_ref.shape[1], slice_ref.shape[2]
    width = width3 // 3
    seq_bits = list(bits_high_first(n_seq))
    greet(
        [{"seq": me ^ bit} for bit in seq_bits]
        + [{"dp": lax.rem(dp + k, n_dp)} for k in range(1, n_dp)]
    )

    def put(place, bit, index):
        return pltpu.make_async_remote_copy(
            src_ref=h_ref if place == 0 else all_ref.at[me ^ place],
            dst_ref=all_ref.at[me ^ place],
            send_sem=h_send.at[index],
            recv_sem=h_recv.at[index],
            device_id={"seq": me ^ bit},
            device_id_type=MESH,
        )

    plan, arrival = [], {}
    order = [(0, bit) for bit in seq_bits]
    while order:
        place, bit = order.pop(0)
        copy = put(place, bit, len(plan))
        arrival[place ^ bit] = copy
        plan.append((place, copy))
        order += [(place ^ bit, low) for low in seq_bits if low < bit]
    for place, copy in plan:
        if place == 0:
            copy.start()

    for j in range(n_seq):

        @pl.when(me == j)
        def _():
            for c in range(3):
                left = c * width * n_seq + j * width
                slice_ref[dp, :, c * width : (c + 1) * width] = w_ref[:, left : left + width]

    small_buf[dp] = jnp.zeros(small_buf.shape[1:], bf16)
    small_buf[dp, 0:1, :] = again_ref[...]
    small_buf[dp, 1:2, :] = mgain_ref[...]
    small_buf[dp, 2:4, :] = vec_ref[...]
    small_buf[dp, 4:6, :] = mix_ref[0]
    small_buf[dp, 6:8, :] = mix_ref[1]
    small_buf[dp, 8 : 8 + H, :] = router_ref[...].astype(f32).T.astype(bf16)
    copies = []
    for k in range(1, n_dp):
        target = {"dp": lax.rem(dp + k, n_dp)}
        for ref, send, recv in ((slice_ref, w_send, w_recv), (small_buf, s_send, s_recv)):
            copy = pltpu.make_async_remote_copy(
                src_ref=ref.at[dp],
                dst_ref=ref.at[dp],
                send_sem=send.at[k],
                recv_sem=recv.at[k],
                device_id=target,
                device_id_type=MESH,
            )
            copy.start()
            copies.append(copy)
    all_ref[me] = h_ref[...]
    make_slots(route_ref, cot_ref, slot_ref, g_buf)
    for k in range(n_dp):
        g_refs[k][...] = g_buf[(dp ^ k) // owners]
    for place, copy in plan:
        if place != 0:
            arrival[place].wait_recv()
            copy.start()
    for place in arrival:
        if not any(p == place for p, _ in plan):
            arrival[place].wait_recv()
    for _, copy in plan:
        copy.wait_send()
    for copy in copies:
        copy.wait()
    small_ref[...] = jnp.concatenate(
        [small_buf[i].astype(f32) for i in range(n_dp)], axis=1
    )


def start_call(
    n_seq, n_dp, hidden, w_qkv, attn_gain, moe_gain, vec, mix, router, routes, cotangent
):
    tok, shard = hidden.shape[0], w_qkv.shape[0]
    width3 = w_qkv.shape[1] // n_seq
    vmem = pl.BlockSpec(memory_space=pltpu.VMEM)
    hops = n_seq - 1
    dma = pltpu.SemaphoreType.DMA
    return pl.pallas_call(
        functools.partial(start_kernel, n_seq, n_dp),
        out_shape=(
            jax.ShapeDtypeStruct((n_seq, tok, D), bf16),
            jax.ShapeDtypeStruct((n_dp, shard, width3), bf16),
            jax.ShapeDtypeStruct((SMALL, D), f32),
            jax.ShapeDtypeStruct(routes.shape, jnp.int32),
        )
        + (jax.ShapeDtypeStruct((CAP, D), bf16),) * n_dp,
        in_specs=[vmem] * 9,
        out_specs=[vmem] * (4 + n_dp),
        scratch_shapes=[
            pltpu.VMEM((E, CAP, D), bf16),
            pltpu.VMEM((n_dp, SMALL, shard), bf16),
            dma((hops,)),
            dma((hops,)),
            dma((n_dp,)),
            dma((n_dp,)),
            dma((n_dp,)),
            dma((n_dp,)),
        ],
        compiler_params=pltpu.CompilerParams(collective_id=0, has_side_effects=True),
        name="start",
    )(hidden, w_qkv, attn_gain[None], moe_gain[None], vec, mix, router, routes, cotangent)


def qkv_kernel(h_ref, gain_ref, w_ref, cos_ref, sin_ref, attn_ref, out_ref, wt_ref):
    @pl.when((pl.program_id(0) == 0) & (pl.program_id(1) == 0))
    def _():
        wt_ref[...] = w_ref[...].reshape(D, w_ref.shape[2]).T

    x = h_ref[0].astype(f32)
    mean_square = jnp.mean(x * x, axis=-1, keepdims=True)
    attn = (x * lax.rsqrt(mean_square + 1e-06) * gain_ref[...]).astype(bf16)
    attn_ref[...] = attn
    y = mm(wt_ref[...], attn, NT)
    cos, sin = cos_ref[...], sin_ref[...]
    rows = y.shape[0]
    half = HD // 2
    for head in range(2 * rows // (3 * HD)):
        a = y[head * HD : head * HD + half]
        b = y[head * HD + half : (head + 1) * HD]
        out_ref[head * HD : head * HD + half] = (a * cos - b * sin).astype(bf16)
        out_ref[head * HD + half : (head + 1) * HD] = (a * sin + b * cos).astype(bf16)
    out_ref[2 * rows // 3 :] = y[2 * rows // 3 :].astype(bf16)


def qkv_call(blocks, gain, w, cos_t, sin_t):
    parts, tok, _ = blocks.shape
    seq_len, width = parts * tok, w.shape[2]
    per = tok // BLK
    return pl.pallas_call(
        qkv_kernel,
        out_shape=(
            jax.ShapeDtypeStruct((seq_len, D), bf16),
            jax.ShapeDtypeStruct((width, seq_len), bf16),
            jax.ShapeDtypeStruct((width, D), bf16),
        ),
        grid=(parts, per),
        in_specs=[
            pl.BlockSpec((1, BLK, D), lambda b, t: (b, t, 0)),
            pl.BlockSpec((1, D), lambda b, t: (0, 0)),
            pl.BlockSpec(w.shape, lambda b, t: (0, 0, 0)),
            pl.BlockSpec((HD // 2, BLK), lambda b, t: (0, b * per + t)),
            pl.BlockSpec((HD // 2, BLK), lambda b, t: (0, b * per + t)),
        ],
        out_specs=[
            pl.BlockSpec((BLK, D), lambda b, t: (b * per + t, 0)),
            pl.BlockSpec((width, BLK), lambda b, t: (0, b * per + t)),
            pl.BlockSpec((width, D), lambda b, t: (0, 0)),
        ],
        name="qkv",
    )(blocks, gain, w, cos_t, sin_t)


def allowed_block(key_block, query_block, start_row):
    key_pos = key_block * BLK + lax.broadcasted_iota(jnp.int32, (BLK, BLK), 0)
    query_pos = query_block * BLK + lax.broadcasted_iota(jnp.int32, (BLK, BLK), 1)
    return (key_pos >= start_row) & (key_pos <= query_pos)


def attn_kernel(lo_ref, qkv_ref, start_ref, out_ref, exact_ref, log_ref, keys_ref):
    heads, seq_len, _ = keys_ref.shape
    width = heads * HD
    qb = pl.program_id(0)

    @pl.when(qb == 0)
    def _():
        for h in range(heads):
            keys_ref[h] = qkv_ref[width + h * HD : width + (h + 1) * HD, :].T

    here = pl.ds(pl.multiple_of(qb * BLK, BLK), BLK)
    start_row = start_ref[...]

    def step(kb, carry):
        there = pl.ds(pl.multiple_of(kb * BLK, BLK), BLK)
        allowed = allowed_block(kb, qb, start_row)
        new = []
        for h in range(heads):
            top, total, acc = carry[h]
            scores = mm(keys_ref[h, there, :], qkv_ref[h * HD : (h + 1) * HD, here], NN)
            scores = jnp.where(allowed, scores * score_scale, neg_large)
            new_top = jnp.maximum(top, jnp.max(scores, axis=0, keepdims=True))
            fade = jnp.exp2(top - new_top)
            weights = jnp.exp2(scores - new_top)
            total = total * fade + jnp.sum(weights, axis=0, keepdims=True)
            values = qkv_ref[2 * width + h * HD : 2 * width + (h + 1) * HD, there]
            acc = acc * fade + mm(values, weights.astype(bf16), NN)
            new.append((new_top, total, acc))
        return tuple(new)

    first = tuple(
        (
            jnp.full((1, BLK), neg_large, f32),
            jnp.zeros((1, BLK), f32),
            jnp.zeros((HD, BLK), f32),
        )
        for _ in range(heads)
    )
    done = lax.fori_loop(lo_ref[qb], qb + 1, step, first)
    for h in range(heads):
        top, total, acc = done[h]
        attended = acc / total
        exact_ref[h * HD : (h + 1) * HD, :] = attended
        out_ref[0, h * HD : (h + 1) * HD, :] = attended.astype(bf16)
        log_ref[h : h + 1, :] = top + jnp.log2(total)


def attn_call(lows, qkv, start_row, tok):
    width3, seq_len = qkv.shape
    width = width3 // 3
    heads = width // HD
    per = tok // BLK
    return pl.pallas_call(
        attn_kernel,
        out_shape=(
            jax.ShapeDtypeStruct((seq_len // tok, width, tok), bf16),
            jax.ShapeDtypeStruct((width, seq_len), f32),
            jax.ShapeDtypeStruct((heads, seq_len), f32),
        ),
        grid_spec=pltpu.PrefetchScalarGridSpec(
            num_scalar_prefetch=1,
            grid=(seq_len // BLK,),
            in_specs=[
                pl.BlockSpec((width3, seq_len), lambda i, lo: (0, 0)),
                pl.BlockSpec((1, BLK), lambda i, lo: (0, i)),
            ],
            out_specs=[
                pl.BlockSpec((1, width, BLK), lambda i, lo: (i // per, 0, i % per)),
                pl.BlockSpec((width, BLK), lambda i, lo: (0, i)),
                pl.BlockSpec((heads, BLK), lambda i, lo: (0, i)),
            ],
            scratch_shapes=[pltpu.VMEM((heads, seq_len, HD), bf16)],
        ),
        name="attend",
    )(lows, qkv, start_row)


def attn_back_kernel(
    lo_ref, qkv_ref, go_ref, exact_ref, log_ref, start_ref, cos_ref, sin_ref, out_ref,
    keys_ref, values_ref, dk_ref, dv_ref,
):
    heads, seq_len, _ = keys_ref.shape
    width = heads * HD
    half = HD // 2
    qb = pl.program_id(0)

    @pl.when(qb == 0)
    def _():
        for h in range(heads):
            keys_ref[h] = qkv_ref[width + h * HD : width + (h + 1) * HD, :].T
            values_ref[h] = qkv_ref[2 * width + h * HD : 2 * width + (h + 1) * HD, :].T
        dk_ref[...] = jnp.zeros_like(dk_ref)
        dv_ref[...] = jnp.zeros_like(dv_ref)

    here = pl.ds(pl.multiple_of(qb * BLK, BLK), BLK)
    start_row = start_ref[...]
    grad = go_ref[0]
    deltas = [
        jnp.sum(
            exact_ref[h * HD : (h + 1) * HD, :] * grad[h * HD : (h + 1) * HD].astype(f32),
            axis=0,
            keepdims=True,
        )
        for h in range(heads)
    ]

    def step(kb, carry):
        there = pl.ds(pl.multiple_of(kb * BLK, BLK), BLK)
        allowed = allowed_block(kb, qb, start_row)
        new = []
        for h in range(heads):
            rows = slice(h * HD, (h + 1) * HD)
            queries = qkv_ref[rows, here]
            scores = mm(keys_ref[h, there, :], queries, NN)
            scores = jnp.where(allowed, scores * score_scale, neg_large)
            probs = jnp.exp2(scores - log_ref[h : h + 1, :])
            grad_probs = mm(values_ref[h, there, :], grad[rows], NN)
            grad_scores = (probs * (grad_probs - deltas[h])).astype(bf16)
            dv_ref[rows, there] += mm(grad[rows], probs.astype(bf16), NT)
            dk_ref[rows, there] += mm(queries, grad_scores, NT)
            keys = qkv_ref[width + h * HD : width + (h + 1) * HD, there]
            new.append(carry[h] + mm(keys, grad_scores, NN))
        return tuple(new)

    grads = lax.fori_loop(
        lo_ref[qb], qb + 1, step, tuple(jnp.zeros((HD, BLK), f32) for _ in range(heads))
    )

    def turn_back(value, cos, sin):
        value = value.astype(bf16).astype(f32)
        a, b = value[:half], value[half:]
        return (a * cos + b * sin).astype(bf16), (b * cos - a * sin).astype(bf16)

    for h in range(heads):
        a, b = turn_back(grads[h] * 0.125, cos_ref[:, here], sin_ref[:, here])
        out_ref[h * HD : h * HD + half, here] = a
        out_ref[h * HD + half : (h + 1) * HD, here] = b

    @pl.when(qb == pl.num_programs(0) - 1)
    def _():
        cos, sin = cos_ref[...], sin_ref[...]
        for h in range(heads):
            a, b = turn_back(dk_ref[h * HD : (h + 1) * HD, :] * 0.125, cos, sin)
            out_ref[width + h * HD : width + h * HD + half, :] = a
            out_ref[width + h * HD + half : width + (h + 1) * HD, :] = b
        out_ref[2 * width :, :] = dv_ref[...].astype(bf16)


def attn_back_call(lows, qkv, grad_out, exact, logs, start_row, cos_t, sin_t):
    width3, seq_len = qkv.shape
    width = width3 // 3
    heads = width // HD
    per = grad_out.shape[2] // BLK
    return pl.pallas_call(
        attn_back_kernel,
        out_shape=jax.ShapeDtypeStruct((width3, seq_len), bf16),
        grid_spec=pltpu.PrefetchScalarGridSpec(
            num_scalar_prefetch=1,
            grid=(seq_len // BLK,),
            in_specs=[
                pl.BlockSpec((width3, seq_len), lambda i, lo: (0, 0)),
                pl.BlockSpec((1, width, BLK), lambda i, lo: (i // per, 0, i % per)),
                pl.BlockSpec((width, BLK), lambda i, lo: (0, i)),
                pl.BlockSpec((heads, BLK), lambda i, lo: (0, i)),
                pl.BlockSpec((1, BLK), lambda i, lo: (0, i)),
                pl.BlockSpec((HD // 2, seq_len), lambda i, lo: (0, 0)),
                pl.BlockSpec((HD // 2, seq_len), lambda i, lo: (0, 0)),
            ],
            out_specs=pl.BlockSpec((width3, seq_len), lambda i, lo: (0, 0)),
            scratch_shapes=[
                pltpu.VMEM((heads, seq_len, HD), bf16),
                pltpu.VMEM((heads, seq_len, HD), bf16),
                pltpu.VMEM((width, seq_len), f32),
                pltpu.VMEM((width, seq_len), f32),
            ],
        ),
        name="attend_back",
    )(lows, qkv, grad_out, exact, logs, start_row, cos_t, sin_t)


PAIR = 2 * CAP
TILE = 512
UNITS = 256


def moe_kernel(n_dp, n_cross, x_ref, gate_ref, w_hbm, *refs):
    g_refs, refs = refs[:n_dp], refs[n_dp:]
    piece_ref, dots_ref, refs = refs[0], refs[1], refs[2:]
    out_refs, refs = refs[:n_dp], refs[n_dp:]
    units = w_hbm.shape[1]
    tiles = units // UNITS // 2
    sum_refs, refs = refs[:tiles], refs[tiles:]
    far_refs, refs = refs[:n_cross], refs[n_cross:]
    (
        w_ref, x_in, gate_in, gs_ref, hid_ref, gg_ref, gu_ref, oacc_ref, pacc_ref, piece_out,
        dot_out, dw_out, dw_in, w_sem, x_send, x_recv, t_send, t_recv, p_send, p_recv,
        d_send, d_recv, c_send, c_recv, f_send, f_recv,
    ) = refs
    me, dp = lax.axis_index("seq"), lax.axis_index("dp")
    owners = n_dp // E
    pairs = n_dp // 2
    order = [i ^ (i >> 1) for i in range(pairs)]
    greet([{"dp": dp ^ k} for k in range(1, n_dp)] + [{"seq": me ^ 1}, {"seq": me ^ 2}])
    loads = [pltpu.make_async_copy(w_hbm.at[j], w_ref.at[j], w_sem.at[j]) for j in range(3)]
    x_copies, gate_copies = {}, {}
    for p in order:
        for k in (2 * p, 2 * p + 1):
            mine = (dp ^ k) // owners
            if k:
                target = {"dp": dp ^ k}
                gate_copies[k] = remote(
                    gate_ref.at[mine], gate_in.at[k], (t_send, t_recv), k, target
                )
                x_copies[k] = remote(x_ref.at[mine], x_in.at[k], (x_send, x_recv), k, target)
    for load in loads:
        load.start()
    x_in[0] = x_ref[dp // owners]
    gate_in[0] = gate_ref[dp // owners]
    piece_copies, dot_copies = {}, {}
    for count, p in enumerate(order):
        rows = slice(p * PAIR, (p + 1) * PAIR)
        for k in (2 * p, 2 * p + 1):
            if k:
                x_copies[k].wait_recv()
                gate_copies[k].wait_recv()
            column = jnp.broadcast_to(gate_in[k], (CAP, CAP)).T[:, 0:1]
            gs_ref[k * CAP : (k + 1) * CAP] = (g_refs[k][...].astype(f32) * column).astype(bf16)
        if count == 0:
            for load in loads:
                load.wait()
        oacc_ref[...] = jnp.zeros_like(oacc_ref)
        pacc_ref[...] = jnp.zeros_like(pacc_ref)

        @pl.loop(0, units // TILE)
        def _(t):
            part = pl.ds(pl.multiple_of(t * TILE, TILE), TILE)
            x = x_in[2 * p : 2 * p + 2].reshape(PAIR, D)
            gate_pre = mm(x, w_ref[0, part], NT)
            up_pre = mm(x, w_ref[1, part], NT)
            sig = 1.0 / (1.0 + jnp.exp(-gate_pre))
            silu = gate_pre * sig
            hidden = (silu * up_pre).astype(bf16)
            hid_ref[rows, part] = hidden
            oacc_ref[...] += mm(hidden, w_ref[2, part], NN)
            grad_hidden = mm(gs_ref[rows], w_ref[2, part], NT)
            grad_gate = (grad_hidden * up_pre * sig * (1.0 + gate_pre * (1.0 - sig))).astype(bf16)
            grad_up = (grad_hidden * silu).astype(bf16)
            gg_ref[rows, part] = grad_gate
            gu_ref[rows, part] = grad_up
            pacc_ref[...] += mm(grad_gate, w_ref[0, part], NN) + mm(grad_up, w_ref[1, part], NN)

        for k in (2 * p, 2 * p + 1):
            half = slice((k % 2) * CAP, (k % 2 + 1) * CAP)
            out = oacc_ref[half].astype(bf16)
            out_refs[k][...] = out
            product = out.astype(f32) * g_refs[k][...].astype(f32)
            dot_out[k] = lax.dot_general(
                jnp.ones((8, D), f32), product, NT, precision=exact_prec,
                preferred_element_type=f32,
            )[0:1]
            piece_out[k] = pacc_ref[half].astype(bf16)
            if k:
                target = {"dp": dp ^ k}
                dot_copies[k] = remote(
                    dot_out.at[k], dots_ref.at[dp], (d_send, d_recv), k, target
                )
                piece_copies[k] = remote(
                    piece_out.at[k], piece_ref.at[dp], (p_send, p_recv), k, target
                )
            else:
                dots_ref[dp] = dot_out[k]
                piece_ref[dp] = piece_out[k]
    core = me & 1
    x_all = x_in[...].reshape(n_dp * CAP, D)

    def weight_grad(half, t, ref):
        part = pl.ds(pl.multiple_of((half * tiles + t) * UNITS, UNITS), UNITS)
        ref[0] = mm(gg_ref[:, part], x_all, TN).astype(ref.dtype)
        ref[1] = mm(gu_ref[:, part], x_all, TN).astype(ref.dtype)
        ref[2] = mm(hid_ref[:, part], gs_ref[...], TN).astype(ref.dtype)

    core_copies = []
    for t in range(tiles):
        weight_grad(1 - core, t, dw_out.at[t])
        core_copies.append(
            remote(dw_out.at[t], dw_in.at[t], (c_send, c_recv), t, {"seq": me ^ 1})
        )
    far_copies = []
    for t in range(tiles):
        weight_grad(core, t, sum_refs[t])
        core_copies[t].wait_recv()
        sum_refs[t][...] = (sum_refs[t][...].astype(f32) + dw_in[t].astype(f32)).astype(bf16)
        if t < n_cross:
            far_copies.append(
                remote(sum_refs[t], far_refs[t], (f_send, f_recv), t, {"seq": me ^ 2})
            )
    for k in range(1, n_dp):
        piece_copies[k].wait_recv()
        dot_copies[k].wait_recv()
    for copy in far_copies:
        copy.wait_recv()
    for copies in (x_copies, gate_copies, piece_copies, dot_copies):
        for copy in copies.values():
            copy.wait_send()
    for copy in core_copies + far_copies:
        copy.wait_send()


def moe_call(n_dp, n_cross, x_slots, gate_slots, weights, grads):
    units = weights.shape[1]
    rows = n_dp * CAP
    tiles = units // UNITS // 2
    part = (3, UNITS, D)
    vmem = pl.BlockSpec(memory_space=pltpu.VMEM)
    dma = pltpu.SemaphoreType.DMA
    outs = pl.pallas_call(
        functools.partial(moe_kernel, n_dp, n_cross),
        out_shape=(
            jax.ShapeDtypeStruct((n_dp, CAP, D), bf16),
            jax.ShapeDtypeStruct((n_dp, 1, CAP), f32),
        )
        + (jax.ShapeDtypeStruct((CAP, D), bf16),) * n_dp
        + (jax.ShapeDtypeStruct(part, bf16),) * (tiles + n_cross),
        in_specs=[vmem, vmem, pl.BlockSpec(memory_space=pl.ANY)] + [vmem] * n_dp,
        out_specs=[vmem] * (2 + n_dp + tiles + n_cross),
        scratch_shapes=[
            pltpu.VMEM(weights.shape, bf16),
            pltpu.VMEM((n_dp, CAP, D), bf16),
            pltpu.VMEM((n_dp, 1, CAP), f32),
            pltpu.VMEM((rows, D), bf16),
            pltpu.VMEM((rows, units), bf16),
            pltpu.VMEM((rows, units), bf16),
            pltpu.VMEM((rows, units), bf16),
            pltpu.VMEM((PAIR, D), f32),
            pltpu.VMEM((PAIR, D), f32),
            pltpu.VMEM((n_dp, CAP, D), bf16),
            pltpu.VMEM((n_dp, 1, CAP), f32),
            pltpu.VMEM((tiles, *part), bf16),
            pltpu.VMEM((tiles, *part), bf16),
            dma((3,)),
        ]
        + [dma((n_dp,))] * 8
        + [dma((tiles,))] * 2
        + [dma((max(n_cross, 1),))] * 2,
        compiler_params=pltpu.CompilerParams(
            collective_id=4, has_side_effects=True, vmem_limit_bytes=67043328
        ),
        name="experts",
    )(x_slots, gate_slots, weights, *grads)
    piece, dots, outs = outs[0], outs[1], outs[2:]
    return piece, dots, outs[:n_dp], outs[n_dp : n_dp + tiles], outs[n_dp + tiles :]


def remote(src, dst, sems, index, target):
    copy = pltpu.make_async_remote_copy(
        src_ref=src,
        dst_ref=dst,
        send_sem=sems[0].at[index],
        recv_sem=sems[1].at[index],
        device_id=target,
        device_id_type=MESH,
    )
    copy.start()
    return copy


def fill_rows(full_ref, part_refs, dp):
    for k, part in enumerate(part_refs):
        full_ref[dp ^ k] = part[...]


def mid_kernel(n_seq, n_dp, *refs):
    (att_ref, h_ref, prev_ref, carry_ref, small_ref, slot_ref, route_ref), refs = refs[:7], refs[7:]
    parts, refs = refs[:n_dp], refs[n_dp:]
    heads_ref, mid_ref, gate_ref, clog_ref, x_ref, gs_ref, wfull_ref = refs[:7]
    sems = refs[7:]
    me, dp = lax.axis_index("seq"), lax.axis_index("dp")
    tok = h_ref.shape[0]
    greet([{"seq": me ^ place} for place in range(1, n_seq)])
    copies = [
        remote(att_ref.at[me ^ place], heads_ref.at[me], sems, place, {"seq": me ^ place})
        for place in range(1, n_seq)
    ]
    heads_ref[me] = att_ref[me]
    fill_rows(wfull_ref, parts, dp)
    picks = picks_of(slot_ref)
    pick_any = one_hot(picks[0] | picks[1])
    carried = jnp.dot(prev_ref[...], carry_ref[...], precision=exact_prec)
    for copy in copies:
        copy.wait_recv()
    attn_out = mm(heads_ref[...].reshape(D, tok), wfull_ref[...].reshape(D, D), TN)
    resid = h_ref[...].astype(f32) + attn_out
    mid_ref[...] = resid
    rate = lax.rsqrt(jnp.mean(resid * resid, axis=-1, keepdims=True) + 1e-06)
    normed = resid * rate * small_ref[1:2]
    low = normed.astype(bf16)
    x_ref[...] = mm(pick_any, low, TN).astype(bf16).reshape(x_ref.shape)
    logits = mm(low, small_ref[8 : 8 + H].astype(bf16), NT) + carried
    ids = lax.broadcasted_iota(jnp.int32, (tok, H), 1)
    chosen = [
        jnp.sum(jnp.where(route_ref[:, k : k + 1] == ids, logits, 0.0), axis=1, keepdims=True)
        for k in range(2)
    ]
    top = jnp.maximum(chosen[0], chosen[1])
    exps = [jnp.exp(c - top) for c in chosen]
    total = exps[0] + exps[1]
    gates = [e / total for e in exps]
    gate_ref[:, 0:1] = gates[0]
    gate_ref[:, 1:2] = gates[1]
    clog_ref[...] = lax.dot_general(
        normed, small_ref[4:8], NT, precision=exact_prec, preferred_element_type=f32
    )
    slot_gates = jnp.sum(
        jnp.where(picks[0], gates[0], 0.0) + jnp.where(picks[1], gates[1], 0.0),
        axis=0,
        keepdims=True,
    )
    for e in range(E):
        gs_ref[e] = slot_gates[:, e * CAP : (e + 1) * CAP]
    for copy in copies:
        copy.wait_send()


def mid_call(n_seq, n_dp, attended, hidden, prev, carry, small, slot_of, routes, parts):
    tok, width = hidden.shape[0], attended.shape[1]
    shard = parts[0].shape[0]
    vmem = pl.BlockSpec(memory_space=pltpu.VMEM)
    dma = pltpu.SemaphoreType.DMA
    return pl.pallas_call(
        functools.partial(mid_kernel, n_seq, n_dp),
        out_shape=(
            jax.ShapeDtypeStruct((n_seq, width, tok), bf16),
            jax.ShapeDtypeStruct((tok, D), f32),
            jax.ShapeDtypeStruct((tok, 2), f32),
            jax.ShapeDtypeStruct((tok, 4), f32),
            jax.ShapeDtypeStruct((E, CAP, D), bf16),
            jax.ShapeDtypeStruct((E, 1, CAP), f32),
            jax.ShapeDtypeStruct((n_dp, shard, D), bf16),
        ),
        in_specs=[vmem] * (7 + n_dp),
        out_specs=[vmem] * 7,
        scratch_shapes=[dma((n_seq,)), dma((n_seq,))],
        compiler_params=pltpu.CompilerParams(collective_id=2, has_side_effects=True),
        name="mid",
    )(attended, hidden, prev, carry, small, slot_of, routes, *parts)


LINES = 40


def mid_back_kernel(
    n_seq, n_dp, piece_ref, dots_ref, cot_ref, mid_ref, gate_ref, clog_ref, slot_ref, route_ref,
    small_ref, heads_ref, w_ref, prev_ref, carry_ref,
    resid_ref, go_ref, base_ref, dprev_ref, pack_ref, own_ref, cross_ref,
    gh_ref, wo_ref, wo_in, a_send, a_recv, c_send, c_recv,
):
    me = lax.axis_index("seq")
    tok = cot_ref.shape[0]
    width = heads_ref.shape[1]
    owners = n_dp // E
    pairs = n_seq // 2
    greet([{"seq": me ^ place} for place in range(1, n_seq)])
    cot = cot_ref[...]
    grad_top = cot.astype(f32)
    resid_mid = mid_ref[...]
    gain = small_ref[1:2]
    vec, mix = small_ref[2:4], small_ref[4:8]
    rate = lax.rsqrt(jnp.mean(resid_mid * resid_mid, axis=-1, keepdims=True) + 1e-06)
    normed = resid_mid * rate * gain
    picks = picks_of(slot_ref)
    gates = [gate_ref[:, k : k + 1] for k in range(2)]
    routes = [route_ref[:, k : k + 1] for k in range(2)]
    normed_dot = jnp.sum(grad_top * normed, axis=1, keepdims=True)
    vec_dot = mm(cot, vec.astype(bf16), NT)
    alphas, const_dot = [], []
    for j in range(2):
        pair = [clog_ref[:, 2 * j + c : 2 * j + c + 1] for c in range(2)]
        top = jnp.maximum(pair[0], pair[1])
        exps = [jnp.exp(p - top) for p in pair]
        total = exps[0] + exps[1]
        alphas.append([e / total for e in exps])
        const_dot.append(alphas[j][0] * normed_dot + alphas[j][1] * vec_dot[:, j : j + 1])
    slot_dots = jnp.concatenate(
        [sum(dots_ref[e * owners + o] for o in range(owners)) for e in range(E)], axis=1
    )
    out_dots = []
    for k in range(2):
        value = jnp.sum(jnp.where(picks[k], slot_dots, 0.0), axis=1, keepdims=True)
        value = value + jnp.where(routes[k] == E + 1, normed_dot, 0.0)
        for j in range(2):
            value = value + jnp.where(routes[k] == E + 2 + j, const_dot[j], 0.0)
        out_dots.append(value)
    mean_dot = gates[0] * out_dots[0] + gates[1] * out_dots[1]
    ids = lax.broadcasted_iota(jnp.int32, (tok, H), 1)
    grad_logits = sum(
        jnp.where(routes[k] == ids, gates[k] * (out_dots[k] - mean_dot), 0.0) for k in range(2)
    )

    def gate_of(expert):
        return sum(jnp.where(routes[k] == expert, gates[k], 0.0) for k in range(2))

    const_gate = [gate_of(E + 2 + j) for j in range(2)]
    normed_gate = gate_of(E + 1) + sum(const_gate[j] * alphas[j][0] for j in range(2))
    vec_gate = [const_gate[j] * alphas[j][1] for j in range(2)]
    mix_grads = []
    for j in range(2):
        terms = [normed_dot, vec_dot[:, j : j + 1]]
        for c in range(2):
            mix_grads.append(const_gate[j] * alphas[j][c] * (terms[c] - const_dot[j]))
    mix_grads = jnp.concatenate(mix_grads, axis=1)
    pick_any = one_hot(picks[0] | picks[1])
    grad_normed = grad_top * normed_gate
    grad_normed = grad_normed + jnp.dot(
        jnp.concatenate([grad_logits, mix_grads], axis=1),
        jnp.concatenate([small_ref[8 : 8 + H], mix], axis=0),
        precision=exact_prec,
        preferred_element_type=f32,
    )
    pieces = piece_ref[...].reshape(E, owners, CAP, D)
    for o in range(owners):
        grad_normed = grad_normed + mm(pick_any, pieces[:, o].reshape(E * CAP, D), NN)
    back, _ = norm_back(resid_mid, gain, grad_normed)
    grad_resid = grad_top + back
    resid_ref[...] = grad_resid
    grad_attn = grad_resid.astype(bf16)
    gh_ref[...] = mm(w_ref[...].reshape(D, D), grad_attn, NT).astype(bf16).reshape(gh_ref.shape)
    copies = [
        remote(gh_ref.at[me ^ place], go_ref.at[me], (a_send, a_recv), place, {"seq": me ^ place})
        for place in range(1, n_seq)
    ]
    go_ref[me] = gh_ref[me]
    grad_w = mm(heads_ref[...].reshape(D, tok), grad_attn, NN)
    for j in range(n_seq):
        wo_ref[j] = grad_w[:, j * width : (j + 1) * width].astype(bf16)
    core_copies = [
        remote(wo_ref.at[me ^ (2 * i + 1)], wo_in.at[i], (c_send, c_recv), i, {"seq": me ^ 1})
        for i in range(pairs)
    ]
    base = resid_mid + normed * normed_gate
    for j in range(2):
        base = base + vec_gate[j] * vec[j : j + 1]
    base_ref[...] = base
    dprev_ref[...] = lax.dot_general(
        grad_logits, carry_ref[...], NT, precision=exact_prec, preferred_element_type=f32
    )

    def rows_of(left, right):
        return lax.dot_general(left, right, TN, precision=exact_prec, preferred_element_type=f32)

    packed = jnp.concatenate(
        [
            rows_of(grad_logits, normed.astype(bf16).astype(f32)),
            rows_of(mix_grads, normed),
            rows_of(jnp.concatenate(vec_gate, axis=1), grad_top),
            jnp.sum(grad_normed * resid_mid * rate, axis=0, keepdims=True),
        ],
        axis=0,
    )
    carry_grad = rows_of(prev_ref[...], grad_logits)
    lines, shard = packed.shape[0], D // n_dp
    for i in range(n_dp):
        pack_ref[i] = jnp.zeros(pack_ref.shape[1:], f32)
        pack_ref[i, 0:lines, :] = packed[:, i * shard : (i + 1) * shard]
        pack_ref[i, 24 : 24 + H, 0:H] = carry_grad
    for i in range(pairs):
        core_copies[i].wait_recv()
        summed = wo_ref[me ^ (2 * i)].astype(f32) + wo_in[i].astype(f32)
        if i == 0:
            own_ref[...] = summed
        else:
            cross_ref[i - 1] = summed.astype(bf16)
    for copy in copies:
        copy.wait()
    for copy in core_copies:
        copy.wait_send()


def mid_back_call(
    n_seq, n_dp, piece, dots, cot, mid, gates, clog, slot_of, routes, small, heads, w, prev, carry
):
    tok, width = cot.shape[0], heads.shape[1]
    pairs = n_seq // 2
    vmem = pl.BlockSpec(memory_space=pltpu.VMEM)
    dma = pltpu.SemaphoreType.DMA
    return pl.pallas_call(
        functools.partial(mid_back_kernel, n_seq, n_dp),
        out_shape=(
            jax.ShapeDtypeStruct((tok, D), f32),
            jax.ShapeDtypeStruct((n_seq, width, tok), bf16),
            jax.ShapeDtypeStruct((tok, D), f32),
            jax.ShapeDtypeStruct((tok, H), f32),
            jax.ShapeDtypeStruct((n_dp, LINES, D // n_dp), f32),
            jax.ShapeDtypeStruct((D, width), f32),
            jax.ShapeDtypeStruct((pairs - 1, D, width), bf16),
        ),
        in_specs=[vmem] * 13,
        out_specs=[vmem] * 7,
        scratch_shapes=[
            pltpu.VMEM((n_seq, width, tok), bf16),
            pltpu.VMEM((n_seq, D, width), bf16),
            pltpu.VMEM((pairs, D, width), bf16),
            dma((n_seq,)),
            dma((n_seq,)),
            dma((pairs,)),
            dma((pairs,)),
        ],
        compiler_params=pltpu.CompilerParams(collective_id=3, has_side_effects=True),
        name="mid_back",
    )(piece, dots, cot, mid, gates, clog, slot_of, routes, small, heads, w, prev, carry)


def tail_kernel(
    n_seq, n_dp, g_ref, a_ref, wt_ref, h_ref, resid_ref, gain_ref, wq_ref,
    own_ref, cross_ref, pack_ref, gate_ref, slot_ref, base_ref, *refs,
):
    out_parts, refs = refs[:n_dp], refs[n_dp:]
    tail_body(n_seq, n_dp, g_ref, a_ref, wt_ref, h_ref, resid_ref, gain_ref, wq_ref,
              own_ref, cross_ref, pack_ref, gate_ref, slot_ref, base_ref, out_parts, *refs)


def tail_body(
    n_seq, n_dp, g_ref, a_ref, wt_ref, h_ref, resid_ref, gain_ref, wq_ref,
    own_ref, cross_ref, pack_ref, gate_ref, slot_ref, base_ref, out_parts,
    din_ref, dw_ref, dgain_ref, dwo_ref, line_ref, block_ref,
    core_out, core_in, x_out, x_in, part_ref, w_out_buf, w_in, row_buf, row_in,
    cross_in, wo_buf, wo_in, pack_in, line_buf, line_in, rows_ref,
    c_send, c_recv, x_send, x_recv, w_send, w_recv, r_send, r_recv,
    o_send, o_recv, p_send, p_recv, q_send, q_recv, l_send, l_recv,
):
    me, dp = lax.axis_index("seq"), lax.axis_index("dp")
    tok = h_ref.shape[0]
    shard, width3 = w_in.shape[1], w_in.shape[2]
    width = width3 // 3
    owners = n_dp // E
    others = range(1, n_dp)
    greet(
        [{"seq": me ^ place} for place in range(1, n_seq)]
        + [{"dp": lax.rem(dp + k, n_dp)} for k in others]
    )

    def there(k):
        return lax.rem(dp + k, n_dp)

    def term(place):
        columns = pl.ds(pl.multiple_of((me ^ place) * tok, tok), tok)
        return mm(g_ref[:, columns], wt_ref[...], TN)

    pairs = n_seq // 2
    cross_copies = [
        remote(cross_ref.at[i - 1], cross_in.at[i - 1], (o_send, o_recv), i - 1,
               {"seq": me ^ (2 * i)})
        for i in range(1, pairs)
    ]
    pack_copies = [
        remote(pack_ref.at[there(k)], pack_in.at[dp], (p_send, p_recv), k, {"dp": there(k)})
        for k in others
    ]
    pack_in[dp] = pack_ref[dp]
    core_copies = []
    for i in range(pairs):
        core_out[i] = term(2 * i + 1).astype(bf16)
        core_copies.append(
            remote(core_out.at[i], core_in.at[i], (c_send, c_recv), i, {"seq": me ^ 1})
        )
    turned = mm(g_ref[...], a_ref[...], NN)
    w_out_buf[...] = turned.T.astype(bf16).reshape(n_dp, shard, width3)
    w_in[dp] = w_out_buf[dp]
    w_copies = [
        remote(w_out_buf.at[there(k)], w_in.at[dp], (w_send, w_recv), k, {"dp": there(k)})
        for k in others
    ]
    x_copies = []
    for i in range(pairs - 1, -1, -1):
        part = term(2 * i)
        core_copies[i].wait_recv()
        part = part + core_in[i].astype(f32)
        if i == 0:
            part_ref[...] = part
        else:
            x_out[i - 1] = part.astype(bf16)
            x_copies.append(
                remote(x_out.at[i - 1], x_in.at[i - 1], (x_send, x_recv), i - 1,
                       {"seq": me ^ (2 * i)})
            )
    own = own_ref[...]
    for i in range(pairs - 1):
        cross_copies[i].wait_recv()
        own = own + cross_in[i].astype(f32)
    wo_buf[...] = own.astype(bf16).reshape(n_dp, shard, width)
    wo_in[dp] = wo_buf[dp]
    wo_copies = [
        remote(wo_buf.at[there(k)], wo_in.at[dp], (q_send, q_recv), k, {"dp": there(k)})
        for k in others
    ]
    picks = picks_of(slot_ref)
    fill_rows(rows_ref, out_parts, dp)
    rows = rows_ref[...].reshape(E, owners, CAP, D)
    block = base_ref[...]
    for k in range(2):
        hot = one_hot(picks[k])
        picked = sum(mm(hot, rows[:, o].reshape(E * CAP, D), NN) for o in range(owners))
        block = block + gate_ref[:, k : k + 1] * picked
    block_ref[...] = block.astype(bf16)

    for copy in pack_copies:
        copy.wait_recv()
    line_buf[...] = jnp.sum(pack_in[...], axis=0)
    line_in[me] = line_buf[...]
    line_copies = [
        remote(line_buf, line_in.at[me], (l_send, l_recv), place, {"seq": me ^ place})
        for place in range(1, n_seq)
    ]
    for copy in w_copies + wo_copies:
        copy.wait_recv()
    row_buf[:, :width3] = jnp.sum(w_in[...].astype(f32), axis=0).astype(bf16)
    row_buf[:, width3:] = jnp.sum(wo_in[...].astype(f32), axis=0).astype(bf16)
    row_in[me] = row_buf[...]
    row_copies = [
        remote(row_buf, row_in.at[me], (r_send, r_recv), place, {"seq": me ^ place})
        for place in range(1, n_seq)
    ]
    for copy in x_copies:
        copy.wait_recv()
    grad = part_ref[...]
    for i in range(pairs - 1):
        grad = grad + x_in[i].astype(f32)
    values = h_ref[...].astype(f32)
    back, _ = norm_back(values, gain_ref[...], grad)
    din_ref[...] = resid_ref[...] + back
    for copy in line_copies:
        copy.wait_recv()
    line_ref[...] = jnp.sum(line_in[...], axis=0)
    for copy in row_copies:
        copy.wait_recv()
    for j in range(n_seq):
        block = row_in[j].astype(f32)
        for c in range(3):
            left = c * width * n_seq + j * width
            dw_ref[:, left : left + width] = block[:, c * width : (c + 1) * width]
        dwo_ref[:, j * width : (j + 1) * width] = block[:, width3:]
    dgain_ref[...] = jnp.sum(dw_ref[...] * wq_ref[...].astype(f32), axis=1, keepdims=True)
    for copy in (
        core_copies + w_copies + x_copies + row_copies + wo_copies + pack_copies
        + line_copies + cross_copies
    ):
        copy.wait_send()


def tail_call(
    n_seq, n_dp, grad_qkv, attn_in, w_turned, hidden, grad_resid, gain, w_qkv,
    own, cross, pack, gates, slot_of, base, out_parts,
):
    tok, shard = hidden.shape[0], w_qkv.shape[0]
    width3 = grad_qkv.shape[0]
    width = width3 // 3
    pairs = n_seq // 2
    vmem = pl.BlockSpec(memory_space=pltpu.VMEM)
    dma = pltpu.SemaphoreType.DMA
    return pl.pallas_call(
        functools.partial(tail_kernel, n_seq, n_dp),
        out_shape=(
            jax.ShapeDtypeStruct((tok, D), f32),
            jax.ShapeDtypeStruct(w_qkv.shape, f32),
            jax.ShapeDtypeStruct((shard, 1), f32),
            jax.ShapeDtypeStruct((shard, D), f32),
            jax.ShapeDtypeStruct((LINES, shard), f32),
            jax.ShapeDtypeStruct((tok, D), bf16),
        ),
        in_specs=[vmem] * (13 + n_dp),
        out_specs=[vmem] * 6,
        scratch_shapes=[
            pltpu.VMEM((pairs, tok, D), bf16),
            pltpu.VMEM((pairs, tok, D), bf16),
            pltpu.VMEM((pairs - 1, tok, D), bf16),
            pltpu.VMEM((pairs - 1, tok, D), bf16),
            pltpu.VMEM((tok, D), f32),
            pltpu.VMEM((n_dp, shard, width3), bf16),
            pltpu.VMEM((n_dp, shard, width3), bf16),
            pltpu.VMEM((shard, width3 + width), bf16),
            pltpu.VMEM((n_seq, shard, width3 + width), bf16),
            pltpu.VMEM((pairs - 1, D, width), bf16),
            pltpu.VMEM((n_dp, shard, width), bf16),
            pltpu.VMEM((n_dp, shard, width), bf16),
            pltpu.VMEM((n_dp, LINES, shard), f32),
            pltpu.VMEM((LINES, shard), f32),
            pltpu.VMEM((n_seq, LINES, shard), f32),
            pltpu.VMEM((n_dp, CAP, D), bf16),
        ]
        + [dma((pairs,))] * 4
        + [dma((n_dp,))] * 2
        + [dma((n_seq,))] * 2
        + [dma((pairs,))] * 2
        + [dma((n_dp,))] * 4
        + [dma((n_seq,))] * 2,
        compiler_params=pltpu.CompilerParams(collective_id=1, has_side_effects=True),
        name="tail",
    )(
        grad_qkv, attn_in, w_turned, hidden, grad_resid, gain, w_qkv,
        own, cross, pack, gates, slot_of, base, *out_parts,
    )


def rope_tables(seq_len):
    freq_index = jnp.arange(HD // 2, dtype=f32)
    inv_freq = jnp.exp(freq_index * (-2.0 * math.log(10000.0) / HD))
    angles = jnp.arange(seq_len, dtype=jnp.int32).astype(f32)[None, :] * inv_freq[:, None]
    return jnp.cos(angles), jnp.sin(angles)


def norm_back(values, gain, grad):
    rate = lax.rsqrt(jnp.mean(values * values, axis=-1, keepdims=True) + 1e-06)
    scaled = gain * grad
    inner = jnp.mean(values * scaled, axis=-1, keepdims=True)
    return rate * scaled - values * (rate * rate * rate) * inner, rate


def per_device(
    hidden_in,
    prev_logits,
    segments,
    routes,
    attn_gain,
    w_qkv,
    w_out,
    moe_gain,
    w_router,
    w_carry,
    const_vec,
    const_mix,
    experts,
    cotangent,
):
    n_seq, n_dp = lax.axis_size("seq"), lax.axis_size("dp")
    me = lax.axis_index("seq")
    tok = hidden_in.shape[1]
    seq_len = tok * n_seq
    hidden = hidden_in[0]
    grad_low = cotangent[0]
    prev_rows = prev_logits[0]
    route_rows = routes[0]
    carry_f = w_carry.astype(f32)

    blocks, w_slice, small, slot_of, *grad_slots = start_call(
        n_seq, n_dp, hidden, w_qkv, attn_gain, moe_gain, const_vec, const_mix, w_router,
        route_rows, grad_low,
    )
    gain_one = small[0:1]
    w_out_parts = [w_out] + [swap(w_out, "dp", k) for k in range(1, n_dp)]

    def swap_all(parts):
        return [parts[0]] + [swap(parts[k], "dp", k) for k in range(1, n_dp)]

    arrived_grad = swap_all(grad_slots)

    cos_t, sin_t = rope_tables(seq_len)
    seg_row = segments[0]
    doc_ids = jnp.arange(16, dtype=jnp.int32)
    doc_start = jnp.sum((seg_row[None, :] < doc_ids[:, None]).astype(jnp.int32), axis=1)
    start = jnp.sum(jnp.where(seg_row[None, :] == doc_ids[:, None], doc_start[:, None], 0), axis=0)
    start_row = start.astype(jnp.int32)[None, :]
    lows = start[::BLK].astype(jnp.int32) // BLK
    attn_in, qkv, w_turned = qkv_call(blocks, gain_one, w_slice, cos_t, sin_t)
    attended, attended_exact, logs = attn_call(lows, qkv, start_row, tok)

    heads_t, resid_mid, gates, const_logits, x_slots, gate_slots, out_weight = mid_call(
        n_seq, n_dp, attended, hidden, prev_rows, carry_f, small, slot_of, route_rows, w_out_parts
    )
    n_cross = min(N_CROSS, experts.shape[1] // UNITS // 2 - 1)
    back_piece, back_dots, partial, sums, far = moe_call(
        n_dp, n_cross, x_slots, gate_slots, experts, arrived_grad
    )
    back_out = swap_all(partial)
    far = list(far) + [swap(part, "seq", 2) for part in sums[n_cross:]]

    grad_resid, grad_out, base, d_prev, pack, own, cross = mid_back_call(
        n_seq, n_dp, back_piece, back_dots, grad_low, resid_mid, gates, const_logits, slot_of,
        route_rows, small, heads_t, out_weight, prev_rows, carry_f,
    )
    grad_qkv = attn_back_call(
        lows, qkv, grad_out, attended_exact, logs, start_row, cos_t, sin_t
    )
    d_input, d_qkv, gain_sum, d_out, lines, block_out = tail_call(
        n_seq, n_dp, grad_qkv, attn_in, w_turned, hidden, grad_resid, gain_one, w_qkv,
        own, cross, pack, gates, slot_of, base, back_out,
    )
    mine, d_input = lax.optimization_barrier((list(zip(sums, far)), d_input))
    mine = jnp.concatenate(
        [(a.astype(f32) + b.astype(f32)).astype(bf16) for a, b in mine], axis=1
    )
    other = swap(mine, "seq", 1)
    core = me & 1
    d_experts = jnp.concatenate(
        [jnp.where(core == 0, mine, other), jnp.where(core == 0, other, mine)], axis=1
    ).astype(f32)
    return (
        block_out[None],
        d_input[None],
        d_prev[None],
        gain_sum[:, 0] / attn_gain.astype(f32),
        d_qkv,
        d_out,
        lines[H + 6],
        lines[:H].T,
        lines[24 : 24 + H, :H],
        lines[H + 4 : H + 6],
        lines[H : H + 4].reshape(2, 2, -1),
        d_experts,
    )


def solution(mesh):
    return jax.shard_map(
        per_device,
        mesh=mesh,
        in_specs=(
            P("dp", "seq", None),
            P("dp", "seq", None),
            P("dp", None),
            P("dp", "seq", None),
            P("dp"),
            P("dp", None),
            P("dp", None),
            P("dp"),
            P("dp", None),
            P(),
            P(None, "dp"),
            P(None, None, "dp"),
            P(None, "dp", None),
            P("dp", "seq", None),
        ),
        out_specs=(
            P("dp", "seq", None),
            P("dp", "seq", None),
            P("dp", "seq", None),
            P("dp"),
            P("dp", None),
            P("dp", None),
            P("dp"),
            P("dp", None),
            P(),
            P(None, "dp"),
            P(None, None, "dp"),
            P(None, "dp", None),
        ),
        check_vma=False,
    )
```

```python
import functools
import math

import jax
import jax.numpy as jnp
from jax import lax
from jax.experimental import pallas as pl
from jax.experimental.pallas import tpu as pltpu
from jax.sharding import PartitionSpec as P

D = 768
H = 12
HD = 64
E = 8
CAP = 128
BLK = 256
PAIR = 2 * CAP
TILE = 1024
UNITS = 256
SMALL = 32
LINES = 40

exact_prec = lax.Precision.HIGHEST
neg_large = -1e30
score_scale = 0.125 * math.log2(math.e)
f32 = jnp.float32
bf16 = jnp.bfloat16

NN = (((1,), (0,)), ((), ()))
NT = (((1,), (1,)), ((), ()))
TN = (((0,), (0,)), ((), ()))


MESH = pl.DeviceIdType.MESH
VMEM = pl.BlockSpec(memory_space=pltpu.VMEM)
HBM = pl.BlockSpec(memory_space=pl.ANY)
DMA = pltpu.SemaphoreType.DMA


def mm(a, b, dims):
    return lax.dot_general(a, b, dims, preferred_element_type=f32)


def swap(value, axis, bit):
    size = lax.axis_size(axis)
    return lax.ppermute(value, axis, [(i, i ^ bit) for i in range(size)])


def bits_high_first(size):
    bit = size // 2
    while bit >= 1:
        yield bit
        bit //= 2


def greet(peers):
    barrier = pltpu.get_barrier_semaphore()
    for peer in peers:
        pl.semaphore_signal(barrier, inc=1, device_id=peer, device_id_type=MESH)
    pl.semaphore_wait(barrier, len(peers))


def remote_later(src, dst, sems, index, target):
    return pltpu.make_async_remote_copy(
        src_ref=src,
        dst_ref=dst,
        send_sem=sems[0].at[index],
        recv_sem=sems[1].at[index],
        device_id=target,
        device_id_type=MESH,
    )


def remote(src, dst, sems, index, target):
    copy = remote_later(src, dst, sems, index, target)
    copy.start()
    return copy


def one_hot(condition):
    return jnp.where(condition, 1.0, 0.0).astype(bf16)


def picks_of(slot_ref):
    slots = lax.broadcasted_iota(jnp.int32, (E * CAP, slot_ref.shape[1]), 0)
    return [one_hot(slots == slot_ref[k : k + 1, :]) for k in range(2)]


def split(rows):
    high = rows.astype(bf16)
    rest = rows - high.astype(f32)
    middle = rest.astype(bf16)
    low = (rest - middle.astype(f32)).astype(bf16)
    return jnp.concatenate([high, middle, low], axis=0)


def unsplit(rows):
    third = rows.shape[0] // 3
    return rows[:third] + rows[third : 2 * third] + rows[2 * third :]


def column_to_row(column):
    return jnp.broadcast_to(column, (column.shape[0], 128)).T[0:1]


def norm_back(values, gain, grad):
    rate = lax.rsqrt(jnp.mean(values * values, axis=-1, keepdims=True) + 1e-06)
    scaled = gain * grad
    inner = jnp.mean(values * scaled, axis=-1, keepdims=True)
    return rate * scaled - values * (rate * rate * rate) * inner


def make_slots(route_ref, cot_ref, slot_ref, g_ref):
    tok = route_ref.shape[1]
    ids = lax.broadcasted_iota(jnp.int32, (E, tok), 0)
    named = [route_ref[k : k + 1, :] == ids for k in range(2)]
    earlier = lax.broadcasted_iota(jnp.int32, (tok, tok), 0) < lax.broadcasted_iota(
        jnp.int32, (tok, tok), 1
    )
    ranks = mm(one_hot(named[0] | named[1]), one_hot(earlier), NN)
    for k in range(2):
        route = route_ref[k : k + 1, :]
        rank = jnp.sum(jnp.where(named[k], ranks, 0.0), axis=0, keepdims=True)
        slot_ref[k : k + 1, :] = jnp.where(
            route < E, route * CAP + rank.astype(jnp.int32), E * CAP
        )
    picks = picks_of(slot_ref)
    g_ref[...] = mm(picks[0] + picks[1], cot_ref[...], NN).astype(bf16).reshape(g_ref.shape)


def start_kernel(
    n_seq, n_dp, h_ref, w_ref, again_ref, mgain_ref, vec_ref, mix_ref, router_ref,
    route_ref, cot_ref, cos_ref, sin_ref, wo_ref,
    attn_ref, qkv_ref, wt_ref, small_ref, slot_ref, g_ref, wo_all,
    all_ref, slice_ref, small_buf, h_send, h_recv, w_send, w_recv, s_send, s_recv,
    o_send, o_recv, c_send, c_recv,
):
    me, dp = lax.axis_index("seq"), lax.axis_index("dp")
    tok = h_ref.shape[0]
    width = slice_ref.shape[2] // 3
    seq_bits = list(bits_high_first(n_seq))
    greet(
        [{"seq": me ^ bit} for bit in seq_bits]
        + [{"dp": lax.rem(dp + k, n_dp)} for k in range(1, n_dp)]
    )

    plan, arrival = [], {}
    order = [(0, bit) for bit in seq_bits]
    while order:
        place, bit = order.pop(0)
        copy = remote_later(
            h_ref if place == 0 else all_ref.at[me ^ place],
            all_ref.at[me ^ place],
            (h_send, h_recv),
            len(plan),
            {"seq": me ^ bit},
        )
        arrival[place ^ bit] = copy
        plan.append((place, copy))
        order += [(place ^ bit, low) for low in seq_bits if low < bit]
    for place, copy in plan:
        if place == 0:
            copy.start()

    for j in range(n_seq):

        @pl.when(me == j)
        def _():
            for c in range(3):
                left = c * width * n_seq + j * width
                slice_ref[dp, :, c * width : (c + 1) * width] = w_ref[:, left : left + width]

    small_buf[dp] = jnp.zeros(small_buf.shape[1:], bf16)
    small_buf[dp, 0:1, :] = again_ref[...]
    small_buf[dp, 1:2, :] = mgain_ref[...]
    small_buf[dp, 2:4, :] = vec_ref[...]
    small_buf[dp, 4:6, :] = mix_ref[0]
    small_buf[dp, 6:8, :] = mix_ref[1]
    small_buf[dp, 8 : 8 + H, :] = router_ref[...]
    small_copies, w_copies = [], []
    for k in range(1, n_dp):
        target = {"dp": lax.rem(dp + k, n_dp)}
        small_copies.append(
            remote(small_buf.at[dp], small_buf.at[dp], (s_send, s_recv), k, target)
        )
        w_copies.append(remote(slice_ref.at[dp], slice_ref.at[dp], (w_send, w_recv), k, target))
    cols = pl.ds(pl.multiple_of((me & 1) * (D // 2), D // 2), D // 2)
    wo_copies = [
        remote(
            wo_ref.at[:, cols], wo_all.at[dp, :, cols], (o_send, o_recv), k,
            {"dp": lax.rem(dp + k, n_dp)},
        )
        for k in range(1, n_dp)
    ]
    make_slots(route_ref, cot_ref, slot_ref, g_ref)
    for copy in small_copies:
        copy.wait()
    small_ref[...] = jnp.concatenate([small_buf[i].astype(f32) for i in range(n_dp)], axis=1)

    def normalize(block, ref):
        x = ref.astype(f32)
        mean_square = jnp.mean(x * x, axis=-1, keepdims=True)
        rows = pl.ds(pl.multiple_of(block * tok, tok), tok)
        attn_ref[rows, :] = (x * lax.rsqrt(mean_square + 1e-06) * small_ref[0:1]).astype(bf16)

    normalize(me, h_ref[...])
    for place in arrival:
        arrival[place].wait_recv()
        for source, copy in plan:
            if source == place:
                copy.start()
        normalize(me ^ place, all_ref[me ^ place])
    for copy in w_copies:
        copy.wait()
    wt_ref[...] = slice_ref[...].reshape(D, 3 * width).T
    half = HD // 2

    @pl.loop(0, attn_ref.shape[0] // BLK)
    def _(i):
        rows = pl.ds(pl.multiple_of(i * BLK, BLK), BLK)
        y = mm(wt_ref[...], attn_ref[rows, :], NT)
        cos, sin = cos_ref[:, rows], sin_ref[:, rows]
        for head in range(2 * width // HD):
            low, middle, high = head * HD, head * HD + half, (head + 1) * HD
            a, b = y[low:middle], y[middle:high]
            qkv_ref[low:middle, rows] = (a * cos - b * sin).astype(bf16)
            qkv_ref[middle:high, rows] = (a * sin + b * cos).astype(bf16)
        qkv_ref[2 * width :, rows] = y[2 * width :].astype(bf16)

    for copy in wo_copies:
        copy.wait()
    wo_all[dp, :, cols] = wo_ref[:, cols]
    trade = remote(
        wo_all.at[:, :, cols], wo_all.at[:, :, cols], (c_send, c_recv), 0, {"seq": me ^ 1}
    )
    for _, copy in plan:
        copy.wait_send()
    trade.wait()


def start_call(
    n_seq, n_dp, hidden, w_qkv, attn_gain, moe_gain, vec, mix, router, routes, cotangent, cos, sin,
    w_out,
):
    tok, shard = hidden.shape[0], w_qkv.shape[0]
    width3 = w_qkv.shape[1] // n_seq
    hops = n_seq - 1
    return pl.pallas_call(
        functools.partial(start_kernel, n_seq, n_dp),
        out_shape=(
            jax.ShapeDtypeStruct((n_seq * tok, D), bf16),
            jax.ShapeDtypeStruct((width3, n_seq * tok), bf16),
            jax.ShapeDtypeStruct((width3, D), bf16),
            jax.ShapeDtypeStruct((SMALL, D), f32),
            jax.ShapeDtypeStruct(routes.shape, jnp.int32),
            jax.ShapeDtypeStruct((E, CAP, D), bf16),
            jax.ShapeDtypeStruct((n_dp, shard, D), bf16),
        ),
        in_specs=[VMEM] * 12,
        out_specs=[VMEM] * 7,
        scratch_shapes=[
            pltpu.VMEM((n_seq, tok, D), bf16),
            pltpu.VMEM((n_dp, shard, width3), bf16),
            pltpu.VMEM((n_dp, SMALL, shard), bf16),
            DMA((hops,)),
            DMA((hops,)),
            DMA((n_dp,)),
            DMA((n_dp,)),
            DMA((n_dp,)),
            DMA((n_dp,)),
            DMA((n_dp,)),
            DMA((n_dp,)),
            DMA((1,)),
            DMA((1,)),
        ],
        compiler_params=pltpu.CompilerParams(collective_id=0, has_side_effects=True),
        name="start",
    )(
        hidden, w_qkv, attn_gain[None], moe_gain[None], vec, mix, router, routes, cotangent,
        cos, sin, w_out,
    )


def allowed_block(key_block, query_block, start_row):
    key_pos = key_block * BLK + lax.broadcasted_iota(jnp.int32, (BLK, BLK), 0)
    query_pos = query_block * BLK + lax.broadcasted_iota(jnp.int32, (BLK, BLK), 1)
    return (key_pos >= start_row) & (key_pos <= query_pos)


def attn_kernel(lo_ref, qkv_ref, start_ref, out_ref, exact_ref, log_ref, keys_ref):
    heads, seq_len, _ = keys_ref.shape
    width = heads * HD
    qb = pl.program_id(0)

    @pl.when(qb == 0)
    def _():
        for h in range(heads):
            keys_ref[h] = qkv_ref[width + h * HD : width + (h + 1) * HD, :].T

    here = pl.ds(pl.multiple_of(qb * BLK, BLK), BLK)
    start_row = start_ref[...]

    def step(kb, carry):
        there = pl.ds(pl.multiple_of(kb * BLK, BLK), BLK)
        allowed = allowed_block(kb, qb, start_row)
        new = []
        for h in range(heads):
            top, total, acc = carry[h]
            scores = mm(keys_ref[h, there, :], qkv_ref[h * HD : (h + 1) * HD, here], NN)
            scores = jnp.where(allowed, scores * score_scale, neg_large)
            new_top = jnp.maximum(top, jnp.max(scores, axis=0, keepdims=True))
            fade = jnp.exp2(top - new_top)
            weights = jnp.exp2(scores - new_top)
            total = total * fade + jnp.sum(weights, axis=0, keepdims=True)
            values = qkv_ref[2 * width + h * HD : 2 * width + (h + 1) * HD, there]
            acc = acc * fade + mm(values, weights.astype(bf16), NN)
            new.append((new_top, total, acc))
        return tuple(new)

    first = tuple(
        (
            jnp.full((1, BLK), neg_large, f32),
            jnp.zeros((1, BLK), f32),
            jnp.zeros((HD, BLK), f32),
        )
        for _ in range(heads)
    )
    done = lax.fori_loop(lo_ref[qb], qb + 1, step, first)
    for h in range(heads):
        top, total, acc = done[h]
        attended = acc / total
        exact_ref[h * HD : (h + 1) * HD, :] = attended
        out_ref[0, h * HD : (h + 1) * HD, :] = attended.astype(bf16)
        log_ref[h : h + 1, :] = top + jnp.log2(total)


def attn_call(lows, qkv, start_row, tok):
    width3, seq_len = qkv.shape
    width = width3 // 3
    heads = width // HD
    per = tok // BLK
    return pl.pallas_call(
        attn_kernel,
        out_shape=(
            jax.ShapeDtypeStruct((seq_len // tok, width, tok), bf16),
            jax.ShapeDtypeStruct((width, seq_len), f32),
            jax.ShapeDtypeStruct((heads, seq_len), f32),
        ),
        grid_spec=pltpu.PrefetchScalarGridSpec(
            num_scalar_prefetch=1,
            grid=(seq_len // BLK,),
            in_specs=[
                pl.BlockSpec((width3, seq_len), lambda i, lo: (0, 0)),
                pl.BlockSpec((1, BLK), lambda i, lo: (0, i)),
            ],
            out_specs=[
                pl.BlockSpec((1, width, BLK), lambda i, lo: (i // per, 0, i % per)),
                pl.BlockSpec((width, BLK), lambda i, lo: (0, i)),
                pl.BlockSpec((heads, BLK), lambda i, lo: (0, i)),
            ],
            scratch_shapes=[pltpu.VMEM((heads, seq_len, HD), bf16)],
        ),
        cost_estimate=pl.CostEstimate(
            flops=16_000_000_000, transcendentals=0, bytes_accessed=16_000_000
        ),
        name="attend",
    )(lows, qkv, start_row)


def attn_back_kernel(
    lo_ref, qkv_ref, go_ref, exact_ref, log_ref, start_ref, cos_ref, sin_ref, out_ref,
    keys_ref, values_ref, dk_ref, dv_ref,
):
    heads, seq_len, _ = keys_ref.shape
    width = heads * HD
    half = HD // 2
    qb = pl.program_id(0)

    @pl.when(qb == 0)
    def _():
        for h in range(heads):
            keys_ref[h] = qkv_ref[width + h * HD : width + (h + 1) * HD, :].T
            values_ref[h] = qkv_ref[2 * width + h * HD : 2 * width + (h + 1) * HD, :].T
        dk_ref[...] = jnp.zeros_like(dk_ref)
        dv_ref[...] = jnp.zeros_like(dv_ref)

    here = pl.ds(pl.multiple_of(qb * BLK, BLK), BLK)
    start_row = start_ref[...]
    grad = go_ref[0]
    deltas = [
        jnp.sum(
            exact_ref[h * HD : (h + 1) * HD, :] * grad[h * HD : (h + 1) * HD].astype(f32),
            axis=0,
            keepdims=True,
        )
        for h in range(heads)
    ]

    def step(kb, carry):
        there = pl.ds(pl.multiple_of(kb * BLK, BLK), BLK)
        allowed = allowed_block(kb, qb, start_row)
        new = []
        for h in range(heads):
            rows = slice(h * HD, (h + 1) * HD)
            queries = qkv_ref[rows, here]
            scores = mm(keys_ref[h, there, :], queries, NN)
            scores = jnp.where(allowed, scores * score_scale, neg_large)
            probs = jnp.exp2(scores - log_ref[h : h + 1, :])
            grad_probs = mm(values_ref[h, there, :], grad[rows], NN)
            grad_scores = (probs * (grad_probs - deltas[h])).astype(bf16)
            dv_ref[rows, there] += mm(grad[rows], probs.astype(bf16), NT)
            dk_ref[rows, there] += mm(queries, grad_scores, NT)
            keys = qkv_ref[width + h * HD : width + (h + 1) * HD, there]
            new.append(carry[h] + mm(keys, grad_scores, NN))
        return tuple(new)

    grads = lax.fori_loop(
        lo_ref[qb], qb + 1, step, tuple(jnp.zeros((HD, BLK), f32) for _ in range(heads))
    )

    def turn_back(value, cos, sin):
        value = value.astype(bf16).astype(f32)
        a, b = value[:half], value[half:]
        return (a * cos + b * sin).astype(bf16), (b * cos - a * sin).astype(bf16)

    for h in range(heads):
        a, b = turn_back(grads[h] * 0.125, cos_ref[:, here], sin_ref[:, here])
        out_ref[h * HD : h * HD + half, here] = a
        out_ref[h * HD + half : (h + 1) * HD, here] = b

    @pl.when(qb == pl.num_programs(0) - 1)
    def _():
        cos, sin = cos_ref[...], sin_ref[...]
        for h in range(heads):
            a, b = turn_back(dk_ref[h * HD : (h + 1) * HD, :] * 0.125, cos, sin)
            out_ref[width + h * HD : width + h * HD + half, :] = a
            out_ref[width + h * HD + half : width + (h + 1) * HD, :] = b
        out_ref[2 * width :, :] = dv_ref[...].astype(bf16)


def attn_back_call(lows, qkv, grad_out, exact, logs, start_row, cos_t, sin_t):
    width3, seq_len = qkv.shape
    width = width3 // 3
    heads = width // HD
    per = grad_out.shape[2] // BLK
    return pl.pallas_call(
        attn_back_kernel,
        out_shape=jax.ShapeDtypeStruct((width3, seq_len), bf16),
        grid_spec=pltpu.PrefetchScalarGridSpec(
            num_scalar_prefetch=1,
            grid=(seq_len // BLK,),
            in_specs=[
                pl.BlockSpec((width3, seq_len), lambda i, lo: (0, 0)),
                pl.BlockSpec((1, width, BLK), lambda i, lo: (i // per, 0, i % per)),
                pl.BlockSpec((width, BLK), lambda i, lo: (0, i)),
                pl.BlockSpec((heads, BLK), lambda i, lo: (0, i)),
                pl.BlockSpec((1, BLK), lambda i, lo: (0, i)),
                pl.BlockSpec((HD // 2, seq_len), lambda i, lo: (0, 0)),
                pl.BlockSpec((HD // 2, seq_len), lambda i, lo: (0, 0)),
            ],
            out_specs=pl.BlockSpec((width3, seq_len), lambda i, lo: (0, 0)),
            scratch_shapes=[
                pltpu.VMEM((heads, seq_len, HD), bf16),
                pltpu.VMEM((heads, seq_len, HD), bf16),
                pltpu.VMEM((width, seq_len), f32),
                pltpu.VMEM((width, seq_len), f32),
            ],
        ),
        cost_estimate=pl.CostEstimate(
            flops=16_000_000_000, transcendentals=0, bytes_accessed=16_000_000
        ),
        name="attend_back",
    )(lows, qkv, grad_out, exact, logs, start_row, cos_t, sin_t)


def moe_kernel(n_dp, n_cross, x_ref, gate_ref, w_hbm, g_ref, *refs):
    piece_ref, dots_ref, out_ref, refs = refs[0], refs[1], refs[2], refs[3:]
    units = w_hbm.shape[1]
    tile = min(TILE, units)
    tiles = units // UNITS // 2
    sum_hbm, refs = refs[:tiles], refs[tiles:]
    far_refs, refs = refs[:n_cross], refs[n_cross:]
    (
        w_ref, x_in, gate_in, gs_ref, hid_ref, gg_ref, gu_ref, piece_out,
        dot_out, dw_out, dw_in, dw_keep, w_sem, x_send, x_recv, t_send, t_recv, p_send, p_recv,
        d_send, d_recv, c_send, c_recv, f_send, f_recv, keep_sem,
    ) = refs
    me, dp = lax.axis_index("seq"), lax.axis_index("dp")
    owners = n_dp // E
    pairs = n_dp // 2
    greet([{"dp": dp ^ k} for k in range(1, n_dp)] + [{"seq": me ^ 1}, {"seq": me ^ 2}])

    def x_copy(k):
        return remote_later(
            x_ref.at[(dp ^ k) // owners], x_in.at[k], (x_send, x_recv), k, {"dp": dp ^ k}
        )

    def gate_copy(k):
        return remote_later(
            gate_ref.at[(dp ^ k) // owners], gate_in.at[k], (t_send, t_recv), k, {"dp": dp ^ k}
        )

    def piece_copy(k):
        return remote_later(
            piece_out.at[k], piece_ref.at[dp], (p_send, p_recv), k, {"dp": dp ^ k}
        )

    def dot_copy(k):
        return remote_later(dot_out.at[k], dots_ref.at[dp], (d_send, d_recv), k, {"dp": dp ^ k})

    def core_copy(t):
        return remote_later(dw_out.at[t], dw_in.at[t], (c_send, c_recv), t, {"seq": me ^ 1})

    def far_copy(t):
        return remote_later(dw_keep.at[t], far_refs[t], (f_send, f_recv), t, {"seq": me ^ 2})

    for p in [0, pairs - 1, *range(1, pairs - 1)]:
        for k in (2 * p, 2 * p + 1):
            if k:
                gate_copy(k).start()
                x_copy(k).start()
    loads = [pltpu.make_async_copy(w_hbm.at[j], w_ref.at[j], w_sem.at[j]) for j in range(3)]
    loads.append(pltpu.make_async_copy(x_ref.at[dp // owners], x_in.at[0], w_sem.at[3]))
    for load in loads:
        load.start()
    gate_in[0] = gate_ref[dp // owners]
    for load in loads:
        load.wait()

    @pl.loop(0, pairs)
    def _(i):
        p = jnp.where(i == 0, 0, 1 + lax.rem(i + pairs - 3, pairs - 1))
        rows = pl.ds(pl.multiple_of(p * PAIR, PAIR), PAIR)

        def arrive(k):
            x_copy(k).wait_recv()
            gate_copy(k).wait_recv()

        @pl.when(p > 0)
        def _():
            arrive(2 * p)

        arrive(2 * p + 1)
        for side in range(2):
            k = 2 * p + side
            column = jnp.broadcast_to(gate_in[k], (CAP, CAP)).T[:, 0:1]
            here = pl.ds(pl.multiple_of(k * CAP, CAP), CAP)
            gs_ref[here] = (g_ref[dp ^ k].astype(f32) * column).astype(bf16)

        @pl.loop(0, units // tile)
        def _(t):
            part = pl.ds(pl.multiple_of(t * tile, tile), tile)
            x = x_in[pl.ds(2 * p, 2)].reshape(PAIR, D)
            gate_pre = mm(x, w_ref[0, part], NT)
            up_pre = mm(x, w_ref[1, part], NT)
            grad_hidden = mm(gs_ref[rows], w_ref[2, part], NT)
            sig = 1.0 / (1.0 + jnp.exp(-gate_pre))
            silu = gate_pre * sig
            hid_ref[rows, part] = (silu * up_pre).astype(bf16)
            gu_ref[rows, part] = (grad_hidden * silu).astype(bf16)
            gg_ref[rows, part] = (
                grad_hidden * up_pre * sig * (1.0 + gate_pre * (1.0 - sig))
            ).astype(bf16)

        pieces = mm(gg_ref[rows], w_ref[0], NN) + mm(gu_ref[rows], w_ref[1], NN)
        piece_out[pl.ds(2 * p, 2)] = pieces.astype(bf16).reshape(2, CAP, D)
        piece_copy(2 * p + 1).start()

        @pl.when(p > 0)
        def _():
            piece_copy(2 * p).start()

        outs = mm(hid_ref[rows], w_ref[2], NN)
        for side in range(2):
            k = 2 * p + side
            out = outs[side * CAP : (side + 1) * CAP].astype(bf16)
            out_ref[dp ^ k] = out
            product = out.astype(f32) * g_ref[dp ^ k].astype(f32)
            dot_out[k] = column_to_row(jnp.sum(product, axis=1, keepdims=True))
        dot_copy(2 * p + 1).start()

        @pl.when(p > 0)
        def _():
            dot_copy(2 * p).start()

    piece_ref[dp] = piece_out[0]
    dots_ref[dp] = dot_out[0]
    core = me & 1

    def weight_grad(half, t, ref):
        part = pl.ds(pl.multiple_of((half * tiles + t) * UNITS, UNITS), UNITS)
        x_all = x_in[...].reshape(n_dp * CAP, D)
        ref[0] = mm(gg_ref[:, part], x_all, TN).astype(ref.dtype)
        ref[1] = mm(gu_ref[:, part], x_all, TN).astype(ref.dtype)
        ref[2] = mm(hid_ref[:, part], gs_ref[...], TN).astype(ref.dtype)

    @pl.loop(0, tiles)
    def _(t):
        weight_grad(1 - core, t, dw_out.at[t])
        core_copy(t).start()
        weight_grad(core, t, dw_keep.at[t])
        core_copy(t).wait_recv()
        dw_keep[t] = (dw_keep[t].astype(f32) + dw_in[t].astype(f32)).astype(bf16)
        for c in range(n_cross):

            @pl.when(t == c)
            def _():
                far_copy(c).start()

    keeps = [
        pltpu.make_async_copy(dw_keep.at[t], sum_hbm[t], keep_sem.at[t]) for t in range(tiles)
    ]
    for keep in keeps:
        keep.start()
    for k in range(1, n_dp):
        piece_copy(k).wait()
        dot_copy(k).wait()
        x_copy(k).wait_send()
        gate_copy(k).wait_send()
    for t in range(n_cross):
        far_copy(t).wait()
    for t in range(tiles):
        core_copy(t).wait_send()
    for keep in keeps:
        keep.wait()


def moe_call(n_dp, n_cross, x_slots, gate_slots, weights, grads):
    units = weights.shape[1]
    rows = n_dp * CAP
    tiles = units // UNITS // 2
    part = (3, UNITS, D)
    outs = pl.pallas_call(
        functools.partial(moe_kernel, n_dp, n_cross),
        out_shape=(
            jax.ShapeDtypeStruct((n_dp, CAP, D), bf16),
            jax.ShapeDtypeStruct((n_dp, 1, CAP), f32),
            jax.ShapeDtypeStruct((n_dp, CAP, D), bf16),
        )
        + (jax.ShapeDtypeStruct(part, bf16),) * (tiles + n_cross),
        in_specs=[HBM, VMEM, HBM, VMEM],
        out_specs=[VMEM] * 3 + [HBM] * tiles + [VMEM] * n_cross,
        scratch_shapes=[
            pltpu.VMEM(weights.shape, bf16),
            pltpu.VMEM((n_dp, CAP, D), bf16),
            pltpu.VMEM((n_dp, 1, CAP), f32),
            pltpu.VMEM((rows, D), bf16),
            pltpu.VMEM((rows, units), bf16),
            pltpu.VMEM((rows, units), bf16),
            pltpu.VMEM((rows, units), bf16),
            pltpu.VMEM((n_dp, CAP, D), bf16),
            pltpu.VMEM((n_dp, 1, CAP), f32),
            pltpu.VMEM((tiles, *part), bf16),
            pltpu.VMEM((tiles, *part), bf16),
            pltpu.VMEM((tiles, *part), bf16),
            DMA((4,)),
        ]
        + [DMA((n_dp,))] * 8
        + [DMA((tiles,))] * 2
        + [DMA((max(n_cross, 1),))] * 2
        + [DMA((tiles,))],
        compiler_params=pltpu.CompilerParams(
            collective_id=4, has_side_effects=True, vmem_limit_bytes=67043328
        ),
        name="experts",
    )(x_slots, gate_slots, weights, grads)
    return outs[0], outs[1], outs[2], outs[3 : 3 + tiles], outs[3 + tiles :]


def mid_kernel(
    n_seq, att_ref, h_ref, prev_ref, carry_ref, small_ref, slot_ref, route_ref, w_ref,
    heads_ref, mid_ref, gate_ref, x_ref, gs_ref, send_sem, recv_sem,
):
    me = lax.axis_index("seq")
    tok = h_ref.shape[0]
    greet([{"seq": me ^ place} for place in range(1, n_seq)])
    copies = [
        remote(
            att_ref.at[me ^ place], heads_ref.at[me], (send_sem, recv_sem), place,
            {"seq": me ^ place},
        )
        for place in range(1, n_seq)
    ]
    heads_ref[me] = att_ref[me]
    picks = picks_of(slot_ref)
    pick_any = picks[0] + picks[1]
    carried = lax.dot_general(
        carry_ref[...].astype(f32), prev_ref[:, 0, :], TN, precision=exact_prec,
        preferred_element_type=f32,
    )
    for copy in copies:
        copy.wait_recv()
    attn_out = mm(heads_ref[...].reshape(D, tok), w_ref[...].reshape(D, D), TN)
    resid = h_ref[...].astype(f32) + attn_out
    mid_ref[...] = resid
    rate = lax.rsqrt(jnp.mean(resid * resid, axis=-1, keepdims=True) + 1e-06)
    normed = resid * rate * small_ref[1:2]
    low = normed.astype(bf16)
    x_ref[...] = mm(pick_any, low, NN).astype(bf16).reshape(x_ref.shape)
    heads_rows = small_ref[4 : 8 + H].astype(bf16)
    products = mm(heads_rows, low, NT)
    rest = mm(heads_rows, (normed - low.astype(f32)).astype(bf16), NT)
    logits = products[4:] + carried
    ids = lax.broadcasted_iota(jnp.int32, (H, tok), 0)
    chosen = [
        jnp.sum(jnp.where(route_ref[k : k + 1, :] == ids, logits, 0.0), axis=0, keepdims=True)
        for k in range(2)
    ]
    top = jnp.maximum(chosen[0], chosen[1])
    exps = [jnp.exp(c - top) for c in chosen]
    total = exps[0] + exps[1]
    gates = [e / total for e in exps]
    gate_ref[...] = jnp.concatenate(
        [gates[0], gates[1], products[:4] + rest[:4], jnp.zeros((2, tok), f32)], axis=0
    )
    slot_gates = sum(unsplit(mm(split(gates[k]), picks[k], NT)) for k in range(2))
    for e in range(E):
        gs_ref[e] = slot_gates[:, e * CAP : (e + 1) * CAP]
    for copy in copies:
        copy.wait_send()


def mid_call(n_seq, attended, hidden, prev, carry, small, slot_of, routes, w_out):
    tok, width = hidden.shape[0], attended.shape[1]
    return pl.pallas_call(
        functools.partial(mid_kernel, n_seq),
        out_shape=(
            jax.ShapeDtypeStruct((n_seq, width, tok), bf16),
            jax.ShapeDtypeStruct((tok, D), f32),
            jax.ShapeDtypeStruct((8, tok), f32),
            jax.ShapeDtypeStruct((E, CAP, D), bf16),
            jax.ShapeDtypeStruct((E, 1, CAP), f32),
        ),
        in_specs=[VMEM] * 8,
        out_specs=[VMEM] * 5,
        scratch_shapes=[DMA((n_seq,)), DMA((n_seq,))],
        compiler_params=pltpu.CompilerParams(collective_id=2, has_side_effects=True),
        name="mid",
    )(attended, hidden, prev, carry, small, slot_of, routes, w_out)


def mid_back_kernel(
    n_seq, n_dp, piece_ref, dots_ref, cot_ref, mid_ref, gate_ref, slot_ref, route_ref,
    small_ref, heads_ref, w_ref, prev_ref, carry_ref,
    resid_ref, go_ref, base_ref, dprev_ref, pack_ref, wo_sum_ref,
    gh_ref, wo_ref, wo_in, a_send, a_recv, c_send, c_recv,
):
    me = lax.axis_index("seq")
    tok = cot_ref.shape[0]
    width = heads_ref.shape[1]
    owners = n_dp // E
    pairs = n_seq // 2
    greet([{"seq": me ^ place} for place in range(1, n_seq)])
    cot = cot_ref[...]
    grad_top = cot.astype(f32)
    resid_mid = mid_ref[...]
    gain = small_ref[1:2]
    rate = lax.rsqrt(jnp.mean(resid_mid * resid_mid, axis=-1, keepdims=True) + 1e-06)
    normed = resid_mid * rate * gain
    low = normed.astype(bf16)
    picks = picks_of(slot_ref)
    gates = [gate_ref[k : k + 1, :] for k in range(2)]
    routes = [route_ref[k : k + 1, :] for k in range(2)]
    normed_dot = column_to_row(jnp.sum(grad_top * normed, axis=1, keepdims=True))
    vecs = small_ref[2:4].astype(bf16)
    vec_dot = mm(vecs, cot, NT)
    alphas, const_dot = [], []
    for j in range(2):
        pair = [gate_ref[2 + 2 * j + c : 3 + 2 * j + c, :] for c in range(2)]
        top = jnp.maximum(pair[0], pair[1])
        exps = [jnp.exp(p - top) for p in pair]
        total = exps[0] + exps[1]
        alphas.append([e / total for e in exps])
        const_dot.append(alphas[j][0] * normed_dot + alphas[j][1] * vec_dot[j : j + 1])
    slot_dots = split(
        jnp.concatenate(
            [sum(dots_ref[e * owners + o] for o in range(owners)) for e in range(E)], axis=1
        )
    )
    out_dots = []
    for k in range(2):
        value = unsplit(mm(slot_dots, picks[k], NN))
        value = value + jnp.where(routes[k] == E + 1, normed_dot, 0.0)
        for j in range(2):
            value = value + jnp.where(routes[k] == E + 2 + j, const_dot[j], 0.0)
        out_dots.append(value)
    mean_dot = gates[0] * out_dots[0] + gates[1] * out_dots[1]
    ids = lax.broadcasted_iota(jnp.int32, (H, tok), 0)
    grad_logits = sum(
        jnp.where(routes[k] == ids, gates[k] * (out_dots[k] - mean_dot), 0.0) for k in range(2)
    )

    def gate_of(expert):
        return sum(jnp.where(routes[k] == expert, gates[k], 0.0) for k in range(2))

    const_gate = [gate_of(E + 2 + j) for j in range(2)]
    normed_gate = gate_of(E + 1) + sum(const_gate[j] * alphas[j][0] for j in range(2))
    vec_gate = split(jnp.concatenate([const_gate[j] * alphas[j][1] for j in range(2)], axis=0))
    mix_grads = []
    for j in range(2):
        terms = [normed_dot, vec_dot[j : j + 1]]
        for c in range(2):
            mix_grads.append(const_gate[j] * alphas[j][c] * (terms[c] - const_dot[j]))
    token_rows = split(jnp.concatenate(mix_grads + [grad_logits], axis=0))
    normed_column = jnp.broadcast_to(normed_gate, (8, tok)).T[:, 0:1]
    heads_rows = small_ref[4 : 8 + H].astype(bf16)
    pick_any = picks[0] + picks[1]
    grad_normed = grad_top * normed_column
    grad_normed = grad_normed + mm(
        token_rows, jnp.concatenate([heads_rows] * 3, axis=0), TN
    )
    pieces = piece_ref[...].reshape(E, owners, CAP, D)
    for o in range(owners):
        grad_normed = grad_normed + mm(pick_any, pieces[:, o].reshape(E * CAP, D), TN)
    grad_resid = grad_top + norm_back(resid_mid, gain, grad_normed)
    resid_ref[...] = grad_resid
    grad_attn = grad_resid.astype(bf16)
    gh_ref[...] = mm(w_ref[...].reshape(D, D), grad_attn, NT).astype(bf16).reshape(gh_ref.shape)
    copies = [
        remote(gh_ref.at[me ^ place], go_ref.at[me], (a_send, a_recv), place, {"seq": me ^ place})
        for place in range(1, n_seq)
    ]
    go_ref[me] = gh_ref[me]
    grad_w = mm(heads_ref[...].reshape(D, tok), grad_attn, NN)
    for j in range(n_seq):
        wo_ref[j] = grad_w[:, j * width : (j + 1) * width].astype(bf16)
    core_copies = [
        remote(wo_ref.at[me ^ (2 * i + 1)], wo_in.at[i], (c_send, c_recv), i, {"seq": me ^ 1})
        for i in range(pairs)
    ]
    base_ref[...] = (
        resid_mid
        + normed * normed_column
        + mm(vec_gate, jnp.concatenate([vecs] * 3, axis=0), TN)
    )
    dprev_ref[:, 0, :] = lax.dot_general(
        carry_ref[...].astype(f32), grad_logits, NN, precision=exact_prec,
        preferred_element_type=f32,
    )
    rest = (normed - low.astype(f32)).astype(bf16)
    row_sums = unsplit(mm(token_rows, low, NN))
    mix_sums = row_sums[:4] + unsplit(mm(token_rows, rest, NN))[:4]
    vec_sums = unsplit(mm(vec_gate, cot, NN))
    gain_sum = jnp.sum(grad_normed * resid_mid * rate, axis=0, keepdims=True)
    carry_grad = lax.dot_general(
        prev_ref[:, 0, :], grad_logits, NT, precision=exact_prec, preferred_element_type=f32
    )
    packed = jnp.concatenate([mix_sums, row_sums[4:], vec_sums, gain_sum], axis=0)
    lines, shard = packed.shape[0], D // n_dp
    for i in range(n_dp):
        pack_ref[i] = jnp.zeros(pack_ref.shape[1:], f32)
        pack_ref[i, 0:lines, :] = packed[:, i * shard : (i + 1) * shard]
        pack_ref[i, 24 : 24 + H, 0:H] = carry_grad
    for i in range(pairs):
        core_copies[i].wait_recv()
        wo_sum_ref[i] = (
            wo_ref[me ^ (2 * i)].astype(f32) + wo_in[i].astype(f32)
        ).astype(bf16)
    for copy in copies:
        copy.wait()
    for copy in core_copies:
        copy.wait_send()


def mid_back_call(
    n_seq, n_dp, piece, dots, cot, mid, gates, slot_of, routes, small, heads, w, prev, carry
):
    tok, width = cot.shape[0], heads.shape[1]
    pairs = n_seq // 2
    return pl.pallas_call(
        functools.partial(mid_back_kernel, n_seq, n_dp),
        out_shape=(
            jax.ShapeDtypeStruct((tok, D), f32),
            jax.ShapeDtypeStruct((n_seq, width, tok), bf16),
            jax.ShapeDtypeStruct((tok, D), f32),
            jax.ShapeDtypeStruct((H, 1, tok), f32),
            jax.ShapeDtypeStruct((n_dp, LINES, D // n_dp), f32),
            jax.ShapeDtypeStruct((pairs, D, width), bf16),
        ),
        in_specs=[VMEM] * 12,
        out_specs=[VMEM] * 6,
        scratch_shapes=[
            pltpu.VMEM((n_seq, width, tok), bf16),
            pltpu.VMEM((n_seq, D, width), bf16),
            pltpu.VMEM((pairs, D, width), bf16),
            DMA((n_seq,)),
            DMA((n_seq,)),
            DMA((pairs,)),
            DMA((pairs,)),
        ],
        compiler_params=pltpu.CompilerParams(collective_id=3, has_side_effects=True),
        name="mid_back",
    )(piece, dots, cot, mid, gates, slot_of, routes, small, heads, w, prev, carry)


def tail_kernel(
    n_seq, n_dp, tiles, g_ref, wt_ref, wo_ref, pack_ref, gate_ref, slot_ref, gain_ref,
    a_hbm, h_hbm, resid_hbm, base_hbm, out_hbm, *refs,
):
    sum_hbm, refs = refs[:tiles], refs[tiles:]
    n_far = tiles - 1
    far_hbm, refs = refs[:n_far], refs[n_far:]
    din_ref, row_in, line_ref, block_ref, both_ref, refs = *refs[:5], refs[5:]
    (
        a_ref, h_ref, resid_ref, base_ref, rows_ref, far_ref, sum_ref, fin_ref,
        core_out, core_in, x_out, x_in, part_ref, w_out_buf, w_in, wo_buf, wo_in, wo_x, wo_far,
        row_buf, pack_in, line_buf, line_in, load_sem, c_sems, x_sems, w_sems, r_sems, o_sems,
        p_sems, q_sems, l_sems, t_sems, f_sems, keep_sem,
    ) = refs
    me, dp = lax.axis_index("seq"), lax.axis_index("dp")
    tok = h_ref.shape[0]
    shard, width3 = w_in.shape[1], w_in.shape[2]
    width = width3 // 3
    owners = n_dp // E
    pairs = n_seq // 2
    others = range(1, n_dp)

    def both(sems):
        return sems.at[0], sems.at[1]

    c_sems, x_sems, w_sems, r_sems, o_sems, p_sems, q_sems, l_sems, t_sems, f_sems = (
        both(sems)
        for sems in (
            c_sems, x_sems, w_sems, r_sems, o_sems, p_sems, q_sems, l_sems, t_sems, f_sems
        )
    )

    loads = []
    for src, dst in [
        (a_hbm, a_ref), (out_hbm, rows_ref), (base_hbm, base_ref), (h_hbm, h_ref),
        (resid_hbm, resid_ref),
    ] + [(far_hbm[t], far_ref.at[t]) for t in range(n_far)] + [
        (sum_hbm[t], sum_ref.at[t]) for t in range(n_far)
    ]:
        load = pltpu.make_async_copy(src, dst, load_sem.at[len(loads)])
        load.start()
        loads.append(load)
    greet(
        [{"seq": me ^ place} for place in range(1, n_seq)]
        + [{"dp": lax.rem(dp + k, n_dp)} for k in others]
    )

    def there(k):
        return lax.rem(dp + k, n_dp)

    def term(place):
        columns = pl.ds(pl.multiple_of((me ^ place) * tok, tok), tok)
        return mm(g_ref[:, columns], wt_ref[...], TN)

    last, cut = sum_hbm[tiles - 1], UNITS // 2
    tile_copies = []

    def send_part(i):
        part = pl.ds(i * cut, cut)
        tile_copies.append(
            remote(last.at[:, part], far_ref.at[tiles - 1, :, part], t_sems, i, {"seq": me ^ 2})
        )

    send_part(0)
    last_load = pltpu.make_async_copy(last, sum_ref.at[tiles - 1], load_sem.at[len(loads)])
    last_load.start()
    pack_copies = [
        remote(pack_ref.at[there(k)], pack_in.at[dp], p_sems, k, {"dp": there(k)}) for k in others
    ]
    pack_in[dp] = pack_ref[dp]
    for i in range(pairs):
        wo_buf[:, :, i * width : (i + 1) * width] = wo_ref[i].reshape(n_dp, shard, width)
    wo_in[dp] = wo_buf[dp]
    wo_copies = [
        remote(wo_buf.at[there(k)], wo_in.at[dp], q_sems, k, {"dp": there(k)}) for k in others
    ]
    core_copies = []
    for i in range(pairs - 1, -1, -1):
        core_out[i] = term(2 * i + 1).astype(bf16)
        core_copies.insert(0, remote(core_out.at[i], core_in.at[i], c_sems, i, {"seq": me ^ 1}))
    x_copies = []
    for i in range(pairs - 1, 0, -1):
        part = term(2 * i)
        core_copies[i].wait_recv()
        x_out[i - 1] = (part + core_in[i].astype(f32)).astype(bf16)
        x_copies.append(
            remote(x_out.at[i - 1], x_in.at[i - 1], x_sems, i - 1, {"seq": me ^ (2 * i)})
        )
    send_part(1)
    loads[0].wait()
    turned = mm(g_ref[...], a_ref[...], NN)
    w_out_buf[...] = turned.T.astype(bf16).reshape(n_dp, shard, width3)
    w_in[dp] = w_out_buf[dp]
    w_copies = [
        remote(w_out_buf.at[there(k)], w_in.at[dp], w_sems, k, {"dp": there(k)}) for k in others
    ]
    part = term(0)
    core_copies[0].wait_recv()
    part_ref[...] = part + core_in[0].astype(f32)

    for copy in pack_copies:
        copy.wait_recv()
    line_buf[...] = jnp.sum(pack_in[...], axis=0)
    line_in[me] = line_buf[...]
    line_copies = [
        remote(line_buf, line_in.at[me], l_sems, place, {"seq": me ^ place})
        for place in range(1, n_seq)
    ]

    fin_copies, keeps = [], []

    def finish(t):
        fin_ref[t] = (sum_ref[t].astype(f32) + far_ref[t].astype(f32)).astype(bf16)
        fin_copies.append(remote(fin_ref.at[t], both_ref.at[1, t], f_sems, t, {"seq": me ^ 1}))
        keep = pltpu.make_async_copy(fin_ref.at[t], both_ref.at[0, t], keep_sem.at[t])
        keep.start()
        keeps.append(keep)

    for t in range(n_far):
        loads[5 + t].wait()
        loads[5 + n_far + t].wait()
        finish(t)

    for copy in wo_copies:
        copy.wait_recv()
    wo_total = jnp.sum(wo_in[...].astype(f32), axis=0)
    wo_cross = []
    for i in range(1, pairs):
        wo_x[i - 1] = wo_total[:, i * width : (i + 1) * width].astype(bf16)
        wo_cross.append(
            remote(wo_x.at[i - 1], wo_far.at[i - 1], o_sems, i - 1, {"seq": me ^ (2 * i)})
        )

    loads[1].wait()
    loads[2].wait()
    picks = picks_of(slot_ref)
    rows = rows_ref[...].reshape(E, owners, CAP, D)
    columns = gate_ref[...].T
    block = base_ref[...]
    for k in range(2):
        picked = sum(
            mm(picks[k], rows[:, o].reshape(E * CAP, D), TN) for o in range(owners)
        )
        block = block + columns[:, k : k + 1] * picked
    block_ref[...] = block.astype(bf16)

    for copy in x_copies:
        copy.wait_recv()
    grad = part_ref[...]
    for i in range(pairs - 1):
        grad = grad + x_in[i].astype(f32)
    loads[3].wait()
    loads[4].wait()
    din_ref[...] = resid_ref[...] + norm_back(h_ref[...].astype(f32), gain_ref[0:1], grad)

    for copy in w_copies + wo_cross:
        copy.wait_recv()
    row_buf[:, :width3] = jnp.sum(w_in[...].astype(f32), axis=0).astype(bf16)
    wo_mine = wo_total[:, :width]
    for i in range(pairs - 1):
        wo_mine = wo_mine + wo_far[i].astype(f32)
    row_buf[:, width3:] = wo_mine.astype(bf16)
    row_in[me] = row_buf[...]
    row_copies = [
        remote(row_buf, row_in.at[me], r_sems, place, {"seq": me ^ place})
        for place in range(1, n_seq)
    ]
    for copy in line_copies:
        copy.wait_recv()
    line_ref[...] = jnp.sum(line_in[...], axis=0)
    last_load.wait()
    for copy in tile_copies:
        copy.wait_recv()
    finish(tiles - 1)
    for copy in row_copies + fin_copies:
        copy.wait_recv()
    for copy in (
        core_copies + w_copies + x_copies + row_copies + wo_copies + pack_copies
        + line_copies + wo_cross + tile_copies + fin_copies
    ):
        copy.wait_send()
    for keep in keeps:
        keep.wait()


def tail_call(
    n_seq, n_dp, grad_qkv, w_turned, wo_sum, pack, gates, slot_of, small,
    attn_in, hidden, grad_resid, base, back_out, sums, far,
):
    tok = hidden.shape[0]
    shard, width3 = D // n_dp, grad_qkv.shape[0]
    width = width3 // 3
    pairs = n_seq // 2
    tiles = len(sums)
    part = sums[0].shape
    return pl.pallas_call(
        functools.partial(tail_kernel, n_seq, n_dp, tiles),
        out_shape=(
            jax.ShapeDtypeStruct((tok, D), f32),
            jax.ShapeDtypeStruct((n_seq, shard, width3 + width), bf16),
            jax.ShapeDtypeStruct((LINES, shard), f32),
            jax.ShapeDtypeStruct((tok, D), bf16),
            jax.ShapeDtypeStruct((2, tiles, *part), bf16),
        ),
        in_specs=[VMEM] * 7 + [HBM] * (5 + tiles + len(far)),
        out_specs=[VMEM] * 4 + [HBM],
        scratch_shapes=[
            pltpu.VMEM((n_seq * tok, D), bf16),
            pltpu.VMEM((tok, D), bf16),
            pltpu.VMEM((tok, D), f32),
            pltpu.VMEM((tok, D), f32),
            pltpu.VMEM((n_dp, CAP, D), bf16),
            pltpu.VMEM((tiles, *part), bf16),
            pltpu.VMEM((tiles, *part), bf16),
            pltpu.VMEM((tiles, *part), bf16),
            pltpu.VMEM((pairs, tok, D), bf16),
            pltpu.VMEM((pairs, tok, D), bf16),
            pltpu.VMEM((pairs - 1, tok, D), bf16),
            pltpu.VMEM((pairs - 1, tok, D), bf16),
            pltpu.VMEM((tok, D), f32),
            pltpu.VMEM((n_dp, shard, width3), bf16),
            pltpu.VMEM((n_dp, shard, width3), bf16),
            pltpu.VMEM((n_dp, shard, pairs * width), bf16),
            pltpu.VMEM((n_dp, shard, pairs * width), bf16),
            pltpu.VMEM((pairs - 1, shard, width), bf16),
            pltpu.VMEM((pairs - 1, shard, width), bf16),
            pltpu.VMEM((shard, width3 + width), bf16),
            pltpu.VMEM((n_dp, LINES, shard), f32),
            pltpu.VMEM((LINES, shard), f32),
            pltpu.VMEM((n_seq, LINES, shard), f32),
            DMA((4 + 2 * tiles,)),
            DMA((2, pairs)),
            DMA((2, pairs)),
            DMA((2, n_dp)),
            DMA((2, n_seq)),
            DMA((2, pairs)),
            DMA((2, n_dp)),
            DMA((2, n_dp)),
            DMA((2, n_seq)),
            DMA((2, 2)),
            DMA((2, tiles)),
            DMA((tiles,)),
        ],
        compiler_params=pltpu.CompilerParams(
            collective_id=1, has_side_effects=True, vmem_limit_bytes=67043328
        ),
        name="tail",
    )(
        grad_qkv, w_turned, wo_sum, pack, gates, slot_of, small,
        attn_in, hidden, grad_resid, base, back_out, *sums, *far,
    )


def finish_kernel(
    n_seq, me_ref, both_ref, row_ref, line_ref, wq_ref, gain_ref,
    de_ref, dw_ref, dwo_ref, again_ref, mgain_ref, router_ref, carry_ref, vec_ref, mix_ref,
):
    de_ref[...] = both_ref[0, 0].astype(f32)

    @pl.when(pl.program_id(0) == 0)
    def _():
        width = row_ref.shape[2] // 4
        for j in range(n_seq):
            block = row_ref[j].astype(f32)
            for c in range(3):
                left = c * width * n_seq + j * width
                dw_ref[:, left : left + width] = block[:, c * width : (c + 1) * width]
            dwo_ref[:, j * width : (j + 1) * width] = block[:, 3 * width :]
        sums = jnp.sum(dw_ref[...] * wq_ref[...].astype(f32), axis=1, keepdims=True)
        again_ref[...] = column_to_row(sums) / gain_ref[...].astype(f32)
        mix_ref[0] = line_ref[0:2]
        mix_ref[1] = line_ref[2:4]
        router_ref[...] = line_ref[4 : 4 + H]
        vec_ref[...] = line_ref[4 + H : 6 + H]
        mgain_ref[...] = line_ref[6 + H : 7 + H]
        carry_ref[...] = line_ref[24 : 24 + H, 0:H]


def finish_call(n_seq, me, both, row_in, lines, w_qkv, attn_gain):
    shard = w_qkv.shape[0]
    _, tiles, three, step, _ = both.shape
    units = 2 * tiles * step

    def whole(shape):
        return pl.BlockSpec(shape, lambda i, me_ref: (0,) * len(shape))

    shapes = [(shard, 3 * D), (shard, D), (1, shard), (1, shard), (H, shard), (H, H), (2, shard),
              (2, 2, shard)]
    return pl.pallas_call(
        functools.partial(finish_kernel, n_seq),
        out_shape=[jax.ShapeDtypeStruct((three, units, D), f32)]
        + [jax.ShapeDtypeStruct(shape, f32) for shape in shapes],
        grid_spec=pltpu.PrefetchScalarGridSpec(
            num_scalar_prefetch=1,
            grid=(2 * tiles,),
            in_specs=[
                pl.BlockSpec(
                    (1, 1, three, step, D),
                    lambda i, me_ref: ((i // tiles) ^ (me_ref[0] & 1), i % tiles, 0, 0, 0),
                ),
                whole(row_in.shape),
                whole(lines.shape),
                whole(w_qkv.shape),
                whole((1, shard)),
            ],
            out_specs=[pl.BlockSpec((three, step, D), lambda i, me_ref: (0, i, 0))]
            + [whole(shape) for shape in shapes],
        ),
        name="finish",
    )(me, both, row_in, lines, w_qkv, attn_gain[None])


def rope_tables(seq_len):
    freq_index = jnp.arange(HD // 2, dtype=f32)
    inv_freq = jnp.exp(freq_index * (-2.0 * math.log(10000.0) / HD))
    angles = jnp.arange(seq_len, dtype=jnp.int32).astype(f32)[None, :] * inv_freq[:, None]
    return jnp.cos(angles), jnp.sin(angles)


def per_device(
    hidden_in,
    prev_logits,
    segments,
    routes,
    attn_gain,
    w_qkv,
    w_out,
    moe_gain,
    w_router,
    w_carry,
    const_vec,
    const_mix,
    experts,
    cotangent,
):
    n_seq, n_dp = lax.axis_size("seq"), lax.axis_size("dp")
    owners = n_dp // E
    me = lax.axis_index("seq")
    tok = hidden_in.shape[1]
    hidden, cot = hidden_in[0], cotangent[0]
    prev_t = jnp.transpose(prev_logits, (2, 0, 1))
    routes_t = routes[0].T

    def to_owners(values):
        return lax.all_to_all(
            jnp.repeat(values, owners, axis=0), "dp", split_axis=0, concat_axis=0, tiled=True
        )

    def to_sources(values):
        return lax.all_to_all(values, "dp", split_axis=0, concat_axis=0, tiled=True)

    cos_t, sin_t = rope_tables(tok * n_seq)
    attn_in, qkv, w_turned, small, slot_of, grad_slots, out_weight = start_call(
        n_seq, n_dp, hidden, w_qkv, attn_gain, moe_gain, const_vec, const_mix, w_router.T,
        routes_t, cot, cos_t, sin_t, w_out,
    )
    arrived_grad = to_owners(grad_slots)

    seg_row = segments[0]
    doc_ids = jnp.arange(16, dtype=jnp.int32)
    doc_start = jnp.sum((seg_row[None, :] < doc_ids[:, None]).astype(jnp.int32), axis=1)
    start = jnp.sum(jnp.where(seg_row[None, :] == doc_ids[:, None], doc_start[:, None], 0), axis=0)
    start_row = start.astype(jnp.int32)[None, :]
    lows = start[::BLK].astype(jnp.int32) // BLK
    attended, attended_exact, logs = attn_call(lows, qkv, start_row, tok)

    heads_t, resid_mid, gates, x_slots, gate_slots = mid_call(
        n_seq, attended, hidden, prev_t, w_carry, small, slot_of, routes_t, out_weight
    )
    tiles = experts.shape[1] // UNITS // 2
    n_cross = 1 if tiles > 1 else 0
    piece, dots, partial, sums, far = moe_call(
        n_dp, n_cross, x_slots, gate_slots, experts, arrived_grad
    )
    far = list(far) + [swap(part, "seq", 2) for part in sums[n_cross : min(2, tiles - 1)]]
    back_out = to_sources(partial)

    grad_resid, grad_out, base, d_prev, pack, wo_sum = mid_back_call(
        n_seq, n_dp, piece, dots, cot, resid_mid, gates, slot_of, routes_t, small, heads_t,
        out_weight, prev_t, w_carry,
    )
    later, grad_out = lax.optimization_barrier((list(sums[2 : tiles - 1]), grad_out))
    far += [swap(part, "seq", 2) for part in later]
    grad_qkv = attn_back_call(
        lows, qkv, grad_out, attended_exact, logs, start_row, cos_t, sin_t
    )
    d_input, row_in, lines, block_out, both = tail_call(
        n_seq, n_dp, grad_qkv, w_turned, wo_sum, pack, gates, slot_of, small,
        attn_in, hidden, grad_resid, base, back_out, sums, far,
    )
    d_experts, d_qkv, d_out, again, mgain, router, carry, vec, mix = finish_call(
        n_seq, me.astype(jnp.int32).reshape(1), both, row_in, lines, w_qkv, attn_gain
    )
    return (
        block_out[None],
        d_input[None],
        jnp.transpose(d_prev, (1, 2, 0)),
        again[0],
        d_qkv,
        d_out,
        mgain[0],
        router.T,
        carry,
        vec,
        mix,
        d_experts,
    )


def solution(mesh):
    return jax.shard_map(
        per_device,
        mesh=mesh,
        in_specs=(
            P("dp", "seq", None),
            P("dp", "seq", None),
            P("dp", None),
            P("dp", "seq", None),
            P("dp"),
            P("dp", None),
            P("dp", None),
            P("dp"),
            P("dp", None),
            P(),
            P(None, "dp"),
            P(None, None, "dp"),
            P(None, "dp", None),
            P("dp", "seq", None),
        ),
        out_specs=(
            P("dp", "seq", None),
            P("dp", "seq", None),
            P("dp", "seq", None),
            P("dp"),
            P("dp", None),
            P("dp", None),
            P("dp"),
            P("dp", None),
            P(),
            P(None, "dp"),
            P(None, None, "dp"),
            P(None, "dp", None),
        ),
        check_vma=False,
    )
```

```python
import functools
import math

import jax
import jax.numpy as jnp
from jax import lax
from jax.experimental import pallas as pl
from jax.experimental.pallas import tpu as pltpu
from jax.sharding import PartitionSpec as P

D = 768
H = 12
HD = 64
E = 8
CAP = 128
BLK = 256
PAIR = 2 * CAP
UNITS = 256
PART = 128
SMALL = 32
LINES = 40

exact_prec = lax.Precision.HIGHEST
neg_large = -1e30
score_scale = 0.125 * math.log2(math.e)
f32 = jnp.float32
bf16 = jnp.bfloat16

NN = (((1,), (0,)), ((), ()))
NT = (((1,), (1,)), ((), ()))
TN = (((0,), (0,)), ((), ()))


MESH = pl.DeviceIdType.MESH
VMEM = pl.BlockSpec(memory_space=pltpu.VMEM)
HBM = pl.BlockSpec(memory_space=pl.ANY)
DMA = pltpu.SemaphoreType.DMA


def mm(a, b, dims):
    return lax.dot_general(a, b, dims, preferred_element_type=f32)


def swap(value, axis, bit):
    size = lax.axis_size(axis)
    return lax.ppermute(value, axis, [(i, i ^ bit) for i in range(size)])


def bits_high_first(size):
    bit = size // 2
    while bit >= 1:
        yield bit
        bit //= 2


def greet(peers):
    barrier = pltpu.get_barrier_semaphore()
    for peer in peers:
        pl.semaphore_signal(barrier, inc=1, device_id=peer, device_id_type=MESH)
    pl.semaphore_wait(barrier, len(peers))


def remote_later(src, dst, sems, index, target):
    return pltpu.make_async_remote_copy(
        src_ref=src,
        dst_ref=dst,
        send_sem=sems[0].at[index],
        recv_sem=sems[1].at[index],
        device_id=target,
        device_id_type=MESH,
    )


def remote(src, dst, sems, index, target):
    copy = remote_later(src, dst, sems, index, target)
    copy.start()
    return copy


def one_hot(condition):
    return jnp.where(condition, 1.0, 0.0).astype(bf16)


def picks_of(slot_ref):
    slots = lax.broadcasted_iota(jnp.int32, (E * CAP, slot_ref.shape[1]), 0)
    return [one_hot(slots == slot_ref[k : k + 1, :]) for k in range(2)]


def split(rows):
    high = rows.astype(bf16)
    rest = rows - high.astype(f32)
    middle = rest.astype(bf16)
    low = (rest - middle.astype(f32)).astype(bf16)
    return jnp.concatenate([high, middle, low], axis=0)


def unsplit(rows):
    third = rows.shape[0] // 3
    return rows[:third] + rows[third : 2 * third] + rows[2 * third :]


def column_to_row(column):
    return jnp.broadcast_to(column, (column.shape[0], 128)).T[0:1]


def norm_back(values, gain, grad):
    rate = lax.rsqrt(jnp.mean(values * values, axis=-1, keepdims=True) + 1e-06)
    scaled = gain * grad
    inner = jnp.mean(values * scaled, axis=-1, keepdims=True)
    return rate * scaled - values * (rate * rate * rate) * inner


def make_slots(route_ref, cot_ref, slot_ref, g_ref):
    tok = route_ref.shape[1]
    ids = lax.broadcasted_iota(jnp.int32, (E, tok), 0)
    named = [route_ref[k : k + 1, :] == ids for k in range(2)]
    earlier = lax.broadcasted_iota(jnp.int32, (tok, tok), 0) < lax.broadcasted_iota(
        jnp.int32, (tok, tok), 1
    )
    ranks = mm(one_hot(named[0] | named[1]), one_hot(earlier), NN)
    for k in range(2):
        route = route_ref[k : k + 1, :]
        rank = jnp.sum(jnp.where(named[k], ranks, 0.0), axis=0, keepdims=True)
        slot_ref[k : k + 1, :] = jnp.where(
            route < E, route * CAP + rank.astype(jnp.int32), E * CAP
        )
    picks = picks_of(slot_ref)
    g_ref[...] = mm(picks[0] + picks[1], cot_ref[...], NN).astype(bf16).reshape(g_ref.shape)


def start_kernel(
    n_seq, n_dp, h_ref, w_ref, again_ref, mgain_ref, vec_ref, mix_ref, router_ref,
    route_ref, cot_ref, cos_ref, sin_ref, wo_ref,
    attn_ref, qkv_ref, wt_ref, small_ref, slot_ref, g_ref, wo_all,
    all_ref, slice_ref, small_buf, h_send, h_recv, near_send, near_recv, next_send, next_recv,
    c_send, c_recv,
):
    me, dp = lax.axis_index("seq"), lax.axis_index("dp")
    tok = h_ref.shape[0]
    width = slice_ref.shape[2] // 3
    seq_bits = list(bits_high_first(n_seq))
    greet(
        [{"seq": me ^ bit} for bit in seq_bits]
        + [{"dp": dp ^ 1}]
        + [{"dp": dp ^ (2 * j)} for j in range(1, n_dp // 2)]
    )

    plan, arrival = [], {}
    order = [(0, bit) for bit in seq_bits]
    while order:
        place, bit = order.pop(0)
        copy = remote_later(
            h_ref if place == 0 else all_ref.at[me ^ place],
            all_ref.at[me ^ place],
            (h_send, h_recv),
            len(plan),
            {"seq": me ^ bit},
        )
        arrival[place ^ bit] = copy
        plan.append((place, copy))
        order += [(place ^ bit, low) for low in seq_bits if low < bit]
    for place, copy in plan:
        if place == 0:
            copy.start()

    for j in range(n_seq):

        @pl.when(me == j)
        def _():
            for c in range(3):
                left = c * width * n_seq + j * width
                slice_ref[dp, :, c * width : (c + 1) * width] = w_ref[:, left : left + width]

    small_buf[dp] = jnp.zeros(small_buf.shape[1:], bf16)
    small_buf[dp, 0:1, :] = again_ref[...]
    small_buf[dp, 1:2, :] = mgain_ref[...]
    small_buf[dp, 2:4, :] = vec_ref[...]
    small_buf[dp, 4:6, :] = mix_ref[0]
    small_buf[dp, 6:8, :] = mix_ref[1]
    small_buf[dp, 8 : 8 + H, :] = router_ref[...]
    cols = pl.ds(pl.multiple_of((me & 1) * (D // 2), D // 2), D // 2)
    wo_all[dp, :, cols] = wo_ref[:, cols]

    def rows_of(kind, source):
        return (small_buf.at[source], slice_ref.at[source], wo_all.at[source, :, cols])[kind]

    def first_copy(kind, j):
        return remote_later(
            rows_of(kind, dp), rows_of(kind, dp), (near_send.at[kind], near_recv.at[kind]), j,
            {"dp": dp ^ (2 * j)},
        )

    def next_copy(kind, j):
        return remote_later(
            rows_of(kind, dp ^ (2 * j)), rows_of(kind, dp ^ (2 * j)),
            (next_send.at[kind], next_recv.at[kind]), j, {"dp": dp ^ 1},
        )

    places = range(1, n_dp // 2)
    for kind in range(3):
        for j in places:
            first_copy(kind, j).start()
        next_copy(kind, 0).start()
    make_slots(route_ref, cot_ref, slot_ref, g_ref)

    def pass_on(kind):
        for j in places:
            first_copy(kind, j).wait_recv()
            next_copy(kind, j).start()

    def complete(kind):
        for j in range(n_dp // 2):
            next_copy(kind, j).wait_recv()

    pass_on(0)
    complete(0)
    small_ref[...] = jnp.concatenate([small_buf[i].astype(f32) for i in range(n_dp)], axis=1)

    def normalize(block, ref):
        x = ref.astype(f32)
        mean_square = jnp.mean(x * x, axis=-1, keepdims=True)
        rows = pl.ds(pl.multiple_of(block * tok, tok), tok)
        attn_ref[rows, :] = (x * lax.rsqrt(mean_square + 1e-06) * small_ref[0:1]).astype(bf16)

    normalize(me, h_ref[...])
    pass_on(1)
    for place in arrival:
        arrival[place].wait_recv()
        for source, copy in plan:
            if source == place:
                copy.start()
        normalize(me ^ place, all_ref[me ^ place])
    complete(1)
    pass_on(2)
    wt_ref[...] = slice_ref[...].reshape(D, 3 * width).T
    half = HD // 2

    @pl.loop(0, attn_ref.shape[0] // BLK)
    def _(i):
        rows = pl.ds(pl.multiple_of(i * BLK, BLK), BLK)
        y = mm(wt_ref[...], attn_ref[rows, :], NT)
        cos, sin = cos_ref[:, rows], sin_ref[:, rows]
        for head in range(2 * width // HD):
            low, middle, high = head * HD, head * HD + half, (head + 1) * HD
            a, b = y[low:middle], y[middle:high]
            qkv_ref[low:middle, rows] = (a * cos - b * sin).astype(bf16)
            qkv_ref[middle:high, rows] = (a * sin + b * cos).astype(bf16)
        qkv_ref[2 * width :, rows] = y[2 * width :].astype(bf16)

    complete(2)
    trade = remote(
        wo_all.at[:, :, cols], wo_all.at[:, :, cols], (c_send, c_recv), 0, {"seq": me ^ 1}
    )
    for _, copy in plan:
        copy.wait_send()
    for kind in range(3):
        for j in places:
            first_copy(kind, j).wait_send()
        for j in range(n_dp // 2):
            next_copy(kind, j).wait_send()
    trade.wait()


def start_call(
    n_seq, n_dp, hidden, w_qkv, attn_gain, moe_gain, vec, mix, router, routes, cotangent, cos, sin,
    w_out,
):
    tok, shard = hidden.shape[0], w_qkv.shape[0]
    width3 = w_qkv.shape[1] // n_seq
    hops = n_seq - 1
    return pl.pallas_call(
        functools.partial(start_kernel, n_seq, n_dp),
        out_shape=(
            jax.ShapeDtypeStruct((n_seq * tok, D), bf16),
            jax.ShapeDtypeStruct((width3, n_seq * tok), bf16),
            jax.ShapeDtypeStruct((width3, D), bf16),
            jax.ShapeDtypeStruct((SMALL, D), f32),
            jax.ShapeDtypeStruct(routes.shape, jnp.int32),
            jax.ShapeDtypeStruct((E, CAP, D), bf16),
            jax.ShapeDtypeStruct((n_dp, shard, D), bf16),
        ),
        in_specs=[VMEM] * 12,
        out_specs=[VMEM] * 7,
        scratch_shapes=[
            pltpu.VMEM((n_seq, tok, D), bf16),
            pltpu.VMEM((n_dp, shard, width3), bf16),
            pltpu.VMEM((n_dp, SMALL, shard), bf16),
            DMA((hops,)),
            DMA((hops,)),
            DMA((3, n_dp // 2)),
            DMA((3, n_dp // 2)),
            DMA((3, n_dp // 2)),
            DMA((3, n_dp // 2)),
            DMA((1,)),
            DMA((1,)),
        ],
        compiler_params=pltpu.CompilerParams(collective_id=0, has_side_effects=True),
        name="start",
    )(
        hidden, w_qkv, attn_gain[None], moe_gain[None], vec, mix, router, routes, cotangent,
        cos, sin, w_out,
    )


def allowed_block(key_block, query_block, start_row):
    key_pos = key_block * BLK + lax.broadcasted_iota(jnp.int32, (BLK, BLK), 0)
    query_pos = query_block * BLK + lax.broadcasted_iota(jnp.int32, (BLK, BLK), 1)
    return (key_pos >= start_row) & (key_pos <= query_pos)


def attn_kernel(lo_ref, qkv_ref, start_ref, out_ref, exact_ref, log_ref, keys_ref):
    heads, seq_len, _ = keys_ref.shape
    width = heads * HD
    qb = pl.program_id(0)

    @pl.when(qb == 0)
    def _():
        for h in range(heads):
            keys_ref[h] = qkv_ref[width + h * HD : width + (h + 1) * HD, :].T

    here = pl.ds(pl.multiple_of(qb * BLK, BLK), BLK)
    start_row = start_ref[...]

    def step(kb, carry):
        there = pl.ds(pl.multiple_of(kb * BLK, BLK), BLK)
        allowed = allowed_block(kb, qb, start_row)
        new = []
        for h in range(heads):
            top, total, acc = carry[h]
            scores = mm(keys_ref[h, there, :], qkv_ref[h * HD : (h + 1) * HD, here], NN)
            scores = jnp.where(allowed, scores * score_scale, neg_large)
            new_top = jnp.maximum(top, jnp.max(scores, axis=0, keepdims=True))
            fade = jnp.exp2(top - new_top)
            weights = jnp.exp2(scores - new_top)
            total = total * fade + jnp.sum(weights, axis=0, keepdims=True)
            values = qkv_ref[2 * width + h * HD : 2 * width + (h + 1) * HD, there]
            acc = acc * fade + mm(values, weights.astype(bf16), NN)
            new.append((new_top, total, acc))
        return tuple(new)

    first = tuple(
        (
            jnp.full((1, BLK), neg_large, f32),
            jnp.zeros((1, BLK), f32),
            jnp.zeros((HD, BLK), f32),
        )
        for _ in range(heads)
    )
    done = lax.fori_loop(lo_ref[qb], qb + 1, step, first)
    for h in range(heads):
        top, total, acc = done[h]
        attended = acc / total
        exact_ref[h * HD : (h + 1) * HD, :] = attended
        out_ref[0, h * HD : (h + 1) * HD, :] = attended.astype(bf16)
        log_ref[h : h + 1, :] = top + jnp.log2(total)


def attn_call(lows, qkv, start_row, tok):
    width3, seq_len = qkv.shape
    width = width3 // 3
    heads = width // HD
    per = tok // BLK
    return pl.pallas_call(
        attn_kernel,
        out_shape=(
            jax.ShapeDtypeStruct((seq_len // tok, width, tok), bf16),
            jax.ShapeDtypeStruct((width, seq_len), f32),
            jax.ShapeDtypeStruct((heads, seq_len), f32),
        ),
        grid_spec=pltpu.PrefetchScalarGridSpec(
            num_scalar_prefetch=1,
            grid=(seq_len // BLK,),
            in_specs=[
                pl.BlockSpec((width3, seq_len), lambda i, lo: (0, 0)),
                pl.BlockSpec((1, BLK), lambda i, lo: (0, i)),
            ],
            out_specs=[
                pl.BlockSpec((1, width, BLK), lambda i, lo: (i // per, 0, i % per)),
                pl.BlockSpec((width, BLK), lambda i, lo: (0, i)),
                pl.BlockSpec((heads, BLK), lambda i, lo: (0, i)),
            ],
            scratch_shapes=[pltpu.VMEM((heads, seq_len, HD), bf16)],
        ),
        cost_estimate=pl.CostEstimate(
            flops=16_000_000_000, transcendentals=0, bytes_accessed=16_000_000
        ),
        name="attend",
    )(lows, qkv, start_row)


def attn_back_kernel(
    lo_ref, qkv_ref, go_ref, exact_ref, log_ref, start_ref, cos_ref, sin_ref, out_ref,
    keys_ref, values_ref, dk_ref, dv_ref,
):
    heads, seq_len, _ = keys_ref.shape
    width = heads * HD
    half = HD // 2
    qb = pl.program_id(0)

    @pl.when(qb == 0)
    def _():
        for h in range(heads):
            keys_ref[h] = qkv_ref[width + h * HD : width + (h + 1) * HD, :].T
            values_ref[h] = qkv_ref[2 * width + h * HD : 2 * width + (h + 1) * HD, :].T
        dk_ref[...] = jnp.zeros_like(dk_ref)
        dv_ref[...] = jnp.zeros_like(dv_ref)

    here = pl.ds(pl.multiple_of(qb * BLK, BLK), BLK)
    start_row = start_ref[...]
    grad = go_ref[0]
    deltas = [
        jnp.sum(
            exact_ref[h * HD : (h + 1) * HD, :] * grad[h * HD : (h + 1) * HD].astype(f32),
            axis=0,
            keepdims=True,
        )
        for h in range(heads)
    ]

    def step(kb, carry):
        there = pl.ds(pl.multiple_of(kb * BLK, BLK), BLK)
        allowed = allowed_block(kb, qb, start_row)
        new = []
        for h in range(heads):
            rows = slice(h * HD, (h + 1) * HD)
            queries = qkv_ref[rows, here]
            scores = mm(keys_ref[h, there, :], queries, NN)
            scores = jnp.where(allowed, scores * score_scale, neg_large)
            probs = jnp.exp2(scores - log_ref[h : h + 1, :])
            grad_probs = mm(values_ref[h, there, :], grad[rows], NN)
            grad_scores = (probs * (grad_probs - deltas[h])).astype(bf16)
            dv_ref[rows, there] += mm(grad[rows], probs.astype(bf16), NT)
            dk_ref[rows, there] += mm(queries, grad_scores, NT)
            keys = qkv_ref[width + h * HD : width + (h + 1) * HD, there]
            new.append(carry[h] + mm(keys, grad_scores, NN))
        return tuple(new)

    grads = lax.fori_loop(
        lo_ref[qb], qb + 1, step, tuple(jnp.zeros((HD, BLK), f32) for _ in range(heads))
    )

    def turn_back(value, cos, sin):
        value = value.astype(bf16).astype(f32)
        a, b = value[:half], value[half:]
        return (a * cos + b * sin).astype(bf16), (b * cos - a * sin).astype(bf16)

    for h in range(heads):
        a, b = turn_back(grads[h] * 0.125, cos_ref[:, here], sin_ref[:, here])
        out_ref[h * HD : h * HD + half, here] = a
        out_ref[h * HD + half : (h + 1) * HD, here] = b

    @pl.when(qb == pl.num_programs(0) - 1)
    def _():
        cos, sin = cos_ref[...], sin_ref[...]
        for h in range(heads):
            a, b = turn_back(dk_ref[h * HD : (h + 1) * HD, :] * 0.125, cos, sin)
            out_ref[width + h * HD : width + h * HD + half, :] = a
            out_ref[width + h * HD + half : width + (h + 1) * HD, :] = b
        out_ref[2 * width :, :] = dv_ref[...].astype(bf16)


def attn_back_call(lows, qkv, grad_out, exact, logs, start_row, cos_t, sin_t):
    width3, seq_len = qkv.shape
    width = width3 // 3
    heads = width // HD
    per = grad_out.shape[2] // BLK
    return pl.pallas_call(
        attn_back_kernel,
        out_shape=jax.ShapeDtypeStruct((width3, seq_len), bf16),
        grid_spec=pltpu.PrefetchScalarGridSpec(
            num_scalar_prefetch=1,
            grid=(seq_len // BLK,),
            in_specs=[
                pl.BlockSpec((width3, seq_len), lambda i, lo: (0, 0)),
                pl.BlockSpec((1, width, BLK), lambda i, lo: (i // per, 0, i % per)),
                pl.BlockSpec((width, BLK), lambda i, lo: (0, i)),
                pl.BlockSpec((heads, BLK), lambda i, lo: (0, i)),
                pl.BlockSpec((1, BLK), lambda i, lo: (0, i)),
                pl.BlockSpec((HD // 2, seq_len), lambda i, lo: (0, 0)),
                pl.BlockSpec((HD // 2, seq_len), lambda i, lo: (0, 0)),
            ],
            out_specs=pl.BlockSpec((width3, seq_len), lambda i, lo: (0, 0)),
            scratch_shapes=[
                pltpu.VMEM((heads, seq_len, HD), bf16),
                pltpu.VMEM((heads, seq_len, HD), bf16),
                pltpu.VMEM((width, seq_len), f32),
                pltpu.VMEM((width, seq_len), f32),
            ],
        ),
        cost_estimate=pl.CostEstimate(
            flops=16_000_000_000, transcendentals=0, bytes_accessed=16_000_000
        ),
        name="attend_back",
    )(lows, qkv, grad_out, exact, logs, start_row, cos_t, sin_t)


def gates_back(grad_hidden, gate_pre, up_pre):
    sig = 1.0 / (1.0 + jnp.exp(-gate_pre))
    silu = gate_pre * sig
    grad_gate = grad_hidden * up_pre * sig * (1.0 + gate_pre * (1.0 - sig))
    return (
        (silu * up_pre).astype(bf16),
        grad_gate.astype(bf16),
        (grad_hidden * silu).astype(bf16),
    )


def moe_kernel(n_dp, parts, x_ref, gate_ref, w_hbm, g_ref, *refs):
    piece_ref, dots_ref, out_ref, refs = refs[0], refs[1], refs[2], refs[3:]
    fin_hbm, refs = refs[:parts], refs[parts:]
    (
        w_ref, x_in, x_far, g_far, gate_in, gate_far, gs_ref, gs_far, pair_ref, near_ref, far_ref,
        own_ref, piece_out, dot_out, dw_out, dw_in, fin_ref,
        w_sem, x_send, x_recv, t_send, t_recv, p_send, p_recv, d_send, d_recv,
        xf_send, xf_recv, gf_send, gf_recv, tf_send, tf_recv, c_send, c_recv, keep_sem,
    ) = refs
    me, dp = lax.axis_index("seq"), lax.axis_index("dp")
    owners = n_dp // E
    pairs = n_dp // 2
    half = near_ref.shape[2]
    core, plane = me & 1, lax.div(me, 2)
    greet([{"dp": dp ^ k} for k in range(1, n_dp)] + [{"seq": me ^ 1}, {"seq": me ^ 2}])

    def x_copy(k):
        return remote_later(
            x_ref.at[(dp ^ k) // owners], x_in.at[k], (x_send, x_recv), k, {"dp": dp ^ k}
        )

    def gate_copy(k):
        return remote_later(
            gate_ref.at[(dp ^ k) // owners], gate_in.at[k], (t_send, t_recv), k, {"dp": dp ^ k}
        )

    def piece_copy(k):
        return remote_later(
            piece_out.at[k], piece_ref.at[dp], (p_send, p_recv), k, {"dp": dp ^ k}
        )

    def dot_copy(k):
        return remote_later(dot_out.at[k], dots_ref.at[dp], (d_send, d_recv), k, {"dp": dp ^ k})

    def far_copies(k):
        across = {"seq": me ^ 2}
        return [
            remote_later(gate_in.at[k], gate_far.at[k], (tf_send, tf_recv), k, across),
            remote_later(g_ref.at[dp ^ k], g_far.at[k], (gf_send, gf_recv), k, across),
            remote_later(x_in.at[k], x_far.at[k], (xf_send, xf_recv), k, across),
        ]

    def core_copy(t):
        return remote_later(dw_out.at[t], dw_in.at[t], (c_send, c_recv), t, {"seq": me ^ 1})

    for p in [0, pairs - 1, *range(1, pairs - 1)]:
        for k in (2 * p, 2 * p + 1):
            if k:
                gate_copy(k).start()
                x_copy(k).start()
    loads = [pltpu.make_async_copy(w_hbm.at[j], w_ref.at[j], w_sem.at[j]) for j in range(3)]
    loads.append(pltpu.make_async_copy(x_ref.at[dp // owners], x_in.at[0], w_sem.at[3]))
    for load in loads:
        load.start()
    gate_in[0] = gate_ref[dp // owners]
    for load in loads:
        load.wait()

    def place(i):
        return jnp.where(i == 0, 0, 1 + lax.rem(i + pairs - 3, pairs - 1))

    def scale(ref, rows, gate, k):
        column = jnp.broadcast_to(gate, (CAP, CAP)).T[:, 0:1]
        here = pl.ds(pl.multiple_of(k * CAP, CAP), CAP)
        ref[here] = (rows.astype(f32) * column).astype(bf16)

    @pl.loop(0, pairs)
    def _(i):
        p = place(i)
        rows = pl.ds(pl.multiple_of(p * PAIR, PAIR), PAIR)

        def arrive(k):
            x_copy(k).wait_recv()
            gate_copy(k).wait_recv()

        @pl.when(p > 0)
        def _():
            arrive(2 * p)

        arrive(2 * p + 1)
        for side in range(2):
            k = 2 * p + side
            for copy in far_copies(k):
                copy.start()
            scale(gs_ref, g_ref[dp ^ k], gate_in[k], k)

        @pl.loop(0, 2)
        def _(t):
            part = pl.ds(pl.multiple_of(t * half, half), half)
            x = x_in[pl.ds(2 * p, 2)].reshape(PAIR, D)
            gate_pre = mm(x, w_ref[0, part], NT)
            up_pre = mm(x, w_ref[1, part], NT)
            grad_hidden = mm(gs_ref[rows], w_ref[2, part], NT)
            results = gates_back(grad_hidden, gate_pre, up_pre)
            for j in range(3):
                pair_ref[j, :, part] = results[j]

            @pl.when(t == plane)
            def _():
                for j in range(3):
                    near_ref[j, rows] = results[j]

        pieces = mm(pair_ref[1], w_ref[0], NN) + mm(pair_ref[2], w_ref[1], NN)
        piece_out[pl.ds(2 * p, 2)] = pieces.astype(bf16).reshape(2, CAP, D)
        piece_copy(2 * p + 1).start()

        @pl.when(p > 0)
        def _():
            piece_copy(2 * p).start()

        outs = mm(pair_ref[0], w_ref[2], NN)
        for side in range(2):
            k = 2 * p + side
            out = outs[side * CAP : (side + 1) * CAP].astype(bf16)
            out_ref[dp ^ k] = out
            product = out.astype(f32) * g_ref[dp ^ k].astype(f32)
            dot_out[k] = column_to_row(jnp.sum(product, axis=1, keepdims=True))
        dot_copy(2 * p + 1).start()

        @pl.when(p > 0)
        def _():
            dot_copy(2 * p).start()

    piece_ref[dp] = piece_out[0]
    dots_ref[dp] = dot_out[0]

    def weight_grad(source, x, gs, j, part):
        left = source[(1, 2, 0)[j], :, part]
        return mm(left, gs[...] if j == 2 else x[...].reshape(n_dp * CAP, D), TN)

    @pl.loop(0, half // UNITS)
    def _(t):
        part = pl.ds(pl.multiple_of(t * UNITS, UNITS), UNITS)
        for j in range(3):
            own_ref[j, part] = weight_grad(near_ref, x_in, gs_ref, j, part)

    @pl.loop(0, pairs)
    def _(i):
        p = place(i)
        rows = pl.ds(pl.multiple_of(p * PAIR, PAIR), PAIR)
        for side in range(2):
            k = 2 * p + side
            for copy in far_copies(k):
                copy.wait_recv()
            scale(gs_far, g_far[k], gate_far[k], k)
        part = pl.ds(pl.multiple_of(plane * half, half), half)
        x = x_far[pl.ds(2 * p, 2)].reshape(PAIR, D)
        results = gates_back(
            mm(gs_far[rows], w_ref[2, part], NT),
            mm(x, w_ref[0, part], NT),
            mm(x, w_ref[1, part], NT),
        )
        for j in range(3):
            far_ref[j, rows] = results[j]

    tiles = half // UNITS // 2

    def both_rows(side, t, j):
        part = pl.ds(pl.multiple_of((side * tiles + t) * UNITS, UNITS), UNITS)
        return own_ref[j, part] + weight_grad(far_ref, x_far, gs_far, j, part)

    @pl.loop(0, tiles)
    def _(t):
        for j in range(3):
            dw_out[t, j] = both_rows(1 - core, t, j).astype(bf16)
        core_copy(t).start()

    @pl.loop(0, tiles)
    def _(t):
        core_copy(t).wait_recv()
        for j in range(3):
            total = (both_rows(core, t, j) + dw_in[t, j].astype(f32)).astype(bf16)
            for u in range(UNITS // PART):
                fin_ref[t * (UNITS // PART) + u, j] = total[u * PART : (u + 1) * PART]

    keeps = [
        pltpu.make_async_copy(fin_ref.at[t], fin_hbm[t], keep_sem.at[t]) for t in range(parts)
    ]
    for keep in keeps:
        keep.start()
    for k in range(1, n_dp):
        piece_copy(k).wait()
        dot_copy(k).wait()
        x_copy(k).wait_send()
        gate_copy(k).wait_send()
    for k in range(n_dp):
        for copy in far_copies(k):
            copy.wait_send()
    for t in range(tiles):
        core_copy(t).wait_send()
    for keep in keeps:
        keep.wait()


def moe_call(n_dp, x_slots, gate_slots, weights, grads):
    units = weights.shape[1]
    half = units // 2
    rows = n_dp * CAP
    parts = units // 4 // PART
    tiles = half // UNITS // 2
    outs = pl.pallas_call(
        functools.partial(moe_kernel, n_dp, parts),
        out_shape=(
            jax.ShapeDtypeStruct((n_dp, CAP, D), bf16),
            jax.ShapeDtypeStruct((n_dp, 1, CAP), f32),
            jax.ShapeDtypeStruct((n_dp, CAP, D), bf16),
        )
        + (jax.ShapeDtypeStruct((3, PART, D), bf16),) * parts,
        in_specs=[HBM, VMEM, HBM, VMEM],
        out_specs=[VMEM] * 3 + [HBM] * parts,
        scratch_shapes=[
            pltpu.VMEM(weights.shape, bf16),
            pltpu.VMEM((n_dp, CAP, D), bf16),
            pltpu.VMEM((n_dp, CAP, D), bf16),
            pltpu.VMEM((n_dp, CAP, D), bf16),
            pltpu.VMEM((n_dp, 1, CAP), f32),
            pltpu.VMEM((n_dp, 1, CAP), f32),
            pltpu.VMEM((rows, D), bf16),
            pltpu.VMEM((rows, D), bf16),
            pltpu.VMEM((3, PAIR, units), bf16),
            pltpu.VMEM((3, rows, half), bf16),
            pltpu.VMEM((3, rows, half), bf16),
            pltpu.VMEM((3, half, D), f32),
            pltpu.VMEM((n_dp, CAP, D), bf16),
            pltpu.VMEM((n_dp, 1, CAP), f32),
            pltpu.VMEM((tiles, 3, UNITS, D), bf16),
            pltpu.VMEM((tiles, 3, UNITS, D), bf16),
            pltpu.VMEM((parts, 3, PART, D), bf16),
            DMA((4,)),
        ]
        + [DMA((n_dp,))] * 14
        + [DMA((tiles,))] * 2
        + [DMA((parts,))],
        compiler_params=pltpu.CompilerParams(
            collective_id=4, has_side_effects=True, vmem_limit_bytes=67043328
        ),
        name="experts",
    )(x_slots, gate_slots, weights, grads)
    return outs[0], outs[1], outs[2], list(outs[3:])


def experts_plain(to_owners, to_sources, n_dp, x_slots, gate_slots, weights, grads):
    rows = n_dp * CAP
    x = to_owners(x_slots).reshape(rows, D)
    gate = to_owners(gate_slots).reshape(rows, 1)
    g = grads.reshape(rows, D)
    gs = (g.astype(f32) * gate).astype(bf16)
    hidden, grad_gate, grad_up = gates_back(
        mm(gs, weights[2], NT), mm(x, weights[0], NT), mm(x, weights[1], NT)
    )
    out = mm(hidden, weights[2], NN).astype(bf16)
    piece = (mm(grad_gate, weights[0], NN) + mm(grad_up, weights[1], NN)).astype(bf16)
    dw = jnp.stack([mm(grad_gate, x, TN), mm(grad_up, x, TN), mm(hidden, gs, TN)])
    dots = jnp.sum(out.astype(f32) * g.astype(f32), axis=-1)
    return (
        to_sources(piece.reshape(n_dp, CAP, D)),
        to_sources(dots.reshape(n_dp, 1, CAP)),
        out.reshape(n_dp, CAP, D),
        lax.psum(dw, "seq"),
    )


def mid_kernel(
    n_seq, att_ref, h_ref, prev_ref, carry_ref, small_ref, slot_ref, route_ref, w_ref,
    heads_ref, mid_ref, gate_ref, x_ref, gs_ref, send_sem, recv_sem,
):
    me = lax.axis_index("seq")
    tok = h_ref.shape[0]
    greet([{"seq": me ^ place} for place in range(1, n_seq)])
    copies = [
        remote(
            att_ref.at[me ^ place], heads_ref.at[me], (send_sem, recv_sem), place,
            {"seq": me ^ place},
        )
        for place in range(1, n_seq)
    ]
    heads_ref[me] = att_ref[me]
    picks = picks_of(slot_ref)
    pick_any = picks[0] + picks[1]
    carried = lax.dot_general(
        carry_ref[...].astype(f32), prev_ref[:, 0, :], TN, precision=exact_prec,
        preferred_element_type=f32,
    )
    for copy in copies:
        copy.wait_recv()
    attn_out = mm(heads_ref[...].reshape(D, tok), w_ref[...].reshape(D, D), TN)
    resid = h_ref[...].astype(f32) + attn_out
    mid_ref[...] = resid
    rate = lax.rsqrt(jnp.mean(resid * resid, axis=-1, keepdims=True) + 1e-06)
    normed = resid * rate * small_ref[1:2]
    low = normed.astype(bf16)
    x_ref[...] = mm(pick_any, low, NN).astype(bf16).reshape(x_ref.shape)
    heads_rows = small_ref[4 : 8 + H].astype(bf16)
    products = mm(heads_rows, low, NT)
    rest = mm(heads_rows, (normed - low.astype(f32)).astype(bf16), NT)
    logits = products[4:] + carried
    ids = lax.broadcasted_iota(jnp.int32, (H, tok), 0)
    chosen = [
        jnp.sum(jnp.where(route_ref[k : k + 1, :] == ids, logits, 0.0), axis=0, keepdims=True)
        for k in range(2)
    ]
    top = jnp.maximum(chosen[0], chosen[1])
    exps = [jnp.exp(c - top) for c in chosen]
    total = exps[0] + exps[1]
    gates = [e / total for e in exps]
    gate_ref[...] = jnp.concatenate(
        [gates[0], gates[1], products[:4] + rest[:4], jnp.zeros((2, tok), f32)], axis=0
    )
    slot_gates = sum(unsplit(mm(split(gates[k]), picks[k], NT)) for k in range(2))
    for e in range(E):
        gs_ref[e] = slot_gates[:, e * CAP : (e + 1) * CAP]
    for copy in copies:
        copy.wait_send()


def mid_call(n_seq, attended, hidden, prev, carry, small, slot_of, routes, w_out):
    tok, width = hidden.shape[0], attended.shape[1]
    return pl.pallas_call(
        functools.partial(mid_kernel, n_seq),
        out_shape=(
            jax.ShapeDtypeStruct((n_seq, width, tok), bf16),
            jax.ShapeDtypeStruct((tok, D), f32),
            jax.ShapeDtypeStruct((8, tok), f32),
            jax.ShapeDtypeStruct((E, CAP, D), bf16),
            jax.ShapeDtypeStruct((E, 1, CAP), f32),
        ),
        in_specs=[VMEM] * 8,
        out_specs=[VMEM] * 5,
        scratch_shapes=[DMA((n_seq,)), DMA((n_seq,))],
        compiler_params=pltpu.CompilerParams(collective_id=2, has_side_effects=True),
        name="mid",
    )(attended, hidden, prev, carry, small, slot_of, routes, w_out)


def mid_back_kernel(
    n_seq, n_dp, n_tile, piece_ref, dots_ref, cot_ref, mid_ref, gate_ref, slot_ref, route_ref,
    small_ref, heads_ref, w_ref, prev_ref, carry_ref, *refs,
):
    tile_refs, refs = refs[:n_tile], refs[n_tile:]
    resid_ref, go_ref, base_ref, dprev_ref, pack_ref, wo_sum_ref, *refs = refs
    far_refs, refs = refs[:n_tile], refs[n_tile:]
    gh_ref, wo_ref, wo_in, a_send, a_recv, c_send, c_recv, t_send, t_recv = refs
    me = lax.axis_index("seq")
    tok = cot_ref.shape[0]
    width = heads_ref.shape[1]
    owners = n_dp // E
    pairs = n_seq // 2
    greet([{"seq": me ^ place} for place in range(1, n_seq)])
    tile_copies = [
        remote(tile_refs[t], far_refs[t], (t_send, t_recv), t, {"seq": me ^ 2})
        for t in range(n_tile)
    ]
    cot = cot_ref[...]
    grad_top = cot.astype(f32)
    resid_mid = mid_ref[...]
    gain = small_ref[1:2]
    rate = lax.rsqrt(jnp.mean(resid_mid * resid_mid, axis=-1, keepdims=True) + 1e-06)
    normed = resid_mid * rate * gain
    low = normed.astype(bf16)
    picks = picks_of(slot_ref)
    gates = [gate_ref[k : k + 1, :] for k in range(2)]
    routes = [route_ref[k : k + 1, :] for k in range(2)]
    normed_dot = column_to_row(jnp.sum(grad_top * normed, axis=1, keepdims=True))
    vecs = small_ref[2:4].astype(bf16)
    vec_dot = mm(vecs, cot, NT)
    alphas, const_dot = [], []
    for j in range(2):
        pair = [gate_ref[2 + 2 * j + c : 3 + 2 * j + c, :] for c in range(2)]
        top = jnp.maximum(pair[0], pair[1])
        exps = [jnp.exp(p - top) for p in pair]
        total = exps[0] + exps[1]
        alphas.append([e / total for e in exps])
        const_dot.append(alphas[j][0] * normed_dot + alphas[j][1] * vec_dot[j : j + 1])
    slot_dots = split(
        jnp.concatenate(
            [sum(dots_ref[e * owners + o] for o in range(owners)) for e in range(E)], axis=1
        )
    )
    out_dots = []
    for k in range(2):
        value = unsplit(mm(slot_dots, picks[k], NN))
        value = value + jnp.where(routes[k] == E + 1, normed_dot, 0.0)
        for j in range(2):
            value = value + jnp.where(routes[k] == E + 2 + j, const_dot[j], 0.0)
        out_dots.append(value)
    mean_dot = gates[0] * out_dots[0] + gates[1] * out_dots[1]
    ids = lax.broadcasted_iota(jnp.int32, (H, tok), 0)
    grad_logits = sum(
        jnp.where(routes[k] == ids, gates[k] * (out_dots[k] - mean_dot), 0.0) for k in range(2)
    )

    def gate_of(expert):
        return sum(jnp.where(routes[k] == expert, gates[k], 0.0) for k in range(2))

    const_gate = [gate_of(E + 2 + j) for j in range(2)]
    normed_gate = gate_of(E + 1) + sum(const_gate[j] * alphas[j][0] for j in range(2))
    vec_gate = split(jnp.concatenate([const_gate[j] * alphas[j][1] for j in range(2)], axis=0))
    mix_grads = []
    for j in range(2):
        terms = [normed_dot, vec_dot[j : j + 1]]
        for c in range(2):
            mix_grads.append(const_gate[j] * alphas[j][c] * (terms[c] - const_dot[j]))
    token_rows = split(jnp.concatenate(mix_grads + [grad_logits], axis=0))
    normed_column = jnp.broadcast_to(normed_gate, (8, tok)).T[:, 0:1]
    heads_rows = small_ref[4 : 8 + H].astype(bf16)
    pick_any = picks[0] + picks[1]
    grad_normed = grad_top * normed_column
    grad_normed = grad_normed + mm(
        token_rows, jnp.concatenate([heads_rows] * 3, axis=0), TN
    )
    pieces = piece_ref[...].reshape(E, owners, CAP, D)
    for o in range(owners):
        grad_normed = grad_normed + mm(pick_any, pieces[:, o].reshape(E * CAP, D), TN)
    grad_resid = grad_top + norm_back(resid_mid, gain, grad_normed)
    resid_ref[...] = grad_resid
    grad_attn = grad_resid.astype(bf16)
    gh_ref[...] = mm(w_ref[...].reshape(D, D), grad_attn, NT).astype(bf16).reshape(gh_ref.shape)
    copies = [
        remote(gh_ref.at[me ^ place], go_ref.at[me], (a_send, a_recv), place, {"seq": me ^ place})
        for place in range(1, n_seq)
    ]
    go_ref[me] = gh_ref[me]
    grad_w = mm(heads_ref[...].reshape(D, tok), grad_attn, NN)
    for j in range(n_seq):
        wo_ref[j] = grad_w[:, j * width : (j + 1) * width].astype(bf16)
    core_copies = [
        remote(wo_ref.at[me ^ (2 * i + 1)], wo_in.at[i], (c_send, c_recv), i, {"seq": me ^ 1})
        for i in range(pairs)
    ]
    base_ref[...] = (
        resid_mid
        + normed * normed_column
        + mm(vec_gate, jnp.concatenate([vecs] * 3, axis=0), TN)
    )
    dprev_ref[:, 0, :] = lax.dot_general(
        carry_ref[...].astype(f32), grad_logits, NN, precision=exact_prec,
        preferred_element_type=f32,
    )
    rest = (normed - low.astype(f32)).astype(bf16)
    row_sums = unsplit(mm(token_rows, low, NN))
    mix_sums = row_sums[:4] + unsplit(mm(token_rows, rest, NN))[:4]
    vec_sums = unsplit(mm(vec_gate, cot, NN))
    gain_sum = jnp.sum(grad_normed * resid_mid * rate, axis=0, keepdims=True)
    carry_grad = lax.dot_general(
        prev_ref[:, 0, :], grad_logits, NT, precision=exact_prec, preferred_element_type=f32
    )
    packed = jnp.concatenate([mix_sums, row_sums[4:], vec_sums, gain_sum], axis=0)
    lines, shard = packed.shape[0], D // n_dp
    for i in range(n_dp):
        pack_ref[i] = jnp.zeros(pack_ref.shape[1:], f32)
        pack_ref[i, 0:lines, :] = packed[:, i * shard : (i + 1) * shard]
        pack_ref[i, 24 : 24 + H, 0:H] = carry_grad
    for i in range(pairs):
        core_copies[i].wait_recv()
        wo_sum_ref[i] = (
            wo_ref[me ^ (2 * i)].astype(f32) + wo_in[i].astype(f32)
        ).astype(bf16)
    for copy in copies + tile_copies:
        copy.wait()
    for copy in core_copies:
        copy.wait_send()


def mid_back_call(
    n_seq, n_dp, piece, dots, cot, mid, gates, slot_of, routes, small, heads, w, prev, carry,
    parts,
):
    tok, width = cot.shape[0], heads.shape[1]
    pairs = n_seq // 2
    n_tile = len(parts)
    outs = pl.pallas_call(
        functools.partial(mid_back_kernel, n_seq, n_dp, n_tile),
        out_shape=(
            jax.ShapeDtypeStruct((tok, D), f32),
            jax.ShapeDtypeStruct((n_seq, width, tok), bf16),
            jax.ShapeDtypeStruct((tok, D), f32),
            jax.ShapeDtypeStruct((H, 1, tok), f32),
            jax.ShapeDtypeStruct((n_dp, LINES, D // n_dp), f32),
            jax.ShapeDtypeStruct((pairs, D, width), bf16),
        )
        + tuple(jax.ShapeDtypeStruct(part.shape, bf16) for part in parts),
        in_specs=[VMEM] * 12 + [HBM] * n_tile,
        out_specs=[VMEM] * 6 + [HBM] * n_tile,
        scratch_shapes=[
            pltpu.VMEM((n_seq, width, tok), bf16),
            pltpu.VMEM((n_seq, D, width), bf16),
            pltpu.VMEM((pairs, D, width), bf16),
            DMA((n_seq,)),
            DMA((n_seq,)),
            DMA((pairs,)),
            DMA((pairs,)),
            DMA((max(n_tile, 1),)),
            DMA((max(n_tile, 1),)),
        ],
        compiler_params=pltpu.CompilerParams(collective_id=3, has_side_effects=True),
        name="mid_back",
    )(piece, dots, cot, mid, gates, slot_of, routes, small, heads, w, prev, carry, *parts)
    return outs[:6], list(outs[6:])


def tail_kernel(
    n_seq, n_dp, parts, g_ref, wt_ref, wo_ref, pack_ref, gate_ref, slot_ref, gain_ref,
    a_hbm, h_hbm, resid_hbm, base_hbm, out_hbm, *refs,
):
    n_far = max(parts - 1, 0)
    fin_hbm, refs = refs[:parts], refs[parts:]
    far_hbm, refs = refs[:n_far], refs[n_far:]
    din_ref, row_in, line_ref, block_ref, both_ref, refs = *refs[:5], refs[5:]
    (
        a_ref, h_ref, resid_ref, base_ref, rows_ref, far_ref, fin_ref,
        core_out, core_in, x_out, x_in, part_ref, w_out_buf, w_in, wo_buf, wo_in, wo_x, wo_far,
        row_buf, pack_in, line_buf, line_in, load_sem, c_sems, x_sems, w_sems, r_sems, o_sems,
        p_sems, q_sems, l_sems, t_sems, f_sems, keep_sem,
    ) = refs
    me, dp = lax.axis_index("seq"), lax.axis_index("dp")
    tok = h_ref.shape[0]
    shard, width3 = w_in.shape[1], w_in.shape[2]
    width = width3 // 3
    owners = n_dp // E
    pairs = n_seq // 2
    others = range(1, n_dp)

    def both(sems):
        return sems.at[0], sems.at[1]

    c_sems, x_sems, w_sems, r_sems, o_sems, p_sems, q_sems, l_sems, t_sems, f_sems = (
        both(sems)
        for sems in (
            c_sems, x_sems, w_sems, r_sems, o_sems, p_sems, q_sems, l_sems, t_sems, f_sems
        )
    )

    loads = []
    for src, dst in [
        (a_hbm, a_ref), (out_hbm, rows_ref), (base_hbm, base_ref), (h_hbm, h_ref),
        (resid_hbm, resid_ref),
    ] + [(fin_hbm[t], fin_ref.at[t]) for t in range(parts)] + [
        (far_hbm[t], far_ref.at[t]) for t in range(n_far)
    ]:
        load = pltpu.make_async_copy(src, dst, load_sem.at[len(loads)])
        load.start()
        loads.append(load)
    greet(
        [{"seq": me ^ place} for place in range(1, n_seq)]
        + [{"dp": lax.rem(dp + k, n_dp)} for k in others]
    )

    def there(k):
        return lax.rem(dp + k, n_dp)

    def term(place):
        columns = pl.ds(pl.multiple_of((me ^ place) * tok, tok), tok)
        return mm(g_ref[:, columns], wt_ref[...], TN)

    part_copies = [
        remote(fin_hbm[t], far_ref.at[t], t_sems, 0, {"seq": me ^ 2}) for t in range(n_far, parts)
    ]
    pack_copies = [
        remote(pack_ref.at[there(k)], pack_in.at[dp], p_sems, k, {"dp": there(k)}) for k in others
    ]
    pack_in[dp] = pack_ref[dp]
    for i in range(pairs):
        wo_buf[:, :, i * width : (i + 1) * width] = wo_ref[i].reshape(n_dp, shard, width)
    wo_in[dp] = wo_buf[dp]
    wo_copies = [
        remote(wo_buf.at[there(k)], wo_in.at[dp], q_sems, k, {"dp": there(k)}) for k in others
    ]
    core_copies = []
    for i in range(pairs - 1, -1, -1):
        core_out[i] = term(2 * i + 1).astype(bf16)
        core_copies.insert(0, remote(core_out.at[i], core_in.at[i], c_sems, i, {"seq": me ^ 1}))
    x_copies = []
    for i in range(pairs - 1, 0, -1):
        part = term(2 * i)
        core_copies[i].wait_recv()
        x_out[i - 1] = (part + core_in[i].astype(f32)).astype(bf16)
        x_copies.append(
            remote(x_out.at[i - 1], x_in.at[i - 1], x_sems, i - 1, {"seq": me ^ (2 * i)})
        )
    loads[0].wait()
    turned = mm(g_ref[...], a_ref[...], NN)
    w_out_buf[...] = turned.T.astype(bf16).reshape(n_dp, shard, width3)
    w_in[dp] = w_out_buf[dp]
    w_copies = [
        remote(w_out_buf.at[there(k)], w_in.at[dp], w_sems, k, {"dp": there(k)}) for k in others
    ]
    part = term(0)
    core_copies[0].wait_recv()
    part_ref[...] = part + core_in[0].astype(f32)

    for copy in pack_copies:
        copy.wait_recv()
    line_buf[...] = jnp.sum(pack_in[...], axis=0)
    line_in[me] = line_buf[...]
    line_copies = [
        remote(line_buf, line_in.at[me], l_sems, place, {"seq": me ^ place})
        for place in range(1, n_seq)
    ]

    fin_copies, keeps = [], []

    def hand_over(ref, row, t):
        index = row * parts + t
        fin_copies.append(
            remote(ref.at[t], both_ref.at[2 * row + 1, t], f_sems, index, {"seq": me ^ 1})
        )
        keep = pltpu.make_async_copy(ref.at[t], both_ref.at[2 * row, t], keep_sem.at[index])
        keep.start()
        keeps.append(keep)

    for t in range(parts):
        loads[5 + t].wait()
        hand_over(fin_ref, 0, t)
    for t in range(n_far):
        loads[5 + parts + t].wait()
        hand_over(far_ref, 1, t)

    for copy in wo_copies:
        copy.wait_recv()
    wo_total = jnp.sum(wo_in[...].astype(f32), axis=0)
    wo_cross = []
    for i in range(1, pairs):
        wo_x[i - 1] = wo_total[:, i * width : (i + 1) * width].astype(bf16)
        wo_cross.append(
            remote(wo_x.at[i - 1], wo_far.at[i - 1], o_sems, i - 1, {"seq": me ^ (2 * i)})
        )

    loads[1].wait()
    loads[2].wait()
    picks = picks_of(slot_ref)
    rows = rows_ref[...].reshape(E, owners, CAP, D)
    columns = gate_ref[...].T
    block = base_ref[...]
    for k in range(2):
        picked = sum(
            mm(picks[k], rows[:, o].reshape(E * CAP, D), TN) for o in range(owners)
        )
        block = block + columns[:, k : k + 1] * picked
    block_ref[...] = block.astype(bf16)

    for copy in x_copies:
        copy.wait_recv()
    grad = part_ref[...]
    for i in range(pairs - 1):
        grad = grad + x_in[i].astype(f32)
    loads[3].wait()
    loads[4].wait()
    din_ref[...] = resid_ref[...] + norm_back(h_ref[...].astype(f32), gain_ref[0:1], grad)

    for copy in w_copies + wo_cross:
        copy.wait_recv()
    row_buf[:, :width3] = jnp.sum(w_in[...].astype(f32), axis=0).astype(bf16)
    wo_mine = wo_total[:, :width]
    for i in range(pairs - 1):
        wo_mine = wo_mine + wo_far[i].astype(f32)
    row_buf[:, width3:] = wo_mine.astype(bf16)
    row_in[me] = row_buf[...]
    row_copies = [
        remote(row_buf, row_in.at[me], r_sems, place, {"seq": me ^ place})
        for place in range(1, n_seq)
    ]
    for copy in line_copies:
        copy.wait_recv()
    line_ref[...] = jnp.sum(line_in[...], axis=0)
    for copy in part_copies:
        copy.wait_recv()
        hand_over(far_ref, 1, n_far)
    for copy in row_copies + fin_copies:
        copy.wait_recv()
    for copy in (
        core_copies + w_copies + x_copies + row_copies + wo_copies + pack_copies
        + line_copies + wo_cross + part_copies + fin_copies
    ):
        copy.wait_send()
    for keep in keeps:
        keep.wait()


def tail_call(
    n_seq, n_dp, grad_qkv, w_turned, wo_sum, pack, gates, slot_of, small,
    attn_in, hidden, grad_resid, base, back_out, fin, far,
):
    tok = hidden.shape[0]
    shard, width3 = D // n_dp, grad_qkv.shape[0]
    width = width3 // 3
    pairs = n_seq // 2
    parts, room = len(fin), max(len(fin), 1)
    part = (3, PART, D)
    return pl.pallas_call(
        functools.partial(tail_kernel, n_seq, n_dp, parts),
        out_shape=(
            jax.ShapeDtypeStruct((tok, D), f32),
            jax.ShapeDtypeStruct((n_seq, shard, width3 + width), bf16),
            jax.ShapeDtypeStruct((LINES, shard), f32),
            jax.ShapeDtypeStruct((tok, D), bf16),
            jax.ShapeDtypeStruct((n_seq, room, *part), bf16),
        ),
        in_specs=[VMEM] * 7 + [HBM] * (5 + parts + len(far)),
        out_specs=[VMEM] * 4 + [HBM],
        scratch_shapes=[
            pltpu.VMEM((n_seq * tok, D), bf16),
            pltpu.VMEM((tok, D), bf16),
            pltpu.VMEM((tok, D), f32),
            pltpu.VMEM((tok, D), f32),
            pltpu.VMEM((n_dp, CAP, D), bf16),
            pltpu.VMEM((room, *part), bf16),
            pltpu.VMEM((room, *part), bf16),
            pltpu.VMEM((pairs, tok, D), bf16),
            pltpu.VMEM((pairs, tok, D), bf16),
            pltpu.VMEM((pairs - 1, tok, D), bf16),
            pltpu.VMEM((pairs - 1, tok, D), bf16),
            pltpu.VMEM((tok, D), f32),
            pltpu.VMEM((n_dp, shard, width3), bf16),
            pltpu.VMEM((n_dp, shard, width3), bf16),
            pltpu.VMEM((n_dp, shard, pairs * width), bf16),
            pltpu.VMEM((n_dp, shard, pairs * width), bf16),
            pltpu.VMEM((pairs - 1, shard, width), bf16),
            pltpu.VMEM((pairs - 1, shard, width), bf16),
            pltpu.VMEM((shard, width3 + width), bf16),
            pltpu.VMEM((n_dp, LINES, shard), f32),
            pltpu.VMEM((LINES, shard), f32),
            pltpu.VMEM((n_seq, LINES, shard), f32),
            DMA((5 + 2 * room,)),
            DMA((2, pairs)),
            DMA((2, pairs)),
            DMA((2, n_dp)),
            DMA((2, n_seq)),
            DMA((2, pairs)),
            DMA((2, n_dp)),
            DMA((2, n_dp)),
            DMA((2, n_seq)),
            DMA((2, 1)),
            DMA((2, 2 * room)),
            DMA((2 * room,)),
        ],
        compiler_params=pltpu.CompilerParams(
            collective_id=1, has_side_effects=True, vmem_limit_bytes=67043328
        ),
        name="tail",
    )(
        grad_qkv, w_turned, wo_sum, pack, gates, slot_of, small,
        attn_in, hidden, grad_resid, base, back_out, *fin, *far,
    )


def finish_kernel(
    n_seq, me_ref, both_ref, row_ref, line_ref, wq_ref, gain_ref,
    de_ref, dw_ref, dwo_ref, again_ref, mgain_ref, router_ref, carry_ref, vec_ref, mix_ref,
):
    de_ref[...] = both_ref[0, 0].astype(f32)

    @pl.when(pl.program_id(0) == 0)
    def _():
        width = row_ref.shape[2] // 4
        for j in range(n_seq):
            block = row_ref[j].astype(f32)
            for c in range(3):
                left = c * width * n_seq + j * width
                dw_ref[:, left : left + width] = block[:, c * width : (c + 1) * width]
            dwo_ref[:, j * width : (j + 1) * width] = block[:, 3 * width :]
        sums = jnp.sum(dw_ref[...] * wq_ref[...].astype(f32), axis=1, keepdims=True)
        again_ref[...] = column_to_row(sums) / gain_ref[...].astype(f32)
        mix_ref[0] = line_ref[0:2]
        mix_ref[1] = line_ref[2:4]
        router_ref[...] = line_ref[4 : 4 + H]
        vec_ref[...] = line_ref[4 + H : 6 + H]
        mgain_ref[...] = line_ref[6 + H : 7 + H]
        carry_ref[...] = line_ref[24 : 24 + H, 0:H]


def finish_call(n_seq, me, both, row_in, lines, w_qkv, attn_gain):
    shard = w_qkv.shape[0]
    _, parts, three, step, _ = both.shape
    units = n_seq * parts * step

    def whole(shape):
        return pl.BlockSpec(shape, lambda i, me_ref: (0,) * len(shape))

    shapes = [(shard, 3 * D), (shard, D), (1, shard), (1, shard), (H, shard), (H, H), (2, shard),
              (2, 2, shard)]
    return pl.pallas_call(
        functools.partial(finish_kernel, n_seq),
        out_shape=[jax.ShapeDtypeStruct((three, units, D), f32)]
        + [jax.ShapeDtypeStruct(shape, f32) for shape in shapes],
        grid_spec=pltpu.PrefetchScalarGridSpec(
            num_scalar_prefetch=1,
            grid=(n_seq * parts,),
            in_specs=[
                pl.BlockSpec(
                    (1, 1, three, step, D),
                    lambda i, me_ref: ((i // parts) ^ me_ref[0], i % parts, 0, 0, 0),
                ),
                whole(row_in.shape),
                whole(lines.shape),
                whole(w_qkv.shape),
                whole((1, shard)),
            ],
            out_specs=[pl.BlockSpec((three, step, D), lambda i, me_ref: (0, i, 0))]
            + [whole(shape) for shape in shapes],
        ),
        name="finish",
    )(me, both, row_in, lines, w_qkv, attn_gain[None])


def rope_tables(seq_len):
    freq_index = jnp.arange(HD // 2, dtype=f32)
    inv_freq = jnp.exp(freq_index * (-2.0 * math.log(10000.0) / HD))
    angles = jnp.arange(seq_len, dtype=jnp.int32).astype(f32)[None, :] * inv_freq[:, None]
    return jnp.cos(angles), jnp.sin(angles)


def per_device(
    hidden_in,
    prev_logits,
    segments,
    routes,
    attn_gain,
    w_qkv,
    w_out,
    moe_gain,
    w_router,
    w_carry,
    const_vec,
    const_mix,
    experts,
    cotangent,
):
    n_seq, n_dp = lax.axis_size("seq"), lax.axis_size("dp")
    owners = n_dp // E
    me = lax.axis_index("seq")
    tok = hidden_in.shape[1]
    hidden, cot = hidden_in[0], cotangent[0]
    prev_t = jnp.transpose(prev_logits, (2, 0, 1))
    routes_t = routes[0].T

    def to_owners(values):
        return lax.all_to_all(
            jnp.repeat(values, owners, axis=0), "dp", split_axis=0, concat_axis=0, tiled=True
        )

    def to_sources(values):
        return lax.all_to_all(values, "dp", split_axis=0, concat_axis=0, tiled=True)

    cos_t, sin_t = rope_tables(tok * n_seq)
    attn_in, qkv, w_turned, small, slot_of, grad_slots, out_weight = start_call(
        n_seq, n_dp, hidden, w_qkv, attn_gain, moe_gain, const_vec, const_mix, w_router.T,
        routes_t, cot, cos_t, sin_t, w_out,
    )
    arrived_grad = to_owners(grad_slots)

    seg_row = segments[0]
    doc_ids = jnp.arange(16, dtype=jnp.int32)
    doc_start = jnp.sum((seg_row[None, :] < doc_ids[:, None]).astype(jnp.int32), axis=1)
    start = jnp.sum(jnp.where(seg_row[None, :] == doc_ids[:, None], doc_start[:, None], 0), axis=0)
    start_row = start.astype(jnp.int32)[None, :]
    lows = start[::BLK].astype(jnp.int32) // BLK
    attended, attended_exact, logs = attn_call(lows, qkv, start_row, tok)

    heads_t, resid_mid, gates, x_slots, gate_slots = mid_call(
        n_seq, attended, hidden, prev_t, w_carry, small, slot_of, routes_t, out_weight
    )
    if n_dp * CAP > 1024:
        piece, dots, partial, d_plain = experts_plain(
            to_owners, to_sources, n_dp, x_slots, gate_slots, experts, arrived_grad
        )
        fin = []
    else:
        piece, dots, partial, fin = moe_call(
            n_dp, x_slots, gate_slots, experts, arrived_grad
        )
    back_out = to_sources(partial)

    (grad_resid, grad_out, base, d_prev, pack, wo_sum), far_back = mid_back_call(
        n_seq, n_dp, piece, dots, cot, resid_mid, gates, slot_of, routes_t, small, heads_t,
        out_weight, prev_t, w_carry, fin[:1],
    )
    later, grad_out = lax.optimization_barrier((fin[1:-1], grad_out))
    far = far_back + [swap(part, "seq", 2) for part in later]
    grad_qkv = attn_back_call(
        lows, qkv, grad_out, attended_exact, logs, start_row, cos_t, sin_t
    )
    d_input, row_in, lines, block_out, both = tail_call(
        n_seq, n_dp, grad_qkv, w_turned, wo_sum, pack, gates, slot_of, small,
        attn_in, hidden, grad_resid, base, back_out, fin, far,
    )
    d_experts, d_qkv, d_out, again, mgain, router, carry, vec, mix = finish_call(
        n_seq, me.astype(jnp.int32).reshape(1), both, row_in, lines, w_qkv, attn_gain
    )
    if not fin:
        d_experts = d_plain
    return (
        block_out[None],
        d_input[None],
        jnp.transpose(d_prev, (1, 2, 0)),
        again[0],
        d_qkv,
        d_out,
        mgain[0],
        router.T,
        carry,
        vec,
        mix,
        d_experts,
    )


def solution(mesh):
    return jax.shard_map(
        per_device,
        mesh=mesh,
        in_specs=(
            P("dp", "seq", None),
            P("dp", "seq", None),
            P("dp", None),
            P("dp", "seq", None),
            P("dp"),
            P("dp", None),
            P("dp", None),
            P("dp"),
            P("dp", None),
            P(),
            P(None, "dp"),
            P(None, None, "dp"),
            P(None, "dp", None),
            P("dp", "seq", None),
        ),
        out_specs=(
            P("dp", "seq", None),
            P("dp", "seq", None),
            P("dp", "seq", None),
            P("dp"),
            P("dp", None),
            P("dp", None),
            P("dp"),
            P("dp", None),
            P(),
            P(None, "dp"),
            P(None, None, "dp"),
            P(None, "dp", None),
        ),
        check_vma=False,
    )
```

```python
import functools
import math

import jax
import jax.numpy as jnp
from jax import lax
from jax.experimental import pallas as pl
from jax.experimental.pallas import tpu as pltpu
from jax.sharding import PartitionSpec as P

D = 768
H = 12
HD = 64
E = 8
CAP = 128
BLK = 256
PAIR = 2 * CAP
UNITS = 256
PART = 64
EARLY = 2
LATE = 2
SMALL = 32
LINES = 40

exact_prec = lax.Precision.HIGHEST
neg_large = -1e30
score_scale = 0.125 * math.log2(math.e)
f32 = jnp.float32
bf16 = jnp.bfloat16

NN = (((1,), (0,)), ((), ()))
NT = (((1,), (1,)), ((), ()))
TN = (((0,), (0,)), ((), ()))


MESH = pl.DeviceIdType.MESH
VMEM = pl.BlockSpec(memory_space=pltpu.VMEM)
HBM = pl.BlockSpec(memory_space=pl.ANY)
DMA = pltpu.SemaphoreType.DMA


def mm(a, b, dims):
    return lax.dot_general(a, b, dims, preferred_element_type=f32)


def swap(value, axis, bit):
    size = lax.axis_size(axis)
    return lax.ppermute(value, axis, [(i, i ^ bit) for i in range(size)])


def bits_high_first(size):
    bit = size // 2
    while bit >= 1:
        yield bit
        bit //= 2


def greet(peers):
    barrier = pltpu.get_barrier_semaphore()
    for peer in peers:
        pl.semaphore_signal(barrier, inc=1, device_id=peer, device_id_type=MESH)
    pl.semaphore_wait(barrier, len(peers))


def remote_later(src, dst, sems, index, target):
    return pltpu.make_async_remote_copy(
        src_ref=src,
        dst_ref=dst,
        send_sem=sems[0].at[index],
        recv_sem=sems[1].at[index],
        device_id=target,
        device_id_type=MESH,
    )


def remote(src, dst, sems, index, target):
    copy = remote_later(src, dst, sems, index, target)
    copy.start()
    return copy


def one_hot(condition):
    return jnp.where(condition, 1.0, 0.0).astype(bf16)


def picks_of(slot_ref):
    slots = lax.broadcasted_iota(jnp.int32, (E * CAP, slot_ref.shape[1]), 0)
    return [one_hot(slots == slot_ref[k : k + 1, :]) for k in range(2)]


def split(rows):
    high = rows.astype(bf16)
    rest = rows - high.astype(f32)
    middle = rest.astype(bf16)
    low = (rest - middle.astype(f32)).astype(bf16)
    return jnp.concatenate([high, middle, low], axis=0)


def unsplit(rows):
    third = rows.shape[0] // 3
    return rows[:third] + rows[third : 2 * third] + rows[2 * third :]


def column_to_row(column):
    return jnp.broadcast_to(column, (column.shape[0], 128)).T[0:1]


def norm_back(values, gain, grad):
    rate = lax.rsqrt(jnp.mean(values * values, axis=-1, keepdims=True) + 1e-06)
    scaled = gain * grad
    inner = jnp.mean(values * scaled, axis=-1, keepdims=True)
    return rate * scaled - values * (rate * rate * rate) * inner


def make_slots(route_ref, cot_ref, slot_ref, g_ref):
    tok = route_ref.shape[1]
    ids = lax.broadcasted_iota(jnp.int32, (E, tok), 0)
    named = [route_ref[k : k + 1, :] == ids for k in range(2)]
    earlier = lax.broadcasted_iota(jnp.int32, (tok, tok), 0) < lax.broadcasted_iota(
        jnp.int32, (tok, tok), 1
    )
    ranks = mm(one_hot(named[0] | named[1]), one_hot(earlier), NN)
    for k in range(2):
        route = route_ref[k : k + 1, :]
        rank = jnp.sum(jnp.where(named[k], ranks, 0.0), axis=0, keepdims=True)
        slot_ref[k : k + 1, :] = jnp.where(
            route < E, route * CAP + rank.astype(jnp.int32), E * CAP
        )
    picks = picks_of(slot_ref)
    g_ref[...] = mm(picks[0] + picks[1], cot_ref[...], NN).astype(bf16).reshape(g_ref.shape)


def start_kernel(
    n_seq, n_dp, h_ref, w_ref, again_ref, mgain_ref, vec_ref, mix_ref, router_ref,
    route_ref, cot_ref, cos_ref, sin_ref, wo_ref,
    attn_ref, qkv_ref, wt_ref, small_ref, slot_ref, g_ref, wo_all,
    all_ref, slice_ref, small_buf, h_send, h_recv, near_send, near_recv, next_send, next_recv,
    c_send, c_recv,
):
    me, dp = lax.axis_index("seq"), lax.axis_index("dp")
    tok = h_ref.shape[0]
    width = slice_ref.shape[2] // 3
    seq_bits = list(bits_high_first(n_seq))
    greet(
        [{"seq": me ^ bit} for bit in seq_bits]
        + [{"dp": dp ^ 1}]
        + [{"dp": dp ^ (2 * j)} for j in range(1, n_dp // 2)]
    )

    plan, arrival = [], {}
    order = [(0, bit) for bit in seq_bits]
    while order:
        place, bit = order.pop(0)
        copy = remote_later(
            h_ref if place == 0 else all_ref.at[me ^ place],
            all_ref.at[me ^ place],
            (h_send, h_recv),
            len(plan),
            {"seq": me ^ bit},
        )
        arrival[place ^ bit] = copy
        plan.append((place, copy))
        order += [(place ^ bit, low) for low in seq_bits if low < bit]
    for place, copy in plan:
        if place == 0:
            copy.start()

    for j in range(n_seq):

        @pl.when(me == j)
        def _():
            for c in range(3):
                left = c * width * n_seq + j * width
                slice_ref[dp, :, c * width : (c + 1) * width] = w_ref[:, left : left + width]

    small_buf[dp] = jnp.zeros(small_buf.shape[1:], bf16)
    small_buf[dp, 0:1, :] = again_ref[...]
    small_buf[dp, 1:2, :] = mgain_ref[...]
    small_buf[dp, 2:4, :] = vec_ref[...]
    small_buf[dp, 4:6, :] = mix_ref[0]
    small_buf[dp, 6:8, :] = mix_ref[1]
    small_buf[dp, 8 : 8 + H, :] = router_ref[...]
    cols = pl.ds(pl.multiple_of((me & 1) * (D // 2), D // 2), D // 2)
    wo_all[dp, :, cols] = wo_ref[:, cols]

    def rows_of(kind, source):
        return (small_buf.at[source], slice_ref.at[source], wo_all.at[source, :, cols])[kind]

    def first_copy(kind, j):
        return remote_later(
            rows_of(kind, dp), rows_of(kind, dp), (near_send.at[kind], near_recv.at[kind]), j,
            {"dp": dp ^ (2 * j)},
        )

    def next_copy(kind, j):
        return remote_later(
            rows_of(kind, dp ^ (2 * j)), rows_of(kind, dp ^ (2 * j)),
            (next_send.at[kind], next_recv.at[kind]), j, {"dp": dp ^ 1},
        )

    places = range(1, n_dp // 2)
    for kind in range(3):
        for j in places:
            first_copy(kind, j).start()
        next_copy(kind, 0).start()
    make_slots(route_ref, cot_ref, slot_ref, g_ref)

    def pass_on(kind):
        for j in places:
            first_copy(kind, j).wait_recv()
            next_copy(kind, j).start()

    def complete(kind):
        for j in range(n_dp // 2):
            next_copy(kind, j).wait_recv()

    pass_on(0)
    complete(0)
    small_ref[...] = jnp.concatenate([small_buf[i].astype(f32) for i in range(n_dp)], axis=1)

    def normalize(block, ref):
        x = ref.astype(f32)
        mean_square = jnp.mean(x * x, axis=-1, keepdims=True)
        rows = pl.ds(pl.multiple_of(block * tok, tok), tok)
        attn_ref[rows, :] = (x * lax.rsqrt(mean_square + 1e-06) * small_ref[0:1]).astype(bf16)

    normalize(me, h_ref[...])
    pass_on(1)
    for place in arrival:
        arrival[place].wait_recv()
        for source, copy in plan:
            if source == place:
                copy.start()
        normalize(me ^ place, all_ref[me ^ place])
    complete(1)
    pass_on(2)
    wt_ref[...] = slice_ref[...].reshape(D, 3 * width).T
    half = HD // 2

    @pl.loop(0, attn_ref.shape[0] // BLK)
    def _(i):
        rows = pl.ds(pl.multiple_of(i * BLK, BLK), BLK)
        y = mm(wt_ref[...], attn_ref[rows, :], NT)
        cos, sin = cos_ref[:, rows], sin_ref[:, rows]
        for head in range(2 * width // HD):
            low, middle, high = head * HD, head * HD + half, (head + 1) * HD
            a, b = y[low:middle], y[middle:high]
            qkv_ref[low:middle, rows] = (a * cos - b * sin).astype(bf16)
            qkv_ref[middle:high, rows] = (a * sin + b * cos).astype(bf16)
        qkv_ref[2 * width :, rows] = y[2 * width :].astype(bf16)

    complete(2)
    trade = remote(
        wo_all.at[:, :, cols], wo_all.at[:, :, cols], (c_send, c_recv), 0, {"seq": me ^ 1}
    )
    for _, copy in plan:
        copy.wait_send()
    for kind in range(3):
        for j in places:
            first_copy(kind, j).wait_send()
        for j in range(n_dp // 2):
            next_copy(kind, j).wait_send()
    trade.wait()


def start_call(
    n_seq, n_dp, hidden, w_qkv, attn_gain, moe_gain, vec, mix, router, routes, cotangent, cos, sin,
    w_out,
):
    tok, shard = hidden.shape[0], w_qkv.shape[0]
    width3 = w_qkv.shape[1] // n_seq
    hops = n_seq - 1
    return pl.pallas_call(
        functools.partial(start_kernel, n_seq, n_dp),
        out_shape=(
            jax.ShapeDtypeStruct((n_seq * tok, D), bf16),
            jax.ShapeDtypeStruct((width3, n_seq * tok), bf16),
            jax.ShapeDtypeStruct((width3, D), bf16),
            jax.ShapeDtypeStruct((SMALL, D), f32),
            jax.ShapeDtypeStruct(routes.shape, jnp.int32),
            jax.ShapeDtypeStruct((E, CAP, D), bf16),
            jax.ShapeDtypeStruct((n_dp, shard, D), bf16),
        ),
        in_specs=[VMEM] * 12,
        out_specs=[VMEM] * 7,
        scratch_shapes=[
            pltpu.VMEM((n_seq, tok, D), bf16),
            pltpu.VMEM((n_dp, shard, width3), bf16),
            pltpu.VMEM((n_dp, SMALL, shard), bf16),
            DMA((hops,)),
            DMA((hops,)),
            DMA((3, n_dp // 2)),
            DMA((3, n_dp // 2)),
            DMA((3, n_dp // 2)),
            DMA((3, n_dp // 2)),
            DMA((1,)),
            DMA((1,)),
        ],
        compiler_params=pltpu.CompilerParams(collective_id=0, has_side_effects=True),
        name="start",
    )(
        hidden, w_qkv, attn_gain[None], moe_gain[None], vec, mix, router, routes, cotangent,
        cos, sin, w_out,
    )


def allowed_block(key_block, query_block, start_row):
    key_pos = key_block * BLK + lax.broadcasted_iota(jnp.int32, (BLK, BLK), 0)
    query_pos = query_block * BLK + lax.broadcasted_iota(jnp.int32, (BLK, BLK), 1)
    return (key_pos >= start_row) & (key_pos <= query_pos)


def attn_kernel(lo_ref, qkv_ref, start_ref, out_ref, exact_ref, log_ref, keys_ref):
    heads, seq_len, _ = keys_ref.shape
    width = heads * HD
    qb = pl.program_id(0)

    @pl.when(qb == 0)
    def _():
        for h in range(heads):
            keys_ref[h] = qkv_ref[width + h * HD : width + (h + 1) * HD, :].T

    here = pl.ds(pl.multiple_of(qb * BLK, BLK), BLK)
    start_row = start_ref[...]

    def step(kb, carry):
        there = pl.ds(pl.multiple_of(kb * BLK, BLK), BLK)
        allowed = allowed_block(kb, qb, start_row)
        scores = [
            mm(keys_ref[h, there, :], qkv_ref[h * HD : (h + 1) * HD, here], NN)
            for h in range(heads)
        ]
        stats, weights = [], []
        for h in range(heads):
            top, total, acc = carry[h]
            masked = jnp.where(allowed, scores[h] * score_scale, neg_large)
            new_top = jnp.maximum(top, jnp.max(masked, axis=0, keepdims=True))
            fade = jnp.exp2(top - new_top)
            weight = jnp.exp2(masked - new_top)
            total = total * fade + jnp.sum(weight, axis=0, keepdims=True)
            stats.append((new_top, total, acc * fade))
            weights.append(weight.astype(bf16))
        new = []
        for h in range(heads):
            values = qkv_ref[2 * width + h * HD : 2 * width + (h + 1) * HD, there]
            top, total, acc = stats[h]
            new.append((top, total, acc + mm(values, weights[h], NN)))
        return tuple(new)

    first = tuple(
        (
            jnp.full((1, BLK), neg_large, f32),
            jnp.zeros((1, BLK), f32),
            jnp.zeros((HD, BLK), f32),
        )
        for _ in range(heads)
    )
    done = lax.fori_loop(lo_ref[qb], qb + 1, step, first)
    for h in range(heads):
        top, total, acc = done[h]
        attended = acc / total
        exact_ref[h * HD : (h + 1) * HD, :] = attended
        out_ref[0, h * HD : (h + 1) * HD, :] = attended.astype(bf16)
        log_ref[h : h + 1, :] = top + jnp.log2(total)


def attn_call(lows, qkv, start_row, tok):
    width3, seq_len = qkv.shape
    width = width3 // 3
    heads = width // HD
    per = tok // BLK
    return pl.pallas_call(
        attn_kernel,
        out_shape=(
            jax.ShapeDtypeStruct((seq_len // tok, width, tok), bf16),
            jax.ShapeDtypeStruct((width, seq_len), f32),
            jax.ShapeDtypeStruct((heads, seq_len), f32),
        ),
        grid_spec=pltpu.PrefetchScalarGridSpec(
            num_scalar_prefetch=1,
            grid=(seq_len // BLK,),
            in_specs=[
                pl.BlockSpec((width3, seq_len), lambda i, lo: (0, 0)),
                pl.BlockSpec((1, BLK), lambda i, lo: (0, i)),
            ],
            out_specs=[
                pl.BlockSpec((1, width, BLK), lambda i, lo: (i // per, 0, i % per)),
                pl.BlockSpec((width, BLK), lambda i, lo: (0, i)),
                pl.BlockSpec((heads, BLK), lambda i, lo: (0, i)),
            ],
            scratch_shapes=[pltpu.VMEM((heads, seq_len, HD), bf16)],
        ),
        cost_estimate=pl.CostEstimate(
            flops=16_000_000_000, transcendentals=0, bytes_accessed=16_000_000
        ),
        name="attend",
    )(lows, qkv, start_row)


def attn_back_kernel(
    lo_ref, qkv_ref, go_ref, exact_ref, log_ref, start_ref, cos_ref, sin_ref, out_ref,
    keys_ref, values_ref, dk_ref, dv_ref,
):
    heads, seq_len, _ = keys_ref.shape
    width = heads * HD
    half = HD // 2
    qb = pl.program_id(0)

    @pl.when(qb == 0)
    def _():
        for h in range(heads):
            keys_ref[h] = qkv_ref[width + h * HD : width + (h + 1) * HD, :].T
            values_ref[h] = qkv_ref[2 * width + h * HD : 2 * width + (h + 1) * HD, :].T
        dk_ref[...] = jnp.zeros_like(dk_ref)
        dv_ref[...] = jnp.zeros_like(dv_ref)

    here = pl.ds(pl.multiple_of(qb * BLK, BLK), BLK)
    start_row = start_ref[...]
    grad = go_ref[0]
    deltas = [
        jnp.sum(
            exact_ref[h * HD : (h + 1) * HD, :] * grad[h * HD : (h + 1) * HD].astype(f32),
            axis=0,
            keepdims=True,
        )
        for h in range(heads)
    ]

    def step(kb, carry):
        there = pl.ds(pl.multiple_of(kb * BLK, BLK), BLK)
        allowed = allowed_block(kb, qb, start_row)
        spans = [slice(h * HD, (h + 1) * HD) for h in range(heads)]
        queries = [qkv_ref[rows, here] for rows in spans]
        scores = [mm(keys_ref[h, there, :], queries[h], NN) for h in range(heads)]
        grad_probs = [mm(values_ref[h, there, :], grad[spans[h]], NN) for h in range(heads)]
        probs, grad_scores = [], []
        for h in range(heads):
            masked = jnp.where(allowed, scores[h] * score_scale, neg_large)
            prob = jnp.exp2(masked - log_ref[h : h + 1, :])
            probs.append(prob.astype(bf16))
            grad_scores.append((prob * (grad_probs[h] - deltas[h])).astype(bf16))
        new = []
        for h in range(heads):
            dv_ref[spans[h], there] += mm(grad[spans[h]], probs[h], NT)
        for h in range(heads):
            dk_ref[spans[h], there] += mm(queries[h], grad_scores[h], NT)
        for h in range(heads):
            keys = qkv_ref[width + h * HD : width + (h + 1) * HD, there]
            new.append(carry[h] + mm(keys, grad_scores[h], NN))
        return tuple(new)

    grads = lax.fori_loop(
        lo_ref[qb], qb + 1, step, tuple(jnp.zeros((HD, BLK), f32) for _ in range(heads))
    )

    def turn_back(value, cos, sin):
        value = value.astype(bf16).astype(f32)
        a, b = value[:half], value[half:]
        return (a * cos + b * sin).astype(bf16), (b * cos - a * sin).astype(bf16)

    for h in range(heads):
        a, b = turn_back(grads[h] * 0.125, cos_ref[:, here], sin_ref[:, here])
        out_ref[h * HD : h * HD + half, here] = a
        out_ref[h * HD + half : (h + 1) * HD, here] = b

    @pl.when(qb == pl.num_programs(0) - 1)
    def _():
        cos, sin = cos_ref[...], sin_ref[...]
        for h in range(heads):
            a, b = turn_back(dk_ref[h * HD : (h + 1) * HD, :] * 0.125, cos, sin)
            out_ref[width + h * HD : width + h * HD + half, :] = a
            out_ref[width + h * HD + half : width + (h + 1) * HD, :] = b
        out_ref[2 * width :, :] = dv_ref[...].astype(bf16)


def attn_back_call(lows, qkv, grad_out, exact, logs, start_row, cos_t, sin_t):
    width3, seq_len = qkv.shape
    width = width3 // 3
    heads = width // HD
    per = grad_out.shape[2] // BLK
    return pl.pallas_call(
        attn_back_kernel,
        out_shape=jax.ShapeDtypeStruct((width3, seq_len), bf16),
        grid_spec=pltpu.PrefetchScalarGridSpec(
            num_scalar_prefetch=1,
            grid=(seq_len // BLK,),
            in_specs=[
                pl.BlockSpec((width3, seq_len), lambda i, lo: (0, 0)),
                pl.BlockSpec((1, width, BLK), lambda i, lo: (i // per, 0, i % per)),
                pl.BlockSpec((width, BLK), lambda i, lo: (0, i)),
                pl.BlockSpec((heads, BLK), lambda i, lo: (0, i)),
                pl.BlockSpec((1, BLK), lambda i, lo: (0, i)),
                pl.BlockSpec((HD // 2, seq_len), lambda i, lo: (0, 0)),
                pl.BlockSpec((HD // 2, seq_len), lambda i, lo: (0, 0)),
            ],
            out_specs=pl.BlockSpec((width3, seq_len), lambda i, lo: (0, 0)),
            scratch_shapes=[
                pltpu.VMEM((heads, seq_len, HD), bf16),
                pltpu.VMEM((heads, seq_len, HD), bf16),
                pltpu.VMEM((width, seq_len), f32),
                pltpu.VMEM((width, seq_len), f32),
            ],
        ),
        cost_estimate=pl.CostEstimate(
            flops=16_000_000_000, transcendentals=0, bytes_accessed=16_000_000
        ),
        name="attend_back",
    )(lows, qkv, grad_out, exact, logs, start_row, cos_t, sin_t)


def gates_back(grad_hidden, gate_pre, up_pre):
    sig = 1.0 / (1.0 + jnp.exp(-gate_pre))
    silu = gate_pre * sig
    grad_gate = grad_hidden * up_pre * sig * (1.0 + gate_pre * (1.0 - sig))
    return (
        (silu * up_pre).astype(bf16),
        grad_gate.astype(bf16),
        (grad_hidden * silu).astype(bf16),
    )


def moe_kernel(n_dp, parts, x_ref, gate_ref, w_hbm, g_ref, *refs):
    piece_ref, dots_ref, out_ref, refs = refs[0], refs[1], refs[2], refs[3:]
    fin_hbm, refs = refs[:parts], refs[parts:]
    cross_hbm, refs = refs[:EARLY], refs[EARLY:]
    (
        w_ref, x_in, x_far, g_far, gate_in, gate_far, gs_ref, gs_far, pair_ref, near_ref, far_ref,
        own_ref, piece_out, dot_out, dw_out, dw_in, fin_ref,
        w_sem, x_send, x_recv, t_send, t_recv, p_send, p_recv, d_send, d_recv,
        xf_send, xf_recv, gf_send, gf_recv, tf_send, tf_recv, c_send, c_recv, e_send, e_recv, keep_sem,
    ) = refs
    me, dp = lax.axis_index("seq"), lax.axis_index("dp")
    owners = n_dp // E
    pairs = n_dp // 2
    half = near_ref.shape[2]
    core, plane = me & 1, lax.div(me, 2)
    greet([{"dp": dp ^ k} for k in range(1, n_dp)] + [{"seq": me ^ 1}, {"seq": me ^ 2}])

    def x_copy(k):
        return remote_later(
            x_ref.at[(dp ^ k) // owners], x_in.at[k], (x_send, x_recv), k, {"dp": dp ^ k}
        )

    def gate_copy(k):
        return remote_later(
            gate_ref.at[(dp ^ k) // owners], gate_in.at[k], (t_send, t_recv), k, {"dp": dp ^ k}
        )

    def piece_copy(k):
        return remote_later(
            piece_out.at[k], piece_ref.at[dp], (p_send, p_recv), k, {"dp": dp ^ k}
        )

    def dot_copy(k):
        return remote_later(dot_out.at[k], dots_ref.at[dp], (d_send, d_recv), k, {"dp": dp ^ k})

    def far_copies(k):
        across = {"seq": me ^ 2}
        return [
            remote_later(gate_in.at[k], gate_far.at[k], (tf_send, tf_recv), k, across),
            remote_later(g_ref.at[dp ^ k], g_far.at[k], (gf_send, gf_recv), k, across),
            remote_later(x_in.at[k], x_far.at[k], (xf_send, xf_recv), k, across),
        ]

    def core_copy(t):
        return remote_later(dw_out.at[t], dw_in.at[t], (c_send, c_recv), t, {"seq": me ^ 1})

    for p in [0, pairs - 1, *range(1, pairs - 1)]:
        for k in (2 * p, 2 * p + 1):
            if k:
                gate_copy(k).start()
                x_copy(k).start()
    loads = [pltpu.make_async_copy(w_hbm.at[j], w_ref.at[j], w_sem.at[j]) for j in range(3)]
    loads.append(pltpu.make_async_copy(x_ref.at[dp // owners], x_in.at[0], w_sem.at[3]))
    for load in loads:
        load.start()
    gate_in[0] = gate_ref[dp // owners]
    for load in loads:
        load.wait()

    def place(i):
        return jnp.where(i == 0, 0, 1 + lax.rem(i + pairs - 3, pairs - 1))

    def scale(ref, rows, gate, k):
        column = jnp.broadcast_to(gate, (CAP, CAP)).T[:, 0:1]
        here = pl.ds(pl.multiple_of(k * CAP, CAP), CAP)
        ref[here] = (rows.astype(f32) * column).astype(bf16)

    @pl.loop(0, pairs)
    def _(i):
        p = place(i)
        rows = pl.ds(pl.multiple_of(p * PAIR, PAIR), PAIR)

        def arrive(k):
            x_copy(k).wait_recv()
            gate_copy(k).wait_recv()

        @pl.when(p > 0)
        def _():
            arrive(2 * p)

        arrive(2 * p + 1)
        for side in range(2):
            k = 2 * p + side
            for copy in far_copies(k):
                copy.start()
            scale(gs_ref, g_ref[dp ^ k], gate_in[k], k)

        @pl.loop(0, 2)
        def _(t):
            part = pl.ds(pl.multiple_of(t * half, half), half)
            x = x_in[pl.ds(2 * p, 2)].reshape(PAIR, D)
            gate_pre = mm(x, w_ref[0, part], NT)
            up_pre = mm(x, w_ref[1, part], NT)
            grad_hidden = mm(gs_ref[rows], w_ref[2, part], NT)
            results = gates_back(grad_hidden, gate_pre, up_pre)
            for j in range(3):
                pair_ref[j, :, part] = results[j]

            @pl.when(t == plane)
            def _():
                for j in range(3):
                    near_ref[j, rows] = results[j]

        pieces = mm(pair_ref[1], w_ref[0], NN) + mm(pair_ref[2], w_ref[1], NN)
        piece_out[pl.ds(2 * p, 2)] = pieces.astype(bf16).reshape(2, CAP, D)
        piece_copy(2 * p + 1).start()

        @pl.when(p > 0)
        def _():
            piece_copy(2 * p).start()

        outs = mm(pair_ref[0], w_ref[2], NN)
        for side in range(2):
            k = 2 * p + side
            out = outs[side * CAP : (side + 1) * CAP].astype(bf16)
            out_ref[dp ^ k] = out
            product = out.astype(f32) * g_ref[dp ^ k].astype(f32)
            dot_out[k] = column_to_row(jnp.sum(product, axis=1, keepdims=True))
        dot_copy(2 * p + 1).start()

        @pl.when(p > 0)
        def _():
            dot_copy(2 * p).start()

    piece_ref[dp] = piece_out[0]
    dots_ref[dp] = dot_out[0]

    def weight_grad(source, x, gs, j, part):
        left = source[(1, 2, 0)[j], :, part]
        return mm(left, gs[...] if j == 2 else x[...].reshape(n_dp * CAP, D), TN)

    @pl.loop(0, half // UNITS)
    def _(t):
        part = pl.ds(pl.multiple_of(t * UNITS, UNITS), UNITS)
        for j in range(3):
            own_ref[j, part] = weight_grad(near_ref, x_in, gs_ref, j, part)

    def far_grad(rows, j, part):
        left = far_ref[(1, 2, 0)[j], :, part]
        if j == 2:
            right = gs_far[rows]
        elif isinstance(rows, slice):
            right = x_far[rows.start // CAP : rows.stop // CAP].reshape(PAIR, D)
        else:
            right = x_far[pl.ds(lax.div(rows.start, CAP), 2)].reshape(PAIR, D)
        return mm(left, right, TN)

    @pl.loop(0, pairs)
    def _(i):
        p = place(i)
        rows = pl.ds(pl.multiple_of(p * PAIR, PAIR), PAIR)
        for side in range(2):
            k = 2 * p + side
            for copy in far_copies(k):
                copy.wait_recv()
            scale(gs_far, g_far[k], gate_far[k], k)
        part = pl.ds(pl.multiple_of(plane * half, half), half)
        x = x_far[pl.ds(2 * p, 2)].reshape(PAIR, D)
        results = gates_back(
            mm(gs_far[rows], w_ref[2, part], NT),
            mm(x, w_ref[0, part], NT),
            mm(x, w_ref[1, part], NT),
        )
        for j in range(3):
            far_ref[j] = results[j]

        @pl.when(i < pairs - 1)
        def _():
            @pl.loop(0, half // UNITS)
            def _(t):
                part = pl.ds(pl.multiple_of(t * UNITS, UNITS), UNITS)
                for j in range(3):
                    own_ref[j, part] += far_grad(rows, j, part)

    tiles = half // UNITS // 2
    final = slice((pairs - 2) * PAIR, (pairs - 1) * PAIR)

    def both_rows(side, t, j):
        part = pl.ds(pl.multiple_of((side * tiles + t) * UNITS, UNITS), UNITS)
        return own_ref[j, part] + far_grad(final, j, part)

    @pl.loop(0, tiles)
    def _(t):
        for j in range(3):
            dw_out[t, j] = both_rows(1 - core, t, j).astype(bf16)
        core_copy(t).start()

    def early_copy(t):
        return remote_later(fin_ref.at[t], cross_hbm[t], (e_send, e_recv), t, {"seq": me ^ 2})

    @pl.loop(0, tiles)
    def _(t):
        core_copy(t).wait_recv()
        for j in range(3):
            total = (both_rows(core, t, j) + dw_in[t, j].astype(f32)).astype(bf16)
            for u in range(UNITS // PART):
                fin_ref[t * (UNITS // PART) + u, j] = total[u * PART : (u + 1) * PART]

        @pl.when(t == 0)
        def _():
            for e in range(EARLY):
                early_copy(e).start()

    keeps = [
        pltpu.make_async_copy(fin_ref.at[t], fin_hbm[t], keep_sem.at[t]) for t in range(parts)
    ]
    for keep in keeps:
        keep.start()
    for k in range(1, n_dp):
        piece_copy(k).wait()
        dot_copy(k).wait()
        x_copy(k).wait_send()
        gate_copy(k).wait_send()
    for k in range(n_dp):
        for copy in far_copies(k):
            copy.wait_send()
    for t in range(tiles):
        core_copy(t).wait_send()
    for t in range(EARLY):
        early_copy(t).wait()
    for keep in keeps:
        keep.wait()


def moe_call(n_dp, x_slots, gate_slots, weights, grads):
    units = weights.shape[1]
    half = units // 2
    rows = n_dp * CAP
    parts = units // 4 // PART
    tiles = half // UNITS // 2
    outs = pl.pallas_call(
        functools.partial(moe_kernel, n_dp, parts),
        out_shape=(
            jax.ShapeDtypeStruct((n_dp, CAP, D), bf16),
            jax.ShapeDtypeStruct((n_dp, 1, CAP), f32),
            jax.ShapeDtypeStruct((n_dp, CAP, D), bf16),
        )
        + (jax.ShapeDtypeStruct((3, PART, D), bf16),) * (parts + EARLY),
        in_specs=[HBM, VMEM, HBM, VMEM],
        out_specs=[VMEM] * 3 + [HBM] * (parts + EARLY),
        scratch_shapes=[
            pltpu.VMEM(weights.shape, bf16),
            pltpu.VMEM((n_dp, CAP, D), bf16),
            pltpu.VMEM((n_dp, CAP, D), bf16),
            pltpu.VMEM((n_dp, CAP, D), bf16),
            pltpu.VMEM((n_dp, 1, CAP), f32),
            pltpu.VMEM((n_dp, 1, CAP), f32),
            pltpu.VMEM((rows, D), bf16),
            pltpu.VMEM((rows, D), bf16),
            pltpu.VMEM((3, PAIR, units), bf16),
            pltpu.VMEM((3, rows, half), bf16),
            pltpu.VMEM((3, PAIR, half), bf16),
            pltpu.VMEM((3, half, D), f32),
            pltpu.VMEM((n_dp, CAP, D), bf16),
            pltpu.VMEM((n_dp, 1, CAP), f32),
            pltpu.VMEM((tiles, 3, UNITS, D), bf16),
            pltpu.VMEM((tiles, 3, UNITS, D), bf16),
            pltpu.VMEM((parts, 3, PART, D), bf16),
            DMA((4,)),
        ]
        + [DMA((n_dp,))] * 14
        + [DMA((tiles,))] * 2
        + [DMA((EARLY,))] * 2
        + [DMA((parts,))],
        compiler_params=pltpu.CompilerParams(
            collective_id=4, has_side_effects=True, vmem_limit_bytes=67043328
        ),
        name="experts",
    )(x_slots, gate_slots, weights, grads)
    return outs[0], outs[1], outs[2], list(outs[3 : 3 + parts]), list(outs[3 + parts :])


def experts_plain(to_owners, to_sources, n_dp, x_slots, gate_slots, weights, grads):
    rows = n_dp * CAP
    x = to_owners(x_slots).reshape(rows, D)
    gate = to_owners(gate_slots).reshape(rows, 1)
    g = grads.reshape(rows, D)
    gs = (g.astype(f32) * gate).astype(bf16)
    hidden, grad_gate, grad_up = gates_back(
        mm(gs, weights[2], NT), mm(x, weights[0], NT), mm(x, weights[1], NT)
    )
    out = mm(hidden, weights[2], NN).astype(bf16)
    piece = (mm(grad_gate, weights[0], NN) + mm(grad_up, weights[1], NN)).astype(bf16)
    dw = jnp.stack([mm(grad_gate, x, TN), mm(grad_up, x, TN), mm(hidden, gs, TN)])
    dots = jnp.sum(out.astype(f32) * g.astype(f32), axis=-1)
    return (
        to_sources(piece.reshape(n_dp, CAP, D)),
        to_sources(dots.reshape(n_dp, 1, CAP)),
        out.reshape(n_dp, CAP, D),
        lax.psum(dw, "seq"),
    )


def mid_kernel(
    n_seq, att_ref, h_ref, prev_ref, carry_ref, small_ref, slot_ref, route_ref, w_ref,
    heads_ref, mid_ref, gate_ref, x_ref, gs_ref, send_sem, recv_sem,
):
    me = lax.axis_index("seq")
    tok = h_ref.shape[0]
    greet([{"seq": me ^ place} for place in range(1, n_seq)])
    copies = [
        remote(
            att_ref.at[me ^ place], heads_ref.at[me], (send_sem, recv_sem), place,
            {"seq": me ^ place},
        )
        for place in range(1, n_seq)
    ]
    heads_ref[me] = att_ref[me]
    picks = picks_of(slot_ref)
    pick_any = picks[0] + picks[1]
    carried = lax.dot_general(
        carry_ref[...].astype(f32), prev_ref[:, 0, :], TN, precision=exact_prec,
        preferred_element_type=f32,
    )
    for copy in copies:
        copy.wait_recv()
    attn_out = mm(heads_ref[...].reshape(D, tok), w_ref[...].reshape(D, D), TN)
    resid = h_ref[...].astype(f32) + attn_out
    mid_ref[...] = resid
    rate = lax.rsqrt(jnp.mean(resid * resid, axis=-1, keepdims=True) + 1e-06)
    normed = resid * rate * small_ref[1:2]
    low = normed.astype(bf16)
    x_ref[...] = mm(pick_any, low, NN).astype(bf16).reshape(x_ref.shape)
    heads_rows = small_ref[4 : 8 + H].astype(bf16)
    products = mm(heads_rows, low, NT)
    rest = mm(heads_rows, (normed - low.astype(f32)).astype(bf16), NT)
    logits = products[4:] + carried
    ids = lax.broadcasted_iota(jnp.int32, (H, tok), 0)
    chosen = [
        jnp.sum(jnp.where(route_ref[k : k + 1, :] == ids, logits, 0.0), axis=0, keepdims=True)
        for k in range(2)
    ]
    top = jnp.maximum(chosen[0], chosen[1])
    exps = [jnp.exp(c - top) for c in chosen]
    total = exps[0] + exps[1]
    gates = [e / total for e in exps]
    gate_ref[...] = jnp.concatenate(
        [gates[0], gates[1], products[:4] + rest[:4], jnp.zeros((2, tok), f32)], axis=0
    )
    slot_gates = sum(unsplit(mm(split(gates[k]), picks[k], NT)) for k in range(2))
    for e in range(E):
        gs_ref[e] = slot_gates[:, e * CAP : (e + 1) * CAP]
    for copy in copies:
        copy.wait_send()


def mid_call(n_seq, attended, hidden, prev, carry, small, slot_of, routes, w_out):
    tok, width = hidden.shape[0], attended.shape[1]
    return pl.pallas_call(
        functools.partial(mid_kernel, n_seq),
        out_shape=(
            jax.ShapeDtypeStruct((n_seq, width, tok), bf16),
            jax.ShapeDtypeStruct((tok, D), f32),
            jax.ShapeDtypeStruct((8, tok), f32),
            jax.ShapeDtypeStruct((E, CAP, D), bf16),
            jax.ShapeDtypeStruct((E, 1, CAP), f32),
        ),
        in_specs=[VMEM] * 8,
        out_specs=[VMEM] * 5,
        scratch_shapes=[DMA((n_seq,)), DMA((n_seq,))],
        compiler_params=pltpu.CompilerParams(collective_id=2, has_side_effects=True),
        name="mid",
    )(attended, hidden, prev, carry, small, slot_of, routes, w_out)


def mid_back_kernel(
    n_seq, n_dp, n_tile, piece_ref, dots_ref, cot_ref, mid_ref, gate_ref, slot_ref, route_ref,
    small_ref, heads_ref, w_ref, prev_ref, carry_ref, *refs,
):
    tile_refs, refs = refs[:n_tile], refs[n_tile:]
    resid_ref, go_ref, base_ref, dprev_ref, pack_ref, wo_sum_ref, *refs = refs
    far_refs, refs = refs[:n_tile], refs[n_tile:]
    gh_ref, wo_ref, wo_in, a_send, a_recv, c_send, c_recv, t_send, t_recv = refs
    me = lax.axis_index("seq")
    tok = cot_ref.shape[0]
    width = heads_ref.shape[1]
    owners = n_dp // E
    pairs = n_seq // 2
    greet([{"seq": me ^ place} for place in range(1, n_seq)])
    tile_copies = [
        remote(tile_refs[t], far_refs[t], (t_send, t_recv), t, {"seq": me ^ 2})
        for t in range(n_tile)
    ]
    cot = cot_ref[...]
    grad_top = cot.astype(f32)
    resid_mid = mid_ref[...]
    gain = small_ref[1:2]
    rate = lax.rsqrt(jnp.mean(resid_mid * resid_mid, axis=-1, keepdims=True) + 1e-06)
    normed = resid_mid * rate * gain
    low = normed.astype(bf16)
    picks = picks_of(slot_ref)
    gates = [gate_ref[k : k + 1, :] for k in range(2)]
    routes = [route_ref[k : k + 1, :] for k in range(2)]
    normed_dot = column_to_row(jnp.sum(grad_top * normed, axis=1, keepdims=True))
    vecs = small_ref[2:4].astype(bf16)
    vec_dot = mm(vecs, cot, NT)
    alphas, const_dot = [], []
    for j in range(2):
        pair = [gate_ref[2 + 2 * j + c : 3 + 2 * j + c, :] for c in range(2)]
        top = jnp.maximum(pair[0], pair[1])
        exps = [jnp.exp(p - top) for p in pair]
        total = exps[0] + exps[1]
        alphas.append([e / total for e in exps])
        const_dot.append(alphas[j][0] * normed_dot + alphas[j][1] * vec_dot[j : j + 1])
    slot_dots = split(
        jnp.concatenate(
            [sum(dots_ref[e * owners + o] for o in range(owners)) for e in range(E)], axis=1
        )
    )
    out_dots = []
    for k in range(2):
        value = unsplit(mm(slot_dots, picks[k], NN))
        value = value + jnp.where(routes[k] == E + 1, normed_dot, 0.0)
        for j in range(2):
            value = value + jnp.where(routes[k] == E + 2 + j, const_dot[j], 0.0)
        out_dots.append(value)
    mean_dot = gates[0] * out_dots[0] + gates[1] * out_dots[1]
    ids = lax.broadcasted_iota(jnp.int32, (H, tok), 0)
    grad_logits = sum(
        jnp.where(routes[k] == ids, gates[k] * (out_dots[k] - mean_dot), 0.0) for k in range(2)
    )

    def gate_of(expert):
        return sum(jnp.where(routes[k] == expert, gates[k], 0.0) for k in range(2))

    const_gate = [gate_of(E + 2 + j) for j in range(2)]
    normed_gate = gate_of(E + 1) + sum(const_gate[j] * alphas[j][0] for j in range(2))
    vec_gate = split(jnp.concatenate([const_gate[j] * alphas[j][1] for j in range(2)], axis=0))
    mix_grads = []
    for j in range(2):
        terms = [normed_dot, vec_dot[j : j + 1]]
        for c in range(2):
            mix_grads.append(const_gate[j] * alphas[j][c] * (terms[c] - const_dot[j]))
    token_rows = split(jnp.concatenate(mix_grads + [grad_logits], axis=0))
    normed_column = jnp.broadcast_to(normed_gate, (8, tok)).T[:, 0:1]
    heads_rows = small_ref[4 : 8 + H].astype(bf16)
    pick_any = picks[0] + picks[1]
    grad_normed = grad_top * normed_column
    grad_normed = grad_normed + mm(
        token_rows, jnp.concatenate([heads_rows] * 3, axis=0), TN
    )
    pieces = piece_ref[...].reshape(E, owners, CAP, D)
    for o in range(owners):
        grad_normed = grad_normed + mm(pick_any, pieces[:, o].reshape(E * CAP, D), TN)
    grad_resid = grad_top + norm_back(resid_mid, gain, grad_normed)
    resid_ref[...] = grad_resid
    grad_attn = grad_resid.astype(bf16)
    gh_ref[...] = mm(w_ref[...].reshape(D, D), grad_attn, NT).astype(bf16).reshape(gh_ref.shape)
    copies = [
        remote(gh_ref.at[me ^ place], go_ref.at[me], (a_send, a_recv), place, {"seq": me ^ place})
        for place in range(1, n_seq)
    ]
    go_ref[me] = gh_ref[me]
    grad_w = mm(heads_ref[...].reshape(D, tok), grad_attn, NN)
    for j in range(n_seq):
        wo_ref[j] = grad_w[:, j * width : (j + 1) * width].astype(bf16)
    core_copies = [
        remote(wo_ref.at[me ^ (2 * i + 1)], wo_in.at[i], (c_send, c_recv), i, {"seq": me ^ 1})
        for i in range(pairs)
    ]
    base_ref[...] = (
        resid_mid
        + normed * normed_column
        + mm(vec_gate, jnp.concatenate([vecs] * 3, axis=0), TN)
    )
    dprev_ref[:, 0, :] = lax.dot_general(
        carry_ref[...].astype(f32), grad_logits, NN, precision=exact_prec,
        preferred_element_type=f32,
    )
    rest = (normed - low.astype(f32)).astype(bf16)
    row_sums = unsplit(mm(token_rows, low, NN))
    mix_sums = row_sums[:4] + unsplit(mm(token_rows, rest, NN))[:4]
    vec_sums = unsplit(mm(vec_gate, cot, NN))
    gain_sum = jnp.sum(grad_normed * resid_mid * rate, axis=0, keepdims=True)
    carry_grad = lax.dot_general(
        prev_ref[:, 0, :], grad_logits, NT, precision=exact_prec, preferred_element_type=f32
    )
    packed = jnp.concatenate([mix_sums, row_sums[4:], vec_sums, gain_sum], axis=0)
    lines, shard = packed.shape[0], D // n_dp
    for i in range(n_dp):
        pack_ref[i] = jnp.zeros(pack_ref.shape[1:], f32)
        pack_ref[i, 0:lines, :] = packed[:, i * shard : (i + 1) * shard]
        pack_ref[i, 24 : 24 + H, 0:H] = carry_grad
    for i in range(pairs):
        core_copies[i].wait_recv()
        wo_sum_ref[i] = (
            wo_ref[me ^ (2 * i)].astype(f32) + wo_in[i].astype(f32)
        ).astype(bf16)
    for copy in copies + tile_copies:
        copy.wait()
    for copy in core_copies:
        copy.wait_send()


def mid_back_call(
    n_seq, n_dp, piece, dots, cot, mid, gates, slot_of, routes, small, heads, w, prev, carry,
    parts,
):
    tok, width = cot.shape[0], heads.shape[1]
    pairs = n_seq // 2
    n_tile = len(parts)
    outs = pl.pallas_call(
        functools.partial(mid_back_kernel, n_seq, n_dp, n_tile),
        out_shape=(
            jax.ShapeDtypeStruct((tok, D), f32),
            jax.ShapeDtypeStruct((n_seq, width, tok), bf16),
            jax.ShapeDtypeStruct((tok, D), f32),
            jax.ShapeDtypeStruct((H, 1, tok), f32),
            jax.ShapeDtypeStruct((n_dp, LINES, D // n_dp), f32),
            jax.ShapeDtypeStruct((pairs, D, width), bf16),
        )
        + tuple(jax.ShapeDtypeStruct(part.shape, bf16) for part in parts),
        in_specs=[VMEM] * 12 + [HBM] * n_tile,
        out_specs=[VMEM] * 6 + [HBM] * n_tile,
        scratch_shapes=[
            pltpu.VMEM((n_seq, width, tok), bf16),
            pltpu.VMEM((n_seq, D, width), bf16),
            pltpu.VMEM((pairs, D, width), bf16),
            DMA((n_seq,)),
            DMA((n_seq,)),
            DMA((pairs,)),
            DMA((pairs,)),
            DMA((max(n_tile, 1),)),
            DMA((max(n_tile, 1),)),
        ],
        compiler_params=pltpu.CompilerParams(collective_id=3, has_side_effects=True),
        name="mid_back",
    )(piece, dots, cot, mid, gates, slot_of, routes, small, heads, w, prev, carry, *parts)
    return outs[:6], list(outs[6:])


def tail_kernel(
    n_seq, n_dp, parts, g_ref, wt_ref, wo_ref, pack_ref, gate_ref, slot_ref, gain_ref,
    a_hbm, h_hbm, resid_hbm, base_hbm, out_hbm, *refs,
):
    n_far = max(parts - LATE, 0)
    fin_hbm, refs = refs[:parts], refs[parts:]
    far_hbm, refs = refs[:n_far], refs[n_far:]
    din_ref, row_in, line_ref, block_ref, both_ref, refs = *refs[:5], refs[5:]
    (
        a_ref, h_ref, resid_ref, base_ref, rows_ref, far_ref, fin_ref,
        core_out, core_in, x_out, x_in, part_ref, w_out_buf, w_in, wo_buf, wo_in, wo_x, wo_far,
        w_mid, wo_mid,
        row_buf, pack_in, line_buf, line_in, load_sem, c_sems, x_sems, w_sems, v_sems, r_sems, o_sems,
        p_sems, q_sems, u_sems, l_sems, t_sems, f_sems, keep_sem,
    ) = refs
    me, dp = lax.axis_index("seq"), lax.axis_index("dp")
    tok = h_ref.shape[0]
    shard, width3 = w_in.shape[1], w_in.shape[2]
    width = width3 // 3
    owners = n_dp // E
    pairs = n_seq // 2
    others = range(1, n_dp)

    def both(sems):
        return sems.at[0], sems.at[1]

    c_sems, x_sems, w_sems, v_sems, r_sems, o_sems, p_sems, q_sems, u_sems, l_sems, t_sems, f_sems = (
        both(sems)
        for sems in (
            c_sems, x_sems, w_sems, v_sems, r_sems, o_sems, p_sems, q_sems, u_sems, l_sems, t_sems,
            f_sems,
        )
    )

    loads = []
    for src, dst in [
        (a_hbm, a_ref), (out_hbm, rows_ref), (base_hbm, base_ref), (h_hbm, h_ref),
        (resid_hbm, resid_ref),
    ] + [(fin_hbm[t], fin_ref.at[t]) for t in range(parts)] + [
        (far_hbm[t], far_ref.at[t]) for t in range(n_far)
    ]:
        load = pltpu.make_async_copy(src, dst, load_sem.at[len(loads)])
        load.start()
        loads.append(load)
    greet(
        [{"seq": me ^ place} for place in range(1, n_seq)]
        + [{"dp": lax.rem(dp + k, n_dp)} for k in others]
    )

    def there(k):
        return lax.rem(dp + k, n_dp)

    spots = [*range(n_dp // 2 - 1, -1, -1)]

    def to_neighbour(buf, near, sems):
        return {
            j: remote(buf.at[dp ^ (2 * j) ^ 1], near.at[j], sems, j, {"dp": dp ^ 1}) for j in spots
        }

    def pass_sums(copies, buf, near, mid, sems):
        passed = []
        for j in spots:
            copies[j].wait_recv()
            total = buf[dp ^ (2 * j)].astype(f32) + near[j].astype(f32)
            mid[j] = total.astype(bf16)
            if j:
                passed.append(
                    remote(mid.at[j], near.at[n_dp // 2 + j], sems, j, {"dp": dp ^ (2 * j)})
                )
        return passed

    def collect(passed, near, mid):
        for copy in passed:
            copy.wait_recv()
        return sum((near[n_dp // 2 + j].astype(f32) for j in spots[:-1]), mid[0].astype(f32))

    def term(place):
        columns = pl.ds(pl.multiple_of((me ^ place) * tok, tok), tok)
        return mm(g_ref[:, columns], wt_ref[...], TN)

    part_copies = [
        remote(fin_hbm[t], far_ref.at[t], t_sems, t - n_far, {"seq": me ^ 2})
        for t in range(n_far, parts)
    ]
    pack_copies = [
        remote(pack_ref.at[there(k)], pack_in.at[dp], p_sems, k, {"dp": there(k)}) for k in others
    ]
    pack_in[dp] = pack_ref[dp]
    for i in range(pairs):
        wo_buf[:, :, i * width : (i + 1) * width] = wo_ref[i].reshape(n_dp, shard, width)
    wo_near = to_neighbour(wo_buf, wo_in, q_sems)
    core_copies = []
    for i in range(pairs - 1, -1, -1):
        core_out[i] = term(2 * i + 1).astype(bf16)
        core_copies.insert(0, remote(core_out.at[i], core_in.at[i], c_sems, i, {"seq": me ^ 1}))
    x_copies = []
    for i in range(pairs - 1, 0, -1):
        part = term(2 * i)
        core_copies[i].wait_recv()
        x_out[i - 1] = (part + core_in[i].astype(f32)).astype(bf16)
        x_copies.append(
            remote(x_out.at[i - 1], x_in.at[i - 1], x_sems, i - 1, {"seq": me ^ (2 * i)})
        )
    loads[0].wait()
    turned = mm(g_ref[...], a_ref[...], NN)
    w_out_buf[...] = turned.T.astype(bf16).reshape(n_dp, shard, width3)
    w_near = to_neighbour(w_out_buf, w_in, w_sems)
    wo_copies = pass_sums(wo_near, wo_buf, wo_in, wo_mid, u_sems)
    w_copies = pass_sums(w_near, w_out_buf, w_in, w_mid, v_sems)
    part = term(0)
    core_copies[0].wait_recv()
    part_ref[...] = part + core_in[0].astype(f32)

    for copy in pack_copies:
        copy.wait_recv()
    line_buf[...] = jnp.sum(pack_in[...], axis=0)
    line_in[me] = line_buf[...]
    line_copies = [
        remote(line_buf, line_in.at[me], l_sems, place, {"seq": me ^ place})
        for place in range(1, n_seq)
    ]

    fin_copies, keeps = [], []

    def hand_over(ref, row, t):
        index = row * parts + t
        fin_copies.append(
            remote(ref.at[t], both_ref.at[2 * row + 1, t], f_sems, index, {"seq": me ^ 1})
        )
        keep = pltpu.make_async_copy(ref.at[t], both_ref.at[2 * row, t], keep_sem.at[index])
        keep.start()
        keeps.append(keep)

    for t in range(parts):
        loads[5 + t].wait()
        hand_over(fin_ref, 0, t)
    for t in range(n_far):
        loads[5 + parts + t].wait()
        hand_over(far_ref, 1, t)

    wo_total = collect(wo_copies, wo_in, wo_mid)
    wo_cross = []
    for i in range(1, pairs):
        wo_x[i - 1] = wo_total[:, i * width : (i + 1) * width].astype(bf16)
        wo_cross.append(
            remote(wo_x.at[i - 1], wo_far.at[i - 1], o_sems, i - 1, {"seq": me ^ (2 * i)})
        )

    loads[1].wait()
    loads[2].wait()
    picks = picks_of(slot_ref)
    rows = rows_ref[...].reshape(E, owners, CAP, D)
    columns = gate_ref[...].T
    block = base_ref[...]
    for k in range(2):
        picked = sum(
            mm(picks[k], rows[:, o].reshape(E * CAP, D), TN) for o in range(owners)
        )
        block = block + columns[:, k : k + 1] * picked
    block_ref[...] = block.astype(bf16)

    for copy in x_copies:
        copy.wait_recv()
    grad = part_ref[...]
    for i in range(pairs - 1):
        grad = grad + x_in[i].astype(f32)
    loads[3].wait()
    loads[4].wait()
    din_ref[...] = resid_ref[...] + norm_back(h_ref[...].astype(f32), gain_ref[0:1], grad)

    row_buf[:, :width3] = collect(w_copies, w_in, w_mid).astype(bf16)
    for copy in wo_cross:
        copy.wait_recv()
    wo_mine = wo_total[:, :width]
    for i in range(pairs - 1):
        wo_mine = wo_mine + wo_far[i].astype(f32)
    row_buf[:, width3:] = wo_mine.astype(bf16)
    row_in[me] = row_buf[...]
    row_copies = [
        remote(row_buf, row_in.at[me], r_sems, place, {"seq": me ^ place})
        for place in range(1, n_seq)
    ]
    for copy in line_copies:
        copy.wait_recv()
    line_ref[...] = jnp.sum(line_in[...], axis=0)
    for t, copy in enumerate(part_copies):
        copy.wait_recv()
        hand_over(far_ref, 1, n_far + t)
    for copy in row_copies + fin_copies:
        copy.wait_recv()
    for copy in (
        core_copies + [*w_near.values()] + [*wo_near.values()] + w_copies + x_copies + row_copies + wo_copies + pack_copies
        + line_copies + wo_cross + part_copies + fin_copies
    ):
        copy.wait_send()
    for keep in keeps:
        keep.wait()


def tail_call(
    n_seq, n_dp, grad_qkv, w_turned, wo_sum, pack, gates, slot_of, small,
    attn_in, hidden, grad_resid, base, back_out, fin, far,
):
    tok = hidden.shape[0]
    shard, width3 = D // n_dp, grad_qkv.shape[0]
    width = width3 // 3
    pairs = n_seq // 2
    parts, room = len(fin), max(len(fin), 1)
    part = (3, PART, D)
    return pl.pallas_call(
        functools.partial(tail_kernel, n_seq, n_dp, parts),
        out_shape=(
            jax.ShapeDtypeStruct((tok, D), f32),
            jax.ShapeDtypeStruct((n_seq, shard, width3 + width), bf16),
            jax.ShapeDtypeStruct((LINES, shard), f32),
            jax.ShapeDtypeStruct((tok, D), bf16),
            jax.ShapeDtypeStruct((n_seq, room, *part), bf16),
        ),
        in_specs=[VMEM] * 7 + [HBM] * (5 + parts + len(far)),
        out_specs=[VMEM] * 4 + [HBM],
        scratch_shapes=[
            pltpu.VMEM((n_seq * tok, D), bf16),
            pltpu.VMEM((tok, D), bf16),
            pltpu.VMEM((tok, D), f32),
            pltpu.VMEM((tok, D), f32),
            pltpu.VMEM((n_dp, CAP, D), bf16),
            pltpu.VMEM((room, *part), bf16),
            pltpu.VMEM((room, *part), bf16),
            pltpu.VMEM((pairs, tok, D), bf16),
            pltpu.VMEM((pairs, tok, D), bf16),
            pltpu.VMEM((pairs - 1, tok, D), bf16),
            pltpu.VMEM((pairs - 1, tok, D), bf16),
            pltpu.VMEM((tok, D), f32),
            pltpu.VMEM((n_dp, shard, width3), bf16),
            pltpu.VMEM((n_dp, shard, width3), bf16),
            pltpu.VMEM((n_dp, shard, pairs * width), bf16),
            pltpu.VMEM((n_dp, shard, pairs * width), bf16),
            pltpu.VMEM((pairs - 1, shard, width), bf16),
            pltpu.VMEM((pairs - 1, shard, width), bf16),
            pltpu.VMEM((n_dp // 2, shard, width3), bf16),
            pltpu.VMEM((n_dp // 2, shard, pairs * width), bf16),
            pltpu.VMEM((shard, width3 + width), bf16),
            pltpu.VMEM((n_dp, LINES, shard), f32),
            pltpu.VMEM((LINES, shard), f32),
            pltpu.VMEM((n_seq, LINES, shard), f32),
            DMA((5 + 2 * room,)),
            DMA((2, pairs)),
            DMA((2, pairs)),
            DMA((2, n_dp // 2)),
            DMA((2, n_dp // 2)),
            DMA((2, n_seq)),
            DMA((2, pairs)),
            DMA((2, n_dp)),
            DMA((2, n_dp // 2)),
            DMA((2, n_dp // 2)),
            DMA((2, n_seq)),
            DMA((2, LATE)),
            DMA((2, 2 * room)),
            DMA((2 * room,)),
        ],
        compiler_params=pltpu.CompilerParams(
            collective_id=1, has_side_effects=True, vmem_limit_bytes=67043328
        ),
        name="tail",
    )(
        grad_qkv, w_turned, wo_sum, pack, gates, slot_of, small,
        attn_in, hidden, grad_resid, base, back_out, *fin, *far,
    )


def finish_kernel(
    n_seq, me_ref, both_ref, row_ref, line_ref, wq_ref, gain_ref,
    de_ref, dw_ref, dwo_ref, again_ref, mgain_ref, router_ref, carry_ref, vec_ref, mix_ref,
):
    step = both_ref.shape[3]
    for t in range(both_ref.shape[1]):
        de_ref[:, t * step : (t + 1) * step] = both_ref[0, t].astype(f32)

    @pl.when(pl.program_id(0) == 0)
    def _():
        width = row_ref.shape[2] // 4
        for j in range(n_seq):
            block = row_ref[j].astype(f32)
            for c in range(3):
                left = c * width * n_seq + j * width
                dw_ref[:, left : left + width] = block[:, c * width : (c + 1) * width]
            dwo_ref[:, j * width : (j + 1) * width] = block[:, 3 * width :]
        sums = jnp.sum(dw_ref[...] * wq_ref[...].astype(f32), axis=1, keepdims=True)
        again_ref[...] = column_to_row(sums) / gain_ref[...].astype(f32)
        mix_ref[0] = line_ref[0:2]
        mix_ref[1] = line_ref[2:4]
        router_ref[...] = line_ref[4 : 4 + H]
        vec_ref[...] = line_ref[4 + H : 6 + H]
        mgain_ref[...] = line_ref[6 + H : 7 + H]
        carry_ref[...] = line_ref[24 : 24 + H, 0:H]


def finish_call(n_seq, me, both, row_in, lines, w_qkv, attn_gain):
    shard = w_qkv.shape[0]
    _, parts, three, step, _ = both.shape
    units = n_seq * parts * step
    group = 4 if parts % 4 == 0 else 1
    steps = parts // group

    def whole(shape):
        return pl.BlockSpec(shape, lambda i, me_ref: (0,) * len(shape))

    shapes = [(shard, 3 * D), (shard, D), (1, shard), (1, shard), (H, shard), (H, H), (2, shard),
              (2, 2, shard)]
    return pl.pallas_call(
        functools.partial(finish_kernel, n_seq),
        out_shape=[jax.ShapeDtypeStruct((three, units, D), f32)]
        + [jax.ShapeDtypeStruct(shape, f32) for shape in shapes],
        grid_spec=pltpu.PrefetchScalarGridSpec(
            num_scalar_prefetch=1,
            grid=(n_seq * steps,),
            in_specs=[
                pl.BlockSpec(
                    (1, group, three, step, D),
                    lambda i, me_ref: ((i // steps) ^ me_ref[0], i % steps, 0, 0, 0),
                ),
                whole(row_in.shape),
                whole(lines.shape),
                whole(w_qkv.shape),
                whole((1, shard)),
            ],
            out_specs=[pl.BlockSpec((three, group * step, D), lambda i, me_ref: (0, i, 0))]
            + [whole(shape) for shape in shapes],
        ),
        name="finish",
    )(me, both, row_in, lines, w_qkv, attn_gain[None])


def rope_tables(seq_len):
    freq_index = jnp.arange(HD // 2, dtype=f32)
    inv_freq = jnp.exp(freq_index * (-2.0 * math.log(10000.0) / HD))
    angles = jnp.arange(seq_len, dtype=jnp.int32).astype(f32)[None, :] * inv_freq[:, None]
    return jnp.cos(angles), jnp.sin(angles)


def per_device(
    hidden_in,
    prev_logits,
    segments,
    routes,
    attn_gain,
    w_qkv,
    w_out,
    moe_gain,
    w_router,
    w_carry,
    const_vec,
    const_mix,
    experts,
    cotangent,
):
    n_seq, n_dp = lax.axis_size("seq"), lax.axis_size("dp")
    owners = n_dp // E
    me = lax.axis_index("seq")
    tok = hidden_in.shape[1]
    hidden, cot = hidden_in[0], cotangent[0]
    prev_t = jnp.transpose(prev_logits, (2, 0, 1))
    routes_t = routes[0].T

    def to_owners(values):
        return lax.all_to_all(
            jnp.repeat(values, owners, axis=0), "dp", split_axis=0, concat_axis=0, tiled=True
        )

    def to_sources(values):
        return lax.all_to_all(values, "dp", split_axis=0, concat_axis=0, tiled=True)

    cos_t, sin_t = rope_tables(tok * n_seq)
    attn_in, qkv, w_turned, small, slot_of, grad_slots, out_weight = start_call(
        n_seq, n_dp, hidden, w_qkv, attn_gain, moe_gain, const_vec, const_mix, w_router.T,
        routes_t, cot, cos_t, sin_t, w_out,
    )
    arrived_grad = to_owners(grad_slots)

    seg_row = segments[0]
    doc_ids = jnp.arange(16, dtype=jnp.int32)
    doc_start = jnp.sum((seg_row[None, :] < doc_ids[:, None]).astype(jnp.int32), axis=1)
    start = jnp.sum(jnp.where(seg_row[None, :] == doc_ids[:, None], doc_start[:, None], 0), axis=0)
    start_row = start.astype(jnp.int32)[None, :]
    lows = start[::BLK].astype(jnp.int32) // BLK
    attended, attended_exact, logs = attn_call(lows, qkv, start_row, tok)

    heads_t, resid_mid, gates, x_slots, gate_slots = mid_call(
        n_seq, attended, hidden, prev_t, w_carry, small, slot_of, routes_t, out_weight
    )
    if n_dp * CAP > 1024:
        piece, dots, partial, d_plain = experts_plain(
            to_owners, to_sources, n_dp, x_slots, gate_slots, experts, arrived_grad
        )
        fin, far = [], []
    else:
        piece, dots, partial, fin, far = moe_call(
            n_dp, x_slots, gate_slots, experts, arrived_grad
        )
    back_out = to_sources(partial)

    (grad_resid, grad_out, base, d_prev, pack, wo_sum), far_back = mid_back_call(
        n_seq, n_dp, piece, dots, cot, resid_mid, gates, slot_of, routes_t, small, heads_t,
        out_weight, prev_t, w_carry, fin[EARLY : EARLY + 1],
    )
    later, grad_out = lax.optimization_barrier((fin[EARLY + 1 : -LATE], grad_out))
    far = far + far_back + [swap(part, "seq", 2) for part in later]
    grad_qkv = attn_back_call(
        lows, qkv, grad_out, attended_exact, logs, start_row, cos_t, sin_t
    )
    d_input, row_in, lines, block_out, both = tail_call(
        n_seq, n_dp, grad_qkv, w_turned, wo_sum, pack, gates, slot_of, small,
        attn_in, hidden, grad_resid, base, back_out, fin, far,
    )
    d_experts, d_qkv, d_out, again, mgain, router, carry, vec, mix = finish_call(
        n_seq, me.astype(jnp.int32).reshape(1), both, row_in, lines, w_qkv, attn_gain
    )
    if not fin:
        d_experts = d_plain
    return (
        block_out[None],
        d_input[None],
        jnp.transpose(d_prev, (1, 2, 0)),
        again[0],
        d_qkv,
        d_out,
        mgain[0],
        router.T,
        carry,
        vec,
        mix,
        d_experts,
    )


def solution(mesh):
    return jax.shard_map(
        per_device,
        mesh=mesh,
        in_specs=(
            P("dp", "seq", None),
            P("dp", "seq", None),
            P("dp", None),
            P("dp", "seq", None),
            P("dp"),
            P("dp", None),
            P("dp", None),
            P("dp"),
            P("dp", None),
            P(),
            P(None, "dp"),
            P(None, None, "dp"),
            P(None, "dp", None),
            P("dp", "seq", None),
        ),
        out_specs=(
            P("dp", "seq", None),
            P("dp", "seq", None),
            P("dp", "seq", None),
            P("dp"),
            P("dp", None),
            P("dp", None),
            P("dp"),
            P("dp", None),
            P(),
            P(None, "dp"),
            P(None, None, "dp"),
            P(None, "dp", None),
        ),
        check_vma=False,
    )
```

```python
import functools
import math

import jax
import jax.numpy as jnp
from jax import lax
from jax.experimental import pallas as pl
from jax.experimental.pallas import tpu as pltpu
from jax.sharding import PartitionSpec as P

D = 768
H = 12
HD = 64
E = 8
CAP = 128
BLK = 256
PAIR = 2 * CAP
UNITS = 256
PART = 64
EARLY = 1
LATE = 2
SMALL = 32
LINES = 40

exact_prec = lax.Precision.HIGHEST
neg_large = -1e30
score_scale = 0.125 * math.log2(math.e)
f32 = jnp.float32
bf16 = jnp.bfloat16

NN = (((1,), (0,)), ((), ()))
NT = (((1,), (1,)), ((), ()))
TN = (((0,), (0,)), ((), ()))


MESH = pl.DeviceIdType.MESH
VMEM = pl.BlockSpec(memory_space=pltpu.VMEM)
HBM = pl.BlockSpec(memory_space=pl.ANY)
DMA = pltpu.SemaphoreType.DMA


def mm(a, b, dims):
    return lax.dot_general(a, b, dims, preferred_element_type=f32)


def swap(value, axis, bit):
    size = lax.axis_size(axis)
    return lax.ppermute(value, axis, [(i, i ^ bit) for i in range(size)])


def bits_high_first(size):
    bit = size // 2
    while bit >= 1:
        yield bit
        bit //= 2


def greet(peers):
    barrier = pltpu.get_barrier_semaphore()
    for peer in peers:
        pl.semaphore_signal(barrier, inc=1, device_id=peer, device_id_type=MESH)
    pl.semaphore_wait(barrier, len(peers))


def remote_later(src, dst, sems, index, target):
    return pltpu.make_async_remote_copy(
        src_ref=src,
        dst_ref=dst,
        send_sem=sems[0].at[index],
        recv_sem=sems[1].at[index],
        device_id=target,
        device_id_type=MESH,
    )


def remote(src, dst, sems, index, target):
    copy = remote_later(src, dst, sems, index, target)
    copy.start()
    return copy


def one_hot(condition):
    return jnp.where(condition, 1.0, 0.0).astype(bf16)


def picks_of(slot_ref):
    slots = lax.broadcasted_iota(jnp.int32, (E * CAP, slot_ref.shape[1]), 0)
    return [one_hot(slots == slot_ref[k : k + 1, :]) for k in range(2)]


def split(rows):
    high = rows.astype(bf16)
    rest = rows - high.astype(f32)
    middle = rest.astype(bf16)
    low = (rest - middle.astype(f32)).astype(bf16)
    return jnp.concatenate([high, middle, low], axis=0)


def unsplit(rows):
    third = rows.shape[0] // 3
    return rows[:third] + rows[third : 2 * third] + rows[2 * third :]


def column_to_row(column):
    return jnp.broadcast_to(column, (column.shape[0], 128)).T[0:1]


def norm_back(values, gain, grad):
    rate = lax.rsqrt(jnp.mean(values * values, axis=-1, keepdims=True) + 1e-06)
    scaled = gain * grad
    inner = jnp.mean(values * scaled, axis=-1, keepdims=True)
    return rate * scaled - values * (rate * rate * rate) * inner


def make_slots(route_ref, cot_ref, slot_ref, g_ref):
    tok = route_ref.shape[1]
    ids = lax.broadcasted_iota(jnp.int32, (E, tok), 0)
    named = [route_ref[k : k + 1, :] == ids for k in range(2)]
    earlier = lax.broadcasted_iota(jnp.int32, (tok, tok), 0) < lax.broadcasted_iota(
        jnp.int32, (tok, tok), 1
    )
    ranks = mm(one_hot(named[0] | named[1]), one_hot(earlier), NN)
    for k in range(2):
        route = route_ref[k : k + 1, :]
        rank = jnp.sum(jnp.where(named[k], ranks, 0.0), axis=0, keepdims=True)
        slot_ref[k : k + 1, :] = jnp.where(
            route < E, route * CAP + rank.astype(jnp.int32), E * CAP
        )
    picks = picks_of(slot_ref)
    g_ref[...] = mm(picks[0] + picks[1], cot_ref[...], NN).astype(bf16).reshape(g_ref.shape)


def start_kernel(
    n_seq, n_dp, h_ref, w_ref, again_ref, mgain_ref, vec_ref, mix_ref, router_ref,
    route_ref, cot_ref, cos_ref, sin_ref, wo_ref,
    attn_ref, qkv_ref, wt_ref, small_ref, slot_ref, g_ref, wo_all,
    all_ref, slice_ref, small_buf, h_send, h_recv, near_send, near_recv, next_send, next_recv,
    c_send, c_recv,
):
    me, dp = lax.axis_index("seq"), lax.axis_index("dp")
    tok = h_ref.shape[0]
    width = slice_ref.shape[2] // 3
    seq_bits = list(bits_high_first(n_seq))
    greet(
        [{"seq": me ^ bit} for bit in seq_bits]
        + [{"dp": dp ^ 1}]
        + [{"dp": dp ^ (2 * j)} for j in range(1, n_dp // 2)]
    )

    plan, arrival = [], {}
    order = [(0, bit) for bit in seq_bits]
    while order:
        place, bit = order.pop(0)
        copy = remote_later(
            h_ref if place == 0 else all_ref.at[me ^ place],
            all_ref.at[me ^ place],
            (h_send, h_recv),
            len(plan),
            {"seq": me ^ bit},
        )
        arrival[place ^ bit] = copy
        plan.append((place, copy))
        order += [(place ^ bit, low) for low in seq_bits if low < bit]
    for place, copy in plan:
        if place == 0:
            copy.start()

    for j in range(n_seq):

        @pl.when(me == j)
        def _():
            for c in range(3):
                left = c * width * n_seq + j * width
                slice_ref[dp, :, c * width : (c + 1) * width] = w_ref[:, left : left + width]

    small_buf[dp] = jnp.zeros(small_buf.shape[1:], bf16)
    small_buf[dp, 0:1, :] = again_ref[...]
    small_buf[dp, 1:2, :] = mgain_ref[...]
    small_buf[dp, 2:4, :] = vec_ref[...]
    small_buf[dp, 4:6, :] = mix_ref[0]
    small_buf[dp, 6:8, :] = mix_ref[1]
    small_buf[dp, 8 : 8 + H, :] = router_ref[...]
    cols = pl.ds(pl.multiple_of((me & 1) * (D // 2), D // 2), D // 2)
    wo_all[dp, :, cols] = wo_ref[:, cols]

    def rows_of(kind, source):
        return (small_buf.at[source], slice_ref.at[source], wo_all.at[source, :, cols])[kind]

    def first_copy(kind, j):
        return remote_later(
            rows_of(kind, dp), rows_of(kind, dp), (near_send.at[kind], near_recv.at[kind]), j,
            {"dp": dp ^ (2 * j)},
        )

    def next_copy(kind, j):
        return remote_later(
            rows_of(kind, dp ^ (2 * j)), rows_of(kind, dp ^ (2 * j)),
            (next_send.at[kind], next_recv.at[kind]), j, {"dp": dp ^ 1},
        )

    places = range(1, n_dp // 2)
    for kind in range(3):
        for j in places:
            first_copy(kind, j).start()
        next_copy(kind, 0).start()
    make_slots(route_ref, cot_ref, slot_ref, g_ref)

    def pass_on(kind):
        for j in places:
            first_copy(kind, j).wait_recv()
            next_copy(kind, j).start()

    def complete(kind):
        for j in range(n_dp // 2):
            next_copy(kind, j).wait_recv()

    pass_on(0)
    complete(0)
    small_ref[...] = jnp.concatenate([small_buf[i].astype(f32) for i in range(n_dp)], axis=1)

    def normalize(block, ref):
        x = ref.astype(f32)
        mean_square = jnp.mean(x * x, axis=-1, keepdims=True)
        rows = pl.ds(pl.multiple_of(block * tok, tok), tok)
        attn_ref[rows, :] = (x * lax.rsqrt(mean_square + 1e-06) * small_ref[0:1]).astype(bf16)

    normalize(me, h_ref[...])
    pass_on(1)
    for place in arrival:
        arrival[place].wait_recv()
        for source, copy in plan:
            if source == place:
                copy.start()
        normalize(me ^ place, all_ref[me ^ place])
    complete(1)
    pass_on(2)
    wt_ref[...] = slice_ref[...].reshape(D, 3 * width).T
    half = HD // 2

    @pl.loop(0, attn_ref.shape[0] // BLK)
    def _(i):
        rows = pl.ds(pl.multiple_of(i * BLK, BLK), BLK)
        y = mm(wt_ref[...], attn_ref[rows, :], NT)
        cos, sin = cos_ref[:, rows], sin_ref[:, rows]
        for head in range(2 * width // HD):
            low, middle, high = head * HD, head * HD + half, (head + 1) * HD
            a, b = y[low:middle], y[middle:high]
            qkv_ref[low:middle, rows] = (a * cos - b * sin).astype(bf16)
            qkv_ref[middle:high, rows] = (a * sin + b * cos).astype(bf16)
        qkv_ref[2 * width :, rows] = y[2 * width :].astype(bf16)

    complete(2)
    trade = remote(
        wo_all.at[:, :, cols], wo_all.at[:, :, cols], (c_send, c_recv), 0, {"seq": me ^ 1}
    )
    for _, copy in plan:
        copy.wait_send()
    for kind in range(3):
        for j in places:
            first_copy(kind, j).wait_send()
        for j in range(n_dp // 2):
            next_copy(kind, j).wait_send()
    trade.wait()


def start_call(
    n_seq, n_dp, hidden, w_qkv, attn_gain, moe_gain, vec, mix, router, routes, cotangent, cos, sin,
    w_out,
):
    tok, shard = hidden.shape[0], w_qkv.shape[0]
    width3 = w_qkv.shape[1] // n_seq
    hops = n_seq - 1
    return pl.pallas_call(
        functools.partial(start_kernel, n_seq, n_dp),
        out_shape=(
            jax.ShapeDtypeStruct((n_seq * tok, D), bf16),
            jax.ShapeDtypeStruct((width3, n_seq * tok), bf16),
            jax.ShapeDtypeStruct((width3, D), bf16),
            jax.ShapeDtypeStruct((SMALL, D), f32),
            jax.ShapeDtypeStruct(routes.shape, jnp.int32),
            jax.ShapeDtypeStruct((E, CAP, D), bf16),
            jax.ShapeDtypeStruct((n_dp, shard, D), bf16),
        ),
        in_specs=[VMEM] * 12,
        out_specs=[VMEM] * 7,
        scratch_shapes=[
            pltpu.VMEM((n_seq, tok, D), bf16),
            pltpu.VMEM((n_dp, shard, width3), bf16),
            pltpu.VMEM((n_dp, SMALL, shard), bf16),
            DMA((hops,)),
            DMA((hops,)),
            DMA((3, n_dp // 2)),
            DMA((3, n_dp // 2)),
            DMA((3, n_dp // 2)),
            DMA((3, n_dp // 2)),
            DMA((1,)),
            DMA((1,)),
        ],
        compiler_params=pltpu.CompilerParams(collective_id=0, has_side_effects=True),
        name="start",
    )(
        hidden, w_qkv, attn_gain[None], moe_gain[None], vec, mix, router, routes, cotangent,
        cos, sin, w_out,
    )


def allowed_block(key_block, query_block, start_row):
    key_pos = key_block * BLK + lax.broadcasted_iota(jnp.int32, (BLK, BLK), 0)
    query_pos = query_block * BLK + lax.broadcasted_iota(jnp.int32, (BLK, BLK), 1)
    return (key_pos >= start_row) & (key_pos <= query_pos)


def attn_kernel(lo_ref, qkv_ref, start_ref, out_ref, exact_ref, log_ref, keys_ref):
    heads, seq_len, _ = keys_ref.shape
    width = heads * HD
    qb = pl.program_id(0)

    @pl.when(qb == 0)
    def _():
        for h in range(heads):
            keys_ref[h] = qkv_ref[width + h * HD : width + (h + 1) * HD, :].T

    here = pl.ds(pl.multiple_of(qb * BLK, BLK), BLK)
    start_row = start_ref[...]

    def step(kb, carry):
        there = pl.ds(pl.multiple_of(kb * BLK, BLK), BLK)
        allowed = allowed_block(kb, qb, start_row)
        scores = [
            mm(keys_ref[h, there, :], qkv_ref[h * HD : (h + 1) * HD, here], NN)
            for h in range(heads)
        ]
        stats, weights = [], []
        for h in range(heads):
            top, total, acc = carry[h]
            masked = jnp.where(allowed, scores[h] * score_scale, neg_large)
            new_top = jnp.maximum(top, jnp.max(masked, axis=0, keepdims=True))
            fade = jnp.exp2(top - new_top)
            weight = jnp.exp2(masked - new_top)
            total = total * fade + jnp.sum(weight, axis=0, keepdims=True)
            stats.append((new_top, total, acc * fade))
            weights.append(weight.astype(bf16))
        new = []
        for h in range(heads):
            values = qkv_ref[2 * width + h * HD : 2 * width + (h + 1) * HD, there]
            top, total, acc = stats[h]
            new.append((top, total, acc + mm(values, weights[h], NN)))
        return tuple(new)

    first = tuple(
        (
            jnp.full((1, BLK), neg_large, f32),
            jnp.zeros((1, BLK), f32),
            jnp.zeros((HD, BLK), f32),
        )
        for _ in range(heads)
    )
    done = lax.fori_loop(lo_ref[qb], qb + 1, step, first)
    for h in range(heads):
        top, total, acc = done[h]
        attended = acc / total
        exact_ref[h * HD : (h + 1) * HD, :] = attended
        out_ref[0, h * HD : (h + 1) * HD, :] = attended.astype(bf16)
        log_ref[h : h + 1, :] = top + jnp.log2(total)


def attn_call(lows, qkv, start_row, tok):
    width3, seq_len = qkv.shape
    width = width3 // 3
    heads = width // HD
    per = tok // BLK
    return pl.pallas_call(
        attn_kernel,
        out_shape=(
            jax.ShapeDtypeStruct((seq_len // tok, width, tok), bf16),
            jax.ShapeDtypeStruct((width, seq_len), f32),
            jax.ShapeDtypeStruct((heads, seq_len), f32),
        ),
        grid_spec=pltpu.PrefetchScalarGridSpec(
            num_scalar_prefetch=1,
            grid=(seq_len // BLK,),
            in_specs=[
                pl.BlockSpec((width3, seq_len), lambda i, lo: (0, 0)),
                pl.BlockSpec((1, BLK), lambda i, lo: (0, i)),
            ],
            out_specs=[
                pl.BlockSpec((1, width, BLK), lambda i, lo: (i // per, 0, i % per)),
                pl.BlockSpec((width, BLK), lambda i, lo: (0, i)),
                pl.BlockSpec((heads, BLK), lambda i, lo: (0, i)),
            ],
            scratch_shapes=[pltpu.VMEM((heads, seq_len, HD), bf16)],
        ),
        cost_estimate=pl.CostEstimate(
            flops=16_000_000_000, transcendentals=0, bytes_accessed=16_000_000
        ),
        name="attend",
    )(lows, qkv, start_row)


def attn_back_kernel(
    lo_ref, qkv_ref, go_ref, exact_ref, log_ref, start_ref, cos_ref, sin_ref, out_ref,
    keys_ref, values_ref, dk_ref, dv_ref,
):
    heads, seq_len, _ = keys_ref.shape
    width = heads * HD
    half = HD // 2
    qb = pl.program_id(0)

    @pl.when(qb == 0)
    def _():
        for h in range(heads):
            keys_ref[h] = qkv_ref[width + h * HD : width + (h + 1) * HD, :].T
            values_ref[h] = qkv_ref[2 * width + h * HD : 2 * width + (h + 1) * HD, :].T
        dk_ref[...] = jnp.zeros_like(dk_ref)
        dv_ref[...] = jnp.zeros_like(dv_ref)

    here = pl.ds(pl.multiple_of(qb * BLK, BLK), BLK)
    start_row = start_ref[...]
    grad = go_ref[0]
    deltas = [
        jnp.sum(
            exact_ref[h * HD : (h + 1) * HD, :] * grad[h * HD : (h + 1) * HD].astype(f32),
            axis=0,
            keepdims=True,
        )
        for h in range(heads)
    ]

    def step(kb, carry):
        there = pl.ds(pl.multiple_of(kb * BLK, BLK), BLK)
        allowed = allowed_block(kb, qb, start_row)
        spans = [slice(h * HD, (h + 1) * HD) for h in range(heads)]
        queries = [qkv_ref[rows, here] for rows in spans]
        scores = [mm(keys_ref[h, there, :], queries[h], NN) for h in range(heads)]
        grad_probs = [mm(values_ref[h, there, :], grad[spans[h]], NN) for h in range(heads)]
        probs, grad_scores = [], []
        for h in range(heads):
            masked = jnp.where(allowed, scores[h] * score_scale, neg_large)
            prob = jnp.exp2(masked - log_ref[h : h + 1, :])
            probs.append(prob.astype(bf16))
            grad_scores.append((prob * (grad_probs[h] - deltas[h])).astype(bf16))
        new = []
        for h in range(heads):
            dv_ref[spans[h], there] += mm(grad[spans[h]], probs[h], NT)
        for h in range(heads):
            dk_ref[spans[h], there] += mm(queries[h], grad_scores[h], NT)
        for h in range(heads):
            keys = qkv_ref[width + h * HD : width + (h + 1) * HD, there]
            new.append(carry[h] + mm(keys, grad_scores[h], NN))
        return tuple(new)

    grads = lax.fori_loop(
        lo_ref[qb], qb + 1, step, tuple(jnp.zeros((HD, BLK), f32) for _ in range(heads))
    )

    def turn_back(value, cos, sin):
        value = value.astype(bf16).astype(f32)
        a, b = value[:half], value[half:]
        return (a * cos + b * sin).astype(bf16), (b * cos - a * sin).astype(bf16)

    for h in range(heads):
        a, b = turn_back(grads[h] * 0.125, cos_ref[:, here], sin_ref[:, here])
        out_ref[h * HD : h * HD + half, here] = a
        out_ref[h * HD + half : (h + 1) * HD, here] = b

    @pl.when(qb == pl.num_programs(0) - 1)
    def _():
        cos, sin = cos_ref[...], sin_ref[...]
        for h in range(heads):
            a, b = turn_back(dk_ref[h * HD : (h + 1) * HD, :] * 0.125, cos, sin)
            out_ref[width + h * HD : width + h * HD + half, :] = a
            out_ref[width + h * HD + half : width + (h + 1) * HD, :] = b
        out_ref[2 * width :, :] = dv_ref[...].astype(bf16)


def attn_back_call(lows, qkv, grad_out, exact, logs, start_row, cos_t, sin_t):
    width3, seq_len = qkv.shape
    width = width3 // 3
    heads = width // HD
    per = grad_out.shape[2] // BLK
    return pl.pallas_call(
        attn_back_kernel,
        out_shape=jax.ShapeDtypeStruct((width3, seq_len), bf16),
        grid_spec=pltpu.PrefetchScalarGridSpec(
            num_scalar_prefetch=1,
            grid=(seq_len // BLK,),
            in_specs=[
                pl.BlockSpec((width3, seq_len), lambda i, lo: (0, 0)),
                pl.BlockSpec((1, width, BLK), lambda i, lo: (i // per, 0, i % per)),
                pl.BlockSpec((width, BLK), lambda i, lo: (0, i)),
                pl.BlockSpec((heads, BLK), lambda i, lo: (0, i)),
                pl.BlockSpec((1, BLK), lambda i, lo: (0, i)),
                pl.BlockSpec((HD // 2, seq_len), lambda i, lo: (0, 0)),
                pl.BlockSpec((HD // 2, seq_len), lambda i, lo: (0, 0)),
            ],
            out_specs=pl.BlockSpec((width3, seq_len), lambda i, lo: (0, 0)),
            scratch_shapes=[
                pltpu.VMEM((heads, seq_len, HD), bf16),
                pltpu.VMEM((heads, seq_len, HD), bf16),
                pltpu.VMEM((width, seq_len), f32),
                pltpu.VMEM((width, seq_len), f32),
            ],
        ),
        cost_estimate=pl.CostEstimate(
            flops=16_000_000_000, transcendentals=0, bytes_accessed=16_000_000
        ),
        name="attend_back",
    )(lows, qkv, grad_out, exact, logs, start_row, cos_t, sin_t)


def gates_back(grad_hidden, gate_pre, up_pre):
    sig = 1.0 / (1.0 + jnp.exp(-gate_pre))
    silu = gate_pre * sig
    grad_gate = grad_hidden * up_pre * sig * (1.0 + gate_pre * (1.0 - sig))
    return (
        (silu * up_pre).astype(bf16),
        grad_gate.astype(bf16),
        (grad_hidden * silu).astype(bf16),
    )


def moe_kernel(n_dp, parts, x_ref, gate_ref, w_hbm, g_ref, *refs):
    piece_ref, dots_ref, out_ref, refs = refs[0], refs[1], refs[2], refs[3:]
    fin_hbm, refs = refs[:parts], refs[parts:]
    cross_hbm, refs = refs[:EARLY], refs[EARLY:]
    (
        w_ref, x_in, x_far, g_far, gate_in, gate_far, gs_ref, gs_far, pair_ref, near_ref, far_ref,
        own_ref, piece_out, dot_out, dw_out, dw_in, fin_ref,
        w_sem, x_send, x_recv, t_send, t_recv, p_send, p_recv, d_send, d_recv,
        xf_send, xf_recv, gf_send, gf_recv, tf_send, tf_recv, c_send, c_recv, e_send, e_recv, keep_sem,
    ) = refs
    me, dp = lax.axis_index("seq"), lax.axis_index("dp")
    owners = n_dp // E
    pairs = n_dp // 2
    half = near_ref.shape[2]
    core, plane = me & 1, lax.div(me, 2)
    greet([{"dp": dp ^ k} for k in range(1, n_dp)] + [{"seq": me ^ 1}, {"seq": me ^ 2}])

    def x_copy(k):
        return remote_later(
            x_ref.at[(dp ^ k) // owners], x_in.at[k], (x_send, x_recv), k, {"dp": dp ^ k}
        )

    def gate_copy(k):
        return remote_later(
            gate_ref.at[(dp ^ k) // owners], gate_in.at[k], (t_send, t_recv), k, {"dp": dp ^ k}
        )

    def piece_copy(k):
        return remote_later(
            piece_out.at[k], piece_ref.at[dp], (p_send, p_recv), k, {"dp": dp ^ k}
        )

    def dot_copy(k):
        return remote_later(dot_out.at[k], dots_ref.at[dp], (d_send, d_recv), k, {"dp": dp ^ k})

    def far_copies(k):
        across = {"seq": me ^ 2}
        return [
            remote_later(gate_in.at[k], gate_far.at[k], (tf_send, tf_recv), k, across),
            remote_later(g_ref.at[dp ^ k], g_far.at[k], (gf_send, gf_recv), k, across),
            remote_later(x_in.at[k], x_far.at[k], (xf_send, xf_recv), k, across),
        ]

    def core_copy(t):
        return remote_later(dw_out.at[t], dw_in.at[t], (c_send, c_recv), t, {"seq": me ^ 1})

    for p in range(pairs):
        for k in (2 * p, 2 * p + 1):
            if k:
                gate_copy(k).start()
                x_copy(k).start()
    loads = [pltpu.make_async_copy(w_hbm.at[j], w_ref.at[j], w_sem.at[j]) for j in range(3)]
    loads.append(pltpu.make_async_copy(x_ref.at[dp // owners], x_in.at[0], w_sem.at[3]))
    for load in loads:
        load.start()
    gate_in[0] = gate_ref[dp // owners]
    for load in loads:
        load.wait()

    def place(i):
        return i + 0

    def scale(ref, rows, gate, k):
        column = jnp.broadcast_to(gate, (CAP, CAP)).T[:, 0:1]
        here = pl.ds(pl.multiple_of(k * CAP, CAP), CAP)
        ref[here] = (rows.astype(f32) * column).astype(bf16)

    @pl.loop(0, pairs)
    def _(i):
        p = place(i)
        rows = pl.ds(pl.multiple_of(p * PAIR, PAIR), PAIR)

        def arrive(k):
            x_copy(k).wait_recv()
            gate_copy(k).wait_recv()

        @pl.when(p > 0)
        def _():
            arrive(2 * p)

        arrive(2 * p + 1)
        for side in range(2):
            k = 2 * p + side
            for copy in far_copies(k):
                copy.start()
            scale(gs_ref, g_ref[dp ^ k], gate_in[k], k)

        @pl.loop(0, 2)
        def _(t):
            part = pl.ds(pl.multiple_of(t * half, half), half)
            x = x_in[pl.ds(2 * p, 2)].reshape(PAIR, D)
            gate_pre = mm(x, w_ref[0, part], NT)
            up_pre = mm(x, w_ref[1, part], NT)
            grad_hidden = mm(gs_ref[rows], w_ref[2, part], NT)
            results = gates_back(grad_hidden, gate_pre, up_pre)
            for j in range(3):
                pair_ref[j, :, part] = results[j]

            @pl.when(t == plane)
            def _():
                for j in range(3):
                    near_ref[j, rows] = results[j]

        pieces = mm(pair_ref[1], w_ref[0], NN) + mm(pair_ref[2], w_ref[1], NN)
        piece_out[pl.ds(2 * p, 2)] = pieces.astype(bf16).reshape(2, CAP, D)
        piece_copy(2 * p + 1).start()

        @pl.when(p > 0)
        def _():
            piece_copy(2 * p).start()

        outs = mm(pair_ref[0], w_ref[2], NN)
        for side in range(2):
            k = 2 * p + side
            out = outs[side * CAP : (side + 1) * CAP].astype(bf16)
            out_ref[dp ^ k] = out
            product = out.astype(f32) * g_ref[dp ^ k].astype(f32)
            dot_out[k] = column_to_row(jnp.sum(product, axis=1, keepdims=True))
        dot_copy(2 * p + 1).start()

        @pl.when(p > 0)
        def _():
            dot_copy(2 * p).start()

    piece_ref[dp] = piece_out[0]
    dots_ref[dp] = dot_out[0]

    def weight_grad(source, x, gs, j, part):
        left = source[(1, 2, 0)[j], :, part]
        return mm(left, gs[...] if j == 2 else x[...].reshape(n_dp * CAP, D), TN)

    @pl.loop(0, half // UNITS)
    def _(t):
        part = pl.ds(pl.multiple_of(t * UNITS, UNITS), UNITS)
        for j in range(3):
            own_ref[j, part] = weight_grad(near_ref, x_in, gs_ref, j, part)

    def far_grad(rows, j, part):
        left = far_ref[(1, 2, 0)[j], :, part]
        if j == 2:
            right = gs_far[rows]
        elif isinstance(rows, slice):
            right = x_far[rows.start // CAP : rows.stop // CAP].reshape(PAIR, D)
        else:
            right = x_far[pl.ds(lax.div(rows.start, CAP), 2)].reshape(PAIR, D)
        return mm(left, right, TN)

    @pl.loop(0, pairs)
    def _(i):
        p = place(i)
        rows = pl.ds(pl.multiple_of(p * PAIR, PAIR), PAIR)
        for side in range(2):
            k = 2 * p + side
            for copy in far_copies(k):
                copy.wait_recv()
            scale(gs_far, g_far[k], gate_far[k], k)
        part = pl.ds(pl.multiple_of(plane * half, half), half)
        x = x_far[pl.ds(2 * p, 2)].reshape(PAIR, D)
        results = gates_back(
            mm(gs_far[rows], w_ref[2, part], NT),
            mm(x, w_ref[0, part], NT),
            mm(x, w_ref[1, part], NT),
        )
        for j in range(3):
            far_ref[j] = results[j]

        @pl.when(i < pairs - 1)
        def _():
            @pl.loop(0, half // UNITS)
            def _(t):
                part = pl.ds(pl.multiple_of(t * UNITS, UNITS), UNITS)
                for j in range(3):
                    own_ref[j, part] += far_grad(rows, j, part)

    tiles = half // UNITS // 2
    final = slice((pairs - 1) * PAIR, pairs * PAIR)

    def both_rows(side, t, j):
        part = pl.ds(pl.multiple_of((side * tiles + t) * UNITS, UNITS), UNITS)
        return own_ref[j, part] + far_grad(final, j, part)

    @pl.loop(0, tiles)
    def _(t):
        for j in range(3):
            dw_out[t, j] = both_rows(1 - core, t, j).astype(bf16)
        core_copy(t).start()

    def early_copy(t):
        return remote_later(fin_ref.at[t], cross_hbm[t], (e_send, e_recv), t, {"seq": me ^ 2})

    @pl.loop(0, tiles)
    def _(t):
        core_copy(t).wait_recv()
        for j in range(3):
            total = (both_rows(core, t, j) + dw_in[t, j].astype(f32)).astype(bf16)
            for u in range(UNITS // PART):
                fin_ref[t * (UNITS // PART) + u, j] = total[u * PART : (u + 1) * PART]

        @pl.when(t == 0)
        def _():
            for e in range(EARLY):
                early_copy(e).start()

    keeps = [
        pltpu.make_async_copy(fin_ref.at[t], fin_hbm[t], keep_sem.at[t]) for t in range(parts)
    ]
    for keep in keeps:
        keep.start()
    for k in range(1, n_dp):
        piece_copy(k).wait()
        dot_copy(k).wait()
        x_copy(k).wait_send()
        gate_copy(k).wait_send()
    for k in range(n_dp):
        for copy in far_copies(k):
            copy.wait_send()
    for t in range(tiles):
        core_copy(t).wait_send()
    for t in range(EARLY):
        early_copy(t).wait()
    for keep in keeps:
        keep.wait()


def moe_call(n_dp, x_slots, gate_slots, weights, grads):
    units = weights.shape[1]
    half = units // 2
    rows = n_dp * CAP
    parts = units // 4 // PART
    tiles = half // UNITS // 2
    outs = pl.pallas_call(
        functools.partial(moe_kernel, n_dp, parts),
        out_shape=(
            jax.ShapeDtypeStruct((n_dp, CAP, D), bf16),
            jax.ShapeDtypeStruct((n_dp, 1, CAP), f32),
            jax.ShapeDtypeStruct((n_dp, CAP, D), bf16),
        )
        + (jax.ShapeDtypeStruct((3, PART, D), bf16),) * (parts + EARLY),
        in_specs=[HBM, VMEM, HBM, VMEM],
        out_specs=[VMEM] * 3 + [HBM] * (parts + EARLY),
        scratch_shapes=[
            pltpu.VMEM(weights.shape, bf16),
            pltpu.VMEM((n_dp, CAP, D), bf16),
            pltpu.VMEM((n_dp, CAP, D), bf16),
            pltpu.VMEM((n_dp, CAP, D), bf16),
            pltpu.VMEM((n_dp, 1, CAP), f32),
            pltpu.VMEM((n_dp, 1, CAP), f32),
            pltpu.VMEM((rows, D), bf16),
            pltpu.VMEM((rows, D), bf16),
            pltpu.VMEM((3, PAIR, units), bf16),
            pltpu.VMEM((3, rows, half), bf16),
            pltpu.VMEM((3, PAIR, half), bf16),
            pltpu.VMEM((3, half, D), f32),
            pltpu.VMEM((n_dp, CAP, D), bf16),
            pltpu.VMEM((n_dp, 1, CAP), f32),
            pltpu.VMEM((tiles, 3, UNITS, D), bf16),
            pltpu.VMEM((tiles, 3, UNITS, D), bf16),
            pltpu.VMEM((parts, 3, PART, D), bf16),
            DMA((4,)),
        ]
        + [DMA((n_dp,))] * 14
        + [DMA((tiles,))] * 2
        + [DMA((EARLY,))] * 2
        + [DMA((parts,))],
        compiler_params=pltpu.CompilerParams(
            collective_id=4, has_side_effects=True, vmem_limit_bytes=67043328
        ),
        name="experts",
    )(x_slots, gate_slots, weights, grads)
    return outs[0], outs[1], outs[2], list(outs[3 : 3 + parts]), list(outs[3 + parts :])


def experts_plain(to_owners, to_sources, n_dp, x_slots, gate_slots, weights, grads):
    rows = n_dp * CAP
    x = to_owners(x_slots).reshape(rows, D)
    gate = to_owners(gate_slots).reshape(rows, 1)
    g = grads.reshape(rows, D)
    gs = (g.astype(f32) * gate).astype(bf16)
    hidden, grad_gate, grad_up = gates_back(
        mm(gs, weights[2], NT), mm(x, weights[0], NT), mm(x, weights[1], NT)
    )
    out = mm(hidden, weights[2], NN).astype(bf16)
    piece = (mm(grad_gate, weights[0], NN) + mm(grad_up, weights[1], NN)).astype(bf16)
    dw = jnp.stack([mm(grad_gate, x, TN), mm(grad_up, x, TN), mm(hidden, gs, TN)])
    dots = jnp.sum(out.astype(f32) * g.astype(f32), axis=-1)
    return (
        to_sources(piece.reshape(n_dp, CAP, D)),
        to_sources(dots.reshape(n_dp, 1, CAP)),
        out.reshape(n_dp, CAP, D),
        lax.psum(dw, "seq"),
    )


def mid_kernel(
    n_seq, att_ref, h_ref, prev_ref, carry_ref, small_ref, slot_ref, route_ref, w_ref,
    heads_ref, mid_ref, gate_ref, x_ref, gs_ref, send_sem, recv_sem,
):
    me = lax.axis_index("seq")
    tok = h_ref.shape[0]
    greet([{"seq": me ^ place} for place in range(1, n_seq)])
    copies = [
        remote(
            att_ref.at[me ^ place], heads_ref.at[me], (send_sem, recv_sem), place,
            {"seq": me ^ place},
        )
        for place in range(1, n_seq)
    ]
    heads_ref[me] = att_ref[me]
    picks = picks_of(slot_ref)
    pick_any = picks[0] + picks[1]
    carried = lax.dot_general(
        carry_ref[...].astype(f32), prev_ref[:, 0, :], TN, precision=exact_prec,
        preferred_element_type=f32,
    )
    for copy in copies:
        copy.wait_recv()
    attn_out = mm(heads_ref[...].reshape(D, tok), w_ref[...].reshape(D, D), TN)
    resid = h_ref[...].astype(f32) + attn_out
    mid_ref[...] = resid
    rate = lax.rsqrt(jnp.mean(resid * resid, axis=-1, keepdims=True) + 1e-06)
    normed = resid * rate * small_ref[1:2]
    low = normed.astype(bf16)
    x_ref[...] = mm(pick_any, low, NN).astype(bf16).reshape(x_ref.shape)
    heads_rows = small_ref[4 : 8 + H].astype(bf16)
    products = mm(heads_rows, low, NT)
    rest = mm(heads_rows, (normed - low.astype(f32)).astype(bf16), NT)
    logits = products[4:] + carried
    ids = lax.broadcasted_iota(jnp.int32, (H, tok), 0)
    chosen = [
        jnp.sum(jnp.where(route_ref[k : k + 1, :] == ids, logits, 0.0), axis=0, keepdims=True)
        for k in range(2)
    ]
    top = jnp.maximum(chosen[0], chosen[1])
    exps = [jnp.exp(c - top) for c in chosen]
    total = exps[0] + exps[1]
    gates = [e / total for e in exps]
    gate_ref[...] = jnp.concatenate(
        [gates[0], gates[1], products[:4] + rest[:4], jnp.zeros((2, tok), f32)], axis=0
    )
    slot_gates = sum(unsplit(mm(split(gates[k]), picks[k], NT)) for k in range(2))
    for e in range(E):
        gs_ref[e] = slot_gates[:, e * CAP : (e + 1) * CAP]
    for copy in copies:
        copy.wait_send()


def mid_call(n_seq, attended, hidden, prev, carry, small, slot_of, routes, w_out):
    tok, width = hidden.shape[0], attended.shape[1]
    return pl.pallas_call(
        functools.partial(mid_kernel, n_seq),
        out_shape=(
            jax.ShapeDtypeStruct((n_seq, width, tok), bf16),
            jax.ShapeDtypeStruct((tok, D), f32),
            jax.ShapeDtypeStruct((8, tok), f32),
            jax.ShapeDtypeStruct((E, CAP, D), bf16),
            jax.ShapeDtypeStruct((E, 1, CAP), f32),
        ),
        in_specs=[VMEM] * 8,
        out_specs=[VMEM] * 5,
        scratch_shapes=[DMA((n_seq,)), DMA((n_seq,))],
        compiler_params=pltpu.CompilerParams(collective_id=2, has_side_effects=True),
        name="mid",
    )(attended, hidden, prev, carry, small, slot_of, routes, w_out)


def mid_back_kernel(
    n_seq, n_dp, n_tile, piece_ref, dots_ref, cot_ref, mid_ref, gate_ref, slot_ref, route_ref,
    small_ref, heads_ref, w_ref, prev_ref, carry_ref, *refs,
):
    tile_refs, refs = refs[:n_tile], refs[n_tile:]
    resid_ref, go_ref, base_ref, dprev_ref, pack_ref, wo_sum_ref, *refs = refs
    far_refs, refs = refs[:n_tile], refs[n_tile:]
    gh_ref, wo_ref, wo_in, a_send, a_recv, c_send, c_recv, t_send, t_recv = refs
    me = lax.axis_index("seq")
    tok = cot_ref.shape[0]
    width = heads_ref.shape[1]
    owners = n_dp // E
    pairs = n_seq // 2
    greet([{"seq": me ^ place} for place in range(1, n_seq)])
    tile_copies = [
        remote(tile_refs[t], far_refs[t], (t_send, t_recv), t, {"seq": me ^ 2})
        for t in range(n_tile)
    ]
    cot = cot_ref[...]
    grad_top = cot.astype(f32)
    resid_mid = mid_ref[...]
    gain = small_ref[1:2]
    rate = lax.rsqrt(jnp.mean(resid_mid * resid_mid, axis=-1, keepdims=True) + 1e-06)
    normed = resid_mid * rate * gain
    low = normed.astype(bf16)
    picks = picks_of(slot_ref)
    gates = [gate_ref[k : k + 1, :] for k in range(2)]
    routes = [route_ref[k : k + 1, :] for k in range(2)]
    normed_dot = column_to_row(jnp.sum(grad_top * normed, axis=1, keepdims=True))
    vecs = small_ref[2:4].astype(bf16)
    vec_dot = mm(vecs, cot, NT)
    alphas, const_dot = [], []
    for j in range(2):
        pair = [gate_ref[2 + 2 * j + c : 3 + 2 * j + c, :] for c in range(2)]
        top = jnp.maximum(pair[0], pair[1])
        exps = [jnp.exp(p - top) for p in pair]
        total = exps[0] + exps[1]
        alphas.append([e / total for e in exps])
        const_dot.append(alphas[j][0] * normed_dot + alphas[j][1] * vec_dot[j : j + 1])
    slot_dots = split(
        jnp.concatenate(
            [sum(dots_ref[e * owners + o] for o in range(owners)) for e in range(E)], axis=1
        )
    )
    out_dots = []
    for k in range(2):
        value = unsplit(mm(slot_dots, picks[k], NN))
        value = value + jnp.where(routes[k] == E + 1, normed_dot, 0.0)
        for j in range(2):
            value = value + jnp.where(routes[k] == E + 2 + j, const_dot[j], 0.0)
        out_dots.append(value)
    mean_dot = gates[0] * out_dots[0] + gates[1] * out_dots[1]
    ids = lax.broadcasted_iota(jnp.int32, (H, tok), 0)
    grad_logits = sum(
        jnp.where(routes[k] == ids, gates[k] * (out_dots[k] - mean_dot), 0.0) for k in range(2)
    )

    def gate_of(expert):
        return sum(jnp.where(routes[k] == expert, gates[k], 0.0) for k in range(2))

    const_gate = [gate_of(E + 2 + j) for j in range(2)]
    normed_gate = gate_of(E + 1) + sum(const_gate[j] * alphas[j][0] for j in range(2))
    vec_gate = split(jnp.concatenate([const_gate[j] * alphas[j][1] for j in range(2)], axis=0))
    mix_grads = []
    for j in range(2):
        terms = [normed_dot, vec_dot[j : j + 1]]
        for c in range(2):
            mix_grads.append(const_gate[j] * alphas[j][c] * (terms[c] - const_dot[j]))
    token_rows = split(jnp.concatenate(mix_grads + [grad_logits], axis=0))
    normed_column = jnp.broadcast_to(normed_gate, (8, tok)).T[:, 0:1]
    heads_rows = small_ref[4 : 8 + H].astype(bf16)
    pick_any = picks[0] + picks[1]
    grad_normed = grad_top * normed_column
    grad_normed = grad_normed + mm(
        token_rows, jnp.concatenate([heads_rows] * 3, axis=0), TN
    )
    pieces = piece_ref[...].reshape(E, owners, CAP, D)
    for o in range(owners):
        grad_normed = grad_normed + mm(pick_any, pieces[:, o].reshape(E * CAP, D), TN)
    grad_resid = grad_top + norm_back(resid_mid, gain, grad_normed)
    resid_ref[...] = grad_resid
    grad_attn = grad_resid.astype(bf16)
    gh_ref[...] = mm(w_ref[...].reshape(D, D), grad_attn, NT).astype(bf16).reshape(gh_ref.shape)
    copies = [
        remote(gh_ref.at[me ^ place], go_ref.at[me], (a_send, a_recv), place, {"seq": me ^ place})
        for place in range(1, n_seq)
    ]
    go_ref[me] = gh_ref[me]
    grad_w = mm(heads_ref[...].reshape(D, tok), grad_attn, NN)
    for j in range(n_seq):
        wo_ref[j] = grad_w[:, j * width : (j + 1) * width].astype(bf16)
    core_copies = [
        remote(wo_ref.at[me ^ (2 * i + 1)], wo_in.at[i], (c_send, c_recv), i, {"seq": me ^ 1})
        for i in range(pairs)
    ]
    base_ref[...] = (
        resid_mid
        + normed * normed_column
        + mm(vec_gate, jnp.concatenate([vecs] * 3, axis=0), TN)
    )
    dprev_ref[:, 0, :] = lax.dot_general(
        carry_ref[...].astype(f32), grad_logits, NN, precision=exact_prec,
        preferred_element_type=f32,
    )
    rest = (normed - low.astype(f32)).astype(bf16)
    row_sums = unsplit(mm(token_rows, low, NN))
    mix_sums = row_sums[:4] + unsplit(mm(token_rows, rest, NN))[:4]
    vec_sums = unsplit(mm(vec_gate, cot, NN))
    gain_sum = jnp.sum(grad_normed * resid_mid * rate, axis=0, keepdims=True)
    carry_grad = lax.dot_general(
        prev_ref[:, 0, :], grad_logits, NT, precision=exact_prec, preferred_element_type=f32
    )
    packed = jnp.concatenate([mix_sums, row_sums[4:], vec_sums, gain_sum], axis=0)
    lines, shard = packed.shape[0], D // n_dp
    for i in range(n_dp):
        pack_ref[i] = jnp.zeros(pack_ref.shape[1:], f32)
        pack_ref[i, 0:lines, :] = packed[:, i * shard : (i + 1) * shard]
        pack_ref[i, 24 : 24 + H, 0:H] = carry_grad
    for i in range(pairs):
        core_copies[i].wait_recv()
        wo_sum_ref[i] = (
            wo_ref[me ^ (2 * i)].astype(f32) + wo_in[i].astype(f32)
        ).astype(bf16)
    for copy in copies + tile_copies:
        copy.wait()
    for copy in core_copies:
        copy.wait_send()


def mid_back_call(
    n_seq, n_dp, piece, dots, cot, mid, gates, slot_of, routes, small, heads, w, prev, carry,
    parts,
):
    tok, width = cot.shape[0], heads.shape[1]
    pairs = n_seq // 2
    n_tile = len(parts)
    outs = pl.pallas_call(
        functools.partial(mid_back_kernel, n_seq, n_dp, n_tile),
        out_shape=(
            jax.ShapeDtypeStruct((tok, D), f32),
            jax.ShapeDtypeStruct((n_seq, width, tok), bf16),
            jax.ShapeDtypeStruct((tok, D), f32),
            jax.ShapeDtypeStruct((H, 1, tok), f32),
            jax.ShapeDtypeStruct((n_dp, LINES, D // n_dp), f32),
            jax.ShapeDtypeStruct((pairs, D, width), bf16),
        )
        + tuple(jax.ShapeDtypeStruct(part.shape, bf16) for part in parts),
        in_specs=[VMEM] * 12 + [HBM] * n_tile,
        out_specs=[VMEM] * 6 + [HBM] * n_tile,
        scratch_shapes=[
            pltpu.VMEM((n_seq, width, tok), bf16),
            pltpu.VMEM((n_seq, D, width), bf16),
            pltpu.VMEM((pairs, D, width), bf16),
            DMA((n_seq,)),
            DMA((n_seq,)),
            DMA((pairs,)),
            DMA((pairs,)),
            DMA((max(n_tile, 1),)),
            DMA((max(n_tile, 1),)),
        ],
        compiler_params=pltpu.CompilerParams(collective_id=3, has_side_effects=True),
        name="mid_back",
    )(piece, dots, cot, mid, gates, slot_of, routes, small, heads, w, prev, carry, *parts)
    return outs[:6], list(outs[6:])


def tail_kernel(
    n_seq, n_dp, parts, g_ref, wt_ref, wo_ref, pack_ref, gate_ref, slot_ref, gain_ref,
    a_hbm, h_hbm, resid_hbm, base_hbm, out_hbm, *refs,
):
    n_far = max(parts - LATE, 0)
    fin_hbm, refs = refs[:parts], refs[parts:]
    far_hbm, refs = refs[:n_far], refs[n_far:]
    din_ref, row_in, line_ref, block_ref, both_ref, refs = *refs[:5], refs[5:]
    (
        a_ref, h_ref, resid_ref, base_ref, rows_ref, far_ref, fin_ref,
        core_out, core_in, x_out, x_in, part_ref, w_out_buf, w_in, wo_buf, wo_in, wo_x, wo_far,
        w_mid, wo_mid,
        row_buf, pack_in, line_buf, line_in, load_sem, c_sems, x_sems, w_sems, v_sems, r_sems, o_sems,
        p_sems, q_sems, u_sems, l_sems, t_sems, f_sems, keep_sem,
    ) = refs
    me, dp = lax.axis_index("seq"), lax.axis_index("dp")
    tok = h_ref.shape[0]
    shard, width3 = w_in.shape[1], w_in.shape[2]
    width = width3 // 3
    owners = n_dp // E
    pairs = n_seq // 2
    others = range(1, n_dp)

    def both(sems):
        return sems.at[0], sems.at[1]

    c_sems, x_sems, w_sems, v_sems, r_sems, o_sems, p_sems, q_sems, u_sems, l_sems, t_sems, f_sems = (
        both(sems)
        for sems in (
            c_sems, x_sems, w_sems, v_sems, r_sems, o_sems, p_sems, q_sems, u_sems, l_sems, t_sems,
            f_sems,
        )
    )

    loads = []
    for src, dst in [
        (a_hbm, a_ref), (out_hbm, rows_ref), (base_hbm, base_ref), (h_hbm, h_ref),
        (resid_hbm, resid_ref),
    ] + [(fin_hbm[t], fin_ref.at[t]) for t in range(parts)] + [
        (far_hbm[t], far_ref.at[t]) for t in range(n_far)
    ]:
        load = pltpu.make_async_copy(src, dst, load_sem.at[len(loads)])
        load.start()
        loads.append(load)
    greet(
        [{"seq": me ^ place} for place in range(1, n_seq)]
        + [{"dp": lax.rem(dp + k, n_dp)} for k in others]
    )

    def there(k):
        return lax.rem(dp + k, n_dp)

    spots = [*range(n_dp // 2 - 1, -1, -1)]

    def to_neighbour(buf, near, sems):
        return {
            j: remote(buf.at[dp ^ (2 * j) ^ 1], near.at[j], sems, j, {"dp": dp ^ 1}) for j in spots
        }

    def pass_sums(copies, buf, near, mid, sems):
        passed = []
        for j in spots:
            copies[j].wait_recv()
            total = buf[dp ^ (2 * j)].astype(f32) + near[j].astype(f32)
            mid[j] = total.astype(bf16)
            if j:
                passed.append(
                    remote(mid.at[j], near.at[n_dp // 2 + j], sems, j, {"dp": dp ^ (2 * j)})
                )
        return passed

    def collect(passed, near, mid):
        for copy in passed:
            copy.wait_recv()
        return sum((near[n_dp // 2 + j].astype(f32) for j in spots[:-1]), mid[0].astype(f32))

    def term(place):
        columns = pl.ds(pl.multiple_of((me ^ place) * tok, tok), tok)
        return mm(g_ref[:, columns], wt_ref[...], TN)

    part_copies = [
        remote(fin_hbm[t], far_ref.at[t], t_sems, t - n_far, {"seq": me ^ 2})
        for t in range(n_far, parts)
    ]
    pack_copies = [
        remote(pack_ref.at[there(k)], pack_in.at[dp], p_sems, k, {"dp": there(k)}) for k in others
    ]
    pack_in[dp] = pack_ref[dp]
    for i in range(pairs):
        wo_buf[:, :, i * width : (i + 1) * width] = wo_ref[i].reshape(n_dp, shard, width)
    wo_near = to_neighbour(wo_buf, wo_in, q_sems)
    core_copies = []
    for i in range(pairs - 1, -1, -1):
        core_out[i] = term(2 * i + 1).astype(bf16)
        core_copies.insert(0, remote(core_out.at[i], core_in.at[i], c_sems, i, {"seq": me ^ 1}))
    x_copies = []
    for i in range(pairs - 1, 0, -1):
        part = term(2 * i)
        core_copies[i].wait_recv()
        x_out[i - 1] = (part + core_in[i].astype(f32)).astype(bf16)
        x_copies.append(
            remote(x_out.at[i - 1], x_in.at[i - 1], x_sems, i - 1, {"seq": me ^ (2 * i)})
        )
    loads[0].wait()
    turned = mm(g_ref[...], a_ref[...], NN)
    w_out_buf[...] = turned.T.astype(bf16).reshape(n_dp, shard, width3)
    w_near = to_neighbour(w_out_buf, w_in, w_sems)
    wo_copies = pass_sums(wo_near, wo_buf, wo_in, wo_mid, u_sems)
    w_copies = pass_sums(w_near, w_out_buf, w_in, w_mid, v_sems)
    part = term(0)
    core_copies[0].wait_recv()
    part_ref[...] = part + core_in[0].astype(f32)

    for copy in pack_copies:
        copy.wait_recv()
    line_buf[...] = jnp.sum(pack_in[...], axis=0)
    line_in[me] = line_buf[...]
    line_copies = [
        remote(line_buf, line_in.at[me], l_sems, place, {"seq": me ^ place})
        for place in range(1, n_seq)
    ]

    fin_copies, keeps = [], []

    def hand_over(ref, row, t):
        index = row * parts + t
        fin_copies.append(
            remote(ref.at[t], both_ref.at[2 * row + 1, t], f_sems, index, {"seq": me ^ 1})
        )
        keep = pltpu.make_async_copy(ref.at[t], both_ref.at[2 * row, t], keep_sem.at[index])
        keep.start()
        keeps.append(keep)

    for t in range(parts):
        loads[5 + t].wait()
        hand_over(fin_ref, 0, t)
    for t in range(n_far):
        loads[5 + parts + t].wait()
        hand_over(far_ref, 1, t)

    wo_total = collect(wo_copies, wo_in, wo_mid)
    wo_cross = []
    for i in range(1, pairs):
        wo_x[i - 1] = wo_total[:, i * width : (i + 1) * width].astype(bf16)
        wo_cross.append(
            remote(wo_x.at[i - 1], wo_far.at[i - 1], o_sems, i - 1, {"seq": me ^ (2 * i)})
        )

    loads[1].wait()
    loads[2].wait()
    picks = picks_of(slot_ref)
    rows = rows_ref[...].reshape(E, owners, CAP, D)
    columns = gate_ref[...].T
    block = base_ref[...]
    for k in range(2):
        picked = sum(
            mm(picks[k], rows[:, o].reshape(E * CAP, D), TN) for o in range(owners)
        )
        block = block + columns[:, k : k + 1] * picked
    block_ref[...] = block.astype(bf16)

    for copy in x_copies:
        copy.wait_recv()
    grad = part_ref[...]
    for i in range(pairs - 1):
        grad = grad + x_in[i].astype(f32)
    loads[3].wait()
    loads[4].wait()
    din_ref[...] = resid_ref[...] + norm_back(h_ref[...].astype(f32), gain_ref[0:1], grad)

    row_buf[:, :width3] = collect(w_copies, w_in, w_mid).astype(bf16)
    for copy in wo_cross:
        copy.wait_recv()
    wo_mine = wo_total[:, :width]
    for i in range(pairs - 1):
        wo_mine = wo_mine + wo_far[i].astype(f32)
    row_buf[:, width3:] = wo_mine.astype(bf16)
    row_in[me] = row_buf[...]
    row_copies = [
        remote(row_buf, row_in.at[me], r_sems, place, {"seq": me ^ place})
        for place in range(1, n_seq)
    ]
    for copy in line_copies:
        copy.wait_recv()
    line_ref[...] = jnp.sum(line_in[...], axis=0)
    for t, copy in enumerate(part_copies):
        copy.wait_recv()
        hand_over(far_ref, 1, n_far + t)
    for copy in row_copies + fin_copies:
        copy.wait_recv()
    for copy in (
        core_copies + [*w_near.values()] + [*wo_near.values()] + w_copies + x_copies + row_copies + wo_copies + pack_copies
        + line_copies + wo_cross + part_copies + fin_copies
    ):
        copy.wait_send()
    for keep in keeps:
        keep.wait()


def tail_call(
    n_seq, n_dp, grad_qkv, w_turned, wo_sum, pack, gates, slot_of, small,
    attn_in, hidden, grad_resid, base, back_out, fin, far,
):
    tok = hidden.shape[0]
    shard, width3 = D // n_dp, grad_qkv.shape[0]
    width = width3 // 3
    pairs = n_seq // 2
    parts, room = len(fin), max(len(fin), 1)
    part = (3, PART, D)
    return pl.pallas_call(
        functools.partial(tail_kernel, n_seq, n_dp, parts),
        out_shape=(
            jax.ShapeDtypeStruct((tok, D), f32),
            jax.ShapeDtypeStruct((n_seq, shard, width3 + width), bf16),
            jax.ShapeDtypeStruct((LINES, shard), f32),
            jax.ShapeDtypeStruct((tok, D), bf16),
            jax.ShapeDtypeStruct((n_seq, room, *part), bf16),
        ),
        in_specs=[VMEM] * 7 + [HBM] * (5 + parts + len(far)),
        out_specs=[VMEM] * 4 + [HBM],
        scratch_shapes=[
            pltpu.VMEM((n_seq * tok, D), bf16),
            pltpu.VMEM((tok, D), bf16),
            pltpu.VMEM((tok, D), f32),
            pltpu.VMEM((tok, D), f32),
            pltpu.VMEM((n_dp, CAP, D), bf16),
            pltpu.VMEM((room, *part), bf16),
            pltpu.VMEM((room, *part), bf16),
            pltpu.VMEM((pairs, tok, D), bf16),
            pltpu.VMEM((pairs, tok, D), bf16),
            pltpu.VMEM((pairs - 1, tok, D), bf16),
            pltpu.VMEM((pairs - 1, tok, D), bf16),
            pltpu.VMEM((tok, D), f32),
            pltpu.VMEM((n_dp, shard, width3), bf16),
            pltpu.VMEM((n_dp, shard, width3), bf16),
            pltpu.VMEM((n_dp, shard, pairs * width), bf16),
            pltpu.VMEM((n_dp, shard, pairs * width), bf16),
            pltpu.VMEM((pairs - 1, shard, width), bf16),
            pltpu.VMEM((pairs - 1, shard, width), bf16),
            pltpu.VMEM((n_dp // 2, shard, width3), bf16),
            pltpu.VMEM((n_dp // 2, shard, pairs * width), bf16),
            pltpu.VMEM((shard, width3 + width), bf16),
            pltpu.VMEM((n_dp, LINES, shard), f32),
            pltpu.VMEM((LINES, shard), f32),
            pltpu.VMEM((n_seq, LINES, shard), f32),
            DMA((5 + 2 * room,)),
            DMA((2, pairs)),
            DMA((2, pairs)),
            DMA((2, n_dp // 2)),
            DMA((2, n_dp // 2)),
            DMA((2, n_seq)),
            DMA((2, pairs)),
            DMA((2, n_dp)),
            DMA((2, n_dp // 2)),
            DMA((2, n_dp // 2)),
            DMA((2, n_seq)),
            DMA((2, LATE)),
            DMA((2, 2 * room)),
            DMA((2 * room,)),
        ],
        compiler_params=pltpu.CompilerParams(
            collective_id=1, has_side_effects=True, vmem_limit_bytes=67043328
        ),
        name="tail",
    )(
        grad_qkv, w_turned, wo_sum, pack, gates, slot_of, small,
        attn_in, hidden, grad_resid, base, back_out, *fin, *far,
    )


def finish_kernel(
    n_seq, me_ref, both_ref, row_ref, line_ref, wq_ref, gain_ref,
    de_ref, dw_ref, dwo_ref, again_ref, mgain_ref, router_ref, carry_ref, vec_ref, mix_ref,
):
    step = both_ref.shape[3]
    for t in range(both_ref.shape[1]):
        de_ref[:, t * step : (t + 1) * step] = both_ref[0, t].astype(f32)

    @pl.when(pl.program_id(0) == 0)
    def _():
        width = row_ref.shape[2] // 4
        for j in range(n_seq):
            block = row_ref[j].astype(f32)
            for c in range(3):
                left = c * width * n_seq + j * width
                dw_ref[:, left : left + width] = block[:, c * width : (c + 1) * width]
            dwo_ref[:, j * width : (j + 1) * width] = block[:, 3 * width :]
        sums = jnp.sum(dw_ref[...] * wq_ref[...].astype(f32), axis=1, keepdims=True)
        again_ref[...] = column_to_row(sums) / gain_ref[...].astype(f32)
        mix_ref[0] = line_ref[0:2]
        mix_ref[1] = line_ref[2:4]
        router_ref[...] = line_ref[4 : 4 + H]
        vec_ref[...] = line_ref[4 + H : 6 + H]
        mgain_ref[...] = line_ref[6 + H : 7 + H]
        carry_ref[...] = line_ref[24 : 24 + H, 0:H]


def finish_call(n_seq, me, both, row_in, lines, w_qkv, attn_gain):
    shard = w_qkv.shape[0]
    _, parts, three, step, _ = both.shape
    units = n_seq * parts * step
    group = 4 if parts % 4 == 0 else 1
    steps = parts // group

    def whole(shape):
        return pl.BlockSpec(shape, lambda i, me_ref: (0,) * len(shape))

    shapes = [(shard, 3 * D), (shard, D), (1, shard), (1, shard), (H, shard), (H, H), (2, shard),
              (2, 2, shard)]
    return pl.pallas_call(
        functools.partial(finish_kernel, n_seq),
        out_shape=[jax.ShapeDtypeStruct((three, units, D), f32)]
        + [jax.ShapeDtypeStruct(shape, f32) for shape in shapes],
        grid_spec=pltpu.PrefetchScalarGridSpec(
            num_scalar_prefetch=1,
            grid=(n_seq * steps,),
            in_specs=[
                pl.BlockSpec(
                    (1, group, three, step, D),
                    lambda i, me_ref: ((i // steps) ^ me_ref[0], i % steps, 0, 0, 0),
                ),
                whole(row_in.shape),
                whole(lines.shape),
                whole(w_qkv.shape),
                whole((1, shard)),
            ],
            out_specs=[pl.BlockSpec((three, group * step, D), lambda i, me_ref: (0, i, 0))]
            + [whole(shape) for shape in shapes],
        ),
        name="finish",
    )(me, both, row_in, lines, w_qkv, attn_gain[None])


def rope_tables(seq_len):
    freq_index = jnp.arange(HD // 2, dtype=f32)
    inv_freq = jnp.exp(freq_index * (-2.0 * math.log(10000.0) / HD))
    angles = jnp.arange(seq_len, dtype=jnp.int32).astype(f32)[None, :] * inv_freq[:, None]
    return jnp.cos(angles), jnp.sin(angles)


def per_device(
    hidden_in,
    prev_logits,
    segments,
    routes,
    attn_gain,
    w_qkv,
    w_out,
    moe_gain,
    w_router,
    w_carry,
    const_vec,
    const_mix,
    experts,
    cotangent,
):
    n_seq, n_dp = lax.axis_size("seq"), lax.axis_size("dp")
    owners = n_dp // E
    me = lax.axis_index("seq")
    tok = hidden_in.shape[1]
    hidden, cot = hidden_in[0], cotangent[0]
    prev_t = jnp.transpose(prev_logits, (2, 0, 1))
    routes_t = routes[0].T

    def to_owners(values):
        return lax.all_to_all(
            jnp.repeat(values, owners, axis=0), "dp", split_axis=0, concat_axis=0, tiled=True
        )

    def to_sources(values):
        return lax.all_to_all(values, "dp", split_axis=0, concat_axis=0, tiled=True)

    cos_t, sin_t = rope_tables(tok * n_seq)
    attn_in, qkv, w_turned, small, slot_of, grad_slots, out_weight = start_call(
        n_seq, n_dp, hidden, w_qkv, attn_gain, moe_gain, const_vec, const_mix, w_router.T,
        routes_t, cot, cos_t, sin_t, w_out,
    )
    arrived_grad = to_owners(grad_slots)

    seg_row = segments[0]
    doc_ids = jnp.arange(16, dtype=jnp.int32)
    doc_start = jnp.sum((seg_row[None, :] < doc_ids[:, None]).astype(jnp.int32), axis=1)
    start = jnp.sum(jnp.where(seg_row[None, :] == doc_ids[:, None], doc_start[:, None], 0), axis=0)
    start_row = start.astype(jnp.int32)[None, :]
    lows = start[::BLK].astype(jnp.int32) // BLK
    attended, attended_exact, logs = attn_call(lows, qkv, start_row, tok)

    heads_t, resid_mid, gates, x_slots, gate_slots = mid_call(
        n_seq, attended, hidden, prev_t, w_carry, small, slot_of, routes_t, out_weight
    )
    if n_dp * CAP > 1024:
        piece, dots, partial, d_plain = experts_plain(
            to_owners, to_sources, n_dp, x_slots, gate_slots, experts, arrived_grad
        )
        fin, far = [], []
    else:
        piece, dots, partial, fin, far = moe_call(
            n_dp, x_slots, gate_slots, experts, arrived_grad
        )
    back_out = to_sources(partial)

    (grad_resid, grad_out, base, d_prev, pack, wo_sum), far_back = mid_back_call(
        n_seq, n_dp, piece, dots, cot, resid_mid, gates, slot_of, routes_t, small, heads_t,
        out_weight, prev_t, w_carry, fin[EARLY : EARLY + 1],
    )
    later, grad_out = lax.optimization_barrier((fin[EARLY + 1 : -LATE], grad_out))
    far = far + far_back + [swap(part, "seq", 2) for part in later]
    grad_qkv = attn_back_call(
        lows, qkv, grad_out, attended_exact, logs, start_row, cos_t, sin_t
    )
    d_input, row_in, lines, block_out, both = tail_call(
        n_seq, n_dp, grad_qkv, w_turned, wo_sum, pack, gates, slot_of, small,
        attn_in, hidden, grad_resid, base, back_out, fin, far,
    )
    d_experts, d_qkv, d_out, again, mgain, router, carry, vec, mix = finish_call(
        n_seq, me.astype(jnp.int32).reshape(1), both, row_in, lines, w_qkv, attn_gain
    )
    if not fin:
        d_experts = d_plain
    return (
        block_out[None],
        d_input[None],
        jnp.transpose(d_prev, (1, 2, 0)),
        again[0],
        d_qkv,
        d_out,
        mgain[0],
        router.T,
        carry,
        vec,
        mix,
        d_experts,
    )


def solution(mesh):
    return jax.shard_map(
        per_device,
        mesh=mesh,
        in_specs=(
            P("dp", "seq", None),
            P("dp", "seq", None),
            P("dp", None),
            P("dp", "seq", None),
            P("dp"),
            P("dp", None),
            P("dp", None),
            P("dp"),
            P("dp", None),
            P(),
            P(None, "dp"),
            P(None, None, "dp"),
            P(None, "dp", None),
            P("dp", "seq", None),
        ),
        out_specs=(
            P("dp", "seq", None),
            P("dp", "seq", None),
            P("dp", "seq", None),
            P("dp"),
            P("dp", None),
            P("dp", None),
            P("dp"),
            P("dp", None),
            P(),
            P(None, "dp"),
            P(None, None, "dp"),
            P(None, "dp", None),
        ),
        check_vma=False,
    )
```

```python
import functools
import math

import jax
import jax.numpy as jnp
from jax import lax
from jax.experimental import pallas as pl
from jax.experimental.pallas import tpu as pltpu
from jax.sharding import PartitionSpec as P

D = 768
H = 12
HD = 64
E = 8
CAP = 128
BLK = 256
PAIR = 2 * CAP
UNITS = 256
PART = 64
EARLY = 1
LATE = 2
SMALL = 32
LINES = 40

exact_prec = lax.Precision.HIGHEST
neg_large = -1e30
score_scale = 0.125 * math.log2(math.e)
f32 = jnp.float32
bf16 = jnp.bfloat16

NN = (((1,), (0,)), ((), ()))
NT = (((1,), (1,)), ((), ()))
TN = (((0,), (0,)), ((), ()))


MESH = pl.DeviceIdType.MESH
VMEM = pl.BlockSpec(memory_space=pltpu.VMEM)
HBM = pl.BlockSpec(memory_space=pl.ANY)
DMA = pltpu.SemaphoreType.DMA


def mm(a, b, dims):
    return lax.dot_general(a, b, dims, preferred_element_type=f32)


def swap(value, axis, bit):
    size = lax.axis_size(axis)
    return lax.ppermute(value, axis, [(i, i ^ bit) for i in range(size)])


def bits_high_first(size):
    bit = size // 2
    while bit >= 1:
        yield bit
        bit //= 2


def greet(peers):
    barrier = pltpu.get_barrier_semaphore()
    for peer in peers:
        pl.semaphore_signal(barrier, inc=1, device_id=peer, device_id_type=MESH)
    pl.semaphore_wait(barrier, len(peers))


def remote_later(src, dst, sems, index, target):
    return pltpu.make_async_remote_copy(
        src_ref=src,
        dst_ref=dst,
        send_sem=sems[0].at[index],
        recv_sem=sems[1].at[index],
        device_id=target,
        device_id_type=MESH,
    )


def remote(src, dst, sems, index, target):
    copy = remote_later(src, dst, sems, index, target)
    copy.start()
    return copy


def one_hot(condition):
    return jnp.where(condition, 1.0, 0.0).astype(bf16)


def picks_of(slot_ref):
    slots = lax.broadcasted_iota(jnp.int32, (E * CAP, slot_ref.shape[1]), 0)
    return [one_hot(slots == slot_ref[k : k + 1, :]) for k in range(2)]


def split(rows):
    high = rows.astype(bf16)
    rest = rows - high.astype(f32)
    middle = rest.astype(bf16)
    low = (rest - middle.astype(f32)).astype(bf16)
    return jnp.concatenate([high, middle, low], axis=0)


def unsplit(rows):
    third = rows.shape[0] // 3
    return rows[:third] + rows[third : 2 * third] + rows[2 * third :]


def column_to_row(column):
    return jnp.broadcast_to(column, (column.shape[0], 128)).T[0:1]


def norm_back(values, gain, grad):
    rate = lax.rsqrt(jnp.mean(values * values, axis=-1, keepdims=True) + 1e-06)
    scaled = gain * grad
    inner = jnp.mean(values * scaled, axis=-1, keepdims=True)
    return rate * scaled - values * (rate * rate * rate) * inner


def make_slots(route_ref, cot_ref, slot_ref, g_ref):
    tok = route_ref.shape[1]
    ids = lax.broadcasted_iota(jnp.int32, (E, tok), 0)
    named = [route_ref[k : k + 1, :] == ids for k in range(2)]
    earlier = lax.broadcasted_iota(jnp.int32, (tok, tok), 0) < lax.broadcasted_iota(
        jnp.int32, (tok, tok), 1
    )
    ranks = mm(one_hot(named[0] | named[1]), one_hot(earlier), NN)
    for k in range(2):
        route = route_ref[k : k + 1, :]
        rank = jnp.sum(jnp.where(named[k], ranks, 0.0), axis=0, keepdims=True)
        slot_ref[k : k + 1, :] = jnp.where(
            route < E, route * CAP + rank.astype(jnp.int32), E * CAP
        )
    picks = picks_of(slot_ref)
    g_ref[...] = mm(picks[0] + picks[1], cot_ref[...], NN).astype(bf16).reshape(g_ref.shape)


def start_kernel(
    n_seq, n_dp, h_ref, w_ref, again_ref, mgain_ref, vec_ref, mix_ref, router_ref,
    route_ref, cot_ref, cos_ref, sin_ref, wo_ref,
    attn_hbm, qkv_ref, wt_ref, small_ref, slot_ref, g_hbm, wo_all,
    attn_ref, g_ref, out_sem, all_ref, slice_ref, small_buf, h_send, h_recv, near_send, near_recv, next_send, next_recv,
    c_send, c_recv,
):
    me, dp = lax.axis_index("seq"), lax.axis_index("dp")
    tok = h_ref.shape[0]
    width = slice_ref.shape[2] // 3
    seq_bits = list(bits_high_first(n_seq))
    greet(
        [{"seq": me ^ bit} for bit in seq_bits]
        + [{"dp": dp ^ 1}]
        + [{"dp": dp ^ (2 * j)} for j in range(1, n_dp // 2)]
    )

    plan, arrival = [], {}
    order = [(0, bit) for bit in seq_bits]
    while order:
        place, bit = order.pop(0)
        copy = remote_later(
            h_ref if place == 0 else all_ref.at[me ^ place],
            all_ref.at[me ^ place],
            (h_send, h_recv),
            len(plan),
            {"seq": me ^ bit},
        )
        arrival[place ^ bit] = copy
        plan.append((place, copy))
        order += [(place ^ bit, low) for low in seq_bits if low < bit]
    for place, copy in plan:
        if place == 0:
            copy.start()

    for j in range(n_seq):

        @pl.when(me == j)
        def _():
            for c in range(3):
                left = c * width * n_seq + j * width
                slice_ref[dp, :, c * width : (c + 1) * width] = w_ref[:, left : left + width]

    small_buf[dp] = jnp.zeros(small_buf.shape[1:], bf16)
    small_buf[dp, 0:1, :] = again_ref[...]
    small_buf[dp, 1:2, :] = mgain_ref[...]
    small_buf[dp, 2:4, :] = vec_ref[...]
    small_buf[dp, 4:6, :] = mix_ref[0]
    small_buf[dp, 6:8, :] = mix_ref[1]
    small_buf[dp, 8 : 8 + H, :] = router_ref[...]
    cols = pl.ds(pl.multiple_of((me & 1) * (D // 2), D // 2), D // 2)
    wo_all[dp, :, cols] = wo_ref[:, cols]

    def rows_of(kind, source):
        return (small_buf.at[source], slice_ref.at[source], wo_all.at[source, :, cols])[kind]

    def first_copy(kind, j):
        return remote_later(
            rows_of(kind, dp), rows_of(kind, dp), (near_send.at[kind], near_recv.at[kind]), j,
            {"dp": dp ^ (2 * j)},
        )

    def next_copy(kind, j):
        return remote_later(
            rows_of(kind, dp ^ (2 * j)), rows_of(kind, dp ^ (2 * j)),
            (next_send.at[kind], next_recv.at[kind]), j, {"dp": dp ^ 1},
        )

    places = range(1, n_dp // 2)
    for kind in range(3):
        for j in places:
            first_copy(kind, j).start()
        next_copy(kind, 0).start()
    make_slots(route_ref, cot_ref, slot_ref, g_ref)
    outs = [pltpu.make_async_copy(g_ref, g_hbm, out_sem.at[0])]
    outs[0].start()

    def pass_on(kind):
        for j in places:
            first_copy(kind, j).wait_recv()
            next_copy(kind, j).start()

    def complete(kind):
        for j in range(n_dp // 2):
            next_copy(kind, j).wait_recv()

    pass_on(0)
    complete(0)
    small_ref[...] = jnp.concatenate([small_buf[i].astype(f32) for i in range(n_dp)], axis=1)

    def normalize(block, ref):
        x = ref.astype(f32)
        mean_square = jnp.mean(x * x, axis=-1, keepdims=True)
        rows = pl.ds(pl.multiple_of(block * tok, tok), tok)
        attn_ref[rows, :] = (x * lax.rsqrt(mean_square + 1e-06) * small_ref[0:1]).astype(bf16)
        outs.append(
            pltpu.make_async_copy(
                attn_ref.at[rows, :], attn_hbm.at[rows, :], out_sem.at[len(outs)]
            )
        )
        outs[-1].start()

    normalize(me, h_ref[...])
    pass_on(1)
    for place in arrival:
        arrival[place].wait_recv()
        for source, copy in plan:
            if source == place:
                copy.start()
        normalize(me ^ place, all_ref[me ^ place])
    complete(1)
    pass_on(2)
    wt_ref[...] = slice_ref[...].reshape(D, 3 * width).T
    half = HD // 2

    @pl.loop(0, attn_ref.shape[0] // BLK)
    def _(i):
        rows = pl.ds(pl.multiple_of(i * BLK, BLK), BLK)
        y = mm(wt_ref[...], attn_ref[rows, :], NT)
        cos, sin = cos_ref[:, rows], sin_ref[:, rows]
        for head in range(2 * width // HD):
            low, middle, high = head * HD, head * HD + half, (head + 1) * HD
            a, b = y[low:middle], y[middle:high]
            qkv_ref[low:middle, rows] = (a * cos - b * sin).astype(bf16)
            qkv_ref[middle:high, rows] = (a * sin + b * cos).astype(bf16)
        qkv_ref[2 * width :, rows] = y[2 * width :].astype(bf16)

    complete(2)
    trade = remote(
        wo_all.at[:, :, cols], wo_all.at[:, :, cols], (c_send, c_recv), 0, {"seq": me ^ 1}
    )
    for _, copy in plan:
        copy.wait_send()
    for kind in range(3):
        for j in places:
            first_copy(kind, j).wait_send()
        for j in range(n_dp // 2):
            next_copy(kind, j).wait_send()
    for copy in outs:
        copy.wait()
    trade.wait()


def start_call(
    n_seq, n_dp, hidden, w_qkv, attn_gain, moe_gain, vec, mix, router, routes, cotangent, cos, sin,
    w_out,
):
    tok, shard = hidden.shape[0], w_qkv.shape[0]
    width3 = w_qkv.shape[1] // n_seq
    hops = n_seq - 1
    return pl.pallas_call(
        functools.partial(start_kernel, n_seq, n_dp),
        out_shape=(
            jax.ShapeDtypeStruct((n_seq * tok, D), bf16),
            jax.ShapeDtypeStruct((width3, n_seq * tok), bf16),
            jax.ShapeDtypeStruct((width3, D), bf16),
            jax.ShapeDtypeStruct((SMALL, D), f32),
            jax.ShapeDtypeStruct(routes.shape, jnp.int32),
            jax.ShapeDtypeStruct((E, CAP, D), bf16),
            jax.ShapeDtypeStruct((n_dp, shard, D), bf16),
        ),
        in_specs=[VMEM] * 12,
        out_specs=[HBM] + [VMEM] * 4 + [HBM, VMEM],
        scratch_shapes=[
            pltpu.VMEM((n_seq * tok, D), bf16),
            pltpu.VMEM((E, CAP, D), bf16),
            DMA((1 + n_seq,)),
            pltpu.VMEM((n_seq, tok, D), bf16),
            pltpu.VMEM((n_dp, shard, width3), bf16),
            pltpu.VMEM((n_dp, SMALL, shard), bf16),
            DMA((hops,)),
            DMA((hops,)),
            DMA((3, n_dp // 2)),
            DMA((3, n_dp // 2)),
            DMA((3, n_dp // 2)),
            DMA((3, n_dp // 2)),
            DMA((1,)),
            DMA((1,)),
        ],
        compiler_params=pltpu.CompilerParams(collective_id=0, has_side_effects=True),
        name="start",
    )(
        hidden, w_qkv, attn_gain[None], moe_gain[None], vec, mix, router, routes, cotangent,
        cos, sin, w_out,
    )


def allowed_block(key_block, query_block, start_row):
    key_pos = key_block * BLK + lax.broadcasted_iota(jnp.int32, (BLK, BLK), 0)
    query_pos = query_block * BLK + lax.broadcasted_iota(jnp.int32, (BLK, BLK), 1)
    return (key_pos >= start_row) & (key_pos <= query_pos)


def attn_kernel(lo_ref, qkv_ref, start_ref, out_ref, exact_ref, log_ref, keys_ref):
    heads, seq_len, _ = keys_ref.shape
    width = heads * HD
    qb = pl.program_id(0)

    @pl.when(qb == 0)
    def _():
        for h in range(heads):
            keys_ref[h] = qkv_ref[width + h * HD : width + (h + 1) * HD, :].T

    here = pl.ds(pl.multiple_of(qb * BLK, BLK), BLK)
    start_row = start_ref[...]

    def step(kb, carry):
        there = pl.ds(pl.multiple_of(kb * BLK, BLK), BLK)
        allowed = allowed_block(kb, qb, start_row)
        scores = [
            mm(keys_ref[h, there, :], qkv_ref[h * HD : (h + 1) * HD, here], NN)
            for h in range(heads)
        ]
        stats, weights = [], []
        for h in range(heads):
            top, total, acc = carry[h]
            masked = jnp.where(allowed, scores[h] * score_scale, neg_large)
            new_top = jnp.maximum(top, jnp.max(masked, axis=0, keepdims=True))
            fade = jnp.exp2(top - new_top)
            weight = jnp.exp2(masked - new_top)
            total = total * fade + jnp.sum(weight, axis=0, keepdims=True)
            stats.append((new_top, total, acc * fade))
            weights.append(weight.astype(bf16))
        new = []
        for h in range(heads):
            values = qkv_ref[2 * width + h * HD : 2 * width + (h + 1) * HD, there]
            top, total, acc = stats[h]
            new.append((top, total, acc + mm(values, weights[h], NN)))
        return tuple(new)

    first = tuple(
        (
            jnp.full((1, BLK), neg_large, f32),
            jnp.zeros((1, BLK), f32),
            jnp.zeros((HD, BLK), f32),
        )
        for _ in range(heads)
    )
    done = lax.fori_loop(lo_ref[qb], qb + 1, step, first)
    for h in range(heads):
        top, total, acc = done[h]
        attended = acc / total
        exact_ref[h * HD : (h + 1) * HD, :] = attended
        out_ref[0, h * HD : (h + 1) * HD, :] = attended.astype(bf16)
        log_ref[h : h + 1, :] = top + jnp.log2(total)


def attn_call(lows, qkv, start_row, tok):
    width3, seq_len = qkv.shape
    width = width3 // 3
    heads = width // HD
    per = tok // BLK
    return pl.pallas_call(
        attn_kernel,
        out_shape=(
            jax.ShapeDtypeStruct((seq_len // tok, width, tok), bf16),
            jax.ShapeDtypeStruct((width, seq_len), f32),
            jax.ShapeDtypeStruct((heads, seq_len), f32),
        ),
        grid_spec=pltpu.PrefetchScalarGridSpec(
            num_scalar_prefetch=1,
            grid=(seq_len // BLK,),
            in_specs=[
                pl.BlockSpec((width3, seq_len), lambda i, lo: (0, 0)),
                pl.BlockSpec((1, BLK), lambda i, lo: (0, i)),
            ],
            out_specs=[
                pl.BlockSpec((1, width, BLK), lambda i, lo: (i // per, 0, i % per)),
                pl.BlockSpec((width, BLK), lambda i, lo: (0, i)),
                pl.BlockSpec((heads, BLK), lambda i, lo: (0, i)),
            ],
            scratch_shapes=[pltpu.VMEM((heads, seq_len, HD), bf16)],
        ),
        cost_estimate=pl.CostEstimate(
            flops=16_000_000_000, transcendentals=0, bytes_accessed=16_000_000
        ),
        name="attend",
    )(lows, qkv, start_row)


def attn_back_kernel(
    lo_ref, qkv_ref, go_ref, exact_ref, log_ref, start_ref, cos_ref, sin_ref, out_ref,
    keys_ref, values_ref, dk_ref, dv_ref,
):
    heads, seq_len, _ = keys_ref.shape
    width = heads * HD
    half = HD // 2
    qb = pl.program_id(0)

    @pl.when(qb == 0)
    def _():
        for h in range(heads):
            keys_ref[h] = qkv_ref[width + h * HD : width + (h + 1) * HD, :].T
            values_ref[h] = qkv_ref[2 * width + h * HD : 2 * width + (h + 1) * HD, :].T
        dk_ref[...] = jnp.zeros_like(dk_ref)
        dv_ref[...] = jnp.zeros_like(dv_ref)

    here = pl.ds(pl.multiple_of(qb * BLK, BLK), BLK)
    start_row = start_ref[...]
    grad = go_ref[0]
    deltas = [
        jnp.sum(
            exact_ref[h * HD : (h + 1) * HD, :] * grad[h * HD : (h + 1) * HD].astype(f32),
            axis=0,
            keepdims=True,
        )
        for h in range(heads)
    ]

    def step(kb, carry):
        there = pl.ds(pl.multiple_of(kb * BLK, BLK), BLK)
        allowed = allowed_block(kb, qb, start_row)
        spans = [slice(h * HD, (h + 1) * HD) for h in range(heads)]
        queries = [qkv_ref[rows, here] for rows in spans]
        scores = [mm(keys_ref[h, there, :], queries[h], NN) for h in range(heads)]
        grad_probs = [mm(values_ref[h, there, :], grad[spans[h]], NN) for h in range(heads)]
        probs, grad_scores = [], []
        for h in range(heads):
            masked = jnp.where(allowed, scores[h] * score_scale, neg_large)
            prob = jnp.exp2(masked - log_ref[h : h + 1, :])
            probs.append(prob.astype(bf16))
            grad_scores.append((prob * (grad_probs[h] - deltas[h])).astype(bf16))
        new = []
        for h in range(heads):
            dv_ref[spans[h], there] += mm(grad[spans[h]], probs[h], NT)
        for h in range(heads):
            dk_ref[spans[h], there] += mm(queries[h], grad_scores[h], NT)
        for h in range(heads):
            keys = qkv_ref[width + h * HD : width + (h + 1) * HD, there]
            new.append(carry[h] + mm(keys, grad_scores[h], NN))
        return tuple(new)

    grads = lax.fori_loop(
        lo_ref[qb], qb + 1, step, tuple(jnp.zeros((HD, BLK), f32) for _ in range(heads))
    )

    def turn_back(value, cos, sin):
        value = value.astype(bf16).astype(f32)
        a, b = value[:half], value[half:]
        return (a * cos + b * sin).astype(bf16), (b * cos - a * sin).astype(bf16)

    for h in range(heads):
        a, b = turn_back(grads[h] * 0.125, cos_ref[:, here], sin_ref[:, here])
        out_ref[h * HD : h * HD + half, here] = a
        out_ref[h * HD + half : (h + 1) * HD, here] = b

    @pl.when(qb == pl.num_programs(0) - 1)
    def _():
        cos, sin = cos_ref[...], sin_ref[...]
        for h in range(heads):
            a, b = turn_back(dk_ref[h * HD : (h + 1) * HD, :] * 0.125, cos, sin)
            out_ref[width + h * HD : width + h * HD + half, :] = a
            out_ref[width + h * HD + half : width + (h + 1) * HD, :] = b
        out_ref[2 * width :, :] = dv_ref[...].astype(bf16)


def attn_back_call(lows, qkv, grad_out, exact, logs, start_row, cos_t, sin_t):
    width3, seq_len = qkv.shape
    width = width3 // 3
    heads = width // HD
    per = grad_out.shape[2] // BLK
    return pl.pallas_call(
        attn_back_kernel,
        out_shape=jax.ShapeDtypeStruct((width3, seq_len), bf16),
        grid_spec=pltpu.PrefetchScalarGridSpec(
            num_scalar_prefetch=1,
            grid=(seq_len // BLK,),
            in_specs=[
                pl.BlockSpec((width3, seq_len), lambda i, lo: (0, 0)),
                pl.BlockSpec((1, width, BLK), lambda i, lo: (i // per, 0, i % per)),
                pl.BlockSpec((width, BLK), lambda i, lo: (0, i)),
                pl.BlockSpec((heads, BLK), lambda i, lo: (0, i)),
                pl.BlockSpec((1, BLK), lambda i, lo: (0, i)),
                pl.BlockSpec((HD // 2, seq_len), lambda i, lo: (0, 0)),
                pl.BlockSpec((HD // 2, seq_len), lambda i, lo: (0, 0)),
            ],
            out_specs=pl.BlockSpec((width3, seq_len), lambda i, lo: (0, 0)),
            scratch_shapes=[
                pltpu.VMEM((heads, seq_len, HD), bf16),
                pltpu.VMEM((heads, seq_len, HD), bf16),
                pltpu.VMEM((width, seq_len), f32),
                pltpu.VMEM((width, seq_len), f32),
            ],
        ),
        cost_estimate=pl.CostEstimate(
            flops=16_000_000_000, transcendentals=0, bytes_accessed=16_000_000
        ),
        name="attend_back",
    )(lows, qkv, grad_out, exact, logs, start_row, cos_t, sin_t)


def gates_back(grad_hidden, gate_pre, up_pre):
    sig = 1.0 / (1.0 + jnp.exp(-gate_pre))
    silu = gate_pre * sig
    grad_gate = grad_hidden * up_pre * sig * (1.0 + gate_pre * (1.0 - sig))
    return (
        (silu * up_pre).astype(bf16),
        grad_gate.astype(bf16),
        (grad_hidden * silu).astype(bf16),
    )


def moe_kernel(n_dp, parts, x_ref, gate_ref, w_hbm, g_ref, *refs):
    piece_ref, dots_ref, out_ref, refs = refs[0], refs[1], refs[2], refs[3:]
    fin_hbm, refs = refs[:parts], refs[parts:]
    cross_hbm, refs = refs[:EARLY], refs[EARLY:]
    (
        w_ref, x_in, x_far, g_far, gate_in, gate_far, gs_ref, gs_far, pair_ref, near_ref, far_ref,
        own_ref, piece_out, dot_out, dw_out, dw_in, fin_ref,
        w_sem, x_send, x_recv, t_send, t_recv, p_send, p_recv, d_send, d_recv,
        xf_send, xf_recv, gf_send, gf_recv, tf_send, tf_recv, c_send, c_recv, e_send, e_recv, keep_sem,
    ) = refs
    me, dp = lax.axis_index("seq"), lax.axis_index("dp")
    owners = n_dp // E
    pairs = n_dp // 2
    half = near_ref.shape[2]
    core, plane = me & 1, lax.div(me, 2)
    greet([{"dp": dp ^ k} for k in range(1, n_dp)] + [{"seq": me ^ 1}, {"seq": me ^ 2}])

    def x_copy(k):
        return remote_later(
            x_ref.at[(dp ^ k) // owners], x_in.at[k], (x_send, x_recv), k, {"dp": dp ^ k}
        )

    def gate_copy(k):
        return remote_later(
            gate_ref.at[(dp ^ k) // owners], gate_in.at[k], (t_send, t_recv), k, {"dp": dp ^ k}
        )

    def piece_copy(k):
        return remote_later(
            piece_out.at[k], piece_ref.at[dp], (p_send, p_recv), k, {"dp": dp ^ k}
        )

    def dot_copy(k):
        return remote_later(dot_out.at[k], dots_ref.at[dp], (d_send, d_recv), k, {"dp": dp ^ k})

    def far_copies(k):
        across = {"seq": me ^ 2}
        return [
            remote_later(gate_in.at[k], gate_far.at[k], (tf_send, tf_recv), k, across),
            remote_later(g_ref.at[dp ^ k], g_far.at[k], (gf_send, gf_recv), k, across),
            remote_later(x_in.at[k], x_far.at[k], (xf_send, xf_recv), k, across),
        ]

    def core_copy(t):
        return remote_later(dw_out.at[t], dw_in.at[t], (c_send, c_recv), t, {"seq": me ^ 1})

    for p in range(pairs):
        for k in (2 * p, 2 * p + 1):
            if k:
                gate_copy(k).start()
                x_copy(k).start()
    loads = [pltpu.make_async_copy(w_hbm.at[j], w_ref.at[j], w_sem.at[j]) for j in range(3)]
    loads.append(pltpu.make_async_copy(x_ref.at[dp // owners], x_in.at[0], w_sem.at[3]))
    for load in loads:
        load.start()
    gate_in[0] = gate_ref[dp // owners]
    for load in loads:
        load.wait()

    def place(i):
        return i + 0

    def scale(ref, rows, gate, k):
        column = jnp.broadcast_to(gate, (CAP, CAP)).T[:, 0:1]
        here = pl.ds(pl.multiple_of(k * CAP, CAP), CAP)
        ref[here] = (rows.astype(f32) * column).astype(bf16)

    @pl.loop(0, pairs)
    def _(i):
        p = place(i)
        rows = pl.ds(pl.multiple_of(p * PAIR, PAIR), PAIR)

        def arrive(k):
            x_copy(k).wait_recv()
            gate_copy(k).wait_recv()

        @pl.when(p > 0)
        def _():
            arrive(2 * p)

        arrive(2 * p + 1)
        for side in range(2):
            k = 2 * p + side
            for copy in far_copies(k):
                copy.start()
            scale(gs_ref, g_ref[dp ^ k], gate_in[k], k)

        @pl.loop(0, 2)
        def _(t):
            part = pl.ds(pl.multiple_of(t * half, half), half)
            x = x_in[pl.ds(2 * p, 2)].reshape(PAIR, D)
            gate_pre = mm(x, w_ref[0, part], NT)
            up_pre = mm(x, w_ref[1, part], NT)
            grad_hidden = mm(gs_ref[rows], w_ref[2, part], NT)
            results = gates_back(grad_hidden, gate_pre, up_pre)
            for j in range(3):
                pair_ref[j, :, part] = results[j]

            @pl.when(t == plane)
            def _():
                for j in range(3):
                    near_ref[j, rows] = results[j]

        pieces = mm(pair_ref[1], w_ref[0], NN) + mm(pair_ref[2], w_ref[1], NN)
        piece_out[pl.ds(2 * p, 2)] = pieces.astype(bf16).reshape(2, CAP, D)
        piece_copy(2 * p + 1).start()

        @pl.when(p > 0)
        def _():
            piece_copy(2 * p).start()

        outs = mm(pair_ref[0], w_ref[2], NN)
        for side in range(2):
            k = 2 * p + side
            out = outs[side * CAP : (side + 1) * CAP].astype(bf16)
            out_ref[dp ^ k] = out
            product = out.astype(f32) * g_ref[dp ^ k].astype(f32)
            dot_out[k] = column_to_row(jnp.sum(product, axis=1, keepdims=True))
        dot_copy(2 * p + 1).start()

        @pl.when(p > 0)
        def _():
            dot_copy(2 * p).start()

    piece_ref[dp] = piece_out[0]
    dots_ref[dp] = dot_out[0]

    def weight_grad(source, x, gs, j, part):
        left = source[(1, 2, 0)[j], :, part]
        return mm(left, gs[...] if j == 2 else x[...].reshape(n_dp * CAP, D), TN)

    @pl.loop(0, half // UNITS)
    def _(t):
        part = pl.ds(pl.multiple_of(t * UNITS, UNITS), UNITS)
        for j in range(3):
            own_ref[j, part] = weight_grad(near_ref, x_in, gs_ref, j, part)

    def far_grad(rows, j, part):
        left = far_ref[(1, 2, 0)[j], :, part]
        if j == 2:
            right = gs_far[rows]
        elif isinstance(rows, slice):
            right = x_far[rows.start // CAP : rows.stop // CAP].reshape(PAIR, D)
        else:
            right = x_far[pl.ds(lax.div(rows.start, CAP), 2)].reshape(PAIR, D)
        return mm(left, right, TN)

    @pl.loop(0, pairs)
    def _(i):
        p = place(i)
        rows = pl.ds(pl.multiple_of(p * PAIR, PAIR), PAIR)
        for side in range(2):
            k = 2 * p + side
            for copy in far_copies(k):
                copy.wait_recv()
            scale(gs_far, g_far[k], gate_far[k], k)
        part = pl.ds(pl.multiple_of(plane * half, half), half)
        x = x_far[pl.ds(2 * p, 2)].reshape(PAIR, D)
        results = gates_back(
            mm(gs_far[rows], w_ref[2, part], NT),
            mm(x, w_ref[0, part], NT),
            mm(x, w_ref[1, part], NT),
        )
        for j in range(3):
            far_ref[j] = results[j]

        @pl.when(i < pairs - 1)
        def _():
            @pl.loop(0, half // UNITS)
            def _(t):
                part = pl.ds(pl.multiple_of(t * UNITS, UNITS), UNITS)
                for j in range(3):
                    own_ref[j, part] += far_grad(rows, j, part)

    tiles = half // UNITS // 2
    final = slice((pairs - 1) * PAIR, pairs * PAIR)

    def both_rows(side, t, j):
        part = pl.ds(pl.multiple_of((side * tiles + t) * UNITS, UNITS), UNITS)
        return own_ref[j, part] + far_grad(final, j, part)

    @pl.loop(0, tiles)
    def _(t):
        for j in range(3):
            dw_out[t, j] = both_rows(1 - core, t, j).astype(bf16)
        core_copy(t).start()

    def early_copy(t):
        return remote_later(fin_ref.at[t], cross_hbm[t], (e_send, e_recv), t, {"seq": me ^ 2})

    @pl.loop(0, tiles)
    def _(t):
        core_copy(t).wait_recv()
        for j in range(3):
            total = (both_rows(core, t, j) + dw_in[t, j].astype(f32)).astype(bf16)
            for u in range(UNITS // PART):
                fin_ref[t * (UNITS // PART) + u, j] = total[u * PART : (u + 1) * PART]

        @pl.when(t == 0)
        def _():
            for e in range(EARLY):
                early_copy(e).start()

    keeps = [
        pltpu.make_async_copy(fin_ref.at[t], fin_hbm[t], keep_sem.at[t]) for t in range(parts)
    ]
    for keep in keeps:
        keep.start()
    for k in range(1, n_dp):
        piece_copy(k).wait()
        dot_copy(k).wait()
        x_copy(k).wait_send()
        gate_copy(k).wait_send()
    for k in range(n_dp):
        for copy in far_copies(k):
            copy.wait_send()
    for t in range(tiles):
        core_copy(t).wait_send()
    for t in range(EARLY):
        early_copy(t).wait()
    for keep in keeps:
        keep.wait()


def moe_call(n_dp, x_slots, gate_slots, weights, grads):
    units = weights.shape[1]
    half = units // 2
    rows = n_dp * CAP
    parts = units // 4 // PART
    tiles = half // UNITS // 2
    outs = pl.pallas_call(
        functools.partial(moe_kernel, n_dp, parts),
        out_shape=(
            jax.ShapeDtypeStruct((n_dp, CAP, D), bf16),
            jax.ShapeDtypeStruct((n_dp, 1, CAP), f32),
            jax.ShapeDtypeStruct((n_dp, CAP, D), bf16),
        )
        + (jax.ShapeDtypeStruct((3, PART, D), bf16),) * (parts + EARLY),
        in_specs=[HBM, VMEM, HBM, VMEM],
        out_specs=[VMEM] * 3 + [HBM] * (parts + EARLY),
        scratch_shapes=[
            pltpu.VMEM(weights.shape, bf16),
            pltpu.VMEM((n_dp, CAP, D), bf16),
            pltpu.VMEM((n_dp, CAP, D), bf16),
            pltpu.VMEM((n_dp, CAP, D), bf16),
            pltpu.VMEM((n_dp, 1, CAP), f32),
            pltpu.VMEM((n_dp, 1, CAP), f32),
            pltpu.VMEM((rows, D), bf16),
            pltpu.VMEM((rows, D), bf16),
            pltpu.VMEM((3, PAIR, units), bf16),
            pltpu.VMEM((3, rows, half), bf16),
            pltpu.VMEM((3, PAIR, half), bf16),
            pltpu.VMEM((3, half, D), f32),
            pltpu.VMEM((n_dp, CAP, D), bf16),
            pltpu.VMEM((n_dp, 1, CAP), f32),
            pltpu.VMEM((tiles, 3, UNITS, D), bf16),
            pltpu.VMEM((tiles, 3, UNITS, D), bf16),
            pltpu.VMEM((parts, 3, PART, D), bf16),
            DMA((4,)),
        ]
        + [DMA((n_dp,))] * 14
        + [DMA((tiles,))] * 2
        + [DMA((EARLY,))] * 2
        + [DMA((parts,))],
        compiler_params=pltpu.CompilerParams(
            collective_id=4, has_side_effects=True, vmem_limit_bytes=67043328
        ),
        name="experts",
    )(x_slots, gate_slots, weights, grads)
    return outs[0], outs[1], outs[2], list(outs[3 : 3 + parts]), list(outs[3 + parts :])


def experts_plain(to_owners, to_sources, n_dp, x_slots, gate_slots, weights, grads):
    rows = n_dp * CAP
    x = to_owners(x_slots).reshape(rows, D)
    gate = to_owners(gate_slots).reshape(rows, 1)
    g = grads.reshape(rows, D)
    gs = (g.astype(f32) * gate).astype(bf16)
    hidden, grad_gate, grad_up = gates_back(
        mm(gs, weights[2], NT), mm(x, weights[0], NT), mm(x, weights[1], NT)
    )
    out = mm(hidden, weights[2], NN).astype(bf16)
    piece = (mm(grad_gate, weights[0], NN) + mm(grad_up, weights[1], NN)).astype(bf16)
    dw = jnp.stack([mm(grad_gate, x, TN), mm(grad_up, x, TN), mm(hidden, gs, TN)])
    dots = jnp.sum(out.astype(f32) * g.astype(f32), axis=-1)
    return (
        to_sources(piece.reshape(n_dp, CAP, D)),
        to_sources(dots.reshape(n_dp, 1, CAP)),
        out.reshape(n_dp, CAP, D),
        lax.psum(dw, "seq"),
    )


def mid_kernel(
    n_seq, att_ref, h_ref, prev_ref, carry_ref, small_ref, slot_ref, route_ref, w_ref,
    heads_ref, mid_ref, gate_ref, x_ref, gs_ref, send_sem, recv_sem,
):
    me = lax.axis_index("seq")
    tok = h_ref.shape[0]
    greet([{"seq": me ^ place} for place in range(1, n_seq)])
    copies = [
        remote(
            att_ref.at[me ^ place], heads_ref.at[me], (send_sem, recv_sem), place,
            {"seq": me ^ place},
        )
        for place in range(1, n_seq)
    ]
    heads_ref[me] = att_ref[me]
    picks = picks_of(slot_ref)
    pick_any = picks[0] + picks[1]
    carried = lax.dot_general(
        carry_ref[...].astype(f32), prev_ref[:, 0, :], TN, precision=exact_prec,
        preferred_element_type=f32,
    )
    for copy in copies:
        copy.wait_recv()
    attn_out = mm(heads_ref[...].reshape(D, tok), w_ref[...].reshape(D, D), TN)
    resid = h_ref[...].astype(f32) + attn_out
    mid_ref[...] = resid
    rate = lax.rsqrt(jnp.mean(resid * resid, axis=-1, keepdims=True) + 1e-06)
    normed = resid * rate * small_ref[1:2]
    low = normed.astype(bf16)
    x_ref[...] = mm(pick_any, low, NN).astype(bf16).reshape(x_ref.shape)
    heads_rows = small_ref[4 : 8 + H].astype(bf16)
    products = mm(heads_rows, low, NT)
    rest = mm(heads_rows, (normed - low.astype(f32)).astype(bf16), NT)
    logits = products[4:] + carried
    ids = lax.broadcasted_iota(jnp.int32, (H, tok), 0)
    chosen = [
        jnp.sum(jnp.where(route_ref[k : k + 1, :] == ids, logits, 0.0), axis=0, keepdims=True)
        for k in range(2)
    ]
    top = jnp.maximum(chosen[0], chosen[1])
    exps = [jnp.exp(c - top) for c in chosen]
    total = exps[0] + exps[1]
    gates = [e / total for e in exps]
    gate_ref[...] = jnp.concatenate(
        [gates[0], gates[1], products[:4] + rest[:4], jnp.zeros((2, tok), f32)], axis=0
    )
    slot_gates = sum(unsplit(mm(split(gates[k]), picks[k], NT)) for k in range(2))
    for e in range(E):
        gs_ref[e] = slot_gates[:, e * CAP : (e + 1) * CAP]
    for copy in copies:
        copy.wait_send()


def mid_call(n_seq, attended, hidden, prev, carry, small, slot_of, routes, w_out):
    tok, width = hidden.shape[0], attended.shape[1]
    return pl.pallas_call(
        functools.partial(mid_kernel, n_seq),
        out_shape=(
            jax.ShapeDtypeStruct((n_seq, width, tok), bf16),
            jax.ShapeDtypeStruct((tok, D), f32),
            jax.ShapeDtypeStruct((8, tok), f32),
            jax.ShapeDtypeStruct((E, CAP, D), bf16),
            jax.ShapeDtypeStruct((E, 1, CAP), f32),
        ),
        in_specs=[VMEM] * 8,
        out_specs=[VMEM] * 5,
        scratch_shapes=[DMA((n_seq,)), DMA((n_seq,))],
        compiler_params=pltpu.CompilerParams(collective_id=2, has_side_effects=True),
        name="mid",
    )(attended, hidden, prev, carry, small, slot_of, routes, w_out)


def mid_back_kernel(
    n_seq, n_dp, n_tile, piece_ref, dots_ref, cot_ref, mid_ref, gate_ref, slot_ref, route_ref,
    small_ref, heads_ref, w_ref, prev_ref, carry_ref, *refs,
):
    tile_refs, refs = refs[:n_tile], refs[n_tile:]
    resid_ref, go_ref, base_ref, dprev_ref, pack_ref, wo_sum_ref, *refs = refs
    far_refs, refs = refs[:n_tile], refs[n_tile:]
    gh_ref, wo_ref, wo_in, a_send, a_recv, c_send, c_recv, t_send, t_recv = refs
    me = lax.axis_index("seq")
    tok = cot_ref.shape[0]
    width = heads_ref.shape[1]
    owners = n_dp // E
    pairs = n_seq // 2
    greet([{"seq": me ^ place} for place in range(1, n_seq)])
    tile_copies = [
        remote(tile_refs[t], far_refs[t], (t_send, t_recv), t, {"seq": me ^ 2})
        for t in range(n_tile)
    ]
    cot = cot_ref[...]
    grad_top = cot.astype(f32)
    resid_mid = mid_ref[...]
    gain = small_ref[1:2]
    rate = lax.rsqrt(jnp.mean(resid_mid * resid_mid, axis=-1, keepdims=True) + 1e-06)
    normed = resid_mid * rate * gain
    low = normed.astype(bf16)
    picks = picks_of(slot_ref)
    gates = [gate_ref[k : k + 1, :] for k in range(2)]
    routes = [route_ref[k : k + 1, :] for k in range(2)]
    normed_dot = column_to_row(jnp.sum(grad_top * normed, axis=1, keepdims=True))
    vecs = small_ref[2:4].astype(bf16)
    vec_dot = mm(vecs, cot, NT)
    alphas, const_dot = [], []
    for j in range(2):
        pair = [gate_ref[2 + 2 * j + c : 3 + 2 * j + c, :] for c in range(2)]
        top = jnp.maximum(pair[0], pair[1])
        exps = [jnp.exp(p - top) for p in pair]
        total = exps[0] + exps[1]
        alphas.append([e / total for e in exps])
        const_dot.append(alphas[j][0] * normed_dot + alphas[j][1] * vec_dot[j : j + 1])
    slot_dots = split(
        jnp.concatenate(
            [sum(dots_ref[e * owners + o] for o in range(owners)) for e in range(E)], axis=1
        )
    )
    out_dots = []
    for k in range(2):
        value = unsplit(mm(slot_dots, picks[k], NN))
        value = value + jnp.where(routes[k] == E + 1, normed_dot, 0.0)
        for j in range(2):
            value = value + jnp.where(routes[k] == E + 2 + j, const_dot[j], 0.0)
        out_dots.append(value)
    mean_dot = gates[0] * out_dots[0] + gates[1] * out_dots[1]
    ids = lax.broadcasted_iota(jnp.int32, (H, tok), 0)
    grad_logits = sum(
        jnp.where(routes[k] == ids, gates[k] * (out_dots[k] - mean_dot), 0.0) for k in range(2)
    )

    def gate_of(expert):
        return sum(jnp.where(routes[k] == expert, gates[k], 0.0) for k in range(2))

    const_gate = [gate_of(E + 2 + j) for j in range(2)]
    normed_gate = gate_of(E + 1) + sum(const_gate[j] * alphas[j][0] for j in range(2))
    vec_gate = split(jnp.concatenate([const_gate[j] * alphas[j][1] for j in range(2)], axis=0))
    mix_grads = []
    for j in range(2):
        terms = [normed_dot, vec_dot[j : j + 1]]
        for c in range(2):
            mix_grads.append(const_gate[j] * alphas[j][c] * (terms[c] - const_dot[j]))
    token_rows = split(jnp.concatenate(mix_grads + [grad_logits], axis=0))
    normed_column = jnp.broadcast_to(normed_gate, (8, tok)).T[:, 0:1]
    heads_rows = small_ref[4 : 8 + H].astype(bf16)
    pick_any = picks[0] + picks[1]
    grad_normed = grad_top * normed_column
    grad_normed = grad_normed + mm(
        token_rows, jnp.concatenate([heads_rows] * 3, axis=0), TN
    )
    pieces = piece_ref[...].reshape(E, owners, CAP, D)
    for o in range(owners):
        grad_normed = grad_normed + mm(pick_any, pieces[:, o].reshape(E * CAP, D), TN)
    grad_resid = grad_top + norm_back(resid_mid, gain, grad_normed)
    resid_ref[...] = grad_resid
    grad_attn = grad_resid.astype(bf16)
    gh_ref[...] = mm(w_ref[...].reshape(D, D), grad_attn, NT).astype(bf16).reshape(gh_ref.shape)
    copies = [
        remote(gh_ref.at[me ^ place], go_ref.at[me], (a_send, a_recv), place, {"seq": me ^ place})
        for place in range(1, n_seq)
    ]
    go_ref[me] = gh_ref[me]
    grad_w = mm(heads_ref[...].reshape(D, tok), grad_attn, NN)
    for j in range(n_seq):
        wo_ref[j] = grad_w[:, j * width : (j + 1) * width].astype(bf16)
    core_copies = [
        remote(wo_ref.at[me ^ (2 * i + 1)], wo_in.at[i], (c_send, c_recv), i, {"seq": me ^ 1})
        for i in range(pairs)
    ]
    base_ref[...] = (
        resid_mid
        + normed * normed_column
        + mm(vec_gate, jnp.concatenate([vecs] * 3, axis=0), TN)
    )
    dprev_ref[:, 0, :] = lax.dot_general(
        carry_ref[...].astype(f32), grad_logits, NN, precision=exact_prec,
        preferred_element_type=f32,
    )
    rest = (normed - low.astype(f32)).astype(bf16)
    row_sums = unsplit(mm(token_rows, low, NN))
    mix_sums = row_sums[:4] + unsplit(mm(token_rows, rest, NN))[:4]
    vec_sums = unsplit(mm(vec_gate, cot, NN))
    gain_sum = jnp.sum(grad_normed * resid_mid * rate, axis=0, keepdims=True)
    carry_grad = lax.dot_general(
        prev_ref[:, 0, :], grad_logits, NT, precision=exact_prec, preferred_element_type=f32
    )
    packed = jnp.concatenate([mix_sums, row_sums[4:], vec_sums, gain_sum], axis=0)
    lines, shard = packed.shape[0], D // n_dp
    for i in range(n_dp):
        pack_ref[i] = jnp.zeros(pack_ref.shape[1:], f32)
        pack_ref[i, 0:lines, :] = packed[:, i * shard : (i + 1) * shard]
        pack_ref[i, 24 : 24 + H, 0:H] = carry_grad
    for i in range(pairs):
        core_copies[i].wait_recv()
        wo_sum_ref[i] = (
            wo_ref[me ^ (2 * i)].astype(f32) + wo_in[i].astype(f32)
        ).astype(bf16)
    for copy in copies + tile_copies:
        copy.wait()
    for copy in core_copies:
        copy.wait_send()


def mid_back_call(
    n_seq, n_dp, piece, dots, cot, mid, gates, slot_of, routes, small, heads, w, prev, carry,
    parts,
):
    tok, width = cot.shape[0], heads.shape[1]
    pairs = n_seq // 2
    n_tile = len(parts)
    outs = pl.pallas_call(
        functools.partial(mid_back_kernel, n_seq, n_dp, n_tile),
        out_shape=(
            jax.ShapeDtypeStruct((tok, D), f32),
            jax.ShapeDtypeStruct((n_seq, width, tok), bf16),
            jax.ShapeDtypeStruct((tok, D), f32),
            jax.ShapeDtypeStruct((H, 1, tok), f32),
            jax.ShapeDtypeStruct((n_dp, LINES, D // n_dp), f32),
            jax.ShapeDtypeStruct((pairs, D, width), bf16),
        )
        + tuple(jax.ShapeDtypeStruct(part.shape, bf16) for part in parts),
        in_specs=[VMEM] * 12 + [HBM] * n_tile,
        out_specs=[VMEM] * 6 + [HBM] * n_tile,
        scratch_shapes=[
            pltpu.VMEM((n_seq, width, tok), bf16),
            pltpu.VMEM((n_seq, D, width), bf16),
            pltpu.VMEM((pairs, D, width), bf16),
            DMA((n_seq,)),
            DMA((n_seq,)),
            DMA((pairs,)),
            DMA((pairs,)),
            DMA((max(n_tile, 1),)),
            DMA((max(n_tile, 1),)),
        ],
        compiler_params=pltpu.CompilerParams(collective_id=3, has_side_effects=True),
        name="mid_back",
    )(piece, dots, cot, mid, gates, slot_of, routes, small, heads, w, prev, carry, *parts)
    return outs[:6], list(outs[6:])


def tail_kernel(
    n_seq, n_dp, parts, g_ref, wt_ref, wo_ref, pack_ref, gate_ref, slot_ref, gain_ref,
    a_hbm, h_hbm, resid_hbm, base_hbm, out_hbm, *refs,
):
    n_far = max(parts - LATE, 0)
    fin_hbm, refs = refs[:parts], refs[parts:]
    far_hbm, refs = refs[:n_far], refs[n_far:]
    din_ref, row_in, line_ref, block_ref, both_ref, refs = *refs[:5], refs[5:]
    (
        a_ref, h_ref, resid_ref, base_ref, rows_ref, far_ref, fin_ref,
        core_out, core_in, x_out, x_in, part_ref, w_out_buf, w_in, wo_buf, wo_in, wo_x, wo_far,
        w_mid, wo_mid,
        row_buf, pack_in, line_buf, line_in, load_sem, c_sems, x_sems, w_sems, v_sems, r_sems, o_sems,
        p_sems, q_sems, u_sems, l_sems, t_sems, f_sems, keep_sem,
    ) = refs
    me, dp = lax.axis_index("seq"), lax.axis_index("dp")
    tok = h_ref.shape[0]
    shard, width3 = w_in.shape[1], w_in.shape[2]
    width = width3 // 3
    owners = n_dp // E
    pairs = n_seq // 2
    others = range(1, n_dp)

    def both(sems):
        return sems.at[0], sems.at[1]

    c_sems, x_sems, w_sems, v_sems, r_sems, o_sems, p_sems, q_sems, u_sems, l_sems, t_sems, f_sems = (
        both(sems)
        for sems in (
            c_sems, x_sems, w_sems, v_sems, r_sems, o_sems, p_sems, q_sems, u_sems, l_sems, t_sems,
            f_sems,
        )
    )

    loads = []
    for src, dst in [
        (a_hbm, a_ref), (out_hbm, rows_ref), (base_hbm, base_ref), (h_hbm, h_ref),
        (resid_hbm, resid_ref),
    ] + [(fin_hbm[t], fin_ref.at[t]) for t in range(parts)] + [
        (far_hbm[t], far_ref.at[t]) for t in range(n_far)
    ]:
        load = pltpu.make_async_copy(src, dst, load_sem.at[len(loads)])
        load.start()
        loads.append(load)
    greet(
        [{"seq": me ^ place} for place in range(1, n_seq)]
        + [{"dp": lax.rem(dp + k, n_dp)} for k in others]
    )

    def there(k):
        return lax.rem(dp + k, n_dp)

    spots = [*range(n_dp // 2 - 1, -1, -1)]

    def to_neighbour(buf, near, sems):
        return {
            j: remote(buf.at[dp ^ (2 * j) ^ 1], near.at[j], sems, j, {"dp": dp ^ 1}) for j in spots
        }

    def pass_sums(copies, buf, near, mid, sems):
        passed = []
        for j in spots:
            copies[j].wait_recv()
            total = buf[dp ^ (2 * j)].astype(f32) + near[j].astype(f32)
            mid[j] = total.astype(bf16)
            if j:
                passed.append(
                    remote(mid.at[j], near.at[n_dp // 2 + j], sems, j, {"dp": dp ^ (2 * j)})
                )
        return passed

    def collect(passed, near, mid):
        for copy in passed:
            copy.wait_recv()
        return sum((near[n_dp // 2 + j].astype(f32) for j in spots[:-1]), mid[0].astype(f32))

    def term(place):
        columns = pl.ds(pl.multiple_of((me ^ place) * tok, tok), tok)
        return mm(g_ref[:, columns], wt_ref[...], TN)

    part_copies = [
        remote(fin_hbm[t], far_ref.at[t], t_sems, t - n_far, {"seq": me ^ 2})
        for t in range(n_far, parts)
    ]
    pack_copies = [
        remote(pack_ref.at[there(k)], pack_in.at[dp], p_sems, k, {"dp": there(k)}) for k in others
    ]
    pack_in[dp] = pack_ref[dp]
    for i in range(pairs):
        wo_buf[:, :, i * width : (i + 1) * width] = wo_ref[i].reshape(n_dp, shard, width)
    wo_near = to_neighbour(wo_buf, wo_in, q_sems)
    core_copies = []
    for i in range(pairs - 1, -1, -1):
        core_out[i] = term(2 * i + 1).astype(bf16)
        core_copies.insert(0, remote(core_out.at[i], core_in.at[i], c_sems, i, {"seq": me ^ 1}))
    x_copies = []
    for i in range(pairs - 1, 0, -1):
        part = term(2 * i)
        core_copies[i].wait_recv()
        x_out[i - 1] = (part + core_in[i].astype(f32)).astype(bf16)
        x_copies.append(
            remote(x_out.at[i - 1], x_in.at[i - 1], x_sems, i - 1, {"seq": me ^ (2 * i)})
        )
    loads[0].wait()
    turned = mm(g_ref[...], a_ref[...], NN)
    w_out_buf[...] = turned.T.astype(bf16).reshape(n_dp, shard, width3)
    w_near = to_neighbour(w_out_buf, w_in, w_sems)
    wo_copies = pass_sums(wo_near, wo_buf, wo_in, wo_mid, u_sems)
    w_copies = pass_sums(w_near, w_out_buf, w_in, w_mid, v_sems)
    part = term(0)
    core_copies[0].wait_recv()
    part_ref[...] = part + core_in[0].astype(f32)

    for copy in pack_copies:
        copy.wait_recv()
    line_buf[...] = jnp.sum(pack_in[...], axis=0)
    line_in[me] = line_buf[...]
    line_copies = [
        remote(line_buf, line_in.at[me], l_sems, place, {"seq": me ^ place})
        for place in range(1, n_seq)
    ]

    fin_copies, keeps = [], []

    def hand_over(ref, row, t):
        index = row * parts + t
        fin_copies.append(
            remote(ref.at[t], both_ref.at[2 * row + 1, t], f_sems, index, {"seq": me ^ 1})
        )
        keep = pltpu.make_async_copy(ref.at[t], both_ref.at[2 * row, t], keep_sem.at[index])
        keep.start()
        keeps.append(keep)

    for t in range(parts):
        loads[5 + t].wait()
        hand_over(fin_ref, 0, t)
    for t in range(n_far):
        loads[5 + parts + t].wait()
        hand_over(far_ref, 1, t)

    wo_total = collect(wo_copies, wo_in, wo_mid)
    wo_cross = []
    for i in range(1, pairs):
        wo_x[i - 1] = wo_total[:, i * width : (i + 1) * width].astype(bf16)
        wo_cross.append(
            remote(wo_x.at[i - 1], wo_far.at[i - 1], o_sems, i - 1, {"seq": me ^ (2 * i)})
        )

    loads[1].wait()
    loads[2].wait()
    picks = picks_of(slot_ref)
    rows = rows_ref[...].reshape(E, owners, CAP, D)
    columns = gate_ref[...].T
    block = base_ref[...]
    for k in range(2):
        picked = sum(
            mm(picks[k], rows[:, o].reshape(E * CAP, D), TN) for o in range(owners)
        )
        block = block + columns[:, k : k + 1] * picked
    block_ref[...] = block.astype(bf16)

    for copy in x_copies:
        copy.wait_recv()
    grad = part_ref[...]
    for i in range(pairs - 1):
        grad = grad + x_in[i].astype(f32)
    loads[3].wait()
    loads[4].wait()
    din_ref[...] = resid_ref[...] + norm_back(h_ref[...].astype(f32), gain_ref[0:1], grad)

    row_buf[:, :width3] = collect(w_copies, w_in, w_mid).astype(bf16)
    for copy in wo_cross:
        copy.wait_recv()
    wo_mine = wo_total[:, :width]
    for i in range(pairs - 1):
        wo_mine = wo_mine + wo_far[i].astype(f32)
    row_buf[:, width3:] = wo_mine.astype(bf16)
    row_in[me] = row_buf[...]
    row_copies = [
        remote(row_buf, row_in.at[me], r_sems, place, {"seq": me ^ place})
        for place in range(1, n_seq)
    ]
    for copy in line_copies:
        copy.wait_recv()
    line_ref[...] = jnp.sum(line_in[...], axis=0)
    for t, copy in enumerate(part_copies):
        copy.wait_recv()
        hand_over(far_ref, 1, n_far + t)
    for copy in row_copies + fin_copies:
        copy.wait_recv()
    for copy in (
        core_copies + [*w_near.values()] + [*wo_near.values()] + w_copies + x_copies + row_copies + wo_copies + pack_copies
        + line_copies + wo_cross + part_copies + fin_copies
    ):
        copy.wait_send()
    for keep in keeps:
        keep.wait()


def tail_call(
    n_seq, n_dp, grad_qkv, w_turned, wo_sum, pack, gates, slot_of, small,
    attn_in, hidden, grad_resid, base, back_out, fin, far,
):
    tok = hidden.shape[0]
    shard, width3 = D // n_dp, grad_qkv.shape[0]
    width = width3 // 3
    pairs = n_seq // 2
    parts, room = len(fin), max(len(fin), 1)
    part = (3, PART, D)
    return pl.pallas_call(
        functools.partial(tail_kernel, n_seq, n_dp, parts),
        out_shape=(
            jax.ShapeDtypeStruct((tok, D), f32),
            jax.ShapeDtypeStruct((n_seq, shard, width3 + width), bf16),
            jax.ShapeDtypeStruct((LINES, shard), f32),
            jax.ShapeDtypeStruct((tok, D), bf16),
            jax.ShapeDtypeStruct((n_seq, room, *part), bf16),
        ),
        in_specs=[VMEM] * 7 + [HBM] * (5 + parts + len(far)),
        out_specs=[VMEM] * 4 + [HBM],
        scratch_shapes=[
            pltpu.VMEM((n_seq * tok, D), bf16),
            pltpu.VMEM((tok, D), bf16),
            pltpu.VMEM((tok, D), f32),
            pltpu.VMEM((tok, D), f32),
            pltpu.VMEM((n_dp, CAP, D), bf16),
            pltpu.VMEM((room, *part), bf16),
            pltpu.VMEM((room, *part), bf16),
            pltpu.VMEM((pairs, tok, D), bf16),
            pltpu.VMEM((pairs, tok, D), bf16),
            pltpu.VMEM((pairs - 1, tok, D), bf16),
            pltpu.VMEM((pairs - 1, tok, D), bf16),
            pltpu.VMEM((tok, D), f32),
            pltpu.VMEM((n_dp, shard, width3), bf16),
            pltpu.VMEM((n_dp, shard, width3), bf16),
            pltpu.VMEM((n_dp, shard, pairs * width), bf16),
            pltpu.VMEM((n_dp, shard, pairs * width), bf16),
            pltpu.VMEM((pairs - 1, shard, width), bf16),
            pltpu.VMEM((pairs - 1, shard, width), bf16),
            pltpu.VMEM((n_dp // 2, shard, width3), bf16),
            pltpu.VMEM((n_dp // 2, shard, pairs * width), bf16),
            pltpu.VMEM((shard, width3 + width), bf16),
            pltpu.VMEM((n_dp, LINES, shard), f32),
            pltpu.VMEM((LINES, shard), f32),
            pltpu.VMEM((n_seq, LINES, shard), f32),
            DMA((5 + 2 * room,)),
            DMA((2, pairs)),
            DMA((2, pairs)),
            DMA((2, n_dp // 2)),
            DMA((2, n_dp // 2)),
            DMA((2, n_seq)),
            DMA((2, pairs)),
            DMA((2, n_dp)),
            DMA((2, n_dp // 2)),
            DMA((2, n_dp // 2)),
            DMA((2, n_seq)),
            DMA((2, LATE)),
            DMA((2, 2 * room)),
            DMA((2 * room,)),
        ],
        compiler_params=pltpu.CompilerParams(
            collective_id=1, has_side_effects=True, vmem_limit_bytes=67043328
        ),
        name="tail",
    )(
        grad_qkv, w_turned, wo_sum, pack, gates, slot_of, small,
        attn_in, hidden, grad_resid, base, back_out, *fin, *far,
    )


def finish_kernel(
    n_seq, me_ref, both_ref, row_ref, line_ref, wq_ref, gain_ref,
    de_ref, dw_ref, dwo_ref, again_ref, mgain_ref, router_ref, carry_ref, vec_ref, mix_ref,
):
    step = both_ref.shape[3]
    for t in range(both_ref.shape[1]):
        de_ref[:, t * step : (t + 1) * step] = both_ref[0, t].astype(f32)

    @pl.when(pl.program_id(0) == 0)
    def _():
        width = row_ref.shape[2] // 4
        for j in range(n_seq):
            block = row_ref[j].astype(f32)
            for c in range(3):
                left = c * width * n_seq + j * width
                dw_ref[:, left : left + width] = block[:, c * width : (c + 1) * width]
            dwo_ref[:, j * width : (j + 1) * width] = block[:, 3 * width :]
        sums = jnp.sum(dw_ref[...] * wq_ref[...].astype(f32), axis=1, keepdims=True)
        again_ref[...] = column_to_row(sums) / gain_ref[...].astype(f32)
        mix_ref[0] = line_ref[0:2]
        mix_ref[1] = line_ref[2:4]
        router_ref[...] = line_ref[4 : 4 + H]
        vec_ref[...] = line_ref[4 + H : 6 + H]
        mgain_ref[...] = line_ref[6 + H : 7 + H]
        carry_ref[...] = line_ref[24 : 24 + H, 0:H]


def finish_call(n_seq, me, both, row_in, lines, w_qkv, attn_gain):
    shard = w_qkv.shape[0]
    _, parts, three, step, _ = both.shape
    units = n_seq * parts * step
    group = 4 if parts % 4 == 0 else 1
    steps = parts // group

    def whole(shape):
        return pl.BlockSpec(shape, lambda i, me_ref: (0,) * len(shape))

    shapes = [(shard, 3 * D), (shard, D), (1, shard), (1, shard), (H, shard), (H, H), (2, shard),
              (2, 2, shard)]
    return pl.pallas_call(
        functools.partial(finish_kernel, n_seq),
        out_shape=[jax.ShapeDtypeStruct((three, units, D), f32)]
        + [jax.ShapeDtypeStruct(shape, f32) for shape in shapes],
        grid_spec=pltpu.PrefetchScalarGridSpec(
            num_scalar_prefetch=1,
            grid=(n_seq * steps,),
            in_specs=[
                pl.BlockSpec(
                    (1, group, three, step, D),
                    lambda i, me_ref: ((i // steps) ^ me_ref[0], i % steps, 0, 0, 0),
                ),
                whole(row_in.shape),
                whole(lines.shape),
                whole(w_qkv.shape),
                whole((1, shard)),
            ],
            out_specs=[pl.BlockSpec((three, group * step, D), lambda i, me_ref: (0, i, 0))]
            + [whole(shape) for shape in shapes],
        ),
        name="finish",
    )(me, both, row_in, lines, w_qkv, attn_gain[None])


def rope_tables(seq_len):
    freq_index = jnp.arange(HD // 2, dtype=f32)
    inv_freq = jnp.exp(freq_index * (-2.0 * math.log(10000.0) / HD))
    angles = jnp.arange(seq_len, dtype=jnp.int32).astype(f32)[None, :] * inv_freq[:, None]
    return jnp.cos(angles), jnp.sin(angles)


def per_device(
    hidden_in,
    prev_logits,
    segments,
    routes,
    attn_gain,
    w_qkv,
    w_out,
    moe_gain,
    w_router,
    w_carry,
    const_vec,
    const_mix,
    experts,
    cotangent,
):
    n_seq, n_dp = lax.axis_size("seq"), lax.axis_size("dp")
    owners = n_dp // E
    me = lax.axis_index("seq")
    tok = hidden_in.shape[1]
    hidden, cot = hidden_in[0], cotangent[0]
    prev_t = jnp.transpose(prev_logits, (2, 0, 1))
    routes_t = routes[0].T

    def to_owners(values):
        return lax.all_to_all(
            jnp.repeat(values, owners, axis=0), "dp", split_axis=0, concat_axis=0, tiled=True
        )

    def to_sources(values):
        return lax.all_to_all(values, "dp", split_axis=0, concat_axis=0, tiled=True)

    cos_t, sin_t = rope_tables(tok * n_seq)
    attn_in, qkv, w_turned, small, slot_of, grad_slots, out_weight = start_call(
        n_seq, n_dp, hidden, w_qkv, attn_gain, moe_gain, const_vec, const_mix, w_router.T,
        routes_t, cot, cos_t, sin_t, w_out,
    )
    arrived_grad = to_owners(grad_slots)

    seg_row = segments[0]
    doc_ids = jnp.arange(16, dtype=jnp.int32)
    doc_start = jnp.sum((seg_row[None, :] < doc_ids[:, None]).astype(jnp.int32), axis=1)
    start = jnp.sum(jnp.where(seg_row[None, :] == doc_ids[:, None], doc_start[:, None], 0), axis=0)
    start_row = start.astype(jnp.int32)[None, :]
    lows = start[::BLK].astype(jnp.int32) // BLK
    attended, attended_exact, logs = attn_call(lows, qkv, start_row, tok)

    heads_t, resid_mid, gates, x_slots, gate_slots = mid_call(
        n_seq, attended, hidden, prev_t, w_carry, small, slot_of, routes_t, out_weight
    )
    if n_dp * CAP > 1024:
        piece, dots, partial, d_plain = experts_plain(
            to_owners, to_sources, n_dp, x_slots, gate_slots, experts, arrived_grad
        )
        fin, far = [], []
    else:
        piece, dots, partial, fin, far = moe_call(
            n_dp, x_slots, gate_slots, experts, arrived_grad
        )
    back_out = to_sources(partial)

    (grad_resid, grad_out, base, d_prev, pack, wo_sum), far_back = mid_back_call(
        n_seq, n_dp, piece, dots, cot, resid_mid, gates, slot_of, routes_t, small, heads_t,
        out_weight, prev_t, w_carry, fin[EARLY : EARLY + 1],
    )
    later, grad_out = lax.optimization_barrier((fin[EARLY + 1 : -LATE], grad_out))
    far = far + far_back + [swap(part, "seq", 2) for part in later]
    grad_qkv = attn_back_call(
        lows, qkv, grad_out, attended_exact, logs, start_row, cos_t, sin_t
    )
    d_input, row_in, lines, block_out, both = tail_call(
        n_seq, n_dp, grad_qkv, w_turned, wo_sum, pack, gates, slot_of, small,
        attn_in, hidden, grad_resid, base, back_out, fin, far,
    )
    d_experts, d_qkv, d_out, again, mgain, router, carry, vec, mix = finish_call(
        n_seq, me.astype(jnp.int32).reshape(1), both, row_in, lines, w_qkv, attn_gain
    )
    if not fin:
        d_experts = d_plain
    return (
        block_out[None],
        d_input[None],
        jnp.transpose(d_prev, (1, 2, 0)),
        again[0],
        d_qkv,
        d_out,
        mgain[0],
        router.T,
        carry,
        vec,
        mix,
        d_experts,
    )


def solution(mesh):
    return jax.shard_map(
        per_device,
        mesh=mesh,
        in_specs=(
            P("dp", "seq", None),
            P("dp", "seq", None),
            P("dp", None),
            P("dp", "seq", None),
            P("dp"),
            P("dp", None),
            P("dp", None),
            P("dp"),
            P("dp", None),
            P(),
            P(None, "dp"),
            P(None, None, "dp"),
            P(None, "dp", None),
            P("dp", "seq", None),
        ),
        out_specs=(
            P("dp", "seq", None),
            P("dp", "seq", None),
            P("dp", "seq", None),
            P("dp"),
            P("dp", None),
            P("dp", None),
            P("dp"),
            P("dp", None),
            P(),
            P(None, "dp"),
            P(None, None, "dp"),
            P(None, "dp", None),
        ),
        check_vma=False,
    )
```

```python
import functools
import math

import jax
import jax.numpy as jnp
import numpy as np
from jax import lax
from jax.experimental import pallas as pl
from jax.experimental.pallas import tpu as pltpu
from jax.sharding import PartitionSpec as P

D = 768
H = 12
HD = 64
E = 8
CAP = 128
BLK = 256
PAIR = 2 * CAP
UNITS = 256
PART = 64
EARLY = 1
LATE = 2
SMALL = 32
LINES = 40

exact_prec = lax.Precision.HIGHEST
neg_large = -1e30
score_scale = 0.125 * math.log2(math.e)
f32 = jnp.float32
bf16 = jnp.bfloat16

NN = (((1,), (0,)), ((), ()))
NT = (((1,), (1,)), ((), ()))
TN = (((0,), (0,)), ((), ()))


MESH = pl.DeviceIdType.MESH
VMEM = pl.BlockSpec(memory_space=pltpu.VMEM)
HBM = pl.BlockSpec(memory_space=pl.ANY)
DMA = pltpu.SemaphoreType.DMA


def mm(a, b, dims):
    return lax.dot_general(a, b, dims, preferred_element_type=f32)


def swap(value, axis, bit):
    size = lax.axis_size(axis)
    return lax.ppermute(value, axis, [(i, i ^ bit) for i in range(size)])


def bits_high_first(size):
    bit = size // 2
    while bit >= 1:
        yield bit
        bit //= 2


def greet(peers):
    barrier = pltpu.get_barrier_semaphore()
    for peer in peers:
        pl.semaphore_signal(barrier, inc=1, device_id=peer, device_id_type=MESH)
    pl.semaphore_wait(barrier, len(peers))


def remote_later(src, dst, sems, index, target):
    return pltpu.make_async_remote_copy(
        src_ref=src,
        dst_ref=dst,
        send_sem=sems[0].at[index],
        recv_sem=sems[1].at[index],
        device_id=target,
        device_id_type=MESH,
    )


def remote(src, dst, sems, index, target):
    copy = remote_later(src, dst, sems, index, target)
    copy.start()
    return copy


def one_hot(condition):
    return jnp.where(condition, 1.0, 0.0).astype(bf16)


def picks_of(slot_ref):
    slots = lax.broadcasted_iota(jnp.int32, (E * CAP, slot_ref.shape[1]), 0)
    return [one_hot(slots == slot_ref[k : k + 1, :]) for k in range(2)]


def split(rows):
    high = rows.astype(bf16)
    rest = rows - high.astype(f32)
    middle = rest.astype(bf16)
    low = (rest - middle.astype(f32)).astype(bf16)
    return jnp.concatenate([high, middle, low], axis=0)


def unsplit(rows):
    third = rows.shape[0] // 3
    return rows[:third] + rows[third : 2 * third] + rows[2 * third :]


def column_to_row(column):
    return jnp.broadcast_to(column, (column.shape[0], 128)).T[0:1]


def norm_back(values, gain, grad):
    rate = lax.rsqrt(jnp.mean(values * values, axis=-1, keepdims=True) + 1e-06)
    scaled = gain * grad
    inner = jnp.mean(values * scaled, axis=-1, keepdims=True)
    return rate * scaled - values * (rate * rate * rate) * inner


def make_slots(route_ref, cot_ref, slot_ref, g_ref):
    tok = route_ref.shape[1]
    ids = lax.broadcasted_iota(jnp.int32, (E, tok), 0)
    named = [route_ref[k : k + 1, :] == ids for k in range(2)]
    earlier = lax.broadcasted_iota(jnp.int32, (tok, tok), 0) < lax.broadcasted_iota(
        jnp.int32, (tok, tok), 1
    )
    ranks = mm(one_hot(named[0] | named[1]), one_hot(earlier), NN)
    for k in range(2):
        route = route_ref[k : k + 1, :]
        rank = jnp.sum(jnp.where(named[k], ranks, 0.0), axis=0, keepdims=True)
        slot_ref[k : k + 1, :] = jnp.where(
            route < E, route * CAP + rank.astype(jnp.int32), E * CAP
        )
    picks = picks_of(slot_ref)
    g_ref[...] = mm(picks[0] + picks[1], cot_ref[...], NN).astype(bf16).reshape(g_ref.shape)


def start_kernel(
    n_seq, n_dp, h_ref, w_ref, again_ref, mgain_ref, vec_ref, mix_ref, router_ref,
    route_ref, cot_ref, fine_ref, coarse_ref, wo_ref,
    attn_hbm, qkv_ref, wt_ref, small_ref, slot_ref, g_hbm, wo_all, cos_ref, sin_ref,
    attn_ref, g_ref, out_sem, all_ref, slice_ref, small_buf, h_send, h_recv, near_send, near_recv, next_send, next_recv,
    c_send, c_recv,
):
    me, dp = lax.axis_index("seq"), lax.axis_index("dp")
    tok = h_ref.shape[0]
    width = slice_ref.shape[2] // 3
    seq_bits = list(bits_high_first(n_seq))
    greet(
        [{"seq": me ^ bit} for bit in seq_bits]
        + [{"dp": dp ^ 1}]
        + [{"dp": dp ^ (2 * j)} for j in range(1, n_dp // 2)]
    )

    plan, arrival = [], {}
    order = [(0, bit) for bit in seq_bits]
    while order:
        place, bit = order.pop(0)
        copy = remote_later(
            h_ref if place == 0 else all_ref.at[me ^ place],
            all_ref.at[me ^ place],
            (h_send, h_recv),
            len(plan),
            {"seq": me ^ bit},
        )
        arrival[place ^ bit] = copy
        plan.append((place, copy))
        order += [(place ^ bit, low) for low in seq_bits if low < bit]
    for place, copy in plan:
        if place == 0:
            copy.start()

    for j in range(n_seq):

        @pl.when(me == j)
        def _():
            for c in range(3):
                left = c * width * n_seq + j * width
                slice_ref[dp, :, c * width : (c + 1) * width] = w_ref[:, left : left + width]

    small_buf[dp] = jnp.zeros(small_buf.shape[1:], bf16)
    small_buf[dp, 0:1, :] = again_ref[...]
    small_buf[dp, 1:2, :] = mgain_ref[...]
    small_buf[dp, 2:4, :] = vec_ref[...]
    small_buf[dp, 4:6, :] = mix_ref[0]
    small_buf[dp, 6:8, :] = mix_ref[1]
    small_buf[dp, 8 : 8 + H, :] = router_ref[...]
    cols = pl.ds(pl.multiple_of((me & 1) * (D // 2), D // 2), D // 2)
    wo_all[dp, :, cols] = wo_ref[:, cols]

    def rows_of(kind, source):
        return (small_buf.at[source], slice_ref.at[source], wo_all.at[source, :, cols])[kind]

    def first_copy(kind, j):
        return remote_later(
            rows_of(kind, dp), rows_of(kind, dp), (near_send.at[kind], near_recv.at[kind]), j,
            {"dp": dp ^ (2 * j)},
        )

    def next_copy(kind, j):
        return remote_later(
            rows_of(kind, dp ^ (2 * j)), rows_of(kind, dp ^ (2 * j)),
            (next_send.at[kind], next_recv.at[kind]), j, {"dp": dp ^ 1},
        )

    places = range(1, n_dp // 2)
    for kind in range(3):
        for j in places:
            first_copy(kind, j).start()
        next_copy(kind, 0).start()
    make_slots(route_ref, cot_ref, slot_ref, g_ref)
    outs = [pltpu.make_async_copy(g_ref, g_hbm, out_sem.at[0])]
    outs[0].start()
    rates = HD // 2
    for b in range(coarse_ref.shape[1]):
        there = slice(b * 128, (b + 1) * 128)
        cos_b, sin_b = coarse_ref[:rates, b : b + 1], coarse_ref[rates:, b : b + 1]
        cos_ref[:, there] = cos_b * fine_ref[:rates] - sin_b * fine_ref[rates:]
        sin_ref[:, there] = sin_b * fine_ref[:rates] + cos_b * fine_ref[rates:]

    def pass_on(kind):
        for j in places:
            first_copy(kind, j).wait_recv()
            next_copy(kind, j).start()

    def complete(kind):
        for j in range(n_dp // 2):
            next_copy(kind, j).wait_recv()

    pass_on(0)
    complete(0)
    small_ref[...] = jnp.concatenate([small_buf[i].astype(f32) for i in range(n_dp)], axis=1)

    def normalize(block, ref):
        x = ref.astype(f32)
        mean_square = jnp.mean(x * x, axis=-1, keepdims=True)
        rows = pl.ds(pl.multiple_of(block * tok, tok), tok)
        attn_ref[rows, :] = (x * lax.rsqrt(mean_square + 1e-06) * small_ref[0:1]).astype(bf16)
        outs.append(
            pltpu.make_async_copy(
                attn_ref.at[rows, :], attn_hbm.at[rows, :], out_sem.at[len(outs)]
            )
        )
        outs[-1].start()

    normalize(me, h_ref[...])
    pass_on(1)
    for place in arrival:
        arrival[place].wait_recv()
        for source, copy in plan:
            if source == place:
                copy.start()
        normalize(me ^ place, all_ref[me ^ place])
    complete(1)
    pass_on(2)
    wt_ref[...] = slice_ref[...].reshape(D, 3 * width).T
    half = HD // 2

    @pl.loop(0, attn_ref.shape[0] // BLK)
    def _(i):
        rows = pl.ds(pl.multiple_of(i * BLK, BLK), BLK)
        y = mm(wt_ref[...], attn_ref[rows, :], NT)
        cos, sin = cos_ref[:, rows], sin_ref[:, rows]
        for head in range(2 * width // HD):
            low, middle, high = head * HD, head * HD + half, (head + 1) * HD
            a, b = y[low:middle], y[middle:high]
            qkv_ref[low:middle, rows] = (a * cos - b * sin).astype(bf16)
            qkv_ref[middle:high, rows] = (a * sin + b * cos).astype(bf16)
        qkv_ref[2 * width :, rows] = y[2 * width :].astype(bf16)

    complete(2)
    trade = remote(
        wo_all.at[:, :, cols], wo_all.at[:, :, cols], (c_send, c_recv), 0, {"seq": me ^ 1}
    )
    for _, copy in plan:
        copy.wait_send()
    for kind in range(3):
        for j in places:
            first_copy(kind, j).wait_send()
        for j in range(n_dp // 2):
            next_copy(kind, j).wait_send()
    for copy in outs:
        copy.wait()
    trade.wait()


def start_call(
    n_seq, n_dp, hidden, w_qkv, attn_gain, moe_gain, vec, mix, router, routes, cotangent, w_out,
):
    tok, shard = hidden.shape[0], w_qkv.shape[0]
    width3 = w_qkv.shape[1] // n_seq
    hops = n_seq - 1
    return pl.pallas_call(
        functools.partial(start_kernel, n_seq, n_dp),
        out_shape=(
            jax.ShapeDtypeStruct((n_seq * tok, D), bf16),
            jax.ShapeDtypeStruct((width3, n_seq * tok), bf16),
            jax.ShapeDtypeStruct((width3, D), bf16),
            jax.ShapeDtypeStruct((SMALL, D), f32),
            jax.ShapeDtypeStruct(routes.shape, jnp.int32),
            jax.ShapeDtypeStruct((E, CAP, D), bf16),
            jax.ShapeDtypeStruct((n_dp, shard, D), bf16),
            jax.ShapeDtypeStruct((HD // 2, n_seq * tok), f32),
            jax.ShapeDtypeStruct((HD // 2, n_seq * tok), f32),
        ),
        in_specs=[VMEM] * 12,
        out_specs=[HBM] + [VMEM] * 4 + [HBM] + [VMEM] * 3,
        scratch_shapes=[
            pltpu.VMEM((n_seq * tok, D), bf16),
            pltpu.VMEM((E, CAP, D), bf16),
            DMA((1 + n_seq,)),
            pltpu.VMEM((n_seq, tok, D), bf16),
            pltpu.VMEM((n_dp, shard, width3), bf16),
            pltpu.VMEM((n_dp, SMALL, shard), bf16),
            DMA((hops,)),
            DMA((hops,)),
            DMA((3, n_dp // 2)),
            DMA((3, n_dp // 2)),
            DMA((3, n_dp // 2)),
            DMA((3, n_dp // 2)),
            DMA((1,)),
            DMA((1,)),
        ],
        compiler_params=pltpu.CompilerParams(collective_id=0, has_side_effects=True),
        name="start",
    )(
        hidden, w_qkv, attn_gain[None], moe_gain[None], vec, mix, router, routes, cotangent,
        *rope_tables(n_seq * tok), w_out,
    )


def allowed_block(key_block, query_block, start_row):
    key_pos = key_block * BLK + lax.broadcasted_iota(jnp.int32, (BLK, BLK), 0)
    query_pos = query_block * BLK + lax.broadcasted_iota(jnp.int32, (BLK, BLK), 1)
    return (key_pos >= start_row) & (key_pos <= query_pos)


def attn_kernel(lo_ref, qkv_ref, start_ref, out_ref, exact_ref, log_ref, keys_ref):
    heads, seq_len, _ = keys_ref.shape
    width = heads * HD
    qb = pl.program_id(0)

    @pl.when(qb == 0)
    def _():
        for h in range(heads):
            keys_ref[h] = qkv_ref[width + h * HD : width + (h + 1) * HD, :].T

    here = pl.ds(pl.multiple_of(qb * BLK, BLK), BLK)
    start_row = start_ref[...]

    def step(kb, carry):
        there = pl.ds(pl.multiple_of(kb * BLK, BLK), BLK)
        allowed = allowed_block(kb, qb, start_row)
        scores = [
            mm(keys_ref[h, there, :], qkv_ref[h * HD : (h + 1) * HD, here], NN)
            for h in range(heads)
        ]
        stats, weights = [], []
        for h in range(heads):
            top, total, acc = carry[h]
            masked = jnp.where(allowed, scores[h] * score_scale, neg_large)
            new_top = jnp.maximum(top, jnp.max(masked, axis=0, keepdims=True))
            fade = jnp.exp2(top - new_top)
            weight = jnp.exp2(masked - new_top)
            total = total * fade + jnp.sum(weight, axis=0, keepdims=True)
            stats.append((new_top, total, acc * fade))
            weights.append(weight.astype(bf16))
        new = []
        for h in range(heads):
            values = qkv_ref[2 * width + h * HD : 2 * width + (h + 1) * HD, there]
            top, total, acc = stats[h]
            new.append((top, total, acc + mm(values, weights[h], NN)))
        return tuple(new)

    first = tuple(
        (
            jnp.full((1, BLK), neg_large, f32),
            jnp.zeros((1, BLK), f32),
            jnp.zeros((HD, BLK), f32),
        )
        for _ in range(heads)
    )
    done = lax.fori_loop(lo_ref[qb], qb + 1, step, first)
    for h in range(heads):
        top, total, acc = done[h]
        attended = acc / total
        exact_ref[h * HD : (h + 1) * HD, :] = attended
        out_ref[0, h * HD : (h + 1) * HD, :] = attended.astype(bf16)
        log_ref[h : h + 1, :] = top + jnp.log2(total)


def attn_call(lows, qkv, start_row, tok):
    width3, seq_len = qkv.shape
    width = width3 // 3
    heads = width // HD
    per = tok // BLK
    return pl.pallas_call(
        attn_kernel,
        out_shape=(
            jax.ShapeDtypeStruct((seq_len // tok, width, tok), bf16),
            jax.ShapeDtypeStruct((width, seq_len), f32),
            jax.ShapeDtypeStruct((heads, seq_len), f32),
        ),
        grid_spec=pltpu.PrefetchScalarGridSpec(
            num_scalar_prefetch=1,
            grid=(seq_len // BLK,),
            in_specs=[
                pl.BlockSpec((width3, seq_len), lambda i, lo: (0, 0)),
                pl.BlockSpec((1, BLK), lambda i, lo: (0, i)),
            ],
            out_specs=[
                pl.BlockSpec((1, width, BLK), lambda i, lo: (i // per, 0, i % per)),
                pl.BlockSpec((width, BLK), lambda i, lo: (0, i)),
                pl.BlockSpec((heads, BLK), lambda i, lo: (0, i)),
            ],
            scratch_shapes=[pltpu.VMEM((heads, seq_len, HD), bf16)],
        ),
        cost_estimate=pl.CostEstimate(
            flops=16_000_000_000, transcendentals=0, bytes_accessed=16_000_000
        ),
        name="attend",
    )(lows, qkv, start_row)


def attn_back_kernel(
    lo_ref, qkv_ref, go_ref, exact_ref, log_ref, start_ref, cos_ref, sin_ref, out_ref,
    keys_ref, values_ref, dk_ref, dv_ref,
):
    heads, seq_len, _ = keys_ref.shape
    width = heads * HD
    half = HD // 2
    qb = pl.program_id(0)

    @pl.when(qb == 0)
    def _():
        for h in range(heads):
            keys_ref[h] = qkv_ref[width + h * HD : width + (h + 1) * HD, :].T
            values_ref[h] = qkv_ref[2 * width + h * HD : 2 * width + (h + 1) * HD, :].T
        dk_ref[...] = jnp.zeros_like(dk_ref)
        dv_ref[...] = jnp.zeros_like(dv_ref)

    here = pl.ds(pl.multiple_of(qb * BLK, BLK), BLK)
    start_row = start_ref[...]
    grad = go_ref[0]
    deltas = [
        jnp.sum(
            exact_ref[h * HD : (h + 1) * HD, :] * grad[h * HD : (h + 1) * HD].astype(f32),
            axis=0,
            keepdims=True,
        )
        for h in range(heads)
    ]

    def step(kb, carry):
        there = pl.ds(pl.multiple_of(kb * BLK, BLK), BLK)
        allowed = allowed_block(kb, qb, start_row)
        spans = [slice(h * HD, (h + 1) * HD) for h in range(heads)]
        queries = [qkv_ref[rows, here] for rows in spans]
        scores = [mm(keys_ref[h, there, :], queries[h], NN) for h in range(heads)]
        grad_probs = [mm(values_ref[h, there, :], grad[spans[h]], NN) for h in range(heads)]
        probs, grad_scores = [], []
        for h in range(heads):
            masked = jnp.where(allowed, scores[h] * score_scale, neg_large)
            prob = jnp.exp2(masked - log_ref[h : h + 1, :])
            probs.append(prob.astype(bf16))
            grad_scores.append((prob * (grad_probs[h] - deltas[h])).astype(bf16))
        new = []
        for h in range(heads):
            dv_ref[spans[h], there] += mm(grad[spans[h]], probs[h], NT)
        for h in range(heads):
            dk_ref[spans[h], there] += mm(queries[h], grad_scores[h], NT)
        for h in range(heads):
            keys = qkv_ref[width + h * HD : width + (h + 1) * HD, there]
            new.append(carry[h] + mm(keys, grad_scores[h], NN))
        return tuple(new)

    grads = lax.fori_loop(
        lo_ref[qb], qb + 1, step, tuple(jnp.zeros((HD, BLK), f32) for _ in range(heads))
    )

    def turn_back(value, cos, sin):
        value = value.astype(bf16).astype(f32)
        a, b = value[:half], value[half:]
        return (a * cos + b * sin).astype(bf16), (b * cos - a * sin).astype(bf16)

    for h in range(heads):
        a, b = turn_back(grads[h] * 0.125, cos_ref[:, here], sin_ref[:, here])
        out_ref[h * HD : h * HD + half, here] = a
        out_ref[h * HD + half : (h + 1) * HD, here] = b

    @pl.when(qb == pl.num_programs(0) - 1)
    def _():
        cos, sin = cos_ref[...], sin_ref[...]
        for h in range(heads):
            a, b = turn_back(dk_ref[h * HD : (h + 1) * HD, :] * 0.125, cos, sin)
            out_ref[width + h * HD : width + h * HD + half, :] = a
            out_ref[width + h * HD + half : width + (h + 1) * HD, :] = b
        out_ref[2 * width :, :] = dv_ref[...].astype(bf16)


def attn_back_call(lows, qkv, grad_out, exact, logs, start_row, cos_t, sin_t):
    width3, seq_len = qkv.shape
    width = width3 // 3
    heads = width // HD
    per = grad_out.shape[2] // BLK
    return pl.pallas_call(
        attn_back_kernel,
        out_shape=jax.ShapeDtypeStruct((width3, seq_len), bf16),
        grid_spec=pltpu.PrefetchScalarGridSpec(
            num_scalar_prefetch=1,
            grid=(seq_len // BLK,),
            in_specs=[
                pl.BlockSpec((width3, seq_len), lambda i, lo: (0, 0)),
                pl.BlockSpec((1, width, BLK), lambda i, lo: (i // per, 0, i % per)),
                pl.BlockSpec((width, BLK), lambda i, lo: (0, i)),
                pl.BlockSpec((heads, BLK), lambda i, lo: (0, i)),
                pl.BlockSpec((1, BLK), lambda i, lo: (0, i)),
                pl.BlockSpec((HD // 2, seq_len), lambda i, lo: (0, 0)),
                pl.BlockSpec((HD // 2, seq_len), lambda i, lo: (0, 0)),
            ],
            out_specs=pl.BlockSpec((width3, seq_len), lambda i, lo: (0, 0)),
            scratch_shapes=[
                pltpu.VMEM((heads, seq_len, HD), bf16),
                pltpu.VMEM((heads, seq_len, HD), bf16),
                pltpu.VMEM((width, seq_len), f32),
                pltpu.VMEM((width, seq_len), f32),
            ],
        ),
        cost_estimate=pl.CostEstimate(
            flops=16_000_000_000, transcendentals=0, bytes_accessed=16_000_000
        ),
        name="attend_back",
    )(lows, qkv, grad_out, exact, logs, start_row, cos_t, sin_t)


def gates_back(grad_hidden, gate_pre, up_pre):
    sig = 1.0 / (1.0 + jnp.exp(-gate_pre))
    silu = gate_pre * sig
    grad_gate = grad_hidden * up_pre * sig * (1.0 + gate_pre * (1.0 - sig))
    return (
        (silu * up_pre).astype(bf16),
        grad_gate.astype(bf16),
        (grad_hidden * silu).astype(bf16),
    )


def moe_kernel(n_dp, parts, x_ref, gate_ref, w_hbm, g_ref, *refs):
    piece_ref, dots_ref, out_ref, refs = refs[0], refs[1], refs[2], refs[3:]
    fin_hbm, refs = refs[:parts], refs[parts:]
    cross_hbm, refs = refs[:EARLY], refs[EARLY:]
    (
        w_ref, x_in, x_far, g_far, gate_in, gate_far, gs_ref, gs_far, pair_ref, near_ref, far_ref,
        own_ref, piece_out, dot_out, dw_out, dw_in, fin_ref,
        w_sem, x_send, x_recv, t_send, t_recv, p_send, p_recv, d_send, d_recv,
        xf_send, xf_recv, gf_send, gf_recv, tf_send, tf_recv, c_send, c_recv, e_send, e_recv, keep_sem,
    ) = refs
    me, dp = lax.axis_index("seq"), lax.axis_index("dp")
    owners = n_dp // E
    pairs = n_dp // 2
    half = near_ref.shape[2]
    core, plane = me & 1, lax.div(me, 2)
    greet([{"dp": dp ^ k} for k in range(1, n_dp)] + [{"seq": me ^ 1}, {"seq": me ^ 2}])

    def x_copy(k):
        return remote_later(
            x_ref.at[(dp ^ k) // owners], x_in.at[k], (x_send, x_recv), k, {"dp": dp ^ k}
        )

    def gate_copy(k):
        return remote_later(
            gate_ref.at[(dp ^ k) // owners], gate_in.at[k], (t_send, t_recv), k, {"dp": dp ^ k}
        )

    def piece_copy(k):
        return remote_later(
            piece_out.at[k], piece_ref.at[dp], (p_send, p_recv), k, {"dp": dp ^ k}
        )

    def dot_copy(k):
        return remote_later(dot_out.at[k], dots_ref.at[dp], (d_send, d_recv), k, {"dp": dp ^ k})

    def far_copies(k):
        across = {"seq": me ^ 2}
        return [
            remote_later(gate_in.at[k], gate_far.at[k], (tf_send, tf_recv), k, across),
            remote_later(g_ref.at[dp ^ k], g_far.at[k], (gf_send, gf_recv), k, across),
            remote_later(x_in.at[k], x_far.at[k], (xf_send, xf_recv), k, across),
        ]

    def core_copy(t):
        return remote_later(dw_out.at[t], dw_in.at[t], (c_send, c_recv), t, {"seq": me ^ 1})

    for p in range(pairs):
        for k in (2 * p, 2 * p + 1):
            if k:
                gate_copy(k).start()
                x_copy(k).start()
    loads = [pltpu.make_async_copy(w_hbm.at[j], w_ref.at[j], w_sem.at[j]) for j in range(3)]
    loads.append(pltpu.make_async_copy(x_ref.at[dp // owners], x_in.at[0], w_sem.at[3]))
    for load in loads:
        load.start()
    gate_in[0] = gate_ref[dp // owners]
    for load in loads:
        load.wait()

    def place(i):
        return i + 0

    def scale(ref, rows, gate, k):
        column = jnp.broadcast_to(gate, (CAP, CAP)).T[:, 0:1]
        here = pl.ds(pl.multiple_of(k * CAP, CAP), CAP)
        ref[here] = (rows.astype(f32) * column).astype(bf16)

    @pl.loop(0, pairs)
    def _(i):
        p = place(i)
        rows = pl.ds(pl.multiple_of(p * PAIR, PAIR), PAIR)

        def arrive(k):
            x_copy(k).wait_recv()
            gate_copy(k).wait_recv()

        @pl.when(p > 0)
        def _():
            arrive(2 * p)

        arrive(2 * p + 1)
        for side in range(2):
            k = 2 * p + side
            for copy in far_copies(k):
                copy.start()
            scale(gs_ref, g_ref[dp ^ k], gate_in[k], k)

        @pl.loop(0, 2)
        def _(t):
            part = pl.ds(pl.multiple_of(t * half, half), half)
            x = x_in[pl.ds(2 * p, 2)].reshape(PAIR, D)
            gate_pre = mm(x, w_ref[0, part], NT)
            up_pre = mm(x, w_ref[1, part], NT)
            grad_hidden = mm(gs_ref[rows], w_ref[2, part], NT)
            results = gates_back(grad_hidden, gate_pre, up_pre)
            for j in range(3):
                pair_ref[j, :, part] = results[j]

            @pl.when(t == plane)
            def _():
                for j in range(3):
                    near_ref[j, rows] = results[j]

        pieces = mm(pair_ref[1], w_ref[0], NN) + mm(pair_ref[2], w_ref[1], NN)
        piece_out[pl.ds(2 * p, 2)] = pieces.astype(bf16).reshape(2, CAP, D)
        piece_copy(2 * p + 1).start()

        @pl.when(p > 0)
        def _():
            piece_copy(2 * p).start()

        outs = mm(pair_ref[0], w_ref[2], NN)
        for side in range(2):
            k = 2 * p + side
            out = outs[side * CAP : (side + 1) * CAP].astype(bf16)
            out_ref[dp ^ k] = out
            product = out.astype(f32) * g_ref[dp ^ k].astype(f32)
            dot_out[k] = column_to_row(jnp.sum(product, axis=1, keepdims=True))
        dot_copy(2 * p + 1).start()

        @pl.when(p > 0)
        def _():
            dot_copy(2 * p).start()

    piece_ref[dp] = piece_out[0]
    dots_ref[dp] = dot_out[0]

    def weight_grad(source, x, gs, j, part):
        left = source[(1, 2, 0)[j], :, part]
        return mm(left, gs[...] if j == 2 else x[...].reshape(n_dp * CAP, D), TN)

    @pl.loop(0, half // UNITS)
    def _(t):
        part = pl.ds(pl.multiple_of(t * UNITS, UNITS), UNITS)
        for j in range(3):
            own_ref[j, part] = weight_grad(near_ref, x_in, gs_ref, j, part)

    def far_grad(rows, j, part):
        left = far_ref[(1, 2, 0)[j], :, part]
        if j == 2:
            right = gs_far[rows]
        elif isinstance(rows, slice):
            right = x_far[rows.start // CAP : rows.stop // CAP].reshape(PAIR, D)
        else:
            right = x_far[pl.ds(lax.div(rows.start, CAP), 2)].reshape(PAIR, D)
        return mm(left, right, TN)

    @pl.loop(0, pairs)
    def _(i):
        p = place(i)
        rows = pl.ds(pl.multiple_of(p * PAIR, PAIR), PAIR)
        for side in range(2):
            k = 2 * p + side
            for copy in far_copies(k):
                copy.wait_recv()
            scale(gs_far, g_far[k], gate_far[k], k)
        part = pl.ds(pl.multiple_of(plane * half, half), half)
        x = x_far[pl.ds(2 * p, 2)].reshape(PAIR, D)
        results = gates_back(
            mm(gs_far[rows], w_ref[2, part], NT),
            mm(x, w_ref[0, part], NT),
            mm(x, w_ref[1, part], NT),
        )
        for j in range(3):
            far_ref[j] = results[j]

        @pl.when(i < pairs - 1)
        def _():
            @pl.loop(0, half // UNITS)
            def _(t):
                part = pl.ds(pl.multiple_of(t * UNITS, UNITS), UNITS)
                for j in range(3):
                    own_ref[j, part] += far_grad(rows, j, part)

    tiles = half // UNITS // 2
    final = slice((pairs - 1) * PAIR, pairs * PAIR)

    def both_rows(side, t, j):
        part = pl.ds(pl.multiple_of((side * tiles + t) * UNITS, UNITS), UNITS)
        return own_ref[j, part] + far_grad(final, j, part)

    @pl.loop(0, tiles)
    def _(t):
        for j in range(3):
            dw_out[t, j] = both_rows(1 - core, t, j).astype(bf16)
        core_copy(t).start()

    def early_copy(t):
        return remote_later(fin_ref.at[t], cross_hbm[t], (e_send, e_recv), t, {"seq": me ^ 2})

    @pl.loop(0, tiles)
    def _(t):
        core_copy(t).wait_recv()
        for j in range(3):
            total = (both_rows(core, t, j) + dw_in[t, j].astype(f32)).astype(bf16)
            for u in range(UNITS // PART):
                fin_ref[t * (UNITS // PART) + u, j] = total[u * PART : (u + 1) * PART]

        @pl.when(t == 0)
        def _():
            for e in range(EARLY):
                early_copy(e).start()

    keeps = [
        pltpu.make_async_copy(fin_ref.at[t], fin_hbm[t], keep_sem.at[t]) for t in range(parts)
    ]
    for keep in keeps:
        keep.start()
    for k in range(1, n_dp):
        piece_copy(k).wait()
        dot_copy(k).wait()
        x_copy(k).wait_send()
        gate_copy(k).wait_send()
    for k in range(n_dp):
        for copy in far_copies(k):
            copy.wait_send()
    for t in range(tiles):
        core_copy(t).wait_send()
    for t in range(EARLY):
        early_copy(t).wait()
    for keep in keeps:
        keep.wait()


def moe_call(n_dp, x_slots, gate_slots, weights, grads):
    units = weights.shape[1]
    half = units // 2
    rows = n_dp * CAP
    parts = units // 4 // PART
    tiles = half // UNITS // 2
    outs = pl.pallas_call(
        functools.partial(moe_kernel, n_dp, parts),
        out_shape=(
            jax.ShapeDtypeStruct((n_dp, CAP, D), bf16),
            jax.ShapeDtypeStruct((n_dp, 1, CAP), f32),
            jax.ShapeDtypeStruct((n_dp, CAP, D), bf16),
        )
        + (jax.ShapeDtypeStruct((3, PART, D), bf16),) * (parts + EARLY),
        in_specs=[HBM, VMEM, HBM, VMEM],
        out_specs=[VMEM] * 3 + [HBM] * (parts + EARLY),
        scratch_shapes=[
            pltpu.VMEM(weights.shape, bf16),
            pltpu.VMEM((n_dp, CAP, D), bf16),
            pltpu.VMEM((n_dp, CAP, D), bf16),
            pltpu.VMEM((n_dp, CAP, D), bf16),
            pltpu.VMEM((n_dp, 1, CAP), f32),
            pltpu.VMEM((n_dp, 1, CAP), f32),
            pltpu.VMEM((rows, D), bf16),
            pltpu.VMEM((rows, D), bf16),
            pltpu.VMEM((3, PAIR, units), bf16),
            pltpu.VMEM((3, rows, half), bf16),
            pltpu.VMEM((3, PAIR, half), bf16),
            pltpu.VMEM((3, half, D), f32),
            pltpu.VMEM((n_dp, CAP, D), bf16),
            pltpu.VMEM((n_dp, 1, CAP), f32),
            pltpu.VMEM((tiles, 3, UNITS, D), bf16),
            pltpu.VMEM((tiles, 3, UNITS, D), bf16),
            pltpu.VMEM((parts, 3, PART, D), bf16),
            DMA((4,)),
        ]
        + [DMA((n_dp,))] * 14
        + [DMA((tiles,))] * 2
        + [DMA((EARLY,))] * 2
        + [DMA((parts,))],
        compiler_params=pltpu.CompilerParams(
            collective_id=4, has_side_effects=True, vmem_limit_bytes=67043328
        ),
        name="experts",
    )(x_slots, gate_slots, weights, grads)
    return outs[0], outs[1], outs[2], list(outs[3 : 3 + parts]), list(outs[3 + parts :])


def experts_plain(to_owners, to_sources, n_dp, x_slots, gate_slots, weights, grads):
    rows = n_dp * CAP
    x = to_owners(x_slots).reshape(rows, D)
    gate = to_owners(gate_slots).reshape(rows, 1)
    g = grads.reshape(rows, D)
    gs = (g.astype(f32) * gate).astype(bf16)
    hidden, grad_gate, grad_up = gates_back(
        mm(gs, weights[2], NT), mm(x, weights[0], NT), mm(x, weights[1], NT)
    )
    out = mm(hidden, weights[2], NN).astype(bf16)
    piece = (mm(grad_gate, weights[0], NN) + mm(grad_up, weights[1], NN)).astype(bf16)
    dw = jnp.stack([mm(grad_gate, x, TN), mm(grad_up, x, TN), mm(hidden, gs, TN)])
    dots = jnp.sum(out.astype(f32) * g.astype(f32), axis=-1)
    return (
        to_sources(piece.reshape(n_dp, CAP, D)),
        to_sources(dots.reshape(n_dp, 1, CAP)),
        out.reshape(n_dp, CAP, D),
        lax.psum(dw, "seq"),
    )


def mid_kernel(
    n_seq, att_ref, h_ref, prev_ref, carry_ref, small_ref, slot_ref, route_ref, w_ref,
    heads_ref, mid_ref, gate_ref, x_ref, gs_ref, send_sem, recv_sem,
):
    me = lax.axis_index("seq")
    tok = h_ref.shape[0]
    greet([{"seq": me ^ place} for place in range(1, n_seq)])
    copies = [
        remote(
            att_ref.at[me ^ place], heads_ref.at[me], (send_sem, recv_sem), place,
            {"seq": me ^ place},
        )
        for place in range(1, n_seq)
    ]
    heads_ref[me] = att_ref[me]
    picks = picks_of(slot_ref)
    pick_any = picks[0] + picks[1]
    carried = lax.dot_general(
        carry_ref[...].astype(f32), prev_ref[:, 0, :], TN, precision=exact_prec,
        preferred_element_type=f32,
    )
    for copy in copies:
        copy.wait_recv()
    attn_out = mm(heads_ref[...].reshape(D, tok), w_ref[...].reshape(D, D), TN)
    resid = h_ref[...].astype(f32) + attn_out
    mid_ref[...] = resid
    rate = lax.rsqrt(jnp.mean(resid * resid, axis=-1, keepdims=True) + 1e-06)
    normed = resid * rate * small_ref[1:2]
    low = normed.astype(bf16)
    x_ref[...] = mm(pick_any, low, NN).astype(bf16).reshape(x_ref.shape)
    heads_rows = small_ref[4 : 8 + H].astype(bf16)
    products = mm(heads_rows, low, NT)
    rest = mm(heads_rows, (normed - low.astype(f32)).astype(bf16), NT)
    logits = products[4:] + carried
    ids = lax.broadcasted_iota(jnp.int32, (H, tok), 0)
    chosen = [
        jnp.sum(jnp.where(route_ref[k : k + 1, :] == ids, logits, 0.0), axis=0, keepdims=True)
        for k in range(2)
    ]
    top = jnp.maximum(chosen[0], chosen[1])
    exps = [jnp.exp(c - top) for c in chosen]
    total = exps[0] + exps[1]
    gates = [e / total for e in exps]
    gate_ref[...] = jnp.concatenate(
        [gates[0], gates[1], products[:4] + rest[:4], jnp.zeros((2, tok), f32)], axis=0
    )
    slot_gates = sum(unsplit(mm(split(gates[k]), picks[k], NT)) for k in range(2))
    for e in range(E):
        gs_ref[e] = slot_gates[:, e * CAP : (e + 1) * CAP]
    for copy in copies:
        copy.wait_send()


def mid_call(n_seq, attended, hidden, prev, carry, small, slot_of, routes, w_out):
    tok, width = hidden.shape[0], attended.shape[1]
    return pl.pallas_call(
        functools.partial(mid_kernel, n_seq),
        out_shape=(
            jax.ShapeDtypeStruct((n_seq, width, tok), bf16),
            jax.ShapeDtypeStruct((tok, D), f32),
            jax.ShapeDtypeStruct((8, tok), f32),
            jax.ShapeDtypeStruct((E, CAP, D), bf16),
            jax.ShapeDtypeStruct((E, 1, CAP), f32),
        ),
        in_specs=[VMEM] * 8,
        out_specs=[VMEM] * 5,
        scratch_shapes=[DMA((n_seq,)), DMA((n_seq,))],
        compiler_params=pltpu.CompilerParams(collective_id=2, has_side_effects=True),
        name="mid",
    )(attended, hidden, prev, carry, small, slot_of, routes, w_out)


def mid_back_kernel(
    n_seq, n_dp, n_tile, piece_ref, dots_ref, cot_ref, mid_ref, gate_ref, slot_ref, route_ref,
    small_ref, heads_ref, w_ref, prev_ref, carry_ref, *refs,
):
    tile_refs, refs = refs[:n_tile], refs[n_tile:]
    resid_ref, go_ref, base_ref, dprev_ref, pack_ref, wo_sum_ref, *refs = refs
    far_refs, refs = refs[:n_tile], refs[n_tile:]
    gh_ref, wo_ref, wo_in, a_send, a_recv, c_send, c_recv, t_send, t_recv = refs
    me = lax.axis_index("seq")
    tok = cot_ref.shape[0]
    width = heads_ref.shape[1]
    owners = n_dp // E
    pairs = n_seq // 2
    greet([{"seq": me ^ place} for place in range(1, n_seq)])
    tile_copies = [
        remote(tile_refs[t], far_refs[t], (t_send, t_recv), t, {"seq": me ^ 2})
        for t in range(n_tile)
    ]
    cot = cot_ref[...]
    grad_top = cot.astype(f32)
    resid_mid = mid_ref[...]
    gain = small_ref[1:2]
    rate = lax.rsqrt(jnp.mean(resid_mid * resid_mid, axis=-1, keepdims=True) + 1e-06)
    normed = resid_mid * rate * gain
    low = normed.astype(bf16)
    picks = picks_of(slot_ref)
    gates = [gate_ref[k : k + 1, :] for k in range(2)]
    routes = [route_ref[k : k + 1, :] for k in range(2)]
    normed_dot = column_to_row(jnp.sum(grad_top * normed, axis=1, keepdims=True))
    vecs = small_ref[2:4].astype(bf16)
    vec_dot = mm(vecs, cot, NT)
    alphas, const_dot = [], []
    for j in range(2):
        pair = [gate_ref[2 + 2 * j + c : 3 + 2 * j + c, :] for c in range(2)]
        top = jnp.maximum(pair[0], pair[1])
        exps = [jnp.exp(p - top) for p in pair]
        total = exps[0] + exps[1]
        alphas.append([e / total for e in exps])
        const_dot.append(alphas[j][0] * normed_dot + alphas[j][1] * vec_dot[j : j + 1])
    slot_dots = split(
        jnp.concatenate(
            [sum(dots_ref[e * owners + o] for o in range(owners)) for e in range(E)], axis=1
        )
    )
    out_dots = []
    for k in range(2):
        value = unsplit(mm(slot_dots, picks[k], NN))
        value = value + jnp.where(routes[k] == E + 1, normed_dot, 0.0)
        for j in range(2):
            value = value + jnp.where(routes[k] == E + 2 + j, const_dot[j], 0.0)
        out_dots.append(value)
    mean_dot = gates[0] * out_dots[0] + gates[1] * out_dots[1]
    ids = lax.broadcasted_iota(jnp.int32, (H, tok), 0)
    grad_logits = sum(
        jnp.where(routes[k] == ids, gates[k] * (out_dots[k] - mean_dot), 0.0) for k in range(2)
    )

    def gate_of(expert):
        return sum(jnp.where(routes[k] == expert, gates[k], 0.0) for k in range(2))

    const_gate = [gate_of(E + 2 + j) for j in range(2)]
    normed_gate = gate_of(E + 1) + sum(const_gate[j] * alphas[j][0] for j in range(2))
    vec_gate = split(jnp.concatenate([const_gate[j] * alphas[j][1] for j in range(2)], axis=0))
    mix_grads = []
    for j in range(2):
        terms = [normed_dot, vec_dot[j : j + 1]]
        for c in range(2):
            mix_grads.append(const_gate[j] * alphas[j][c] * (terms[c] - const_dot[j]))
    token_rows = split(jnp.concatenate(mix_grads + [grad_logits], axis=0))
    normed_column = jnp.broadcast_to(normed_gate, (8, tok)).T[:, 0:1]
    heads_rows = small_ref[4 : 8 + H].astype(bf16)
    pick_any = picks[0] + picks[1]
    grad_normed = grad_top * normed_column
    grad_normed = grad_normed + mm(
        token_rows, jnp.concatenate([heads_rows] * 3, axis=0), TN
    )
    pieces = piece_ref[...].reshape(E, owners, CAP, D)
    for o in range(owners):
        grad_normed = grad_normed + mm(pick_any, pieces[:, o].reshape(E * CAP, D), TN)
    grad_resid = grad_top + norm_back(resid_mid, gain, grad_normed)
    resid_ref[...] = grad_resid
    grad_attn = grad_resid.astype(bf16)
    gh_ref[...] = mm(w_ref[...].reshape(D, D), grad_attn, NT).astype(bf16).reshape(gh_ref.shape)
    copies = [
        remote(gh_ref.at[me ^ place], go_ref.at[me], (a_send, a_recv), place, {"seq": me ^ place})
        for place in range(1, n_seq)
    ]
    go_ref[me] = gh_ref[me]
    grad_w = mm(heads_ref[...].reshape(D, tok), grad_attn, NN)
    for j in range(n_seq):
        wo_ref[j] = grad_w[:, j * width : (j + 1) * width].astype(bf16)
    core_copies = [
        remote(wo_ref.at[me ^ (2 * i + 1)], wo_in.at[i], (c_send, c_recv), i, {"seq": me ^ 1})
        for i in range(pairs)
    ]
    base_ref[...] = (
        resid_mid
        + normed * normed_column
        + mm(vec_gate, jnp.concatenate([vecs] * 3, axis=0), TN)
    )
    dprev_ref[:, 0, :] = lax.dot_general(
        carry_ref[...].astype(f32), grad_logits, NN, precision=exact_prec,
        preferred_element_type=f32,
    )
    rest = (normed - low.astype(f32)).astype(bf16)
    row_sums = unsplit(mm(token_rows, low, NN))
    mix_sums = row_sums[:4] + unsplit(mm(token_rows, rest, NN))[:4]
    vec_sums = unsplit(mm(vec_gate, cot, NN))
    gain_sum = jnp.sum(grad_normed * resid_mid * rate, axis=0, keepdims=True)
    carry_grad = lax.dot_general(
        prev_ref[:, 0, :], grad_logits, NT, precision=exact_prec, preferred_element_type=f32
    )
    packed = jnp.concatenate([mix_sums, row_sums[4:], vec_sums, gain_sum], axis=0)
    lines, shard = packed.shape[0], D // n_dp
    for i in range(n_dp):
        pack_ref[i] = jnp.zeros(pack_ref.shape[1:], f32)
        pack_ref[i, 0:lines, :] = packed[:, i * shard : (i + 1) * shard]
        pack_ref[i, 24 : 24 + H, 0:H] = carry_grad
    for i in range(pairs):
        core_copies[i].wait_recv()
        wo_sum_ref[i] = (
            wo_ref[me ^ (2 * i)].astype(f32) + wo_in[i].astype(f32)
        ).astype(bf16)
    for copy in copies + tile_copies:
        copy.wait()
    for copy in core_copies:
        copy.wait_send()


def mid_back_call(
    n_seq, n_dp, piece, dots, cot, mid, gates, slot_of, routes, small, heads, w, prev, carry,
    parts,
):
    tok, width = cot.shape[0], heads.shape[1]
    pairs = n_seq // 2
    n_tile = len(parts)
    outs = pl.pallas_call(
        functools.partial(mid_back_kernel, n_seq, n_dp, n_tile),
        out_shape=(
            jax.ShapeDtypeStruct((tok, D), f32),
            jax.ShapeDtypeStruct((n_seq, width, tok), bf16),
            jax.ShapeDtypeStruct((tok, D), f32),
            jax.ShapeDtypeStruct((H, 1, tok), f32),
            jax.ShapeDtypeStruct((n_dp, LINES, D // n_dp), f32),
            jax.ShapeDtypeStruct((pairs, D, width), bf16),
        )
        + tuple(jax.ShapeDtypeStruct(part.shape, bf16) for part in parts),
        in_specs=[VMEM] * 12 + [HBM] * n_tile,
        out_specs=[VMEM] * 6 + [HBM] * n_tile,
        scratch_shapes=[
            pltpu.VMEM((n_seq, width, tok), bf16),
            pltpu.VMEM((n_seq, D, width), bf16),
            pltpu.VMEM((pairs, D, width), bf16),
            DMA((n_seq,)),
            DMA((n_seq,)),
            DMA((pairs,)),
            DMA((pairs,)),
            DMA((max(n_tile, 1),)),
            DMA((max(n_tile, 1),)),
        ],
        compiler_params=pltpu.CompilerParams(collective_id=3, has_side_effects=True),
        name="mid_back",
    )(piece, dots, cot, mid, gates, slot_of, routes, small, heads, w, prev, carry, *parts)
    return outs[:6], list(outs[6:])


def tail_kernel(
    n_seq, n_dp, parts, g_ref, wt_ref, wo_ref, pack_ref, gate_ref, slot_ref, gain_ref,
    a_hbm, h_hbm, resid_hbm, base_hbm, out_hbm, *refs,
):
    n_far = max(parts - LATE, 0)
    fin_hbm, refs = refs[:parts], refs[parts:]
    far_hbm, refs = refs[:n_far], refs[n_far:]
    din_ref, row_in, line_ref, block_ref, both_ref, refs = *refs[:5], refs[5:]
    (
        a_ref, h_ref, resid_ref, base_ref, rows_ref, far_ref, fin_ref,
        core_out, core_in, x_out, x_in, part_ref, w_out_buf, w_in, wo_buf, wo_in, wo_x, wo_far,
        w_mid, wo_mid,
        row_buf, pack_in, line_buf, line_in, load_sem, c_sems, x_sems, w_sems, v_sems, r_sems, o_sems,
        p_sems, q_sems, u_sems, l_sems, t_sems, f_sems, keep_sem,
    ) = refs
    me, dp = lax.axis_index("seq"), lax.axis_index("dp")
    tok = h_ref.shape[0]
    shard, width3 = w_in.shape[1], w_in.shape[2]
    width = width3 // 3
    owners = n_dp // E
    pairs = n_seq // 2
    others = range(1, n_dp)

    def both(sems):
        return sems.at[0], sems.at[1]

    c_sems, x_sems, w_sems, v_sems, r_sems, o_sems, p_sems, q_sems, u_sems, l_sems, t_sems, f_sems = (
        both(sems)
        for sems in (
            c_sems, x_sems, w_sems, v_sems, r_sems, o_sems, p_sems, q_sems, u_sems, l_sems, t_sems,
            f_sems,
        )
    )

    loads = []
    for src, dst in [
        (a_hbm, a_ref), (out_hbm, rows_ref), (base_hbm, base_ref), (h_hbm, h_ref),
        (resid_hbm, resid_ref),
    ] + [(fin_hbm[t], fin_ref.at[t]) for t in range(parts)] + [
        (far_hbm[t], far_ref.at[t]) for t in range(n_far)
    ]:
        load = pltpu.make_async_copy(src, dst, load_sem.at[len(loads)])
        load.start()
        loads.append(load)
    greet(
        [{"seq": me ^ place} for place in range(1, n_seq)]
        + [{"dp": lax.rem(dp + k, n_dp)} for k in others]
    )

    def there(k):
        return lax.rem(dp + k, n_dp)

    spots = [*range(n_dp // 2 - 1, -1, -1)]

    def to_neighbour(buf, near, sems):
        return {
            j: remote(buf.at[dp ^ (2 * j) ^ 1], near.at[j], sems, j, {"dp": dp ^ 1}) for j in spots
        }

    def pass_sums(copies, buf, near, mid, sems):
        passed = []
        for j in spots:
            copies[j].wait_recv()
            total = buf[dp ^ (2 * j)].astype(f32) + near[j].astype(f32)
            mid[j] = total.astype(bf16)
            if j:
                passed.append(
                    remote(mid.at[j], near.at[n_dp // 2 + j], sems, j, {"dp": dp ^ (2 * j)})
                )
        return passed

    def collect(passed, near, mid):
        for copy in passed:
            copy.wait_recv()
        return sum((near[n_dp // 2 + j].astype(f32) for j in spots[:-1]), mid[0].astype(f32))

    def term(place):
        columns = pl.ds(pl.multiple_of((me ^ place) * tok, tok), tok)
        return mm(g_ref[:, columns], wt_ref[...], TN)

    part_copies = [
        remote(fin_hbm[t], far_ref.at[t], t_sems, t - n_far, {"seq": me ^ 2})
        for t in range(n_far, parts)
    ]
    pack_copies = [
        remote(pack_ref.at[there(k)], pack_in.at[dp], p_sems, k, {"dp": there(k)}) for k in others
    ]
    pack_in[dp] = pack_ref[dp]
    for i in range(pairs):
        wo_buf[:, :, i * width : (i + 1) * width] = wo_ref[i].reshape(n_dp, shard, width)
    wo_near = to_neighbour(wo_buf, wo_in, q_sems)
    core_copies = []
    for i in range(pairs - 1, -1, -1):
        core_out[i] = term(2 * i + 1).astype(bf16)
        core_copies.insert(0, remote(core_out.at[i], core_in.at[i], c_sems, i, {"seq": me ^ 1}))
    x_copies = []
    for i in range(pairs - 1, 0, -1):
        part = term(2 * i)
        core_copies[i].wait_recv()
        x_out[i - 1] = (part + core_in[i].astype(f32)).astype(bf16)
        x_copies.append(
            remote(x_out.at[i - 1], x_in.at[i - 1], x_sems, i - 1, {"seq": me ^ (2 * i)})
        )
    loads[0].wait()
    turned = mm(g_ref[...], a_ref[...], NN)
    w_out_buf[...] = turned.T.astype(bf16).reshape(n_dp, shard, width3)
    w_near = to_neighbour(w_out_buf, w_in, w_sems)
    wo_copies = pass_sums(wo_near, wo_buf, wo_in, wo_mid, u_sems)
    w_copies = pass_sums(w_near, w_out_buf, w_in, w_mid, v_sems)
    part = term(0)
    core_copies[0].wait_recv()
    part_ref[...] = part + core_in[0].astype(f32)

    for copy in pack_copies:
        copy.wait_recv()
    line_buf[...] = jnp.sum(pack_in[...], axis=0)
    line_in[me] = line_buf[...]
    line_copies = [
        remote(line_buf, line_in.at[me], l_sems, place, {"seq": me ^ place})
        for place in range(1, n_seq)
    ]

    fin_copies, keeps = [], []

    def hand_over(ref, row, t):
        index = row * parts + t
        fin_copies.append(
            remote(ref.at[t], both_ref.at[2 * row + 1, t], f_sems, index, {"seq": me ^ 1})
        )
        keep = pltpu.make_async_copy(ref.at[t], both_ref.at[2 * row, t], keep_sem.at[index])
        keep.start()
        keeps.append(keep)

    for t in range(parts):
        loads[5 + t].wait()
        hand_over(fin_ref, 0, t)
    for t in range(n_far):
        loads[5 + parts + t].wait()
        hand_over(far_ref, 1, t)

    wo_total = collect(wo_copies, wo_in, wo_mid)
    wo_cross = []
    for i in range(1, pairs):
        wo_x[i - 1] = wo_total[:, i * width : (i + 1) * width].astype(bf16)
        wo_cross.append(
            remote(wo_x.at[i - 1], wo_far.at[i - 1], o_sems, i - 1, {"seq": me ^ (2 * i)})
        )

    loads[1].wait()
    loads[2].wait()
    picks = picks_of(slot_ref)
    rows = rows_ref[...].reshape(E, owners, CAP, D)
    columns = gate_ref[...].T
    block = base_ref[...]
    for k in range(2):
        picked = sum(
            mm(picks[k], rows[:, o].reshape(E * CAP, D), TN) for o in range(owners)
        )
        block = block + columns[:, k : k + 1] * picked
    block_ref[...] = block.astype(bf16)

    for copy in x_copies:
        copy.wait_recv()
    grad = part_ref[...]
    for i in range(pairs - 1):
        grad = grad + x_in[i].astype(f32)
    loads[3].wait()
    loads[4].wait()
    din_ref[...] = resid_ref[...] + norm_back(h_ref[...].astype(f32), gain_ref[0:1], grad)

    row_buf[:, :width3] = collect(w_copies, w_in, w_mid).astype(bf16)
    for copy in wo_cross:
        copy.wait_recv()
    wo_mine = wo_total[:, :width]
    for i in range(pairs - 1):
        wo_mine = wo_mine + wo_far[i].astype(f32)
    row_buf[:, width3:] = wo_mine.astype(bf16)
    row_in[me] = row_buf[...]
    row_copies = [
        remote(row_buf, row_in.at[me], r_sems, place, {"seq": me ^ place})
        for place in range(1, n_seq)
    ]
    for copy in line_copies:
        copy.wait_recv()
    line_ref[...] = jnp.sum(line_in[...], axis=0)
    for t, copy in enumerate(part_copies):
        copy.wait_recv()
        hand_over(far_ref, 1, n_far + t)
    for copy in row_copies + fin_copies:
        copy.wait_recv()
    for copy in (
        core_copies + [*w_near.values()] + [*wo_near.values()] + w_copies + x_copies + row_copies + wo_copies + pack_copies
        + line_copies + wo_cross + part_copies + fin_copies
    ):
        copy.wait_send()
    for keep in keeps:
        keep.wait()


def tail_call(
    n_seq, n_dp, grad_qkv, w_turned, wo_sum, pack, gates, slot_of, small,
    attn_in, hidden, grad_resid, base, back_out, fin, far,
):
    tok = hidden.shape[0]
    shard, width3 = D // n_dp, grad_qkv.shape[0]
    width = width3 // 3
    pairs = n_seq // 2
    parts, room = len(fin), max(len(fin), 1)
    part = (3, PART, D)
    return pl.pallas_call(
        functools.partial(tail_kernel, n_seq, n_dp, parts),
        out_shape=(
            jax.ShapeDtypeStruct((tok, D), f32),
            jax.ShapeDtypeStruct((n_seq, shard, width3 + width), bf16),
            jax.ShapeDtypeStruct((LINES, shard), f32),
            jax.ShapeDtypeStruct((tok, D), bf16),
            jax.ShapeDtypeStruct((n_seq, room, *part), bf16),
        ),
        in_specs=[VMEM] * 7 + [HBM] * (5 + parts + len(far)),
        out_specs=[VMEM] * 4 + [HBM],
        scratch_shapes=[
            pltpu.VMEM((n_seq * tok, D), bf16),
            pltpu.VMEM((tok, D), bf16),
            pltpu.VMEM((tok, D), f32),
            pltpu.VMEM((tok, D), f32),
            pltpu.VMEM((n_dp, CAP, D), bf16),
            pltpu.VMEM((room, *part), bf16),
            pltpu.VMEM((room, *part), bf16),
            pltpu.VMEM((pairs, tok, D), bf16),
            pltpu.VMEM((pairs, tok, D), bf16),
            pltpu.VMEM((pairs - 1, tok, D), bf16),
            pltpu.VMEM((pairs - 1, tok, D), bf16),
            pltpu.VMEM((tok, D), f32),
            pltpu.VMEM((n_dp, shard, width3), bf16),
            pltpu.VMEM((n_dp, shard, width3), bf16),
            pltpu.VMEM((n_dp, shard, pairs * width), bf16),
            pltpu.VMEM((n_dp, shard, pairs * width), bf16),
            pltpu.VMEM((pairs - 1, shard, width), bf16),
            pltpu.VMEM((pairs - 1, shard, width), bf16),
            pltpu.VMEM((n_dp // 2, shard, width3), bf16),
            pltpu.VMEM((n_dp // 2, shard, pairs * width), bf16),
            pltpu.VMEM((shard, width3 + width), bf16),
            pltpu.VMEM((n_dp, LINES, shard), f32),
            pltpu.VMEM((LINES, shard), f32),
            pltpu.VMEM((n_seq, LINES, shard), f32),
            DMA((5 + 2 * room,)),
            DMA((2, pairs)),
            DMA((2, pairs)),
            DMA((2, n_dp // 2)),
            DMA((2, n_dp // 2)),
            DMA((2, n_seq)),
            DMA((2, pairs)),
            DMA((2, n_dp)),
            DMA((2, n_dp // 2)),
            DMA((2, n_dp // 2)),
            DMA((2, n_seq)),
            DMA((2, LATE)),
            DMA((2, 2 * room)),
            DMA((2 * room,)),
        ],
        compiler_params=pltpu.CompilerParams(
            collective_id=1, has_side_effects=True, vmem_limit_bytes=67043328
        ),
        name="tail",
    )(
        grad_qkv, w_turned, wo_sum, pack, gates, slot_of, small,
        attn_in, hidden, grad_resid, base, back_out, *fin, *far,
    )


def finish_kernel(
    n_seq, me_ref, both_ref, row_ref, line_ref, wq_ref, gain_ref,
    de_ref, dw_ref, dwo_ref, again_ref, mgain_ref, router_ref, carry_ref, vec_ref, mix_ref,
):
    step = both_ref.shape[3]
    for t in range(both_ref.shape[1]):
        de_ref[:, t * step : (t + 1) * step] = both_ref[0, t].astype(f32)

    @pl.when(pl.program_id(0) == 0)
    def _():
        width = row_ref.shape[2] // 4
        for j in range(n_seq):
            block = row_ref[j].astype(f32)
            for c in range(3):
                left = c * width * n_seq + j * width
                dw_ref[:, left : left + width] = block[:, c * width : (c + 1) * width]
            dwo_ref[:, j * width : (j + 1) * width] = block[:, 3 * width :]
        sums = jnp.sum(dw_ref[...] * wq_ref[...].astype(f32), axis=1, keepdims=True)
        again_ref[...] = column_to_row(sums) / gain_ref[...].astype(f32)
        mix_ref[0] = line_ref[0:2]
        mix_ref[1] = line_ref[2:4]
        router_ref[...] = line_ref[4 : 4 + H]
        vec_ref[...] = line_ref[4 + H : 6 + H]
        mgain_ref[...] = line_ref[6 + H : 7 + H]
        carry_ref[...] = line_ref[24 : 24 + H, 0:H]


def finish_call(n_seq, me, both, row_in, lines, w_qkv, attn_gain):
    shard = w_qkv.shape[0]
    _, parts, three, step, _ = both.shape
    units = n_seq * parts * step
    group = 4 if parts % 4 == 0 else 1
    steps = parts // group

    def whole(shape):
        return pl.BlockSpec(shape, lambda i, me_ref: (0,) * len(shape))

    shapes = [(shard, 3 * D), (shard, D), (1, shard), (1, shard), (H, shard), (H, H), (2, shard),
              (2, 2, shard)]
    return pl.pallas_call(
        functools.partial(finish_kernel, n_seq),
        out_shape=[jax.ShapeDtypeStruct((three, units, D), f32)]
        + [jax.ShapeDtypeStruct(shape, f32) for shape in shapes],
        grid_spec=pltpu.PrefetchScalarGridSpec(
            num_scalar_prefetch=1,
            grid=(n_seq * steps,),
            in_specs=[
                pl.BlockSpec(
                    (1, group, three, step, D),
                    lambda i, me_ref: ((i // steps) ^ me_ref[0], i % steps, 0, 0, 0),
                ),
                whole(row_in.shape),
                whole(lines.shape),
                whole(w_qkv.shape),
                whole((1, shard)),
            ],
            out_specs=[pl.BlockSpec((three, group * step, D), lambda i, me_ref: (0, i, 0))]
            + [whole(shape) for shape in shapes],
        ),
        name="finish",
    )(me, both, row_in, lines, w_qkv, attn_gain[None])


def rope_tables(seq_len):
    rates = 10000.0 ** (np.arange(HD // 2) * (-2.0 / HD))

    def table(positions):
        angles = rates[:, None] * positions[None, :]
        return jnp.asarray(np.concatenate([np.cos(angles), np.sin(angles)]), f32)

    return table(np.arange(128.0)), table(np.arange(0.0, seq_len, 128.0))


def per_device(
    hidden_in,
    prev_logits,
    segments,
    routes,
    attn_gain,
    w_qkv,
    w_out,
    moe_gain,
    w_router,
    w_carry,
    const_vec,
    const_mix,
    experts,
    cotangent,
):
    n_seq, n_dp = lax.axis_size("seq"), lax.axis_size("dp")
    owners = n_dp // E
    me = lax.axis_index("seq")
    tok = hidden_in.shape[1]
    hidden, cot = hidden_in[0], cotangent[0]
    prev_t = jnp.transpose(prev_logits, (2, 0, 1))
    routes_t = routes[0].T

    def to_owners(values):
        return lax.all_to_all(
            jnp.repeat(values, owners, axis=0), "dp", split_axis=0, concat_axis=0, tiled=True
        )

    def to_sources(values):
        return lax.all_to_all(values, "dp", split_axis=0, concat_axis=0, tiled=True)

    attn_in, qkv, w_turned, small, slot_of, grad_slots, out_weight, cos_t, sin_t = start_call(
        n_seq, n_dp, hidden, w_qkv, attn_gain, moe_gain, const_vec, const_mix, w_router.T,
        routes_t, cot, w_out,
    )
    arrived_grad = to_owners(grad_slots)

    seg_row = segments[0]
    doc_ids = jnp.arange(16, dtype=jnp.int32)
    doc_start = jnp.sum((seg_row[None, :] < doc_ids[:, None]).astype(jnp.int32), axis=1)
    start = jnp.sum(jnp.where(seg_row[None, :] == doc_ids[:, None], doc_start[:, None], 0), axis=0)
    start_row = start.astype(jnp.int32)[None, :]
    lows = start[::BLK].astype(jnp.int32) // BLK
    attended, attended_exact, logs = attn_call(lows, qkv, start_row, tok)

    heads_t, resid_mid, gates, x_slots, gate_slots = mid_call(
        n_seq, attended, hidden, prev_t, w_carry, small, slot_of, routes_t, out_weight
    )
    if n_dp * CAP > 1024:
        piece, dots, partial, d_plain = experts_plain(
            to_owners, to_sources, n_dp, x_slots, gate_slots, experts, arrived_grad
        )
        fin, far = [], []
    else:
        piece, dots, partial, fin, far = moe_call(
            n_dp, x_slots, gate_slots, experts, arrived_grad
        )
    back_out = to_sources(partial)

    (grad_resid, grad_out, base, d_prev, pack, wo_sum), far_back = mid_back_call(
        n_seq, n_dp, piece, dots, cot, resid_mid, gates, slot_of, routes_t, small, heads_t,
        out_weight, prev_t, w_carry, fin[EARLY : EARLY + 1],
    )
    later, grad_out = lax.optimization_barrier((fin[EARLY + 1 : -LATE], grad_out))
    far = far + far_back + [swap(part, "seq", 2) for part in later]
    grad_qkv = attn_back_call(
        lows, qkv, grad_out, attended_exact, logs, start_row, cos_t, sin_t
    )
    d_input, row_in, lines, block_out, both = tail_call(
        n_seq, n_dp, grad_qkv, w_turned, wo_sum, pack, gates, slot_of, small,
        attn_in, hidden, grad_resid, base, back_out, fin, far,
    )
    d_experts, d_qkv, d_out, again, mgain, router, carry, vec, mix = finish_call(
        n_seq, me.astype(jnp.int32).reshape(1), both, row_in, lines, w_qkv, attn_gain
    )
    if not fin:
        d_experts = d_plain
    return (
        block_out[None],
        d_input[None],
        jnp.transpose(d_prev, (1, 2, 0)),
        again[0],
        d_qkv,
        d_out,
        mgain[0],
        router.T,
        carry,
        vec,
        mix,
        d_experts,
    )


def solution(mesh):
    return jax.shard_map(
        per_device,
        mesh=mesh,
        in_specs=(
            P("dp", "seq", None),
            P("dp", "seq", None),
            P("dp", None),
            P("dp", "seq", None),
            P("dp"),
            P("dp", None),
            P("dp", None),
            P("dp"),
            P("dp", None),
            P(),
            P(None, "dp"),
            P(None, None, "dp"),
            P(None, "dp", None),
            P("dp", "seq", None),
        ),
        out_specs=(
            P("dp", "seq", None),
            P("dp", "seq", None),
            P("dp", "seq", None),
            P("dp"),
            P("dp", None),
            P("dp", None),
            P("dp"),
            P("dp", None),
            P(),
            P(None, "dp"),
            P(None, None, "dp"),
            P(None, "dp", None),
        ),
        check_vma=False,
    )
```
